128 devices in a mesh: gx: 4 (over x), gy: 8 (over z, core), gz: 4 (over y).
Axes of the slice: x: 4, y: 4, z: 4, core: 2. Of those that a mesh axis runs over, the one named last changes fastest.
Arguments:
- source_field: float32 [128, 256, 512], P('gx', 'gy', 'gz'), may hold values from -20 to 20
- beta_field: float32 [128, 256, 512], P('gx', 'gy', 'gz'), may hold values from 0.5 to 4
Outputs:
- solution: float32 [128, 256, 512], P('gx', 'gy', 'gz')
The draws below stay inside these ranges and needn't reach their ends.
All inputs are finite; a program needn't handle non-finite values.
Results may differ from the reference program's by a relative error of at most 0.0001.
Values sent between devices are 32-bit elements; how exact they have to be, the bound alone decides.
No kernel may reach another device: no remote copies, remote signals or barrier semaphores. Data moves between devices by JAX's collectives and lax.ppermute only.
A program may use at most 128 MiB of HBM per device.

```python
import math
import jax
import jax.numpy as jnp

LEVELS = 4
SMOOTH = 4
BOTTOM = 12
NX = 128
NY = 256
NZ = 512


def draw_source_field(key, part):
    values = 4.0 * jax.random.normal(key, (NX, NY, NZ), jnp.float32)
    values = jnp.clip(values, -20.0, 20.0)
    return values


def block_scale(key, extent, pieces, smallest, top_value):
    def one(dim, shards_of):
        steps = jax.random.uniform(jax.random.fold_in(jax.random.fold_in(key, 6), dim), (shards_of,), jnp.float32, smallest / len(pieces), top_value / len(pieces))
        return jnp.repeat(jnp.exp(steps), extent[dim] // shards_of).reshape((-1,) + (1,) * (len(extent) - dim - 1))

    factor_of = one(*pieces[0])
    for cut in pieces[1:]:
        factor_of = factor_of * one(*cut)
    return factor_of


def setup_inputs(seed: int = 0) -> dict:
    seeds = jax.random.split(jax.random.key(seed), 3)
    return {
        "source_field": draw_source_field(jax.random.fold_in(seeds[2], 71), 0),
        "beta_field": jnp.clip(jnp.exp(math.log(4.0) - 2.0794415 * jax.random.uniform(seeds[1], (NX, NY, NZ), jnp.float32) ** block_scale(seeds[1], (NX, NY, NZ), ((0, 4), (1, 8), (2, 4)), -0.2, 0.2)), 0.5, 4.0),
    }


LOW_EIG = 0.3
HIGH_EIG = 2.0
BOTTOM_LOW = 0.02


def cheb_plan(degree, lowest, highest):
    centre = 0.5 * (highest + lowest)
    radius = 0.5 * (highest - lowest)
    ratio_s = centre / radius
    rho_old = 1.0 / ratio_s
    recipe = [(0.0, 1.0 / centre)]
    for position in range(1, degree):
        rho_new = 1.0 / (2.0 * ratio_s - rho_old)
        recipe.append((rho_new * rho_old, 2.0 * rho_new / radius))
        rho_old = rho_new
    return recipe


def face_terms(padded):
    face_x = 0.5 * (padded[1:, 1:-1, 1:-1] + padded[:-1, 1:-1, 1:-1])
    face_y = 0.5 * (padded[1:-1, 1:, 1:-1] + padded[1:-1, :-1, 1:-1])
    face_z = 0.5 * (padded[1:-1, 1:-1, 1:] + padded[1:-1, 1:-1, :-1])
    diagonal = face_x[:-1] + face_x[1:] + face_y[:, :-1] + face_y[:, 1:] + face_z[:, :, :-1] + face_z[:, :, 1:]
    return face_x, face_y, face_z, diagonal


def apply_operator(padded, values, operator_terms, spacing):
    face_x, face_y, face_z, diagonal = operator_terms
    beside = face_x[:-1] * padded[:-2, 1:-1, 1:-1] + face_x[1:] * padded[2:, 1:-1, 1:-1]
    beside = beside + face_y[:, :-1] * padded[1:-1, :-2, 1:-1] + face_y[:, 1:] * padded[1:-1, 2:, 1:-1]
    beside = beside + face_z[:, :, :-1] * padded[1:-1, 1:-1, :-2] + face_z[:, :, 1:] * padded[1:-1, 1:-1, 2:]
    return spacing * (diagonal * values - beside)


def run_steps(values, source, operator_terms, inverse, spacing, recipe, from_zero, padder):
    update = None
    for position, (retain, factor) in enumerate(recipe):
        if position == 0 and from_zero:
            remain = source
        else:
            remain = source - apply_operator(padder(values), values, operator_terms, spacing)
        if position == 0:
            update = factor * (inverse * remain)
        else:
            update = retain * update + factor * (inverse * remain)
        values = values + update
    return values


def local_pad(values):
    return jnp.pad(values, 1)


def restrict(values):
    first, second, third = values.shape
    return values.reshape(first // 2, 2, second // 2, 2, third // 2, 2).mean(axis=(1, 3, 5))


def prolong(values):
    first, second, third = values.shape
    spread_out = jnp.broadcast_to(values[:, None, :, None, :, None], (first, 2, second, 2, third, 2))
    return spread_out.reshape(2 * first, 2 * second, 2 * third)


def reference(source_field, beta_field):
    beta_levels = [beta_field]
    for level_idx in range(1, LEVELS):
        beta_levels.append(restrict(beta_levels[-1]))
    all_terms = [face_terms(jnp.pad(one_beta, 1)) for one_beta in beta_levels]
    inverses = [1.0 / ((0.25 ** level_idx) * all_terms[level_idx][3]) for level_idx in range(LEVELS)]
    recipe = cheb_plan(SMOOTH, LOW_EIG, HIGH_EIG)
    bottom_recipe = cheb_plan(BOTTOM, BOTTOM_LOW, HIGH_EIG)
    sources = [source_field]
    iterates = []
    for level_idx in range(LEVELS - 1):
        spacing = 0.25 ** level_idx
        values = run_steps(jnp.zeros_like(sources[level_idx]), sources[level_idx], all_terms[level_idx], inverses[level_idx], spacing, recipe, True, local_pad)
        remain = sources[level_idx] - apply_operator(jnp.pad(values, 1), values, all_terms[level_idx], spacing)
        iterates.append(values)
        sources.append(restrict(remain))
    last_level = LEVELS - 1
    coarse = run_steps(jnp.zeros_like(sources[last_level]), sources[last_level], all_terms[last_level], inverses[last_level], 0.25 ** last_level, bottom_recipe, True, local_pad)
    for level_idx in reversed(range(LEVELS - 1)):
        values = iterates[level_idx] + prolong(coarse)
        coarse = run_steps(values, sources[level_idx], all_terms[level_idx], inverses[level_idx], 0.25 ** level_idx, recipe, False, local_pad)
    return coarse
```

```python
import functools

import jax
import jax.numpy as jnp
from jax import lax
from jax.experimental import pallas as pl
from jax.experimental.pallas import tpu as pltpu
from jax.sharding import PartitionSpec as P

SMOOTH = 4
BOTTOM = 12
LOW_EIG = 0.3
HIGH_EIG = 2.0
BOTTOM_LOW = 0.02

AXES = ("gx", "gy", "gz")
F32 = jnp.float32
VMEM_LIMIT = 44 * 1024 * 1024


def cheb_plan(degree, lowest, highest):
    centre = 0.5 * (highest + lowest)
    radius = 0.5 * (highest - lowest)
    ratio_s = centre / radius
    rho_old = 1.0 / ratio_s
    recipe = [(0.0, 1.0 / centre)]
    for position in range(1, degree):
        rho_new = 1.0 / (2.0 * ratio_s - rho_old)
        recipe.append((rho_new * rho_old, 2.0 * rho_new / radius))
        rho_old = rho_new
    return recipe


RECIPE = cheb_plan(SMOOTH, LOW_EIG, HIGH_EIG)
BOTTOM_RECIPE = cheb_plan(BOTTOM, BOTTOM_LOW, HIGH_EIG)


def sds(*shape):
    return jax.ShapeDtypeStruct(shape, F32)


def vm(*shape):
    return pltpu.VMEM(shape, F32)


def call(body, outs, scratch=(), name=None):
    return pl.pallas_call(
        body,
        out_shape=outs,
        scratch_shapes=list(scratch),
        compiler_params=pltpu.CompilerParams(vmem_limit_bytes=VMEM_LIMIT),
        name=name,
    )


def lanes_of(rows):
    return lax.broadcasted_iota(jnp.int32, (rows, 128), 1)


def roll(value, shift):
    if isinstance(shift, int):
        shift = shift % 128
        if shift == 0:
            return value
    return pltpu.roll(value, shift, 1)


def flag(condition):
    return jnp.where(condition, 1.0, 0.0).astype(F32)


def dot(left, right):
    return lax.dot_general(
        left,
        right,
        (((1,), (0,)), ((), ())),
        precision=lax.Precision.HIGHEST,
        preferred_element_type=F32,
    )


def pick(match):
    row = lax.broadcasted_iota(jnp.int32, (128, 128), 0)
    col = lax.broadcasted_iota(jnp.int32, (128, 128), 1)
    return jnp.where(match(row, col), 1.0, 0.0).astype(F32)


def pack_x(src, beta, lo, hi):
    lo[0] = src[0:8]
    lo[1] = beta[0:8]
    hi[0] = src[24:32]
    hi[1] = beta[24:32]


def coarse_beta(beta, out, rows):
    total = []
    for x in range(8):
        s = beta[4 * x] + beta[4 * x + 1] + beta[4 * x + 2] + beta[4 * x + 3]
        rows[...] = s
        t = rows[pl.ds(0, 8, stride=4), :] + rows[pl.ds(1, 8, stride=4), :]
        t = t + rows[pl.ds(2, 8, stride=4), :] + rows[pl.ds(3, 8, stride=4), :]
        total.append(t * (1.0 / 64.0))
    for half in range(2):
        acc = jnp.zeros((8, 128), F32)
        for quarter in range(4):
            weight = pick(lambda r, c: (r // 4 + 32 * quarter) == c)
            acc = acc + dot(total[half * 4 + quarter], weight)
        out[half * 8 : half * 8 + 8, :] = acc


def pack_y(src, beta, from_lo, from_hi, lo, hi):
    index = lax.axis_index("gx")
    low = flag(index > 0)
    high = flag(index < lax.axis_size("gx") - 1)
    for field, ref in enumerate((src, beta)):
        for out, row in ((lo, 0), (hi, 24)):
            out[field, 0:8] = from_lo[field, :, row : row + 8, :] * low
            out[field, 8:40] = ref[:, row : row + 8, :]
            out[field, 40:48] = from_hi[field, :, row : row + 8, :] * high


def pack_z(src, beta, x_lo, x_hi, y_lo, y_hi, s_out, b_out, lo, hi):
    ix = lax.axis_index("gx")
    iy = lax.axis_index("gy")
    x_low = flag(ix > 0)
    x_high = flag(ix < lax.axis_size("gx") - 1)
    y_low = flag(iy > 0)
    y_high = flag(iy < lax.axis_size("gy") - 1)
    for field, (ref, out) in enumerate(((src, s_out), (beta, b_out))):
        out[0:8, 8:40, :] = x_lo[field] * x_low
        out[8:40, 8:40, :] = ref[...]
        out[40:48, 8:40, :] = x_hi[field] * x_high
        out[:, 0:8, :] = y_lo[field] * y_low
        out[:, 40:48, :] = y_hi[field] * y_high
    lane = lanes_of(48)

    def body(xx, carry):
        acc_lo = jnp.zeros((48, 128), F32)
        acc_hi = jnp.zeros((48, 128), F32)
        for g in range(8):
            s = s_out[g * 6 + xx]
            b = b_out[g * 6 + xx]
            first = (lane >= g * 16) & (lane < g * 16 + 8)
            second = (lane >= g * 16 + 8) & (lane < g * 16 + 16)
            acc_lo = jnp.where(first, roll(s, g * 16), acc_lo)
            acc_lo = jnp.where(second, roll(b, g * 16 + 8), acc_lo)
            acc_hi = jnp.where(first, roll(s, g * 16 + 8), acc_hi)
            acc_hi = jnp.where(second, roll(b, g * 16 + 16), acc_hi)
        lo[xx] = acc_lo
        hi[xx] = acc_hi
        return carry

    lax.fori_loop(0, 6, body, 0)


def strip_ghosts(values, ghost):
    lane = lanes_of(48)

    def body(xx, carry):
        acc = jnp.zeros((48, 128), F32)
        for g in range(8):
            acc = jnp.where(lane // 16 == g, roll(values[g * 6 + xx + 1, 8:56, :], g * 16 + 8), acc)
        ghost[xx] = acc
        return carry

    lax.fori_loop(0, 6, body, 0)


def strip_sides(strip, xx):
    after = strip[xx + 1, 8:56, :] if xx < 5 else roll(strip[0, 8:56, :], -16)
    before = strip[xx - 1, 8:56, :] if xx > 0 else roll(strip[5, 8:56, :], 16)
    return before, after


def strip_z(strip, ghost, xx, lane):
    here = strip[xx, 8:56, :]
    up = roll(jnp.where(lane % 16 == 8, ghost[xx], here), -1)
    down = roll(jnp.where(lane % 16 == 7, ghost[xx], here), 1)
    return down, up


def block_z(value, strip, x, lane):
    g = x // 6
    edge = roll(strip[x - g * 6, 8:56, :], 120 - g * 16)
    up = roll(jnp.where(lane == 0, edge, value), -1)
    down = roll(jnp.where(lane == 127, edge, value), 1)
    return down, up


def weights(here, sides):
    sums = [here + side for side in sides]
    total = sums[0] + sums[1] + sums[2] + sums[3] + sums[4] + sums[5]
    inverse = jnp.where(here > 0.0, 1.0 / total, 0.0)
    return [s * inverse for s in sums], inverse, total


def level0_setup(b_pad, bt_pad, ghost, src, src_t, g_main, g_strip, sp, sp_t, total):
    strip_ghosts(b_pad, ghost)
    lane = lanes_of(48)

    def body(x, carry):
        here = b_pad[x + 1, 8:56, :]
        down, up = block_z(here, bt_pad, x, lane)
        faces, inverse, tot = weights(
            here,
            (
                b_pad[x, 8:56, :],
                b_pad[x + 2, 8:56, :],
                b_pad[x + 1, 7:55, :],
                b_pad[x + 1, 9:57, :],
                down,
                up,
            ),
        )
        for i in range(6):
            g_main[i, x] = faces[i]
        sp[x] = src[x] * (2.0 * inverse)
        if total is not None:
            total[x] = tot
        return carry

    lax.fori_loop(0, 48, body, 0)
    for xx in range(6):
        before, after = strip_sides(bt_pad, xx)
        down, up = strip_z(bt_pad, ghost, xx, lane)
        faces, inverse, _ = weights(
            bt_pad[xx, 8:56, :],
            (before, after, bt_pad[xx, 7:55, :], bt_pad[xx, 9:57, :], down, up),
        )
        for i in range(6):
            g_strip[i, xx] = faces[i]
        sp_t[xx] = src_t[xx] * (2.0 * inverse)


def block_rest(v, t, g_main, sp, x, lane):
    here = v[x + 1, 8:56, :]
    down, up = block_z(here, t, x, lane)
    rest = sp[x] - here
    rest = rest + g_main[0, x] * v[x, 8:56, :] + g_main[1, x] * v[x + 2, 8:56, :]
    rest = rest + g_main[2, x] * v[x + 1, 7:55, :] + g_main[3, x] * v[x + 1, 9:57, :]
    rest = rest + g_main[4, x] * down + g_main[5, x] * up
    return here, rest


def level0_step(v, t, v_out, t_out, ghost, g_main, g_strip, sp, sp_t, u, u_t, low, high, retain, factor):
    strip_ghosts(v, ghost)
    lane = lanes_of(48)

    def body(x, carry):
        here, rest = block_rest(v, t, g_main, sp, x, lane)
        new = factor * rest
        if retain is not None:
            new = retain * u[x] + new
        u[x] = new
        v_out[x + 1, 8:56, :] = here + new
        return carry

    lax.fori_loop(low, high, body, 0)
    for xx in range(6):
        here = t[xx, 8:56, :]
        before, after = strip_sides(t, xx)
        down, up = strip_z(t, ghost, xx, lane)
        rest = sp_t[xx] - here
        rest = rest + g_strip[0, xx] * before + g_strip[1, xx] * after
        rest = rest + g_strip[2, xx] * t[xx, 7:55, :] + g_strip[3, xx] * t[xx, 9:57, :]
        rest = rest + g_strip[4, xx] * down + g_strip[5, xx] * up
        new = factor * rest
        if retain is not None:
            new = retain * u_t[xx] + new
        u_t[xx] = new
        t_out[xx, 8:56, :] = here + new


def clear_edges(ref, planes, rows):
    width = ref.shape[1]
    ref[0] = jnp.zeros((width, 128), F32)
    ref[planes + 1] = jnp.zeros((width, 128), F32)

    def body(x, carry):
        ref[x, 0:8, :] = jnp.zeros((8, 128), F32)
        ref[x, 8 + rows : width, :] = jnp.zeros((width - 8 - rows, 128), F32)
        return carry

    lax.fori_loop(0, planes + 2, body, 0)


def clear_strip(ref):
    for xx in range(6):
        ref[xx, 0:8, :] = jnp.zeros((8, 128), F32)
        ref[xx, 56:64, :] = jnp.zeros((8, 128), F32)


def unpack_strip(z_lo, z_hi, src_t, bt_pad):
    iz = lax.axis_index("gz")
    low = flag(iz > 0)
    high = flag(iz < lax.axis_size("gz") - 1)
    lower = lanes_of(48) % 16 < 8
    for xx in range(6):
        before = z_lo[xx] * low
        after = z_hi[xx] * high
        src_t[xx] = jnp.where(lower, before, roll(after, 8))
        bt_pad[xx, 8:56, :] = jnp.where(lower, roll(before, -8), after)


LEVEL0_SCRATCH = [
    vm(50, 64, 128),
    vm(6, 64, 128),
    vm(50, 64, 128),
    vm(50, 64, 128),
    vm(6, 64, 128),
    vm(6, 64, 128),
    vm(6, 48, 128),
    vm(6, 48, 48, 128),
    vm(6, 6, 48, 128),
    vm(48, 48, 128),
    vm(6, 48, 128),
    vm(48, 48, 128),
    vm(6, 48, 128),
    vm(6, 48, 128),
]


def level0_down(
    src, beta, z_lo, z_hi, iter_out, iter_t_out, c_out, c_lo, c_hi,
    b_pad, bt_pad, va, vb, ta, tb, ghost, g_main, g_strip, sp, sp_t, u, u_t, src_t, total, rows,
):
    for ref in (b_pad, va, vb):
        clear_edges(ref, 48, 48)
    for ref in (bt_pad, ta, tb):
        clear_strip(ref)
    b_pad[1:49, 8:56, :] = beta[...]
    unpack_strip(z_lo, z_hi, src_t, bt_pad)
    level0_setup(b_pad, bt_pad, ghost, src, src_t, g_main, g_strip, sp, sp_t, total)

    first = RECIPE[0][1]

    def start(x, carry):
        u[x] = first * sp[x]
        va[x + 1, 8:56, :] = u[x]
        return carry

    lax.fori_loop(0, 48, start, 0)
    for xx in range(6):
        u_t[xx] = first * sp_t[xx]
        ta[xx, 8:56, :] = u_t[xx]
    bufs = [(va, ta), (vb, tb)]
    for k in range(1, SMOOTH):
        (v, t), (w, s) = bufs
        retain, factor = RECIPE[k]
        level0_step(v, t, w, s, ghost, g_main, g_strip, sp, sp_t, u, u_t, k, 48 - k, retain, factor)
        for x in [*range(k), *range(48 - k, 48)]:
            w[x + 1, 8:56, :] = v[x + 1, 8:56, :]
        bufs = [(w, s), (v, t)]
    v, t = bufs[0]
    iter_out[...] = v[1:49, 8:56, :]
    for xx in range(6):
        iter_t_out[xx] = t[xx, 8:56, :]

    lane = lanes_of(48)
    to_low = pick(lambda r, c: r // 2 == c)
    to_high = pick(lambda r, c: r // 2 + 64 == c)

    def restrict(x2, carry):
        parts = []
        for half in range(2):
            x = 8 + 2 * x2 + half
            _, rest = block_rest(v, t, g_main, sp, x, lane)
            parts.append(rest * total[x])
        rows[0] = (parts[0] + parts[1]) * (0.5 / 8.0)
        rows[1] = (b_pad[9 + 2 * x2, 8:56, :] + b_pad[10 + 2 * x2, 8:56, :]) * (1.0 / 8.0)
        res = rows[0, pl.ds(8, 16, stride=2), :] + rows[0, pl.ds(9, 16, stride=2), :]
        bet = rows[1, pl.ds(8, 16, stride=2), :] + rows[1, pl.ds(9, 16, stride=2), :]
        c_out[x2] = dot(res, to_low) + dot(bet, to_high)
        return carry

    lax.fori_loop(0, 16, restrict, 0)
    c_lo[...] = c_out[0:10]
    c_hi[...] = c_out[6:16]


def pack1_y(c, from_lo, from_hi, lo, hi):
    index = lax.axis_index("gx")
    low = flag(index > 0)
    high = flag(index < lax.axis_size("gx") - 1)
    for x in range(36):
        if x < 10:
            plane = from_lo[x] * low
        elif x < 26:
            plane = c[x - 10]
        else:
            plane = from_hi[x - 26] * high
        lo[x * 10 : x * 10 + 10, :] = plane[0:10]
        hi[x * 10 : x * 10 + 10, :] = plane[6:16]


def pack1_z(c, x_lo, x_hi, y_lo, y_hi, ext, lo, hi):
    ix = lax.axis_index("gx")
    iy = lax.axis_index("gy")
    x_low = flag(ix > 0)
    x_high = flag(ix < lax.axis_size("gx") - 1)
    y_low = flag(iy > 0)
    y_high = flag(iy < lax.axis_size("gy") - 1)
    ext[0:10, 10:26, :] = x_lo[...] * x_low
    ext[10:26, 10:26, :] = c[...]
    ext[26:36, 10:26, :] = x_hi[...] * x_high
    for x in range(36):
        ext[x, 0:10, :] = y_lo[x * 10 : x * 10 + 10, :] * y_low
        ext[x, 26:36, :] = y_hi[x * 10 : x * 10 + 10, :] * y_high
        ext[x, 36:40, :] = jnp.zeros((4, 128), F32)
    lane = lanes_of(40)

    def body(xx, carry):
        acc_lo = jnp.zeros((40, 128), F32)
        acc_hi = jnp.zeros((40, 128), F32)
        for g in range(6):
            e = ext[g * 6 + xx]
            first = (lane >= g * 20) & (lane < g * 20 + 10)
            second = (lane >= g * 20 + 10) & (lane < g * 20 + 20)
            middle = roll(e, g * 20 - 54)
            acc_lo = jnp.where(first, roll(e, g * 20), acc_lo)
            acc_lo = jnp.where(second, middle, acc_lo)
            acc_hi = jnp.where(first, middle, acc_hi)
            acc_hi = jnp.where(second, roll(e, g * 20 + 20), acc_hi)
        lo[xx] = acc_lo
        hi[xx] = acc_hi
        return carry

    lax.fori_loop(0, 6, body, 0)


def ring_weights(b_pad, src, g, sp, total, planes, rows, scale, edges=None):
    lane = lanes_of(rows)

    def body(x, carry):
        here = b_pad[x + 1, 8 : 8 + rows, :]
        down = roll(here, 1)
        up = roll(here, -1)
        if edges is not None:
            down = jnp.where(lane == 0, 0.0, down)
            up = jnp.where(lane == 127, 0.0, up)
        faces, inverse, tot = weights(
            here,
            (
                b_pad[x, 8 : 8 + rows, :],
                b_pad[x + 2, 8 : 8 + rows, :],
                b_pad[x + 1, 7 : 7 + rows, :],
                b_pad[x + 1, 9 : 9 + rows, :],
                down,
                up,
            ),
        )
        if edges is not None:
            faces[4] = jnp.where(lane == 0, 0.0, faces[4])
            faces[5] = jnp.where(lane == 127, 0.0, faces[5])
        for i in range(6):
            g[i, x] = faces[i]
        sp[x] = src[x] * (scale * 2.0 * inverse)
        if total is not None:
            total[x] = tot
        return carry

    lax.fori_loop(0, planes, body, 0)


def ring_rest(v, g, sp, x, rows):
    here = v[x + 1, 8 : 8 + rows, :]
    rest = sp[x] - here
    rest = rest + g[0, x] * v[x, 8 : 8 + rows, :] + g[1, x] * v[x + 2, 8 : 8 + rows, :]
    rest = rest + g[2, x] * v[x + 1, 7 : 7 + rows, :] + g[3, x] * v[x + 1, 9 : 9 + rows, :]
    rest = rest + g[4, x] * roll(here, 1) + g[5, x] * roll(here, -1)
    return here, rest


def ring_step(v, v_out, g, sp, u, planes, rows, retain, factor):
    def body(x, carry):
        here, rest = ring_rest(v, g, sp, x, rows)
        new = factor * rest
        if retain is not None:
            new = retain * u[x] + new
        u[x] = new
        v_out[x + 1, 8 : 8 + rows, :] = here + new
        return carry

    lax.fori_loop(0, planes, body, 0)


def ring_zero_start(v, u, sp, planes, rows, factor):
    def body(x, carry):
        u[x] = factor * sp[x]
        v[x + 1, 8 : 8 + rows, :] = u[x]
        return carry

    lax.fori_loop(0, planes, body, 0)


def ring_cheb(va, vb, g, sp, u, planes, rows, recipe, from_zero):
    begin = 0
    if from_zero:
        ring_zero_start(va, u, sp, planes, rows, recipe[0][1])
        begin = 1
    for k in range(begin, len(recipe)):
        retain, factor = recipe[k]
        ring_step(va, vb, g, sp, u, planes, rows, None if k == 0 else retain, factor)
        va, vb = vb, va
    return va


LEVEL1_SCRATCH = [
    vm(38, 56, 128),
    vm(38, 56, 128),
    vm(38, 56, 128),
    vm(6, 36, 40, 128),
    vm(36, 40, 128),
    vm(36, 40, 128),
]


def level1_down(
    ext, z_lo, z_hi, src_out, beta_out, iter_out, chunk,
    b_pad, va, vb, g, sp, u, total, rows,
):
    iz = lax.axis_index("gz")
    low = flag(iz > 0)
    high = flag(iz < lax.axis_size("gz") - 1)
    lane = lanes_of(40)
    inner = lane < 64
    above = (lane >= 64) & (lane < 74)
    below = lane >= 118
    for ref in (b_pad, va, vb):
        clear_edges(ref, 36, 40)

    def unpack(xx, carry):
        before = z_lo[xx] * low
        after = z_hi[xx] * high
        for k in range(6):
            x = k * 6 + xx
            e = ext[x]
            s = jnp.where(inner, e, 0.0)
            s = jnp.where(above, roll(after, 64 - k * 20), s)
            s = jnp.where(below, roll(before, 118 - k * 20), s)
            b = jnp.where(inner, roll(e, 64), 0.0)
            b = jnp.where(above, roll(after, 54 - k * 20), b)
            b = jnp.where(below, roll(before, 108 - k * 20), b)
            src_out[x] = s
            beta_out[x] = b
            b_pad[x + 1, 8:48, :] = b
        return carry

    lax.fori_loop(0, 6, unpack, 0)
    ring_weights(b_pad, src_out, g, sp, total, 36, 40, 4.0)
    v = ring_cheb(va, vb, g, sp, u, 36, 40, RECIPE, True)
    iter_out[...] = v[1:37, 8:48, :]
    summed = []
    for x2 in range(8):
        parts = []
        for half in range(2):
            x = 10 + 2 * x2 + half
            _, rest = ring_rest(v, g, sp, x, 40)
            parts.append(rest * total[x])
        rows[...] = (parts[0] + parts[1]) * (0.25 * 0.5 / 8.0)
        summed.append(rows[pl.ds(10, 8, stride=2), :] + rows[pl.ds(11, 8, stride=2), :])
    packed = []
    for half in range(2):
        acc = jnp.zeros((8, 128), F32)
        for quarter in range(4):
            weight = pick(lambda r, c: (r < 64) & ((r // 2 + 32 * quarter) == c))
            acc = acc + dot(summed[half * 4 + quarter], weight)
        packed.append(acc)
    both = jnp.concatenate(packed, axis=0)

    def spread(d, carry):
        chunk[d] = both
        return carry

    lax.fori_loop(0, 128, spread, 0)


def whole_grid(parts, out, x_pad):
    lane = lanes_of(8)

    def body(i, carry):
        gx = i // 8
        gy = i - gx * 8
        for half in range(2):
            blocks = [parts[i * 4 + gz, half * 8 : half * 8 + 8, :] for gz in range(4)]
            for quarter in range(4):
                acc = roll(blocks[0], -quarter * 32)
                for gz in range(1, 4):
                    acc = jnp.where(lane // 32 == gz, roll(blocks[gz], (gz - quarter) * 32), acc)
                row = pl.multiple_of(8 + gy * 8, 8)
                out[gx * 8 + half * 4 + quarter + x_pad, pl.ds(row, 8), :] = acc
        return carry

    lax.fori_loop(0, 32, body, 0)


def bottom(
    s_parts, b_parts, out,
    s2, b2, va, vb, g, sp, u, total,
    b3, v3a, v3b, g3, sp3, u3, s3, rows, bw, wa, wb, gw, spw, uw, sw,
):
    def zero2(x, carry):
        for ref in (s2, b2, va, vb):
            ref[x] = jnp.zeros((80, 128), F32)
        return carry

    for ref in (s2, b2, va, vb):

        def clear(x, carry, ref=ref):
            ref[x, 0:8, :] = jnp.zeros((8, 128), F32)
            ref[x, 72:80, :] = jnp.zeros((8, 128), F32)
            return carry

        lax.fori_loop(0, 48, clear, 0)
        for x in [*range(8), *range(40, 48)]:
            ref[x, 8:72, :] = jnp.zeros((64, 128), F32)
    whole_grid(s_parts, s2, 8)
    whole_grid(b_parts, b2, 8)
    inner_b = b2.at[7:41]
    inner_s = s2.at[8:40, 8:72]
    ring_weights(inner_b, inner_s, g, sp, total, 32, 64, 16.0, edges=True)
    v = ring_cheb(va.at[7:41], vb.at[7:41], g, sp, u, 32, 64, RECIPE, True)
    iterate = vb if SMOOTH % 2 == 0 else va

    clear_edges(b3, 16, 32)
    clear_edges(v3a, 16, 32)
    clear_edges(v3b, 16, 32)
    half_z = pick(lambda r, c: r // 2 == c)

    def restrict(x2, carry):
        parts = []
        for half in range(2):
            x = 2 * x2 + half
            _, rest = ring_rest(v, g, sp, x, 64)
            parts.append(rest * total[x])
        rows[0] = (parts[0] + parts[1]) * (0.0625 * 0.5 / 8.0)
        rows[1] = (b2[8 + 2 * x2, 8:72, :] + b2[9 + 2 * x2, 8:72, :]) * (1.0 / 8.0)
        res = rows[0, pl.ds(0, 32, stride=2), :] + rows[0, pl.ds(1, 32, stride=2), :]
        bet = rows[1, pl.ds(0, 32, stride=2), :] + rows[1, pl.ds(1, 32, stride=2), :]
        s3[x2] = dot(res, half_z)
        b3[x2 + 1, 8:40, :] = dot(bet, half_z)
        return carry

    lax.fori_loop(0, 16, restrict, 0)
    ring_weights(b3, s3, g3, sp3, None, 16, 32, 64.0)
    c3 = ring_cheb(v3a, v3b, g3, sp3, u3, 16, 32, BOTTOM_RECIPE, True)

    other = va if iterate is vb else vb
    double_z = pick(lambda r, c: c // 2 == r)

    def prolong(x3, carry):
        wide = dot(c3[x3 + 1, 8:40, :], double_z)
        rows[0, pl.ds(0, 32, stride=2), :] = wide
        rows[0, pl.ds(1, 32, stride=2), :] = wide
        for half in range(2):
            x = 8 + 2 * x3 + half
            other[x, 8:72, :] = iterate[x, 8:72, :] + rows[0]
        return carry

    lax.fori_loop(0, 16, prolong, 0)
    ix = lax.axis_index("gx")
    iy = lax.axis_index("gy")
    iz = lax.axis_index("gz")
    clear_edges(bw, 22, 24)
    clear_edges(wa, 22, 24)
    clear_edges(wb, 22, 24)
    row = pl.multiple_of(iy * 8, 8)

    def window(x, carry):
        plane = ix * 8 + 1 + x
        bw[x + 1, 8:32, :] = b2[plane, pl.ds(row, 24), :]
        wa[x + 1, 8:32, :] = other[plane, pl.ds(row, 24), :]
        sw[x] = s2[plane, pl.ds(row, 24), :]
        return carry

    lax.fori_loop(0, 22, window, 0)
    ring_weights(bw, sw, gw, spw, None, 22, 24, 16.0, edges=True)
    c2 = ring_cheb(wa, wb, gw, spw, uw, 22, 24, RECIPE, False)
    shift = (128 - iz * 32) % 128
    for x in range(18):
        out[x] = roll(c2[x + 3, 8:32, :], shift)


BOTTOM_SCRATCH = [
    vm(48, 80, 128),
    vm(48, 80, 128),
    vm(48, 80, 128),
    vm(48, 80, 128),
    vm(6, 32, 64, 128),
    vm(32, 64, 128),
    vm(32, 64, 128),
    vm(32, 64, 128),
    vm(18, 48, 128),
    vm(18, 48, 128),
    vm(18, 48, 128),
    vm(6, 16, 32, 128),
    vm(16, 32, 128),
    vm(16, 32, 128),
    vm(16, 32, 128),
    vm(2, 64, 128),
    vm(24, 40, 128),
    vm(24, 40, 128),
    vm(24, 40, 128),
    vm(6, 22, 24, 128),
    vm(22, 24, 128),
    vm(22, 24, 128),
    vm(22, 24, 128),
]


def level1_up(c2, src, beta, iterate, out, b_pad, va, vb, g, sp, u, wide, rows):
    for ref in (b_pad, va, vb):
        clear_edges(ref, 36, 40)
    b_pad[1:37, 8:48, :] = beta[...]
    ring_weights(b_pad, src, g, sp, None, 36, 40, 4.0)
    spread = pick(lambda r, c: ((c < 74) & (c // 2 == r)) | ((c >= 118) & (c // 2 + 64 == r)))
    rows[...] = jnp.zeros((40, 128), F32)

    def prolong(x2, carry):
        wide[...] = dot(c2[x2], spread)
        part = wide[3:21, :]
        rows[pl.ds(0, 18, stride=2), :] = part
        rows[pl.ds(1, 18, stride=2), :] = part
        for half in range(2):
            x = 2 * x2 + half
            va[x + 1, 8:48, :] = jnp.where(beta[x] > 0.0, iterate[x] + rows[...], 0.0)
        return carry

    lax.fori_loop(0, 18, prolong, 0)
    v = ring_cheb(va, vb, g, sp, u, 36, 40, RECIPE, False)
    out[...] = v[7:31, 14:38, :]


def level0_up(
    c1, src, beta, z_lo, z_hi, iterate, iterate_t, out,
    b_pad, bt_pad, va, vb, ta, tb, ghost, g_main, g_strip, sp, sp_t, u, u_t, src_t, rows,
):
    for ref in (b_pad, va, vb):
        clear_edges(ref, 48, 48)
    for ref in (bt_pad, ta, tb):
        clear_strip(ref)
    b_pad[1:49, 8:56, :] = beta[...]
    unpack_strip(z_lo, z_hi, src_t, bt_pad)
    level0_setup(b_pad, bt_pad, ghost, src, src_t, g_main, g_strip, sp, sp_t, None)
    spread = pick(lambda r, c: c // 2 == r)

    def prolong(x1, carry):
        wide = dot(c1[x1], spread)
        rows[pl.ds(0, 24, stride=2), :] = wide
        rows[pl.ds(1, 24, stride=2), :] = wide
        for half in range(2):
            x = 2 * x1 + half
            va[x + 1, 8:56, :] = jnp.where(beta[x] > 0.0, iterate[x] + rows[...], 0.0)
        return carry

    lax.fori_loop(0, 24, prolong, 0)

    def prolong_strip(m, carry):
        acc = jnp.zeros((24, 128), F32)
        for k in range(8):
            to = pick(
                lambda r, c: (c // 16 == k)
                & (((c % 16 < 8) & (r == 124 + (c % 16) // 2)) | ((c % 16 >= 8) & (r == 64 + (c % 16 - 8) // 2)))
            )
            acc = acc + dot(c1[k * 3 + m], to)
        rows[pl.ds(0, 24, stride=2), :] = acc
        rows[pl.ds(1, 24, stride=2), :] = acc
        for half in range(2):
            xx = 2 * m + half
            ta[xx, 8:56, :] = jnp.where(bt_pad[xx, 8:56, :] > 0.0, iterate_t[xx] + rows[...], 0.0)
        return carry

    lax.fori_loop(0, 3, prolong_strip, 0)
    bufs = [(va, ta), (vb, tb)]
    for k in range(SMOOTH):
        (v, t), (w, s) = bufs
        retain, factor = RECIPE[k]
        if k == 0:
            retain = None
        if k < SMOOTH - 1:
            low, high = 4 + k, 44 - k
            level0_step(
                v, t, w, s, ghost, g_main, g_strip, sp, sp_t, u, u_t, low, high, retain, factor
            )
            for x in [*range(low), *range(high, 48)]:
                w[x + 1, 8:56, :] = v[x + 1, 8:56, :]
        else:
            lane = lanes_of(48)

            def last(x, carry):
                here, rest = block_rest(v, t, g_main, sp, x, lane)
                new = here + retain * u[x] + factor * rest
                rows[...] = new
                out[x - 8] = rows[8:40, :]
                return carry

            lax.fori_loop(8, 40, last, 0)
        bufs = [(w, s), (v, t)]


def ring(value, axis, step):
    count = lax.axis_size(axis)
    return lax.ppermute(value, axis, [(i, (i + step) % count) for i in range(count)])


def trade(lo, hi, axis):
    return ring(hi, axis, 1), ring(lo, axis, -1)


def per_device(source, beta):
    lo, hi = call(pack_x, (sds(2, 8, 32, 128), sds(2, 8, 32, 128)), name="pack_x")(source, beta)
    x_lo, x_hi = trade(lo, hi, "gx")
    beta2 = call(coarse_beta, sds(16, 128), [vm(32, 128)], name="coarse_beta")(beta)
    beta2_all = lax.all_gather(beta2, AXES)
    lo, hi = call(pack_y, (sds(2, 48, 8, 128), sds(2, 48, 8, 128)), name="pack_y")(
        source, beta, x_lo, x_hi
    )
    y_lo, y_hi = trade(lo, hi, "gy")
    src_ext, beta_ext, lo, hi = call(
        pack_z, (sds(48, 48, 128), sds(48, 48, 128), sds(6, 48, 128), sds(6, 48, 128)), name="pack_z"
    )(source, beta, x_lo, x_hi, y_lo, y_hi)
    z_lo, z_hi = trade(lo, hi, "gz")
    iter0, iter0_t, c, lo, hi = call(
        level0_down,
        (sds(48, 48, 128), sds(6, 48, 128), sds(16, 16, 128), sds(10, 16, 128), sds(10, 16, 128)),
        LEVEL0_SCRATCH + [vm(48, 48, 128), vm(2, 48, 128)],
        name="level0_down",
    )(src_ext, beta_ext, z_lo, z_hi)
    x_lo, x_hi = trade(lo, hi, "gx")
    lo, hi = call(pack1_y, (sds(360, 128), sds(360, 128)), name="pack1_y")(c, x_lo, x_hi)
    y_lo, y_hi = trade(lo, hi, "gy")
    ext, lo, hi = call(
        pack1_z, (sds(36, 40, 128), sds(6, 40, 128), sds(6, 40, 128)), name="pack1_z"
    )(c, x_lo, x_hi, y_lo, y_hi)
    z1_lo, z1_hi = trade(lo, hi, "gz")
    src1, beta1, iter1, chunk = call(
        level1_down,
        (sds(36, 40, 128), sds(36, 40, 128), sds(36, 40, 128), sds(128, 16, 128)),
        LEVEL1_SCRATCH + [vm(36, 40, 128), vm(40, 128)],
        name="level1_down",
    )(ext, z1_lo, z1_hi)
    source2_all = lax.all_to_all(chunk, AXES, 0, 0)
    c2 = call(bottom, sds(18, 24, 128), BOTTOM_SCRATCH, name="bottom")(source2_all, beta2_all)
    c1 = call(
        level1_up, sds(24, 24, 128), LEVEL1_SCRATCH + [vm(24, 128), vm(40, 128)], name="level1_up"
    )(c2, src1, beta1, iter1)
    return call(level0_up, sds(32, 32, 128), LEVEL0_SCRATCH + [vm(48, 128)], name="level0_up")(
        c1, src_ext, beta_ext, z_lo, z_hi, iter0, iter0_t
    )


def solution(mesh):
    placed = (P(*AXES), P(*AXES))
    return jax.shard_map(
        per_device, mesh=mesh, in_specs=placed, out_specs=P(*AXES), check_vma=False
    )
```

```python
import jax
import jax.numpy as jnp
from jax import lax
from jax.experimental import pallas as pl
from jax.experimental.pallas import tpu as pltpu
from jax.sharding import PartitionSpec as P

SMOOTH = 4
BOTTOM = 12
LOW_EIG = 0.3
HIGH_EIG = 2.0
BOTTOM_LOW = 0.02

AXES = ("gx", "gy", "gz")
F32 = jnp.float32
MIB = 1024 * 1024


def cheb_plan(degree, lowest, highest):
    centre = 0.5 * (highest + lowest)
    radius = 0.5 * (highest - lowest)
    ratio_s = centre / radius
    rho_old = 1.0 / ratio_s
    recipe = [(0.0, 1.0 / centre)]
    for position in range(1, degree):
        rho_new = 1.0 / (2.0 * ratio_s - rho_old)
        recipe.append((rho_new * rho_old, 2.0 * rho_new / radius))
        rho_old = rho_new
    return recipe


RECIPE = cheb_plan(SMOOTH, LOW_EIG, HIGH_EIG)
BOTTOM_RECIPE = cheb_plan(BOTTOM, BOTTOM_LOW, HIGH_EIG)


def sds(*shape):
    return jax.ShapeDtypeStruct(shape, F32)


def vm(*shape):
    return pltpu.VMEM(shape, F32)


def call(body, outs, scratch=(), name=None, mib=8):
    return pl.pallas_call(
        body,
        out_shape=outs,
        scratch_shapes=list(scratch),
        compiler_params=pltpu.CompilerParams(vmem_limit_bytes=mib * MIB),
        name=name,
    )


def loop(low, high, vectors, body):
    count = high - low
    most = max(1, min(count, 72 // vectors))
    width = max([w for w in range(1, most + 1) if count % w == 0])
    if width * 2 < most:
        width = most
    rounds = count // width

    def chunk(i, carry):
        for k in range(width):
            body(low + i * width + k)
        return carry

    if rounds > 1:
        lax.fori_loop(0, rounds, chunk, 0)
    else:
        chunk(0, 0)
    for x in range(low + rounds * width, high):
        body(x)


def lanes_of(rows):
    return lax.broadcasted_iota(jnp.int32, (rows, 128), 1)


def roll(value, shift):
    if isinstance(shift, int):
        shift = shift % 128
        if shift == 0:
            return value
    return pltpu.roll(value, shift, 1)


def flag(condition):
    return jnp.where(condition, 1.0, 0.0).astype(F32)


def dot(left, right):
    return lax.dot_general(
        left,
        right,
        (((1,), (0,)), ((), ())),
        precision=lax.Precision.HIGHEST,
        preferred_element_type=F32,
    )


def pick(match):
    row = lax.broadcasted_iota(jnp.int32, (128, 128), 0)
    col = lax.broadcasted_iota(jnp.int32, (128, 128), 1)
    return jnp.where(match(row, col), 1.0, 0.0).astype(F32)


def pack_x(src, beta, lo, hi):
    lo[0] = src[0:8]
    lo[1] = beta[0:8]
    hi[0] = src[24:32]
    hi[1] = beta[24:32]


def coarse_beta(beta, out, rows):
    total = []
    for x in range(8):
        s = beta[4 * x] + beta[4 * x + 1] + beta[4 * x + 2] + beta[4 * x + 3]
        rows[...] = s
        t = rows[pl.ds(0, 8, stride=4), :] + rows[pl.ds(1, 8, stride=4), :]
        t = t + rows[pl.ds(2, 8, stride=4), :] + rows[pl.ds(3, 8, stride=4), :]
        total.append(t * (1.0 / 64.0))
    for half in range(2):
        acc = jnp.zeros((8, 128), F32)
        for quarter in range(4):
            weight = pick(lambda r, c: (r // 4 + 32 * quarter) == c)
            acc = acc + dot(total[half * 4 + quarter], weight)
        out[half * 8 : half * 8 + 8, :] = acc


def pack_y(src, beta, from_lo, from_hi, lo, hi):
    index = lax.axis_index("gx")
    low = flag(index > 0)
    high = flag(index < lax.axis_size("gx") - 1)
    for field, ref in enumerate((src, beta)):
        for out, row in ((lo, 0), (hi, 24)):
            out[field, 0:8] = from_lo[field, :, row : row + 8, :] * low
            out[field, 8:40] = ref[:, row : row + 8, :]
            out[field, 40:48] = from_hi[field, :, row : row + 8, :] * high


def pack_z(src, beta, x_lo, x_hi, y_lo, y_hi, s_out, b_out, lo, hi):
    ix = lax.axis_index("gx")
    iy = lax.axis_index("gy")
    x_low = flag(ix > 0)
    x_high = flag(ix < lax.axis_size("gx") - 1)
    y_low = flag(iy > 0)
    y_high = flag(iy < lax.axis_size("gy") - 1)
    for field, (ref, out) in enumerate(((src, s_out), (beta, b_out))):
        out[0:8, 8:40, :] = x_lo[field] * x_low
        out[8:40, 8:40, :] = ref[...]
        out[40:48, 8:40, :] = x_hi[field] * x_high
        out[:, 0:8, :] = y_lo[field] * y_low
        out[:, 40:48, :] = y_hi[field] * y_high
    lane = lanes_of(48)

    def body(xx):
        acc_lo = jnp.zeros((48, 128), F32)
        acc_hi = jnp.zeros((48, 128), F32)
        for g in range(8):
            s = s_out[g * 6 + xx]
            b = b_out[g * 6 + xx]
            first = (lane >= g * 16) & (lane < g * 16 + 8)
            second = (lane >= g * 16 + 8) & (lane < g * 16 + 16)
            acc_lo = jnp.where(first, roll(s, g * 16), acc_lo)
            acc_lo = jnp.where(second, roll(b, g * 16 + 8), acc_lo)
            acc_hi = jnp.where(first, roll(s, g * 16 + 8), acc_hi)
            acc_hi = jnp.where(second, roll(b, g * 16 + 16), acc_hi)
        lo[xx] = acc_lo
        hi[xx] = acc_hi

    loop(0, 6, 36, body)


def strip_ghosts(values, ghost):
    lane = lanes_of(48)

    def body(xx):
        acc = jnp.zeros((48, 128), F32)
        for g in range(8):
            acc = jnp.where(lane // 16 == g, roll(values[g * 6 + xx + 1, 8:56, :], g * 16 + 8), acc)
        ghost[xx] = acc

    loop(0, 6, 36, body)


def strip_sides(strip, xx):
    after = strip[xx + 1, 8:56, :] if xx < 5 else roll(strip[0, 8:56, :], -16)
    before = strip[xx - 1, 8:56, :] if xx > 0 else roll(strip[5, 8:56, :], 16)
    return before, after


def strip_z(strip, ghost, xx, lane):
    here = strip[xx, 8:56, :]
    up = roll(jnp.where(lane % 16 == 8, ghost[xx], here), -1)
    down = roll(jnp.where(lane % 16 == 7, ghost[xx], here), 1)
    return down, up


def block_z(value, strip, x, lane, first=8, count=48):
    g = x // 6
    edge = roll(strip[x - g * 6, first : first + count, :], 120 - g * 16)
    up = roll(jnp.where(lane == 0, edge, value), -1)
    down = roll(jnp.where(lane == 127, edge, value), 1)
    return down, up


def weights(here, sides):
    sums = [here + side for side in sides]
    total = sums[0] + sums[1] + sums[2] + sums[3] + sums[4] + sums[5]
    inverse = jnp.where(here > 0.0, 1.0 / total, 0.0)
    return [s * inverse for s in sums], inverse, total


def level0_setup(b_pad, bt_pad, ghost, src, src_t, g_main, g_strip, sp, sp_t, total):
    strip_ghosts(b_pad, ghost)
    lane = lanes_of(48)

    def body(x):
        here = b_pad[x + 1, 8:56, :]
        down, up = block_z(here, bt_pad, x, lane)
        faces, inverse, tot = weights(
            here,
            (
                b_pad[x, 8:56, :],
                b_pad[x + 2, 8:56, :],
                b_pad[x + 1, 7:55, :],
                b_pad[x + 1, 9:57, :],
                down,
                up,
            ),
        )
        for i in range(6):
            g_main[i, x] = faces[i]
        sp[x] = src[x] * (2.0 * inverse)
        if total is not None:
            total[x] = tot

    loop(0, 48, 12, body)
    for xx in range(6):
        before, after = strip_sides(bt_pad, xx)
        down, up = strip_z(bt_pad, ghost, xx, lane)
        faces, inverse, _ = weights(
            bt_pad[xx, 8:56, :],
            (before, after, bt_pad[xx, 7:55, :], bt_pad[xx, 9:57, :], down, up),
        )
        for i in range(6):
            g_strip[i, xx] = faces[i]
        sp_t[xx] = src_t[xx] * (2.0 * inverse)


def block_rest(v, t, g_main, sp, x, lane, skip=0):
    count = 48 - 2 * skip
    first = 8 + skip
    keep = slice(skip, 48 - skip)
    here = v[x + 1, first : first + count, :]
    down, up = block_z(here, t, x, lane, first, count)
    rest = sp[x, keep] - here
    rest = rest + g_main[0, x, keep] * v[x, first : first + count, :]
    rest = rest + g_main[1, x, keep] * v[x + 2, first : first + count, :]
    rest = rest + g_main[2, x, keep] * v[x + 1, first - 1 : first - 1 + count, :]
    rest = rest + g_main[3, x, keep] * v[x + 1, first + 1 : first + 1 + count, :]
    rest = rest + g_main[4, x, keep] * down + g_main[5, x, keep] * up
    return here, rest


def level0_step(v, t, v_out, t_out, ghost, g_main, g_strip, sp, sp_t, u, u_t, low, high, retain, factor):
    strip_ghosts(v, ghost)
    lane = lanes_of(48)

    def body(x):
        here, rest = block_rest(v, t, g_main, sp, x, lane)
        new = factor * rest
        if retain is not None:
            new = retain * u[x] + new
        u[x] = new
        v_out[x + 1, 8:56, :] = here + new

    loop(low, high, 4, body)
    for xx in range(6):
        here = t[xx, 8:56, :]
        before, after = strip_sides(t, xx)
        down, up = strip_z(t, ghost, xx, lane)
        rest = sp_t[xx] - here
        rest = rest + g_strip[0, xx] * before + g_strip[1, xx] * after
        rest = rest + g_strip[2, xx] * t[xx, 7:55, :] + g_strip[3, xx] * t[xx, 9:57, :]
        rest = rest + g_strip[4, xx] * down + g_strip[5, xx] * up
        new = factor * rest
        if retain is not None:
            new = retain * u_t[xx] + new
        u_t[xx] = new
        t_out[xx, 8:56, :] = here + new


def clear_edges(ref, planes, rows):
    width = ref.shape[1]
    ref[0] = jnp.zeros((width, 128), F32)
    ref[planes + 1] = jnp.zeros((width, 128), F32)

    def body(x):
        ref[x, 0:8, :] = jnp.zeros((8, 128), F32)
        ref[x, 8 + rows : width, :] = jnp.zeros((width - 8 - rows, 128), F32)

    loop(0, planes + 2, 4, body)


def clear_strip(ref):
    for xx in range(6):
        ref[xx, 0:8, :] = jnp.zeros((8, 128), F32)
        ref[xx, 56:64, :] = jnp.zeros((8, 128), F32)


def unpack_strip(z_lo, z_hi, src_t, bt_pad):
    iz = lax.axis_index("gz")
    low = flag(iz > 0)
    high = flag(iz < lax.axis_size("gz") - 1)
    lower = lanes_of(48) % 16 < 8
    for xx in range(6):
        before = z_lo[xx] * low
        after = z_hi[xx] * high
        src_t[xx] = jnp.where(lower, before, roll(after, 8))
        bt_pad[xx, 8:56, :] = jnp.where(lower, roll(before, -8), after)


LEVEL0_SCRATCH = [
    vm(50, 64, 128),
    vm(6, 64, 128),
    vm(50, 64, 128),
    vm(50, 64, 128),
    vm(6, 64, 128),
    vm(6, 64, 128),
    vm(6, 48, 128),
    vm(6, 48, 48, 128),
    vm(6, 6, 48, 128),
    vm(48, 48, 128),
    vm(6, 48, 128),
    vm(48, 48, 128),
    vm(6, 48, 128),
    vm(6, 48, 128),
]


def level0_down(
    src, beta, z_lo, z_hi, iter_out, iter_t_out, c_out, c_lo, c_hi,
    b_pad, bt_pad, va, vb, ta, tb, ghost, g_main, g_strip, sp, sp_t, u, u_t, src_t, total, rows,
):
    for ref in (b_pad, va, vb):
        clear_edges(ref, 48, 48)
    for ref in (bt_pad, ta, tb):
        clear_strip(ref)
    b_pad[1:49, 8:56, :] = beta[...]
    unpack_strip(z_lo, z_hi, src_t, bt_pad)
    level0_setup(b_pad, bt_pad, ghost, src, src_t, g_main, g_strip, sp, sp_t, total)

    first = RECIPE[0][1]

    def start(x):
        u[x] = first * sp[x]
        va[x + 1, 8:56, :] = u[x]

    loop(0, 48, 8, start)
    for xx in range(6):
        u_t[xx] = first * sp_t[xx]
        ta[xx, 8:56, :] = u_t[xx]
    bufs = [(va, ta), (vb, tb)]
    for k in range(1, SMOOTH):
        (v, t), (w, s) = bufs
        retain, factor = RECIPE[k]
        level0_step(v, t, w, s, ghost, g_main, g_strip, sp, sp_t, u, u_t, k, 48 - k, retain, factor)
        for x in [*range(k), *range(48 - k, 48)]:
            w[x + 1, 8:56, :] = v[x + 1, 8:56, :]
        bufs = [(w, s), (v, t)]
    v, t = bufs[0]
    iter_out[...] = v[1:49, 8:56, :]
    for xx in range(6):
        iter_t_out[xx] = t[xx, 8:56, :]

    lane = lanes_of(32)
    to_low = pick(lambda r, c: r // 2 == c)
    to_high = pick(lambda r, c: r // 2 + 64 == c)

    def restrict(x2):
        parts = []
        for half in range(2):
            x = 8 + 2 * x2 + half
            _, rest = block_rest(v, t, g_main, sp, x, lane, 8)
            parts.append(rest * total[x, 8:40])
        rows[0, x2] = (parts[0] + parts[1]) * (0.5 / 8.0)
        rows[1, x2] = (b_pad[9 + 2 * x2, 16:48, :] + b_pad[10 + 2 * x2, 16:48, :]) * (1.0 / 8.0)

    loop(0, 16, 8, restrict)

    def compress(x2):
        res = rows[0, x2, pl.ds(0, 16, stride=2), :] + rows[0, x2, pl.ds(1, 16, stride=2), :]
        bet = rows[1, x2, pl.ds(0, 16, stride=2), :] + rows[1, x2, pl.ds(1, 16, stride=2), :]
        c_out[x2] = dot(res, to_low) + dot(bet, to_high)

    loop(0, 16, 8, compress)
    c_lo[...] = c_out[0:10]
    c_hi[...] = c_out[6:16]


def pack1_y(c, from_lo, from_hi, lo, hi):
    index = lax.axis_index("gx")
    low = flag(index > 0)
    high = flag(index < lax.axis_size("gx") - 1)
    for x in range(36):
        if x < 10:
            plane = from_lo[x] * low
        elif x < 26:
            plane = c[x - 10]
        else:
            plane = from_hi[x - 26] * high
        lo[x * 10 : x * 10 + 10, :] = plane[0:10]
        hi[x * 10 : x * 10 + 10, :] = plane[6:16]


def pack1_z(c, x_lo, x_hi, y_lo, y_hi, ext, lo, hi):
    ix = lax.axis_index("gx")
    iy = lax.axis_index("gy")
    x_low = flag(ix > 0)
    x_high = flag(ix < lax.axis_size("gx") - 1)
    y_low = flag(iy > 0)
    y_high = flag(iy < lax.axis_size("gy") - 1)
    ext[0:10, 10:26, :] = x_lo[...] * x_low
    ext[10:26, 10:26, :] = c[...]
    ext[26:36, 10:26, :] = x_hi[...] * x_high
    for x in range(36):
        ext[x, 0:10, :] = y_lo[x * 10 : x * 10 + 10, :] * y_low
        ext[x, 26:36, :] = y_hi[x * 10 : x * 10 + 10, :] * y_high
        ext[x, 36:40, :] = jnp.zeros((4, 128), F32)
    lane = lanes_of(40)

    def body(xx):
        acc_lo = jnp.zeros((40, 128), F32)
        acc_hi = jnp.zeros((40, 128), F32)
        for g in range(6):
            e = ext[g * 6 + xx]
            first = (lane >= g * 20) & (lane < g * 20 + 10)
            second = (lane >= g * 20 + 10) & (lane < g * 20 + 20)
            middle = roll(e, g * 20 - 54)
            acc_lo = jnp.where(first, roll(e, g * 20), acc_lo)
            acc_lo = jnp.where(second, middle, acc_lo)
            acc_hi = jnp.where(first, middle, acc_hi)
            acc_hi = jnp.where(second, roll(e, g * 20 + 20), acc_hi)
        lo[xx] = acc_lo
        hi[xx] = acc_hi

    loop(0, 6, 36, body)


def ring_weights(b_pad, src, g, sp, total, planes, rows, scale, edges=None):
    lane = lanes_of(rows)

    def body(x):
        here = b_pad[x + 1, 8 : 8 + rows, :]
        down = roll(here, 1)
        up = roll(here, -1)
        if edges is not None:
            down = jnp.where(lane == 0, 0.0, down)
            up = jnp.where(lane == 127, 0.0, up)
        faces, inverse, tot = weights(
            here,
            (
                b_pad[x, 8 : 8 + rows, :],
                b_pad[x + 2, 8 : 8 + rows, :],
                b_pad[x + 1, 7 : 7 + rows, :],
                b_pad[x + 1, 9 : 9 + rows, :],
                down,
                up,
            ),
        )
        if edges is not None:
            faces[4] = jnp.where(lane == 0, 0.0, faces[4])
            faces[5] = jnp.where(lane == 127, 0.0, faces[5])
        for i in range(6):
            g[i, x] = faces[i]
        sp[x] = src[x] * (scale * 2.0 * inverse)
        if total is not None:
            total[x] = tot

    loop(0, planes, rows // 4, body)


def ring_rest(v, g, sp, x, rows):
    here = v[x + 1, 8 : 8 + rows, :]
    rest = sp[x] - here
    rest = rest + g[0, x] * v[x, 8 : 8 + rows, :] + g[1, x] * v[x + 2, 8 : 8 + rows, :]
    rest = rest + g[2, x] * v[x + 1, 7 : 7 + rows, :] + g[3, x] * v[x + 1, 9 : 9 + rows, :]
    rest = rest + g[4, x] * roll(here, 1) + g[5, x] * roll(here, -1)
    return here, rest


def ring_step(v, v_out, g, sp, u, planes, rows, retain, factor):
    def body(x):
        here, rest = ring_rest(v, g, sp, x, rows)
        new = factor * rest
        if retain is not None:
            new = retain * u[x] + new
        u[x] = new
        v_out[x + 1, 8 : 8 + rows, :] = here + new

    loop(0, planes, rows // 16, body)


def ring_zero_start(v, u, sp, planes, rows, factor):
    def body(x):
        u[x] = factor * sp[x]
        v[x + 1, 8 : 8 + rows, :] = u[x]

    loop(0, planes, rows // 8, body)


def ring_cheb(va, vb, g, sp, u, planes, rows, recipe, from_zero):
    begin = 0
    if from_zero:
        ring_zero_start(va, u, sp, planes, rows, recipe[0][1])
        begin = 1
    for k in range(begin, len(recipe)):
        retain, factor = recipe[k]
        ring_step(va, vb, g, sp, u, planes, rows, None if k == 0 else retain, factor)
        va, vb = vb, va
    return va


LEVEL1_SCRATCH = [
    vm(38, 56, 128),
    vm(38, 56, 128),
    vm(38, 56, 128),
    vm(6, 36, 40, 128),
    vm(36, 40, 128),
    vm(36, 40, 128),
]


def level1_down(
    ext, z_lo, z_hi, src_out, beta_out, iter_out, chunk,
    b_pad, va, vb, g, sp, u, total, rows,
):
    iz = lax.axis_index("gz")
    low = flag(iz > 0)
    high = flag(iz < lax.axis_size("gz") - 1)
    lane = lanes_of(40)
    inner = lane < 64
    above = (lane >= 64) & (lane < 74)
    below = lane >= 118
    for ref in (b_pad, va, vb):
        clear_edges(ref, 36, 40)

    def unpack(xx):
        before = z_lo[xx] * low
        after = z_hi[xx] * high
        for k in range(6):
            x = k * 6 + xx
            e = ext[x]
            s = jnp.where(inner, e, 0.0)
            s = jnp.where(above, roll(after, 64 - k * 20), s)
            s = jnp.where(below, roll(before, 118 - k * 20), s)
            b = jnp.where(inner, roll(e, 64), 0.0)
            b = jnp.where(above, roll(after, 54 - k * 20), b)
            b = jnp.where(below, roll(before, 108 - k * 20), b)
            src_out[x] = s
            beta_out[x] = b
            b_pad[x + 1, 8:48, :] = b

    loop(0, 6, 36, unpack)
    ring_weights(b_pad, src_out, g, sp, total, 36, 40, 4.0)
    v = ring_cheb(va, vb, g, sp, u, 36, 40, RECIPE, True)
    iter_out[...] = v[1:37, 8:48, :]
    summed = []
    for x2 in range(8):
        parts = []
        for half in range(2):
            x = 10 + 2 * x2 + half
            _, rest = ring_rest(v, g, sp, x, 40)
            parts.append(rest * total[x])
        rows[x2] = (parts[0] + parts[1]) * (0.25 * 0.5 / 8.0)
        summed.append(rows[x2, pl.ds(10, 8, stride=2), :] + rows[x2, pl.ds(11, 8, stride=2), :])
    packed = []
    for half in range(2):
        acc = jnp.zeros((8, 128), F32)
        for quarter in range(4):
            weight = pick(lambda r, c: (r < 64) & ((r // 2 + 32 * quarter) == c))
            acc = acc + dot(summed[half * 4 + quarter], weight)
        packed.append(acc)
    both = jnp.concatenate(packed, axis=0)

    def spread(d):
        chunk[d] = both

    loop(0, 128, 2, spread)


def whole_grid(parts, out, x_pad):
    lane = lanes_of(8)

    def body(i):
        gx = i // 8
        gy = i - gx * 8
        for half in range(2):
            blocks = [parts[i * 4 + gz, half * 8 : half * 8 + 8, :] for gz in range(4)]
            for quarter in range(4):
                acc = roll(blocks[0], -quarter * 32)
                for gz in range(1, 4):
                    acc = jnp.where(lane // 32 == gz, roll(blocks[gz], (gz - quarter) * 32), acc)
                row = pl.multiple_of(8 + gy * 8, 8)
                out[gx * 8 + half * 4 + quarter + x_pad, pl.ds(row, 8), :] = acc

    loop(0, 32, 18, body)


def bottom(
    s_parts, b_parts, out,
    s2, b2, va, vb, g, sp, u, total,
    b3, v3a, v3b, g3, sp3, u3, s3, rows, bw, wa, wb, gw, spw, uw, sw,
):
    for ref in (s2, b2, va, vb):

        def clear(x, ref=ref):
            ref[x, 0:8, :] = jnp.zeros((8, 128), F32)
            ref[x, 72:80, :] = jnp.zeros((8, 128), F32)

        loop(0, 48, 2, clear)
        for x in [*range(8), *range(40, 48)]:
            ref[x, 8:72, :] = jnp.zeros((64, 128), F32)
    whole_grid(s_parts, s2, 8)
    whole_grid(b_parts, b2, 8)
    inner_b = b2.at[7:41]
    inner_s = s2.at[8:40, 8:72]
    ring_weights(inner_b, inner_s, g, sp, total, 32, 64, 16.0, edges=True)
    v = ring_cheb(va.at[7:41], vb.at[7:41], g, sp, u, 32, 64, RECIPE, True)
    iterate = vb if SMOOTH % 2 == 0 else va

    clear_edges(b3, 16, 32)
    clear_edges(v3a, 16, 32)
    clear_edges(v3b, 16, 32)
    half_z = pick(lambda r, c: r // 2 == c)

    def restrict(x2):
        parts = []
        for half in range(2):
            x = 2 * x2 + half
            _, rest = ring_rest(v, g, sp, x, 64)
            parts.append(rest * total[x])
        rows[0, x2] = (parts[0] + parts[1]) * (0.0625 * 0.5 / 8.0)
        rows[1, x2] = (b2[8 + 2 * x2, 8:72, :] + b2[9 + 2 * x2, 8:72, :]) * (1.0 / 8.0)

    loop(0, 16, 16, restrict)

    def compress(x2):
        res = rows[0, x2, pl.ds(0, 32, stride=2), :] + rows[0, x2, pl.ds(1, 32, stride=2), :]
        bet = rows[1, x2, pl.ds(0, 32, stride=2), :] + rows[1, x2, pl.ds(1, 32, stride=2), :]
        s3[x2] = dot(res, half_z)
        b3[x2 + 1, 8:40, :] = dot(bet, half_z)

    loop(0, 16, 18, compress)
    ring_weights(b3, s3, g3, sp3, None, 16, 32, 64.0)
    c3 = ring_cheb(v3a, v3b, g3, sp3, u3, 16, 32, BOTTOM_RECIPE, True)

    other = va if iterate is vb else vb
    double_z = pick(lambda r, c: c // 2 == r)

    def prolong(x3):
        wide = dot(c3[x3 + 1, 8:40, :], double_z)
        rows[0, x3, pl.ds(0, 32, stride=2), :] = wide
        rows[0, x3, pl.ds(1, 32, stride=2), :] = wide
        for half in range(2):
            x = 8 + 2 * x3 + half
            other[x, 8:72, :] = iterate[x, 8:72, :] + rows[0, x3]

    loop(0, 16, 18, prolong)
    ix = lax.axis_index("gx")
    iy = lax.axis_index("gy")
    iz = lax.axis_index("gz")
    clear_edges(bw, 22, 24)
    clear_edges(wa, 22, 24)
    clear_edges(wb, 22, 24)
    row = pl.multiple_of(iy * 8, 8)

    def window(x):
        plane = ix * 8 + 1 + x
        bw[x + 1, 8:32, :] = b2[plane, pl.ds(row, 24), :]
        wa[x + 1, 8:32, :] = other[plane, pl.ds(row, 24), :]
        sw[x] = s2[plane, pl.ds(row, 24), :]

    loop(0, 22, 6, window)
    ring_weights(bw, sw, gw, spw, None, 22, 24, 16.0, edges=True)
    c2 = ring_cheb(wa, wb, gw, spw, uw, 22, 24, RECIPE, False)
    shift = (128 - iz * 32) % 128
    for x in range(18):
        out[x] = roll(c2[x + 3, 8:32, :], shift)


BOTTOM_SCRATCH = [
    vm(48, 80, 128),
    vm(48, 80, 128),
    vm(48, 80, 128),
    vm(48, 80, 128),
    vm(6, 32, 64, 128),
    vm(32, 64, 128),
    vm(32, 64, 128),
    vm(32, 64, 128),
    vm(18, 48, 128),
    vm(18, 48, 128),
    vm(18, 48, 128),
    vm(6, 16, 32, 128),
    vm(16, 32, 128),
    vm(16, 32, 128),
    vm(16, 32, 128),
    vm(2, 16, 64, 128),
    vm(24, 40, 128),
    vm(24, 40, 128),
    vm(24, 40, 128),
    vm(6, 22, 24, 128),
    vm(22, 24, 128),
    vm(22, 24, 128),
    vm(22, 24, 128),
]


def level1_up(c2, src, beta, iterate, out, b_pad, va, vb, g, sp, u, wide, rows):
    for ref in (b_pad, va, vb):
        clear_edges(ref, 36, 40)
    b_pad[1:37, 8:48, :] = beta[...]
    ring_weights(b_pad, src, g, sp, None, 36, 40, 4.0)
    spread = pick(lambda r, c: ((c < 74) & (c // 2 == r)) | ((c >= 118) & (c // 2 + 64 == r)))
    for x2 in range(18):
        rows[x2, 32:40, :] = jnp.zeros((8, 128), F32)

    def prolong(x2):
        wide[x2] = dot(c2[x2], spread)
        part = wide[x2, 3:21, :]
        rows[x2, pl.ds(0, 18, stride=2), :] = part
        rows[x2, pl.ds(1, 18, stride=2), :] = part
        for half in range(2):
            x = 2 * x2 + half
            va[x + 1, 8:48, :] = jnp.where(beta[x] > 0.0, iterate[x] + rows[x2], 0.0)

    loop(0, 18, 12, prolong)
    v = ring_cheb(va, vb, g, sp, u, 36, 40, RECIPE, False)
    out[...] = v[7:31, 14:38, :]


def level0_up(
    c1, src, beta, z_lo, z_hi, iterate, iterate_t, out,
    b_pad, bt_pad, va, vb, ta, tb, ghost, g_main, g_strip, sp, sp_t, u, u_t, src_t, rows,
):
    for ref in (b_pad, va, vb):
        clear_edges(ref, 48, 48)
    for ref in (bt_pad, ta, tb):
        clear_strip(ref)
    b_pad[1:49, 8:56, :] = beta[...]
    unpack_strip(z_lo, z_hi, src_t, bt_pad)
    level0_setup(b_pad, bt_pad, ghost, src, src_t, g_main, g_strip, sp, sp_t, None)
    spread = pick(lambda r, c: c // 2 == r)

    def prolong(x1):
        wide = dot(c1[x1], spread)
        rows[x1, pl.ds(0, 24, stride=2), :] = wide
        rows[x1, pl.ds(1, 24, stride=2), :] = wide
        for half in range(2):
            x = 2 * x1 + half
            va[x + 1, 8:56, :] = jnp.where(beta[x] > 0.0, iterate[x] + rows[x1], 0.0)

    loop(0, 24, 12, prolong)

    def prolong_strip(m):
        acc = jnp.zeros((24, 128), F32)
        for k in range(8):
            to = pick(
                lambda r, c: (c // 16 == k)
                & (((c % 16 < 8) & (r == 124 + (c % 16) // 2)) | ((c % 16 >= 8) & (r == 64 + (c % 16 - 8) // 2)))
            )
            acc = acc + dot(c1[k * 3 + m], to)
        rows[m, pl.ds(0, 24, stride=2), :] = acc
        rows[m, pl.ds(1, 24, stride=2), :] = acc
        for half in range(2):
            xx = 2 * m + half
            ta[xx, 8:56, :] = jnp.where(bt_pad[xx, 8:56, :] > 0.0, iterate_t[xx] + rows[m], 0.0)

    loop(0, 3, 36, prolong_strip)
    bufs = [(va, ta), (vb, tb)]
    for k in range(SMOOTH):
        (v, t), (w, s) = bufs
        retain, factor = RECIPE[k]
        if k == 0:
            retain = None
        if k < SMOOTH - 1:
            low, high = 4 + k, 44 - k
            level0_step(
                v, t, w, s, ghost, g_main, g_strip, sp, sp_t, u, u_t, low, high, retain, factor
            )
            for x in [*range(low), *range(high, 48)]:
                w[x + 1, 8:56, :] = v[x + 1, 8:56, :]
        else:
            lane = lanes_of(32)

            def last(x):
                here, rest = block_rest(v, t, g_main, sp, x, lane, 8)
                out[x - 8] = here + retain * u[x, 8:40] + factor * rest

            loop(8, 40, 4, last)
        bufs = [(w, s), (v, t)]


def ring(value, axis, step):
    count = lax.axis_size(axis)
    return lax.ppermute(value, axis, [(i, (i + step) % count) for i in range(count)])


def trade(lo, hi, axis):
    return ring(hi, axis, 1), ring(lo, axis, -1)


def per_device(source, beta):
    lo, hi = call(pack_x, (sds(2, 8, 32, 128), sds(2, 8, 32, 128)), name="pack_x")(source, beta)
    x_lo, x_hi = trade(lo, hi, "gx")
    beta2 = call(coarse_beta, sds(16, 128), [vm(32, 128)], name="coarse_beta")(beta)
    beta2_all = lax.all_gather(beta2, AXES)
    lo, hi = call(pack_y, (sds(2, 48, 8, 128), sds(2, 48, 8, 128)), name="pack_y")(
        source, beta, x_lo, x_hi
    )
    y_lo, y_hi = trade(lo, hi, "gy")
    src_ext, beta_ext, lo, hi = call(
        pack_z, (sds(48, 48, 128), sds(48, 48, 128), sds(6, 48, 128), sds(6, 48, 128)), name="pack_z", mib=14
    )(source, beta, x_lo, x_hi, y_lo, y_hi)
    z_lo, z_hi = trade(lo, hi, "gz")
    iter0, iter0_t, c, lo, hi = call(
        level0_down,
        (sds(48, 48, 128), sds(6, 48, 128), sds(16, 16, 128), sds(10, 16, 128), sds(10, 16, 128)),
        LEVEL0_SCRATCH + [vm(48, 48, 128), vm(2, 16, 32, 128)],
        name="level0_down", mib=30,
    )(src_ext, beta_ext, z_lo, z_hi)
    x_lo, x_hi = trade(lo, hi, "gx")
    lo, hi = call(pack1_y, (sds(360, 128), sds(360, 128)), name="pack1_y")(c, x_lo, x_hi)
    y_lo, y_hi = trade(lo, hi, "gy")
    ext, lo, hi = call(
        pack1_z, (sds(36, 40, 128), sds(6, 40, 128), sds(6, 40, 128)), name="pack1_z"
    )(c, x_lo, x_hi, y_lo, y_hi)
    z1_lo, z1_hi = trade(lo, hi, "gz")
    src1, beta1, iter1, chunk = call(
        level1_down,
        (sds(36, 40, 128), sds(36, 40, 128), sds(36, 40, 128), sds(128, 16, 128)),
        LEVEL1_SCRATCH + [vm(36, 40, 128), vm(8, 40, 128)],
        name="level1_down", mib=14,
    )(ext, z1_lo, z1_hi)
    source2_all = lax.all_to_all(chunk, AXES, 0, 0)
    c2 = call(bottom, sds(18, 24, 128), BOTTOM_SCRATCH, name="bottom", mib=34)(source2_all, beta2_all)
    c1 = call(
        level1_up, sds(24, 24, 128), LEVEL1_SCRATCH + [vm(18, 24, 128), vm(18, 40, 128)], name="level1_up", mib=14
    )(c2, src1, beta1, iter1)
    return call(level0_up, sds(32, 32, 128), LEVEL0_SCRATCH + [vm(24, 48, 128)], name="level0_up", mib=32)(
        c1, src_ext, beta_ext, z_lo, z_hi, iter0, iter0_t
    )


def solution(mesh):
    placed = (P(*AXES), P(*AXES))
    return jax.shard_map(
        per_device, mesh=mesh, in_specs=placed, out_specs=P(*AXES), check_vma=False
    )
```

```python
import jax
import jax.numpy as jnp
from jax import lax
from jax.experimental import pallas as pl
from jax.experimental.pallas import tpu as pltpu
from jax.sharding import PartitionSpec as P

SMOOTH = 4
BOTTOM = 12
LOW_EIG = 0.3
HIGH_EIG = 2.0
BOTTOM_LOW = 0.02

AXES = ("gx", "gy", "gz")
F32 = jnp.float32
MIB = 1024 * 1024


def cheb_plan(degree, lowest, highest):
    centre = 0.5 * (highest + lowest)
    radius = 0.5 * (highest - lowest)
    ratio_s = centre / radius
    rho_old = 1.0 / ratio_s
    recipe = [(0.0, 1.0 / centre)]
    for position in range(1, degree):
        rho_new = 1.0 / (2.0 * ratio_s - rho_old)
        recipe.append((rho_new * rho_old, 2.0 * rho_new / radius))
        rho_old = rho_new
    return recipe


RECIPE = cheb_plan(SMOOTH, LOW_EIG, HIGH_EIG)
BOTTOM_RECIPE = cheb_plan(BOTTOM, BOTTOM_LOW, HIGH_EIG)


def sds(*shape):
    return jax.ShapeDtypeStruct(shape, F32)


def vm(*shape):
    return pltpu.VMEM(shape, F32)


def call(body, outs, scratch=(), name=None, mib=2):
    return pl.pallas_call(
        body,
        out_shape=outs,
        scratch_shapes=list(scratch),
        compiler_params=pltpu.CompilerParams(vmem_limit_bytes=mib * MIB),
        name=name,
    )


def loop(low, high, vectors, body):
    count = high - low
    most = max(1, min(count, 72 // vectors))
    width = max([w for w in range(1, most + 1) if count % w == 0])
    if width * 2 < most:
        width = most
    rounds = count // width

    def chunk(i, carry):
        for k in range(width):
            body(low + i * width + k)
        return carry

    if rounds > 1:
        lax.fori_loop(0, rounds, chunk, 0)
    else:
        chunk(0, 0)
    for x in range(low + rounds * width, high):
        body(x)


def lanes_of(rows):
    return lax.broadcasted_iota(jnp.int32, (rows, 128), 1)


def roll(value, shift):
    if isinstance(shift, int):
        shift = shift % 128
        if shift == 0:
            return value
    return pltpu.roll(value, shift, 1)


def flag(condition):
    return jnp.where(condition, 1.0, 0.0).astype(F32)


def dot(left, right):
    return lax.dot_general(
        left,
        right,
        (((1,), (0,)), ((), ())),
        precision=lax.Precision.HIGHEST,
        preferred_element_type=F32,
    )


def pick(match):
    row = lax.broadcasted_iota(jnp.int32, (128, 128), 0)
    col = lax.broadcasted_iota(jnp.int32, (128, 128), 1)
    return jnp.where(match(row, col), 1.0, 0.0).astype(F32)


def coarse_beta(beta, out, rows):
    total = []
    for x in range(8):
        s = beta[4 * x] + beta[4 * x + 1] + beta[4 * x + 2] + beta[4 * x + 3]
        rows[...] = s
        t = rows[pl.ds(0, 8, stride=4), :] + rows[pl.ds(1, 8, stride=4), :]
        t = t + rows[pl.ds(2, 8, stride=4), :] + rows[pl.ds(3, 8, stride=4), :]
        total.append(t * (1.0 / 64.0))
    for half in range(2):
        acc = jnp.zeros((8, 128), F32)
        for quarter in range(4):
            weight = pick(lambda r, c: (r // 4 + 32 * quarter) == c)
            acc = acc + dot(total[half * 4 + quarter], weight)
        out[half * 8 : half * 8 + 8, :] = acc


def pack_y(src, beta, from_lo, from_hi, lo, hi, s_mid, b_mid):
    index = lax.axis_index("gx")
    low = flag(index > 0)
    high = flag(index < lax.axis_size("gx") - 1)
    for field, (ref, mid) in enumerate(((src, s_mid), (beta, b_mid))):
        mid[0:8] = from_lo[field] * low
        mid[8:40] = ref[...]
        mid[40:48] = from_hi[field] * high
        lo[field] = mid[:, 0:8, :]
        hi[field] = mid[:, 24:32, :]


def pack_z(s_mid, b_mid, y_lo, y_hi, s_out, b_out, lo, hi):
    iy = lax.axis_index("gy")
    y_low = flag(iy > 0)
    y_high = flag(iy < lax.axis_size("gy") - 1)
    for field, (mid, out) in enumerate(((s_mid, s_out), (b_mid, b_out))):
        out[:, 8:40, :] = mid[...]
        out[:, 0:8, :] = y_lo[field] * y_low
        out[:, 40:48, :] = y_hi[field] * y_high
    lane = lanes_of(48)

    def body(xx):
        acc_lo = jnp.zeros((48, 128), F32)
        acc_hi = jnp.zeros((48, 128), F32)
        for g in range(8):
            s = s_out[g * 6 + xx]
            b = b_out[g * 6 + xx]
            first = (lane >= g * 16) & (lane < g * 16 + 8)
            second = (lane >= g * 16 + 8) & (lane < g * 16 + 16)
            acc_lo = jnp.where(first, roll(s, g * 16), acc_lo)
            acc_lo = jnp.where(second, roll(b, g * 16 + 8), acc_lo)
            acc_hi = jnp.where(first, roll(s, g * 16 + 8), acc_hi)
            acc_hi = jnp.where(second, roll(b, g * 16 + 16), acc_hi)
        lo[xx] = acc_lo
        hi[xx] = acc_hi

    loop(0, 6, 36, body)


def strip_ghosts(values, ghost):
    lane = lanes_of(48)

    def body(xx):
        acc = jnp.zeros((48, 128), F32)
        for g in range(8):
            acc = jnp.where(lane // 16 == g, roll(values[g * 6 + xx + 1, 8:56, :], g * 16 + 8), acc)
        ghost[xx] = acc

    loop(0, 6, 36, body)


def strip_sides(strip, xx):
    after = strip[xx + 1, 8:56, :] if xx < 5 else roll(strip[0, 8:56, :], -16)
    before = strip[xx - 1, 8:56, :] if xx > 0 else roll(strip[5, 8:56, :], 16)
    return before, after


def strip_z(strip, ghost, xx, lane):
    here = strip[xx, 8:56, :]
    up = roll(jnp.where(lane % 16 == 8, ghost[xx], here), -1)
    down = roll(jnp.where(lane % 16 == 7, ghost[xx], here), 1)
    return down, up


def block_z(value, strip, x, lane, first=8, count=48):
    g = x // 6
    edge = roll(strip[x - g * 6, first : first + count, :], 120 - g * 16)
    up = roll(jnp.where(lane == 0, edge, value), -1)
    down = roll(jnp.where(lane == 127, edge, value), 1)
    return down, up


def weights(here, sides):
    sums = [here + side for side in sides]
    total = sums[0] + sums[1] + sums[2] + sums[3] + sums[4] + sums[5]
    inverse = jnp.where(here > 0.0, 1.0 / total, 0.0)
    return [s * inverse for s in sums], inverse, total


def level0_setup(b_pad, bt_pad, ghost, src, src_t, g_main, g_strip, sp, sp_t, total):
    strip_ghosts(b_pad, ghost)
    lane = lanes_of(48)

    def body(x):
        here = b_pad[x + 1, 8:56, :]
        down, up = block_z(here, bt_pad, x, lane)
        faces, inverse, tot = weights(
            here,
            (
                b_pad[x, 8:56, :],
                b_pad[x + 2, 8:56, :],
                b_pad[x + 1, 7:55, :],
                b_pad[x + 1, 9:57, :],
                down,
                up,
            ),
        )
        for i in range(6):
            g_main[i, x] = faces[i]
        sp[x] = src[x] * (2.0 * inverse)
        if total is not None:
            total[x] = tot

    loop(0, 48, 12, body)
    for xx in range(6):
        before, after = strip_sides(bt_pad, xx)
        down, up = strip_z(bt_pad, ghost, xx, lane)
        faces, inverse, _ = weights(
            bt_pad[xx, 8:56, :],
            (before, after, bt_pad[xx, 7:55, :], bt_pad[xx, 9:57, :], down, up),
        )
        for i in range(6):
            g_strip[i, xx] = faces[i]
        sp_t[xx] = src_t[xx] * (2.0 * inverse)


def block_rest(v, t, g_main, sp, x, lane, skip=0):
    count = 48 - 2 * skip
    first = 8 + skip
    keep = slice(skip, 48 - skip)
    here = v[x + 1, first : first + count, :]
    down, up = block_z(here, t, x, lane, first, count)
    rest = sp[x, keep] - here
    rest = rest + g_main[0, x, keep] * v[x, first : first + count, :]
    rest = rest + g_main[1, x, keep] * v[x + 2, first : first + count, :]
    rest = rest + g_main[2, x, keep] * v[x + 1, first - 1 : first - 1 + count, :]
    rest = rest + g_main[3, x, keep] * v[x + 1, first + 1 : first + 1 + count, :]
    rest = rest + g_main[4, x, keep] * down + g_main[5, x, keep] * up
    return here, rest


def level0_step(v, t, v_out, t_out, ghost, g_main, g_strip, sp, sp_t, u, u_t, low, high, retain, factor):
    strip_ghosts(v, ghost)
    lane = lanes_of(48)

    def body(x):
        here, rest = block_rest(v, t, g_main, sp, x, lane)
        new = factor * rest
        if retain is not None:
            new = retain * u[x] + new
        u[x] = new
        v_out[x + 1, 8:56, :] = here + new

    loop(low, high, 4, body)
    for xx in range(6):
        here = t[xx, 8:56, :]
        before, after = strip_sides(t, xx)
        down, up = strip_z(t, ghost, xx, lane)
        rest = sp_t[xx] - here
        rest = rest + g_strip[0, xx] * before + g_strip[1, xx] * after
        rest = rest + g_strip[2, xx] * t[xx, 7:55, :] + g_strip[3, xx] * t[xx, 9:57, :]
        rest = rest + g_strip[4, xx] * down + g_strip[5, xx] * up
        new = factor * rest
        if retain is not None:
            new = retain * u_t[xx] + new
        u_t[xx] = new
        t_out[xx, 8:56, :] = here + new


def clear_edges(ref, planes, rows):
    width = ref.shape[1]
    ref[0] = jnp.zeros((width, 128), F32)
    ref[planes + 1] = jnp.zeros((width, 128), F32)

    def body(x):
        ref[x, 0:8, :] = jnp.zeros((8, 128), F32)
        ref[x, 8 + rows : width, :] = jnp.zeros((width - 8 - rows, 128), F32)

    loop(0, planes + 2, 4, body)


def clear_strip(ref):
    for xx in range(6):
        ref[xx, 0:8, :] = jnp.zeros((8, 128), F32)
        ref[xx, 56:64, :] = jnp.zeros((8, 128), F32)


def unpack_strip(z_lo, z_hi, src_t, bt_pad):
    iz = lax.axis_index("gz")
    low = flag(iz > 0)
    high = flag(iz < lax.axis_size("gz") - 1)
    lower = lanes_of(48) % 16 < 8
    for xx in range(6):
        before = z_lo[xx] * low
        after = z_hi[xx] * high
        src_t[xx] = jnp.where(lower, before, roll(after, 8))
        bt_pad[xx, 8:56, :] = jnp.where(lower, roll(before, -8), after)


LEVEL0_SCRATCH = [
    vm(50, 64, 128),
    vm(6, 64, 128),
    vm(50, 64, 128),
    vm(50, 64, 128),
    vm(6, 64, 128),
    vm(6, 64, 128),
    vm(6, 48, 128),
    vm(6, 48, 48, 128),
    vm(6, 6, 48, 128),
    vm(48, 48, 128),
    vm(6, 48, 128),
    vm(48, 48, 128),
    vm(6, 48, 128),
    vm(6, 48, 128),
]


def level0_down(
    src, beta, z_lo, z_hi, iter_out, iter_t_out, c_out, c_lo, c_hi,
    b_pad, bt_pad, va, vb, ta, tb, ghost, g_main, g_strip, sp, sp_t, u, u_t, src_t, total, rows,
):
    for ref in (b_pad, va, vb):
        clear_edges(ref, 48, 48)
    for ref in (bt_pad, ta, tb):
        clear_strip(ref)
    b_pad[1:49, 8:56, :] = beta[...]
    unpack_strip(z_lo, z_hi, src_t, bt_pad)
    level0_setup(b_pad, bt_pad, ghost, src, src_t, g_main, g_strip, sp, sp_t, total)

    first = RECIPE[0][1]

    def start(x):
        u[x] = first * sp[x]
        va[x + 1, 8:56, :] = u[x]

    loop(0, 48, 8, start)
    for xx in range(6):
        u_t[xx] = first * sp_t[xx]
        ta[xx, 8:56, :] = u_t[xx]
    bufs = [(va, ta), (vb, tb)]
    for k in range(1, SMOOTH):
        (v, t), (w, s) = bufs
        retain, factor = RECIPE[k]
        level0_step(v, t, w, s, ghost, g_main, g_strip, sp, sp_t, u, u_t, k, 48 - k, retain, factor)
        for x in [*range(k), *range(48 - k, 48)]:
            w[x + 1, 8:56, :] = v[x + 1, 8:56, :]
        bufs = [(w, s), (v, t)]
    v, t = bufs[0]
    iter_out[...] = v[1:49, 8:56, :]
    for xx in range(6):
        iter_t_out[xx] = t[xx, 8:56, :]

    lane = lanes_of(32)
    to_low = pick(lambda r, c: r // 2 == c)
    to_high = pick(lambda r, c: r // 2 + 64 == c)

    def restrict(x2):
        parts = []
        for half in range(2):
            x = 8 + 2 * x2 + half
            _, rest = block_rest(v, t, g_main, sp, x, lane, 8)
            parts.append(rest * total[x, 8:40])
        rows[0, x2] = (parts[0] + parts[1]) * (0.5 / 8.0)
        rows[1, x2] = (b_pad[9 + 2 * x2, 16:48, :] + b_pad[10 + 2 * x2, 16:48, :]) * (1.0 / 8.0)

    loop(0, 16, 8, restrict)

    def compress(x2):
        res = rows[0, x2, pl.ds(0, 16, stride=2), :] + rows[0, x2, pl.ds(1, 16, stride=2), :]
        bet = rows[1, x2, pl.ds(0, 16, stride=2), :] + rows[1, x2, pl.ds(1, 16, stride=2), :]
        c_out[x2] = dot(res, to_low) + dot(bet, to_high)

    loop(0, 16, 8, compress)
    c_lo[...] = c_out[0:10]
    c_hi[...] = c_out[6:16]


def pack1_y(c, from_lo, from_hi, lo, hi):
    index = lax.axis_index("gx")
    low = flag(index > 0)
    high = flag(index < lax.axis_size("gx") - 1)
    for x in range(36):
        if x < 10:
            plane = from_lo[x] * low
        elif x < 26:
            plane = c[x - 10]
        else:
            plane = from_hi[x - 26] * high
        lo[x * 10 : x * 10 + 10, :] = plane[0:10]
        hi[x * 10 : x * 10 + 10, :] = plane[6:16]


def pack1_z(c, x_lo, x_hi, y_lo, y_hi, ext, lo, hi):
    ix = lax.axis_index("gx")
    iy = lax.axis_index("gy")
    x_low = flag(ix > 0)
    x_high = flag(ix < lax.axis_size("gx") - 1)
    y_low = flag(iy > 0)
    y_high = flag(iy < lax.axis_size("gy") - 1)
    ext[0:10, 10:26, :] = x_lo[...] * x_low
    ext[10:26, 10:26, :] = c[...]
    ext[26:36, 10:26, :] = x_hi[...] * x_high
    for x in range(36):
        ext[x, 0:10, :] = y_lo[x * 10 : x * 10 + 10, :] * y_low
        ext[x, 26:36, :] = y_hi[x * 10 : x * 10 + 10, :] * y_high
        ext[x, 36:40, :] = jnp.zeros((4, 128), F32)
    lane = lanes_of(40)

    def body(xx):
        acc_lo = jnp.zeros((40, 128), F32)
        acc_hi = jnp.zeros((40, 128), F32)
        for g in range(6):
            e = ext[g * 6 + xx]
            first = (lane >= g * 20) & (lane < g * 20 + 10)
            second = (lane >= g * 20 + 10) & (lane < g * 20 + 20)
            middle = roll(e, g * 20 - 54)
            acc_lo = jnp.where(first, roll(e, g * 20), acc_lo)
            acc_lo = jnp.where(second, middle, acc_lo)
            acc_hi = jnp.where(first, middle, acc_hi)
            acc_hi = jnp.where(second, roll(e, g * 20 + 20), acc_hi)
        lo[xx] = acc_lo
        hi[xx] = acc_hi

    loop(0, 6, 36, body)


def ring_weights(b_pad, src, g, sp, total, planes, rows, scale, edges=None):
    lane = lanes_of(rows)

    def body(x):
        here = b_pad[x + 1, 8 : 8 + rows, :]
        down = roll(here, 1)
        up = roll(here, -1)
        if edges is not None:
            down = jnp.where(lane == 0, 0.0, down)
            up = jnp.where(lane == 127, 0.0, up)
        faces, inverse, tot = weights(
            here,
            (
                b_pad[x, 8 : 8 + rows, :],
                b_pad[x + 2, 8 : 8 + rows, :],
                b_pad[x + 1, 7 : 7 + rows, :],
                b_pad[x + 1, 9 : 9 + rows, :],
                down,
                up,
            ),
        )
        if edges is not None:
            faces[4] = jnp.where(lane == 0, 0.0, faces[4])
            faces[5] = jnp.where(lane == 127, 0.0, faces[5])
        for i in range(6):
            g[i, x] = faces[i]
        sp[x] = scale * 2.0 * inverse if src is None else src[x] * (scale * 2.0 * inverse)
        if total is not None:
            total[x] = tot

    loop(0, planes, rows // 4, body)


def ring_rest(v, g, sp, x, rows):
    here = v[x + 1, 8 : 8 + rows, :]
    rest = sp[x] - here
    rest = rest + g[0, x] * v[x, 8 : 8 + rows, :] + g[1, x] * v[x + 2, 8 : 8 + rows, :]
    rest = rest + g[2, x] * v[x + 1, 7 : 7 + rows, :] + g[3, x] * v[x + 1, 9 : 9 + rows, :]
    rest = rest + g[4, x] * roll(here, 1) + g[5, x] * roll(here, -1)
    return here, rest


def ring_step(v, v_out, g, sp, u, planes, rows, retain, factor):
    def body(x):
        here, rest = ring_rest(v, g, sp, x, rows)
        new = factor * rest
        if retain is not None:
            new = retain * u[x] + new
        u[x] = new
        v_out[x + 1, 8 : 8 + rows, :] = here + new

    loop(0, planes, rows // 16, body)


def ring_zero_start(v, u, sp, planes, rows, factor):
    def body(x):
        u[x] = factor * sp[x]
        v[x + 1, 8 : 8 + rows, :] = u[x]

    loop(0, planes, rows // 8, body)


def ring_cheb(va, vb, g, sp, u, planes, rows, recipe, from_zero):
    begin = 0
    if from_zero:
        ring_zero_start(va, u, sp, planes, rows, recipe[0][1])
        begin = 1
    for k in range(begin, len(recipe)):
        retain, factor = recipe[k]
        ring_step(va, vb, g, sp, u, planes, rows, None if k == 0 else retain, factor)
        va, vb = vb, va
    return va


LEVEL1_SCRATCH = [
    vm(38, 56, 128),
    vm(38, 56, 128),
    vm(38, 56, 128),
    vm(6, 36, 40, 128),
    vm(36, 40, 128),
    vm(36, 40, 128),
]


def level1_unpack(ext, z_lo, z_hi, source, b_pad, beta_out):
    iz = lax.axis_index("gz")
    low = flag(iz > 0)
    high = flag(iz < lax.axis_size("gz") - 1)
    lane = lanes_of(40)
    inner = lane < 64
    above = (lane >= 64) & (lane < 74)
    below = lane >= 118

    def unpack(xx):
        before = z_lo[xx] * low
        after = z_hi[xx] * high
        for k in range(6):
            x = k * 6 + xx
            e = ext[x]
            s = jnp.where(inner, e, 0.0)
            s = jnp.where(above, roll(after, 64 - k * 20), s)
            s = jnp.where(below, roll(before, 118 - k * 20), s)
            b = jnp.where(inner, roll(e, 64), 0.0)
            b = jnp.where(above, roll(after, 54 - k * 20), b)
            b = jnp.where(below, roll(before, 108 - k * 20), b)
            source[x] = s
            b_pad[x + 1, 8:48, :] = b
            if beta_out is not None:
                beta_out[x] = b

    loop(0, 6, 36, unpack)


def level1_down(
    ext, z_lo, z_hi, iter_out, chunk,
    b_pad, va, vb, g, sp, u, src, total, rows,
):
    for ref in (b_pad, va, vb):
        clear_edges(ref, 36, 40)
    level1_unpack(ext, z_lo, z_hi, src, b_pad, None)
    ring_weights(b_pad, src, g, sp, total, 36, 40, 4.0)
    v = ring_cheb(va, vb, g, sp, u, 36, 40, RECIPE, True)
    iter_out[...] = v[1:37, 8:48, :]
    summed = []
    for x2 in range(8):
        parts = []
        for half in range(2):
            x = 10 + 2 * x2 + half
            _, rest = ring_rest(v, g, sp, x, 40)
            parts.append(rest * total[x])
        rows[x2] = (parts[0] + parts[1]) * (0.25 * 0.5 / 8.0)
        summed.append(rows[x2, pl.ds(10, 8, stride=2), :] + rows[x2, pl.ds(11, 8, stride=2), :])
    for half in range(2):
        acc = jnp.zeros((8, 128), F32)
        for quarter in range(4):
            weight = pick(lambda r, c: (r < 64) & ((r // 2 + 32 * quarter) == c))
            acc = acc + dot(summed[half * 4 + quarter], weight)
        chunk[half * 8 : half * 8 + 8, :] = acc


def level1_prepare(ext, z_lo, z_hi, g, sp, beta_out, b_pad, src):
    clear_edges(b_pad, 36, 40)
    level1_unpack(ext, z_lo, z_hi, src, b_pad, beta_out)
    ring_weights(b_pad, src, g, sp, None, 36, 40, 4.0)


def sender(axis, step):
    count = lax.axis_size(axis)
    return lax.rem(lax.axis_index(axis) + count - step, count)


def gather_z(*refs):
    *parts, out = refs
    lane = lanes_of(8)
    for half in range(2):
        for quarter in range(4):
            acc = jnp.zeros((8, 128), F32)
            for step, part in enumerate(parts):
                owner = sender("gz", step)
                moved = roll(part[half * 8 : half * 8 + 8, :], lax.rem(owner - quarter + 4, 4) * 32)
                acc = jnp.where(lane // 32 == owner, moved, acc)
            out[half * 4 + quarter] = acc


def gather_x(*refs):
    *parts, out = refs
    for step, part in enumerate(parts):
        out[pl.ds(sender("gx", step) * 8, 8)] = part[...]


def gather_y(parts, out):
    for step, part in enumerate(parts):
        row = pl.multiple_of(8 + sender("gy", step) * 8, 8)
        out[8:40, pl.ds(row, 8), :] = part[...]


def whole_grid(parts, out, x_pad):
    lane = lanes_of(8)

    def body(i):
        gx = i // 8
        gy = i - gx * 8
        for half in range(2):
            blocks = [parts[i * 4 + gz, half * 8 : half * 8 + 8, :] for gz in range(4)]
            for quarter in range(4):
                acc = roll(blocks[0], -quarter * 32)
                for gz in range(1, 4):
                    acc = jnp.where(lane // 32 == gz, roll(blocks[gz], (gz - quarter) * 32), acc)
                row = pl.multiple_of(8 + gy * 8, 8)
                out[gx * 8 + half * 4 + quarter + x_pad, pl.ds(row, 8), :] = acc

    loop(0, 32, 18, body)


def clear_whole(ref):
    def clear(x):
        ref[x, 0:8, :] = jnp.zeros((8, 128), F32)
        ref[x, 72:80, :] = jnp.zeros((8, 128), F32)

    loop(0, 48, 2, clear)
    for x in [*range(8), *range(40, 48)]:
        ref[x, 8:72, :] = jnp.zeros((64, 128), F32)


def coarse_prepare(b_parts, g, inv, total, g3, inv3, gw, invw, b2, b3, bw, rows):
    clear_whole(b2)
    clear_edges(b3, 16, 32)
    clear_edges(bw, 22, 24)
    whole_grid(b_parts, b2, 8)
    ring_weights(b2.at[7:41], None, g, inv, total, 32, 64, 16.0, edges=True)
    half_z = pick(lambda r, c: r // 2 == c)

    def restrict(x2):
        rows[x2] = (b2[8 + 2 * x2, 8:72, :] + b2[9 + 2 * x2, 8:72, :]) * (1.0 / 8.0)

    loop(0, 16, 8, restrict)

    def compress(x2):
        bet = rows[x2, pl.ds(0, 32, stride=2), :] + rows[x2, pl.ds(1, 32, stride=2), :]
        b3[x2 + 1, 8:40, :] = dot(bet, half_z)

    loop(0, 16, 9, compress)
    ring_weights(b3, None, g3, inv3, None, 16, 32, 64.0)
    ix = lax.axis_index("gx")
    row = pl.multiple_of(lax.axis_index("gy") * 8, 8)

    def window(x):
        bw[x + 1, 8:32, :] = b2[ix * 8 + 1 + x, pl.ds(row, 24), :]

    loop(0, 22, 6, window)
    ring_weights(bw, None, gw, invw, None, 22, 24, 16.0, edges=True)


COARSE_SHAPES = [
    (6, 32, 64, 128),
    (32, 64, 128),
    (32, 64, 128),
    (6, 16, 32, 128),
    (16, 32, 128),
    (6, 22, 24, 128),
    (22, 24, 128),
]


def bottom(
    p0, p1, p2, p3, p4, p5, p6, p7, g, inv, total, g3, inv3, gw, invw, out,
    s2, va, vb, sp, u, v3a, v3b, sp3, u3, rows, wa, wb, spw, uw,
):
    for ref in (s2, va, vb):
        clear_whole(ref)
    gather_y((p0, p1, p2, p3, p4, p5, p6, p7), s2)

    def scale(x):
        sp[x] = s2[x + 8, 8:72, :] * inv[x]

    loop(0, 32, 8, scale)
    v = ring_cheb(va.at[7:41], vb.at[7:41], g, sp, u, 32, 64, RECIPE, True)
    iterate = vb if SMOOTH % 2 == 0 else va

    clear_edges(v3a, 16, 32)
    clear_edges(v3b, 16, 32)
    half_z = pick(lambda r, c: r // 2 == c)

    def restrict(x2):
        parts = []
        for half in range(2):
            x = 2 * x2 + half
            _, rest = ring_rest(v, g, sp, x, 64)
            parts.append(rest * total[x])
        rows[x2] = (parts[0] + parts[1]) * (0.0625 * 0.5 / 8.0)

    loop(0, 16, 16, restrict)

    def compress(x2):
        res = rows[x2, pl.ds(0, 32, stride=2), :] + rows[x2, pl.ds(1, 32, stride=2), :]
        sp3[x2] = dot(res, half_z) * inv3[x2]

    loop(0, 16, 9, compress)
    c3 = ring_cheb(v3a, v3b, g3, sp3, u3, 16, 32, BOTTOM_RECIPE, True)

    other = va if iterate is vb else vb
    double_z = pick(lambda r, c: c // 2 == r)

    def prolong(x3):
        wide = dot(c3[x3 + 1, 8:40, :], double_z)
        rows[x3, pl.ds(0, 32, stride=2), :] = wide
        rows[x3, pl.ds(1, 32, stride=2), :] = wide
        for half in range(2):
            x = 8 + 2 * x3 + half
            other[x, 8:72, :] = iterate[x, 8:72, :] + rows[x3]

    loop(0, 16, 18, prolong)
    ix = lax.axis_index("gx")
    iz = lax.axis_index("gz")
    clear_edges(wa, 22, 24)
    clear_edges(wb, 22, 24)
    row = pl.multiple_of(lax.axis_index("gy") * 8, 8)

    def window(x):
        plane = ix * 8 + 1 + x
        wa[x + 1, 8:32, :] = other[plane, pl.ds(row, 24), :]
        spw[x] = s2[plane, pl.ds(row, 24), :] * invw[x]

    loop(0, 22, 6, window)
    c2 = ring_cheb(wa, wb, gw, spw, uw, 22, 24, RECIPE, False)
    shift = (128 - iz * 32) % 128
    for x in range(18):
        out[x] = roll(c2[x + 3, 8:32, :], shift)


COARSE_SCRATCH = [
    vm(48, 80, 128),
    vm(18, 48, 128),
    vm(24, 40, 128),
    vm(16, 64, 128),
]
BOTTOM_SCRATCH = [
    vm(48, 80, 128),
    vm(48, 80, 128),
    vm(48, 80, 128),
    vm(32, 64, 128),
    vm(32, 64, 128),
    vm(18, 48, 128),
    vm(18, 48, 128),
    vm(16, 32, 128),
    vm(16, 32, 128),
    vm(16, 64, 128),
    vm(24, 40, 128),
    vm(24, 40, 128),
    vm(22, 24, 128),
    vm(22, 24, 128),
]


def level1_up(c2, g, sp, beta, iterate, out, va, vb, u, wide, rows):
    for ref in (va, vb):
        clear_edges(ref, 36, 40)
    spread = pick(lambda r, c: ((c < 74) & (c // 2 == r)) | ((c >= 118) & (c // 2 + 64 == r)))
    for x2 in range(18):
        rows[x2, 32:40, :] = jnp.zeros((8, 128), F32)

    def prolong(x2):
        wide[x2] = dot(c2[x2], spread)
        part = wide[x2, 3:21, :]
        rows[x2, pl.ds(0, 18, stride=2), :] = part
        rows[x2, pl.ds(1, 18, stride=2), :] = part
        for half in range(2):
            x = 2 * x2 + half
            va[x + 1, 8:48, :] = jnp.where(beta[x] > 0.0, iterate[x] + rows[x2], 0.0)

    loop(0, 18, 12, prolong)
    v = ring_cheb(va, vb, g, sp, u, 36, 40, RECIPE, False)
    out[...] = v[7:31, 14:38, :]


def level0_prepare(src, beta, z_lo, z_hi, g_main, g_strip, sp, sp_t, bt_out, b_pad, bt_pad, ghost, src_t):
    clear_edges(b_pad, 48, 48)
    clear_strip(bt_pad)
    b_pad[1:49, 8:56, :] = beta[...]
    unpack_strip(z_lo, z_hi, src_t, bt_pad)
    for xx in range(6):
        bt_out[xx] = bt_pad[xx, 8:56, :]
    level0_setup(b_pad, bt_pad, ghost, src, src_t, g_main, g_strip, sp, sp_t, None)


def level0_up(
    c1, beta, g_main, g_strip, sp, sp_t, beta_t, iterate, iterate_t, out,
    va, vb, ta, tb, ghost, u, u_t, rows,
):
    for ref in (va, vb):
        clear_edges(ref, 48, 48)
    for ref in (ta, tb):
        clear_strip(ref)
    spread = pick(lambda r, c: c // 2 == r)

    def prolong(x1):
        wide = dot(c1[x1], spread)
        rows[x1, pl.ds(0, 24, stride=2), :] = wide
        rows[x1, pl.ds(1, 24, stride=2), :] = wide
        for half in range(2):
            x = 2 * x1 + half
            va[x + 1, 8:56, :] = jnp.where(beta[x] > 0.0, iterate[x] + rows[x1], 0.0)

    loop(0, 24, 12, prolong)

    def prolong_strip(m):
        acc = jnp.zeros((24, 128), F32)
        for k in range(8):
            to = pick(
                lambda r, c: (c // 16 == k)
                & (((c % 16 < 8) & (r == 124 + (c % 16) // 2)) | ((c % 16 >= 8) & (r == 64 + (c % 16 - 8) // 2)))
            )
            acc = acc + dot(c1[k * 3 + m], to)
        rows[m, pl.ds(0, 24, stride=2), :] = acc
        rows[m, pl.ds(1, 24, stride=2), :] = acc
        for half in range(2):
            xx = 2 * m + half
            ta[xx, 8:56, :] = jnp.where(beta_t[xx] > 0.0, iterate_t[xx] + rows[m], 0.0)

    loop(0, 3, 36, prolong_strip)
    bufs = [(va, ta), (vb, tb)]
    for k in range(SMOOTH):
        (v, t), (w, s) = bufs
        retain, factor = RECIPE[k]
        if k == 0:
            retain = None
        if k < SMOOTH - 1:
            low, high = 4 + k, 44 - k
            level0_step(
                v, t, w, s, ghost, g_main, g_strip, sp, sp_t, u, u_t, low, high, retain, factor
            )
            for x in [*range(low), *range(high, 48)]:
                w[x + 1, 8:56, :] = v[x + 1, 8:56, :]
        else:
            lane = lanes_of(32)

            def last(x):
                here, rest = block_rest(v, t, g_main, sp, x, lane, 8)
                out[x - 8] = here + retain * u[x, 8:40] + factor * rest

            loop(8, 40, 4, last)
        bufs = [(w, s), (v, t)]


def ring(value, axis, step):
    count = lax.axis_size(axis)
    return lax.ppermute(value, axis, [(i, (i + step) % count) for i in range(count)])


def trade(lo, hi, axis):
    return ring(hi, axis, 1), ring(lo, axis, -1)


def around(value, axis):
    return [value] + [ring(value, axis, step) for step in range(1, lax.axis_size(axis))]


def per_device(source, beta):
    lo = jnp.stack([source[0:8], beta[0:8]])
    hi = jnp.stack([source[24:32], beta[24:32]])
    lo, hi, source, beta = lax.optimization_barrier((lo, hi, source, beta))
    x_lo, x_hi = trade(lo, hi, "gx")
    beta2 = call(coarse_beta, sds(16, 128), [vm(32, 128)], name="coarse_beta")(beta)
    beta2_all = lax.all_gather(beta2, AXES)
    slab = sds(2, 48, 8, 128)
    mid = sds(48, 32, 128)
    lo, hi, s_mid, b_mid = call(pack_y, (slab, slab, mid, mid), name="pack_y", mib=4)(
        source, beta, x_lo, x_hi
    )
    y_lo, y_hi = trade(lo, hi, "gy")
    whole = sds(48, 48, 128)
    strip = sds(6, 48, 128)
    src_ext, beta_ext, lo, hi = call(
        pack_z, (whole, whole, strip, strip), name="pack_z", mib=4
    )(s_mid, b_mid, y_lo, y_hi)
    z_lo, z_hi = trade(lo, hi, "gz")
    iter0, iter0_t, c, lo, hi = call(
        level0_down,
        (whole, strip, sds(16, 16, 128), sds(10, 16, 128), sds(10, 16, 128)),
        LEVEL0_SCRATCH + [vm(48, 48, 128), vm(2, 16, 32, 128)],
        name="level0_down",
        mib=24,
    )(src_ext, beta_ext, z_lo, z_hi)
    x_lo, x_hi = trade(lo, hi, "gx")
    lo, hi = call(pack1_y, (sds(360, 128), sds(360, 128)), name="pack1_y")(c, x_lo, x_hi)
    y_lo, y_hi = trade(lo, hi, "gy")
    ext, lo, hi = call(
        pack1_z, (sds(36, 40, 128), sds(6, 40, 128), sds(6, 40, 128)), name="pack1_z"
    )(c, x_lo, x_hi, y_lo, y_hi)
    z1_lo, z1_hi = trade(lo, hi, "gz")
    iter1, chunk = call(
        level1_down,
        (sds(36, 40, 128), sds(16, 128)),
        LEVEL1_SCRATCH + [vm(36, 40, 128), vm(36, 40, 128), vm(8, 40, 128)],
        name="level1_down",
        mib=11,
    )(ext, z1_lo, z1_hi)
    chunk, beta2_all = lax.optimization_barrier((chunk, beta2_all))
    parts = around(chunk, "gz")
    coarse = call(
        coarse_prepare,
        tuple(sds(*shape) for shape in COARSE_SHAPES),
        COARSE_SCRATCH,
        name="coarse_prepare",
        mib=8,
    )(beta2_all)
    block = call(gather_z, sds(8, 8, 128), name="gather_z")(*parts)
    block, ext, z1_lo, z1_hi = lax.optimization_barrier((block, ext, z1_lo, z1_hi))
    parts = around(block, "gx")
    g1, sp1, beta1 = call(
        level1_prepare,
        (sds(6, 36, 40, 128), sds(36, 40, 128), sds(36, 40, 128)),
        [vm(38, 56, 128), vm(36, 40, 128)],
        name="level1_prepare",
        mib=4,
    )(ext, z1_lo, z1_hi)
    slab = call(gather_x, sds(32, 8, 128), name="gather_x")(*parts)
    slab, src_ext, beta_ext, z_lo, z_hi = lax.optimization_barrier(
        (slab, src_ext, beta_ext, z_lo, z_hi)
    )
    parts = around(slab, "gy")
    ready = call(
        level0_prepare,
        (sds(6, 48, 48, 128), sds(6, 6, 48, 128), whole, strip, strip),
        [vm(50, 64, 128), vm(6, 64, 128), vm(6, 48, 128), vm(6, 48, 128)],
        name="level0_prepare",
        mib=6,
    )(src_ext, beta_ext, z_lo, z_hi)
    c2 = call(bottom, sds(18, 24, 128), BOTTOM_SCRATCH, name="bottom", mib=18)(*parts, *coarse)
    c1 = call(
        level1_up,
        sds(24, 24, 128),
        [vm(38, 56, 128), vm(38, 56, 128), vm(36, 40, 128), vm(18, 24, 128), vm(18, 40, 128)],
        name="level1_up",
        mib=6,
    )(c2, g1, sp1, beta1, iter1)
    return call(
        level0_up,
        sds(32, 32, 128),
        [vm(50, 64, 128), vm(50, 64, 128), vm(6, 64, 128), vm(6, 64, 128), vm(6, 48, 128)]
        + [vm(48, 48, 128), vm(6, 48, 128), vm(24, 48, 128)],
        name="level0_up",
        mib=12,
    )(c1, beta_ext, *ready, iter0, iter0_t)


def solution(mesh):
    placed = (P(*AXES), P(*AXES))
    return jax.shard_map(
        per_device, mesh=mesh, in_specs=placed, out_specs=P(*AXES), check_vma=False
    )
```

```python
import jax
import jax.numpy as jnp
from jax import lax
from jax.experimental import pallas as pl
from jax.experimental.pallas import tpu as pltpu
from jax.sharding import PartitionSpec as P

SMOOTH = 4
BOTTOM = 12
LOW_EIG = 0.3
HIGH_EIG = 2.0
BOTTOM_LOW = 0.02

AXES = ("gx", "gy", "gz")
F32 = jnp.float32
MIB = 1024 * 1024


def cheb_plan(degree, lowest, highest):
    centre = 0.5 * (highest + lowest)
    radius = 0.5 * (highest - lowest)
    ratio_s = centre / radius
    rho_old = 1.0 / ratio_s
    recipe = [(0.0, 1.0 / centre)]
    for position in range(1, degree):
        rho_new = 1.0 / (2.0 * ratio_s - rho_old)
        recipe.append((rho_new * rho_old, 2.0 * rho_new / radius))
        rho_old = rho_new
    return recipe


RECIPE = cheb_plan(SMOOTH, LOW_EIG, HIGH_EIG)
BOTTOM_RECIPE = cheb_plan(BOTTOM, BOTTOM_LOW, HIGH_EIG)


def sds(*shape):
    return jax.ShapeDtypeStruct(shape, F32)


def vm(*shape):
    return pltpu.VMEM(shape, F32)


def call(body, outs, scratch=(), name=None, mib=2):
    return pl.pallas_call(
        body,
        out_shape=outs,
        scratch_shapes=list(scratch),
        compiler_params=pltpu.CompilerParams(vmem_limit_bytes=mib * MIB),
        name=name,
    )


def loop(low, high, vectors, body):
    count = high - low
    most = max(1, min(count, 72 // vectors))
    width = max([w for w in range(1, most + 1) if count % w == 0])
    if width * 2 < most:
        width = most
    rounds = count // width

    def chunk(i, carry):
        for k in range(width):
            body(low + i * width + k)
        return carry

    if rounds > 1:
        lax.fori_loop(0, rounds, chunk, 0)
    else:
        chunk(0, 0)
    for x in range(low + rounds * width, high):
        body(x)


def lanes_of(rows):
    return lax.broadcasted_iota(jnp.int32, (rows, 128), 1)


def roll(value, shift):
    if isinstance(shift, int):
        shift = shift % 128
        if shift == 0:
            return value
    return pltpu.roll(value, shift, 1)


def flag(condition):
    return jnp.where(condition, 1.0, 0.0).astype(F32)


def dot(left, right):
    return lax.dot_general(
        left,
        right,
        (((1,), (0,)), ((), ())),
        precision=lax.Precision.HIGHEST,
        preferred_element_type=F32,
    )


def pick(match):
    row = lax.broadcasted_iota(jnp.int32, (128, 128), 0)
    col = lax.broadcasted_iota(jnp.int32, (128, 128), 1)
    return jnp.where(match(row, col), 1.0, 0.0).astype(F32)


def coarse_beta(beta, out, rows):
    total = []
    for x in range(8):
        s = beta[4 * x] + beta[4 * x + 1] + beta[4 * x + 2] + beta[4 * x + 3]
        rows[...] = s
        t = rows[pl.ds(0, 8, stride=4), :] + rows[pl.ds(1, 8, stride=4), :]
        t = t + rows[pl.ds(2, 8, stride=4), :] + rows[pl.ds(3, 8, stride=4), :]
        total.append(t * (1.0 / 64.0))
    for half in range(2):
        acc = jnp.zeros((8, 128), F32)
        for quarter in range(4):
            weight = pick(lambda r, c: (r // 4 + 32 * quarter) == c)
            acc = acc + dot(total[half * 4 + quarter], weight)
        out[half * 8 : half * 8 + 8, :] = acc


def pack_y(src, beta, from_lo, from_hi, lo, hi, s_mid, b_mid):
    index = lax.axis_index("gx")
    low = flag(index > 0)
    high = flag(index < lax.axis_size("gx") - 1)
    for field, (ref, mid) in enumerate(((src, s_mid), (beta, b_mid))):
        mid[0:8] = from_lo[field] * low
        mid[8:40] = ref[...]
        mid[40:48] = from_hi[field] * high
        lo[field] = mid[:, 0:8, :]
        hi[field] = mid[:, 24:32, :]


def pack_z(s_mid, b_mid, y_lo, y_hi, s_out, b_out, lo, hi):
    iy = lax.axis_index("gy")
    y_low = flag(iy > 0)
    y_high = flag(iy < lax.axis_size("gy") - 1)
    for field, (mid, out) in enumerate(((s_mid, s_out), (b_mid, b_out))):
        out[:, 8:40, :] = mid[...]
        out[:, 0:8, :] = y_lo[field] * y_low
        out[:, 40:48, :] = y_hi[field] * y_high
    lane = lanes_of(48)

    def body(xx):
        acc_lo = jnp.zeros((48, 128), F32)
        acc_hi = jnp.zeros((48, 128), F32)
        for g in range(8):
            s = s_out[g * 6 + xx]
            b = b_out[g * 6 + xx]
            first = (lane >= g * 16) & (lane < g * 16 + 8)
            second = (lane >= g * 16 + 8) & (lane < g * 16 + 16)
            acc_lo = jnp.where(first, roll(s, g * 16), acc_lo)
            acc_lo = jnp.where(second, roll(b, g * 16 + 8), acc_lo)
            acc_hi = jnp.where(first, roll(s, g * 16 + 8), acc_hi)
            acc_hi = jnp.where(second, roll(b, g * 16 + 16), acc_hi)
        lo[xx] = acc_lo
        hi[xx] = acc_hi

    loop(0, 6, 36, body)


def strip_ghosts(values, ghost):
    lane = lanes_of(48)

    def body(xx):
        acc = jnp.zeros((48, 128), F32)
        for g in range(8):
            acc = jnp.where(lane // 16 == g, roll(values[g * 6 + xx + 1, 8:56, :], g * 16 + 8), acc)
        ghost[xx] = acc

    loop(0, 6, 36, body)


def strip_sides(strip, xx):
    after = strip[xx + 1, 8:56, :] if xx < 5 else roll(strip[0, 8:56, :], -16)
    before = strip[xx - 1, 8:56, :] if xx > 0 else roll(strip[5, 8:56, :], 16)
    return before, after


def strip_z(strip, ghost, xx, lane):
    here = strip[xx, 8:56, :]
    up = jnp.where(lane % 16 == 8, ghost[xx], roll(here, 1))
    down = jnp.where(lane % 16 == 7, ghost[xx], roll(here, -1))
    return down, up


def block_edge(strip, x, first=8, count=48):
    g = x // 6
    return roll(strip[x - g * 6, first : first + count, :], 120 - g * 16)


def weights(here, sides):
    sums = [here + side for side in sides]
    total = sums[0] + sums[1] + sums[2] + sums[3] + sums[4] + sums[5]
    inverse = jnp.where(here > 0.0, 1.0 / total, 0.0)
    return [s * inverse for s in sums], inverse, total


def level0_setup(b_pad, bt_pad, ghost, src, src_t, g_main, g_strip, sp, sp_t, total):
    strip_ghosts(b_pad, ghost)
    lane = lanes_of(48)

    def body(x):
        here = b_pad[x + 1, 8:56, :]
        edge = block_edge(bt_pad, x)
        down = jnp.where(lane == 0, edge, roll(here, 1))
        up = jnp.where(lane == 127, edge, roll(here, -1))
        faces, inverse, tot = weights(
            here,
            (
                b_pad[x, 8:56, :],
                b_pad[x + 2, 8:56, :],
                b_pad[x + 1, 7:55, :],
                b_pad[x + 1, 9:57, :],
                down,
                up,
            ),
        )
        for i in range(4):
            g_main[i, x] = faces[i]
        g_main[4, x] = jnp.where(lane == 0, 0.0, faces[4])
        g_main[5, x] = jnp.where(lane == 127, 0.0, faces[5])
        g_main[6, x] = jnp.where(lane == 0, faces[4], jnp.where(lane == 127, faces[5], 0.0))
        sp[x] = src[x] * (2.0 * inverse)
        if total is not None:
            total[x] = tot

    loop(0, 48, 12, body)
    for xx in range(6):
        before, after = strip_sides(bt_pad, xx)
        down, up = strip_z(bt_pad, ghost, xx, lane)
        faces, inverse, _ = weights(
            bt_pad[xx, 8:56, :],
            (before, after, bt_pad[xx, 7:55, :], bt_pad[xx, 9:57, :], down, up),
        )
        for i in range(6):
            g_strip[i, xx] = faces[i]
        sp_t[xx] = src_t[xx] * (2.0 * inverse)


def block_rest(v, t, g_main, sp, x, skip=0):
    count = 48 - 2 * skip
    first = 8 + skip
    keep = slice(skip, 48 - skip)
    here = v[x + 1, first : first + count, :]
    rest = sp[x, keep] - here
    rest = rest + g_main[0, x, keep] * v[x, first : first + count, :]
    rest = rest + g_main[1, x, keep] * v[x + 2, first : first + count, :]
    rest = rest + g_main[2, x, keep] * v[x + 1, first - 1 : first - 1 + count, :]
    rest = rest + g_main[3, x, keep] * v[x + 1, first + 1 : first + 1 + count, :]
    rest = rest + g_main[4, x, keep] * roll(here, 1) + g_main[5, x, keep] * roll(here, -1)
    rest = rest + g_main[6, x, keep] * block_edge(t, x, first, count)
    return here, rest


def level0_step(v, t, v_out, t_out, ghost, g_main, g_strip, sp, sp_t, u, u_t, low, high, retain, factor):
    strip_ghosts(v, ghost)
    lane = lanes_of(48)

    def body(x):
        here, rest = block_rest(v, t, g_main, sp, x)
        new = factor * rest
        if retain is not None:
            new = retain * u[x] + new
        u[x] = new
        v_out[x + 1, 8:56, :] = here + new

    loop(low, high, 6, body)
    for xx in range(6):
        here = t[xx, 8:56, :]
        before, after = strip_sides(t, xx)
        down, up = strip_z(t, ghost, xx, lane)
        rest = sp_t[xx] - here
        rest = rest + g_strip[0, xx] * before + g_strip[1, xx] * after
        rest = rest + g_strip[2, xx] * t[xx, 7:55, :] + g_strip[3, xx] * t[xx, 9:57, :]
        rest = rest + g_strip[4, xx] * down + g_strip[5, xx] * up
        new = factor * rest
        if retain is not None:
            new = retain * u_t[xx] + new
        u_t[xx] = new
        t_out[xx, 8:56, :] = here + new


def clear_edges(ref, planes, rows):
    width = ref.shape[1]
    ref[0] = jnp.zeros((width, 128), F32)
    ref[planes + 1] = jnp.zeros((width, 128), F32)

    def body(x):
        ref[x, 0:8, :] = jnp.zeros((8, 128), F32)
        ref[x, 8 + rows : width, :] = jnp.zeros((width - 8 - rows, 128), F32)

    loop(0, planes + 2, 4, body)


def clear_strip(ref):
    for xx in range(6):
        ref[xx, 0:8, :] = jnp.zeros((8, 128), F32)
        ref[xx, 56:64, :] = jnp.zeros((8, 128), F32)


def unpack_strip(z_lo, z_hi, src_t, bt_pad):
    iz = lax.axis_index("gz")
    low = flag(iz > 0)
    high = flag(iz < lax.axis_size("gz") - 1)

    def mirror(first, last):
        return pick(lambda r, c: (r // 16 == c // 16) & ((r % 16 < 8) == first) & (r % 16 + c % 16 == last))

    s_lo, s_hi = mirror(True, 15), mirror(True, 7)
    b_lo, b_hi = mirror(False, 23), mirror(False, 15)
    for xx in range(6):
        before = z_lo[xx] * low
        after = z_hi[xx] * high
        src_t[xx] = dot(before, s_lo) + dot(after, s_hi)
        bt_pad[xx, 8:56, :] = dot(before, b_lo) + dot(after, b_hi)


LEVEL0_SCRATCH = [
    vm(50, 64, 128),
    vm(6, 64, 128),
    vm(50, 64, 128),
    vm(50, 64, 128),
    vm(6, 64, 128),
    vm(6, 64, 128),
    vm(6, 48, 128),
    vm(7, 48, 48, 128),
    vm(6, 6, 48, 128),
    vm(48, 48, 128),
    vm(6, 48, 128),
    vm(48, 48, 128),
    vm(6, 48, 128),
    vm(6, 48, 128),
]


def level0_down(
    src, beta, z_lo, z_hi, iter_out, iter_t_out, c_out, c_lo, c_hi,
    b_pad, bt_pad, va, vb, ta, tb, ghost, g_main, g_strip, sp, sp_t, u, u_t, src_t, total, rows,
):
    for ref in (b_pad, va, vb):
        clear_edges(ref, 48, 48)
    for ref in (bt_pad, ta, tb):
        clear_strip(ref)
    b_pad[1:49, 8:56, :] = beta[...]
    unpack_strip(z_lo, z_hi, src_t, bt_pad)
    level0_setup(b_pad, bt_pad, ghost, src, src_t, g_main, g_strip, sp, sp_t, total)

    first = RECIPE[0][1]

    def start(x):
        u[x] = first * sp[x]
        va[x + 1, 8:56, :] = u[x]

    loop(0, 48, 8, start)
    for xx in range(6):
        u_t[xx] = first * sp_t[xx]
        ta[xx, 8:56, :] = u_t[xx]
    bufs = [(va, ta), (vb, tb)]
    for k in range(1, SMOOTH):
        (v, t), (w, s) = bufs
        retain, factor = RECIPE[k]
        level0_step(v, t, w, s, ghost, g_main, g_strip, sp, sp_t, u, u_t, 0, 48, retain, factor)
        bufs = [(w, s), (v, t)]
    v, t = bufs[0]
    iter_out[...] = v[1:49, 8:56, :]
    for xx in range(6):
        iter_t_out[xx] = t[xx, 8:56, :]

    to_low = pick(lambda r, c: r // 2 == c)
    to_high = pick(lambda r, c: r // 2 + 64 == c)

    def restrict(x2):
        parts = []
        for half in range(2):
            x = 8 + 2 * x2 + half
            _, rest = block_rest(v, t, g_main, sp, x, 8)
            parts.append(rest * total[x, 8:40])
        rows[0, x2] = (parts[0] + parts[1]) * (0.5 / 8.0)
        rows[1, x2] = (b_pad[9 + 2 * x2, 16:48, :] + b_pad[10 + 2 * x2, 16:48, :]) * (1.0 / 8.0)

    loop(0, 16, 8, restrict)

    def compress(x2):
        res = rows[0, x2, pl.ds(0, 16, stride=2), :] + rows[0, x2, pl.ds(1, 16, stride=2), :]
        bet = rows[1, x2, pl.ds(0, 16, stride=2), :] + rows[1, x2, pl.ds(1, 16, stride=2), :]
        c_out[x2] = dot(res, to_low) + dot(bet, to_high)

    loop(0, 16, 8, compress)
    c_lo[...] = c_out[0:10]
    c_hi[...] = c_out[6:16]


def pack1_y(c, from_lo, from_hi, lo, hi):
    index = lax.axis_index("gx")
    low = flag(index > 0)
    high = flag(index < lax.axis_size("gx") - 1)
    for x in range(36):
        if x < 10:
            plane = from_lo[x] * low
        elif x < 26:
            plane = c[x - 10]
        else:
            plane = from_hi[x - 26] * high
        lo[x * 10 : x * 10 + 10, :] = plane[0:10]
        hi[x * 10 : x * 10 + 10, :] = plane[6:16]


def pack1_z(c, x_lo, x_hi, y_lo, y_hi, ext, lo, hi):
    ix = lax.axis_index("gx")
    iy = lax.axis_index("gy")
    x_low = flag(ix > 0)
    x_high = flag(ix < lax.axis_size("gx") - 1)
    y_low = flag(iy > 0)
    y_high = flag(iy < lax.axis_size("gy") - 1)
    ext[0:10, 10:26, :] = x_lo[...] * x_low
    ext[10:26, 10:26, :] = c[...]
    ext[26:36, 10:26, :] = x_hi[...] * x_high
    for x in range(36):
        ext[x, 0:10, :] = y_lo[x * 10 : x * 10 + 10, :] * y_low
        ext[x, 26:36, :] = y_hi[x * 10 : x * 10 + 10, :] * y_high
        ext[x, 36:40, :] = jnp.zeros((4, 128), F32)
    lane = lanes_of(40)

    def body(xx):
        acc_lo = jnp.zeros((40, 128), F32)
        acc_hi = jnp.zeros((40, 128), F32)
        for g in range(6):
            e = ext[g * 6 + xx]
            first = (lane >= g * 20) & (lane < g * 20 + 10)
            second = (lane >= g * 20 + 10) & (lane < g * 20 + 20)
            middle = roll(e, g * 20 - 54)
            acc_lo = jnp.where(first, roll(e, g * 20), acc_lo)
            acc_lo = jnp.where(second, middle, acc_lo)
            acc_hi = jnp.where(first, middle, acc_hi)
            acc_hi = jnp.where(second, roll(e, g * 20 + 20), acc_hi)
        lo[xx] = acc_lo
        hi[xx] = acc_hi

    loop(0, 6, 36, body)


def ring_weights(b_pad, src, g, sp, total, planes, rows, scale, edges=None):
    lane = lanes_of(rows)

    def body(x):
        here = b_pad[x + 1, 8 : 8 + rows, :]
        down = roll(here, 1)
        up = roll(here, -1)
        if edges is not None:
            down = jnp.where(lane == 0, 0.0, down)
            up = jnp.where(lane == 127, 0.0, up)
        faces, inverse, tot = weights(
            here,
            (
                b_pad[x, 8 : 8 + rows, :],
                b_pad[x + 2, 8 : 8 + rows, :],
                b_pad[x + 1, 7 : 7 + rows, :],
                b_pad[x + 1, 9 : 9 + rows, :],
                down,
                up,
            ),
        )
        if edges is not None:
            faces[4] = jnp.where(lane == 0, 0.0, faces[4])
            faces[5] = jnp.where(lane == 127, 0.0, faces[5])
        for i in range(6):
            g[i, x] = faces[i]
        sp[x] = scale * 2.0 * inverse if src is None else src[x] * (scale * 2.0 * inverse)
        if total is not None:
            total[x] = tot

    loop(0, planes, rows // 4, body)


def ring_rest(v, g, sp, x, rows):
    here = v[x + 1, 8 : 8 + rows, :]
    rest = sp[x] - here
    rest = rest + g[0, x] * v[x, 8 : 8 + rows, :] + g[1, x] * v[x + 2, 8 : 8 + rows, :]
    rest = rest + g[2, x] * v[x + 1, 7 : 7 + rows, :] + g[3, x] * v[x + 1, 9 : 9 + rows, :]
    rest = rest + g[4, x] * roll(here, 1) + g[5, x] * roll(here, -1)
    return here, rest


def ring_step(v, v_out, g, sp, u, planes, rows, retain, factor):
    def body(x):
        here, rest = ring_rest(v, g, sp, x, rows)
        new = factor * rest
        if retain is not None:
            new = retain * u[x] + new
        u[x] = new
        v_out[x + 1, 8 : 8 + rows, :] = here + new

    loop(0, planes, rows // 16, body)


def ring_zero_start(v, u, sp, planes, rows, factor):
    def body(x):
        u[x] = factor * sp[x]
        v[x + 1, 8 : 8 + rows, :] = u[x]

    loop(0, planes, rows // 8, body)


def ring_cheb(va, vb, g, sp, u, planes, rows, recipe, from_zero):
    begin = 0
    if from_zero:
        ring_zero_start(va, u, sp, planes, rows, recipe[0][1])
        begin = 1
    for k in range(begin, len(recipe)):
        retain, factor = recipe[k]
        ring_step(va, vb, g, sp, u, planes, rows, None if k == 0 else retain, factor)
        va, vb = vb, va
    return va


LEVEL1_SCRATCH = [
    vm(38, 56, 128),
    vm(38, 56, 128),
    vm(38, 56, 128),
    vm(6, 36, 40, 128),
    vm(36, 40, 128),
    vm(36, 40, 128),
]


def level1_unpack(ext, z_lo, z_hi, source, b_pad, beta_out):
    iz = lax.axis_index("gz")
    low = flag(iz > 0)
    high = flag(iz < lax.axis_size("gz") - 1)
    lane = lanes_of(40)
    inner = lane < 64
    above = (lane >= 64) & (lane < 74)
    below = lane >= 118

    def unpack(xx):
        before = z_lo[xx] * low
        after = z_hi[xx] * high
        for k in range(6):
            x = k * 6 + xx
            e = ext[x]
            s = jnp.where(inner, e, 0.0)
            s = jnp.where(above, roll(after, 64 - k * 20), s)
            s = jnp.where(below, roll(before, 118 - k * 20), s)
            b = jnp.where(inner, roll(e, 64), 0.0)
            b = jnp.where(above, roll(after, 54 - k * 20), b)
            b = jnp.where(below, roll(before, 108 - k * 20), b)
            source[x] = s
            b_pad[x + 1, 8:48, :] = b
            if beta_out is not None:
                beta_out[x] = b

    loop(0, 6, 36, unpack)


def level1_down(
    ext, z_lo, z_hi, iter_out, chunk,
    b_pad, va, vb, g, sp, u, src, total, rows,
):
    for ref in (b_pad, va, vb):
        clear_edges(ref, 36, 40)
    level1_unpack(ext, z_lo, z_hi, src, b_pad, None)
    ring_weights(b_pad, src, g, sp, total, 36, 40, 4.0)
    v = ring_cheb(va, vb, g, sp, u, 36, 40, RECIPE, True)
    iter_out[...] = v[1:37, 8:48, :]
    summed = []
    for x2 in range(8):
        parts = []
        for half in range(2):
            x = 10 + 2 * x2 + half
            _, rest = ring_rest(v, g, sp, x, 40)
            parts.append(rest * total[x])
        rows[x2] = (parts[0] + parts[1]) * (0.25 * 0.5 / 8.0)
        summed.append(rows[x2, pl.ds(10, 8, stride=2), :] + rows[x2, pl.ds(11, 8, stride=2), :])
    for half in range(2):
        acc = jnp.zeros((8, 128), F32)
        for quarter in range(4):
            weight = pick(lambda r, c: (r < 64) & ((r // 2 + 32 * quarter) == c))
            acc = acc + dot(summed[half * 4 + quarter], weight)
        chunk[half * 8 : half * 8 + 8, :] = acc


def level1_prepare(ext, z_lo, z_hi, g, sp, beta_out, b_pad, src):
    clear_edges(b_pad, 36, 40)
    level1_unpack(ext, z_lo, z_hi, src, b_pad, beta_out)
    ring_weights(b_pad, src, g, sp, None, 36, 40, 4.0)


def sender(axis, step):
    count = lax.axis_size(axis)
    return lax.rem(lax.axis_index(axis) + count - step, count)


def gather_z(*refs):
    *parts, out = refs
    lane = lanes_of(8)
    for half in range(2):
        for quarter in range(4):
            acc = jnp.zeros((8, 128), F32)
            for step, part in enumerate(parts):
                owner = sender("gz", step)
                moved = roll(part[half * 8 : half * 8 + 8, :], lax.rem(owner - quarter + 4, 4) * 32)
                acc = jnp.where(lane // 32 == owner, moved, acc)
            out[half * 4 + quarter] = acc


def gather_x(*refs):
    *parts, out = refs
    for step, part in enumerate(parts):
        out[pl.ds(sender("gx", step) * 8, 8)] = part[...]


def gather_y(parts, out):
    for step, part in enumerate(parts):
        row = pl.multiple_of(8 + sender("gy", step) * 8, 8)
        out[8:40, pl.ds(row, 8), :] = part[...]


def whole_grid(parts, out, x_pad):
    lane = lanes_of(8)

    def body(i):
        gx = i // 8
        gy = i - gx * 8
        for half in range(2):
            blocks = [parts[i * 4 + gz, half * 8 : half * 8 + 8, :] for gz in range(4)]
            for quarter in range(4):
                acc = roll(blocks[0], -quarter * 32)
                for gz in range(1, 4):
                    acc = jnp.where(lane // 32 == gz, roll(blocks[gz], (gz - quarter) * 32), acc)
                row = pl.multiple_of(8 + gy * 8, 8)
                out[gx * 8 + half * 4 + quarter + x_pad, pl.ds(row, 8), :] = acc

    loop(0, 32, 18, body)


def clear_whole(ref):
    def clear(x):
        ref[x, 0:8, :] = jnp.zeros((8, 128), F32)
        ref[x, 72:80, :] = jnp.zeros((8, 128), F32)

    loop(0, 48, 2, clear)
    for x in [*range(8), *range(40, 48)]:
        ref[x, 8:72, :] = jnp.zeros((64, 128), F32)


def coarse_prepare(b_parts, g, inv, total, g3, inv3, gw, invw, b2, b3, bw, rows):
    clear_whole(b2)
    clear_edges(b3, 16, 32)
    clear_edges(bw, 22, 24)
    whole_grid(b_parts, b2, 8)
    ring_weights(b2.at[7:41], None, g, inv, total, 32, 64, 16.0, edges=True)
    half_z = pick(lambda r, c: r // 2 == c)

    def restrict(x2):
        rows[x2] = (b2[8 + 2 * x2, 8:72, :] + b2[9 + 2 * x2, 8:72, :]) * (1.0 / 8.0)

    loop(0, 16, 8, restrict)

    def compress(x2):
        bet = rows[x2, pl.ds(0, 32, stride=2), :] + rows[x2, pl.ds(1, 32, stride=2), :]
        b3[x2 + 1, 8:40, :] = dot(bet, half_z)

    loop(0, 16, 9, compress)
    ring_weights(b3, None, g3, inv3, None, 16, 32, 64.0)
    ix = lax.axis_index("gx")
    row = pl.multiple_of(lax.axis_index("gy") * 8, 8)

    def window(x):
        bw[x + 1, 8:32, :] = b2[ix * 8 + 1 + x, pl.ds(row, 24), :]

    loop(0, 22, 6, window)
    ring_weights(bw, None, gw, invw, None, 22, 24, 16.0, edges=True)


COARSE_SHAPES = [
    (6, 32, 64, 128),
    (32, 64, 128),
    (32, 64, 128),
    (6, 16, 32, 128),
    (16, 32, 128),
    (6, 22, 24, 128),
    (22, 24, 128),
]


def bottom(
    p0, p1, p2, p3, p4, p5, p6, p7, g, inv, total, g3, inv3, gw, invw, out,
    s2, va, vb, sp, u, v3a, v3b, sp3, u3, rows, wa, wb, spw, uw,
):
    for ref in (s2, va, vb):
        clear_whole(ref)
    gather_y((p0, p1, p2, p3, p4, p5, p6, p7), s2)

    def scale(x):
        sp[x] = s2[x + 8, 8:72, :] * inv[x]

    loop(0, 32, 8, scale)
    v = ring_cheb(va.at[7:41], vb.at[7:41], g, sp, u, 32, 64, RECIPE, True)
    iterate = vb if SMOOTH % 2 == 0 else va

    clear_edges(v3a, 16, 32)
    clear_edges(v3b, 16, 32)
    half_z = pick(lambda r, c: r // 2 == c)

    def restrict(x2):
        parts = []
        for half in range(2):
            x = 2 * x2 + half
            _, rest = ring_rest(v, g, sp, x, 64)
            parts.append(rest * total[x])
        rows[x2] = (parts[0] + parts[1]) * (0.0625 * 0.5 / 8.0)

    loop(0, 16, 16, restrict)

    def compress(x2):
        res = rows[x2, pl.ds(0, 32, stride=2), :] + rows[x2, pl.ds(1, 32, stride=2), :]
        sp3[x2] = dot(res, half_z) * inv3[x2]

    loop(0, 16, 9, compress)
    c3 = ring_cheb(v3a, v3b, g3, sp3, u3, 16, 32, BOTTOM_RECIPE, True)

    other = va if iterate is vb else vb
    double_z = pick(lambda r, c: c // 2 == r)

    def prolong(x3):
        wide = dot(c3[x3 + 1, 8:40, :], double_z)
        rows[x3, pl.ds(0, 32, stride=2), :] = wide
        rows[x3, pl.ds(1, 32, stride=2), :] = wide
        for half in range(2):
            x = 8 + 2 * x3 + half
            other[x, 8:72, :] = iterate[x, 8:72, :] + rows[x3]

    loop(0, 16, 18, prolong)
    ix = lax.axis_index("gx")
    iz = lax.axis_index("gz")
    clear_edges(wa, 22, 24)
    clear_edges(wb, 22, 24)
    row = pl.multiple_of(lax.axis_index("gy") * 8, 8)

    def window(x):
        plane = ix * 8 + 1 + x
        wa[x + 1, 8:32, :] = other[plane, pl.ds(row, 24), :]
        spw[x] = s2[plane, pl.ds(row, 24), :] * invw[x]

    loop(0, 22, 6, window)
    c2 = ring_cheb(wa, wb, gw, spw, uw, 22, 24, RECIPE, False)
    shift = (128 - iz * 32) % 128
    for x in range(18):
        out[x] = roll(c2[x + 3, 8:32, :], shift)


COARSE_SCRATCH = [
    vm(48, 80, 128),
    vm(18, 48, 128),
    vm(24, 40, 128),
    vm(16, 64, 128),
]
BOTTOM_SCRATCH = [
    vm(48, 80, 128),
    vm(48, 80, 128),
    vm(48, 80, 128),
    vm(32, 64, 128),
    vm(32, 64, 128),
    vm(18, 48, 128),
    vm(18, 48, 128),
    vm(16, 32, 128),
    vm(16, 32, 128),
    vm(16, 64, 128),
    vm(24, 40, 128),
    vm(24, 40, 128),
    vm(22, 24, 128),
    vm(22, 24, 128),
]


def level1_up(c2, g, sp, beta, iterate, out, va, vb, u, wide, rows):
    for ref in (va, vb):
        clear_edges(ref, 36, 40)
    spread = pick(lambda r, c: ((c < 74) & (c // 2 == r)) | ((c >= 118) & (c // 2 + 64 == r)))
    for x2 in range(18):
        rows[x2, 32:40, :] = jnp.zeros((8, 128), F32)

    def prolong(x2):
        wide[x2] = dot(c2[x2], spread)
        part = wide[x2, 3:21, :]
        rows[x2, pl.ds(0, 18, stride=2), :] = part
        rows[x2, pl.ds(1, 18, stride=2), :] = part
        for half in range(2):
            x = 2 * x2 + half
            va[x + 1, 8:48, :] = jnp.where(beta[x] > 0.0, iterate[x] + rows[x2], 0.0)

    loop(0, 18, 12, prolong)
    v = ring_cheb(va, vb, g, sp, u, 36, 40, RECIPE, False)
    out[...] = v[7:31, 14:38, :]


def level0_prepare(src, beta, z_lo, z_hi, g_main, g_strip, sp, sp_t, bt_out, b_pad, bt_pad, ghost, src_t):
    clear_edges(b_pad, 48, 48)
    clear_strip(bt_pad)
    b_pad[1:49, 8:56, :] = beta[...]
    unpack_strip(z_lo, z_hi, src_t, bt_pad)
    for xx in range(6):
        bt_out[xx] = bt_pad[xx, 8:56, :]
    level0_setup(b_pad, bt_pad, ghost, src, src_t, g_main, g_strip, sp, sp_t, None)


def level0_up(
    c1, beta, g_main, g_strip, sp, sp_t, beta_t, iterate, iterate_t, out,
    va, vb, ta, tb, ghost, u, u_t, rows,
):
    for ref in (va, vb):
        clear_edges(ref, 48, 48)
    for ref in (ta, tb):
        clear_strip(ref)
    spread = pick(lambda r, c: c // 2 == r)

    def prolong(x1):
        wide = dot(c1[x1], spread)
        rows[x1, pl.ds(0, 24, stride=2), :] = wide
        rows[x1, pl.ds(1, 24, stride=2), :] = wide
        for half in range(2):
            x = 2 * x1 + half
            va[x + 1, 8:56, :] = jnp.where(beta[x] > 0.0, iterate[x] + rows[x1], 0.0)

    loop(0, 24, 12, prolong)

    def prolong_strip(m):
        acc = jnp.zeros((24, 128), F32)
        for k in range(8):
            to = pick(
                lambda r, c: (c // 16 == k)
                & (
                    ((c % 16 < 8) & (r == 64 + (7 - c % 16) // 2))
                    | ((c % 16 >= 8) & (r == 124 + (15 - c % 16) // 2))
                )
            )
            acc = acc + dot(c1[k * 3 + m], to)
        rows[m, pl.ds(0, 24, stride=2), :] = acc
        rows[m, pl.ds(1, 24, stride=2), :] = acc
        for half in range(2):
            xx = 2 * m + half
            ta[xx, 8:56, :] = jnp.where(beta_t[xx] > 0.0, iterate_t[xx] + rows[m], 0.0)

    loop(0, 3, 36, prolong_strip)
    for x in [*range(6), *range(42, 48)]:
        vb[x + 1, 8:56, :] = jnp.zeros((48, 128), F32)
    bufs = [(va, ta), (vb, tb)]
    for k in range(SMOOTH):
        (v, t), (w, s) = bufs
        retain, factor = RECIPE[k]
        if k == 0:
            retain = None
        if k < SMOOTH - 1:
            low, high = (4, 44) if k < 2 else (6, 42)
            level0_step(
                v, t, w, s, ghost, g_main, g_strip, sp, sp_t, u, u_t, low, high, retain, factor
            )
        else:

            def last(x):
                here, rest = block_rest(v, t, g_main, sp, x, 8)
                out[x - 8] = here + retain * u[x, 8:40] + factor * rest

            loop(8, 40, 4, last)
        bufs = [(w, s), (v, t)]


def ring(value, axis, step):
    count = lax.axis_size(axis)
    return lax.ppermute(value, axis, [(i, (i + step) % count) for i in range(count)])


def trade(lo, hi, axis):
    return ring(hi, axis, 1), ring(lo, axis, -1)


def around(value, axis):
    return [value] + [ring(value, axis, step) for step in range(1, lax.axis_size(axis))]


def per_device(source, beta):
    lo = jnp.stack([source[0:8], beta[0:8]])
    hi = jnp.stack([source[24:32], beta[24:32]])
    lo, hi, source, beta = lax.optimization_barrier((lo, hi, source, beta))
    x_lo, x_hi = trade(lo, hi, "gx")
    beta2 = call(coarse_beta, sds(16, 128), [vm(32, 128)], name="coarse_beta")(beta)
    beta2_all = lax.all_gather(beta2, AXES)
    slab = sds(2, 48, 8, 128)
    mid = sds(48, 32, 128)
    lo, hi, s_mid, b_mid = call(pack_y, (slab, slab, mid, mid), name="pack_y", mib=4)(
        source, beta, x_lo, x_hi
    )
    y_lo, y_hi = trade(lo, hi, "gy")
    whole = sds(48, 48, 128)
    strip = sds(6, 48, 128)
    src_ext, beta_ext, lo, hi = call(
        pack_z, (whole, whole, strip, strip), name="pack_z", mib=4
    )(s_mid, b_mid, y_lo, y_hi)
    z_lo, z_hi = trade(lo, hi, "gz")
    iter0, iter0_t, c, lo, hi = call(
        level0_down,
        (whole, strip, sds(16, 16, 128), sds(10, 16, 128), sds(10, 16, 128)),
        LEVEL0_SCRATCH + [vm(48, 48, 128), vm(2, 16, 32, 128)],
        name="level0_down",
        mib=26,
    )(src_ext, beta_ext, z_lo, z_hi)
    x_lo, x_hi = trade(lo, hi, "gx")
    lo, hi = call(pack1_y, (sds(360, 128), sds(360, 128)), name="pack1_y")(c, x_lo, x_hi)
    y_lo, y_hi = trade(lo, hi, "gy")
    ext, lo, hi = call(
        pack1_z, (sds(36, 40, 128), sds(6, 40, 128), sds(6, 40, 128)), name="pack1_z"
    )(c, x_lo, x_hi, y_lo, y_hi)
    z1_lo, z1_hi = trade(lo, hi, "gz")
    iter1, chunk = call(
        level1_down,
        (sds(36, 40, 128), sds(16, 128)),
        LEVEL1_SCRATCH + [vm(36, 40, 128), vm(36, 40, 128), vm(8, 40, 128)],
        name="level1_down",
        mib=11,
    )(ext, z1_lo, z1_hi)
    chunk, beta2_all = lax.optimization_barrier((chunk, beta2_all))
    parts = around(chunk, "gz")
    coarse = call(
        coarse_prepare,
        tuple(sds(*shape) for shape in COARSE_SHAPES),
        COARSE_SCRATCH,
        name="coarse_prepare",
        mib=8,
    )(beta2_all)
    block = call(gather_z, sds(8, 8, 128), name="gather_z")(*parts)
    block, ext, z1_lo, z1_hi = lax.optimization_barrier((block, ext, z1_lo, z1_hi))
    parts = around(block, "gx")
    g1, sp1, beta1 = call(
        level1_prepare,
        (sds(6, 36, 40, 128), sds(36, 40, 128), sds(36, 40, 128)),
        [vm(38, 56, 128), vm(36, 40, 128)],
        name="level1_prepare",
        mib=4,
    )(ext, z1_lo, z1_hi)
    slab = call(gather_x, sds(32, 8, 128), name="gather_x")(*parts)
    slab, src_ext, beta_ext, z_lo, z_hi = lax.optimization_barrier(
        (slab, src_ext, beta_ext, z_lo, z_hi)
    )
    parts = around(slab, "gy")
    ready = call(
        level0_prepare,
        (sds(7, 48, 48, 128), sds(6, 6, 48, 128), whole, strip, strip),
        [vm(50, 64, 128), vm(6, 64, 128), vm(6, 48, 128), vm(6, 48, 128)],
        name="level0_prepare",
        mib=6,
    )(src_ext, beta_ext, z_lo, z_hi)
    c2 = call(bottom, sds(18, 24, 128), BOTTOM_SCRATCH, name="bottom", mib=18)(*parts, *coarse)
    c1 = call(
        level1_up,
        sds(24, 24, 128),
        [vm(38, 56, 128), vm(38, 56, 128), vm(36, 40, 128), vm(18, 24, 128), vm(18, 40, 128)],
        name="level1_up",
        mib=6,
    )(c2, g1, sp1, beta1, iter1)
    return call(
        level0_up,
        sds(32, 32, 128),
        [vm(50, 64, 128), vm(50, 64, 128), vm(6, 64, 128), vm(6, 64, 128), vm(6, 48, 128)]
        + [vm(48, 48, 128), vm(6, 48, 128), vm(24, 48, 128)],
        name="level0_up",
        mib=12,
    )(c1, beta_ext, *ready, iter0, iter0_t)


def solution(mesh):
    placed = (P(*AXES), P(*AXES))
    return jax.shard_map(
        per_device, mesh=mesh, in_specs=placed, out_specs=P(*AXES), check_vma=False
    )
```

```python
import jax
import jax.numpy as jnp
from jax import lax
from jax.experimental import pallas as pl
from jax.experimental.pallas import tpu as pltpu
from jax.sharding import PartitionSpec as P

SMOOTH = 4
BOTTOM = 12
LOW_EIG = 0.3
HIGH_EIG = 2.0
BOTTOM_LOW = 0.02

AXES = ("gx", "gy", "gz")
F32 = jnp.float32
MIB = 1024 * 1024


def cheb_plan(degree, lowest, highest):
    centre = 0.5 * (highest + lowest)
    radius = 0.5 * (highest - lowest)
    ratio_s = centre / radius
    rho_old = 1.0 / ratio_s
    recipe = [(0.0, 1.0 / centre)]
    for position in range(1, degree):
        rho_new = 1.0 / (2.0 * ratio_s - rho_old)
        recipe.append((rho_new * rho_old, 2.0 * rho_new / radius))
        rho_old = rho_new
    return recipe


RECIPE = cheb_plan(SMOOTH, LOW_EIG, HIGH_EIG)
BOTTOM_RECIPE = cheb_plan(BOTTOM, BOTTOM_LOW, HIGH_EIG)


def sds(*shape):
    return jax.ShapeDtypeStruct(shape, F32)


def vm(*shape):
    return pltpu.VMEM(shape, F32)


def call(body, outs, scratch=(), name=None, mib=2, last_unread=None):
    specs = {}
    if last_unread:
        whole = pl.BlockSpec(memory_space=pltpu.VMEM)
        specs["in_specs"] = [whole] * (last_unread - 1) + [pl.BlockSpec(memory_space=pl.ANY)]
    return pl.pallas_call(
        body,
        out_shape=outs,
        **specs,
        scratch_shapes=list(scratch),
        compiler_params=pltpu.CompilerParams(vmem_limit_bytes=mib * MIB),
        name=name,
    )


def loop(low, high, vectors, body):
    count = high - low
    most = max(1, min(count, 72 // vectors))
    width = max([w for w in range(1, most + 1) if count % w == 0])
    if width * 2 < most:
        width = most
    rounds = count // width

    def chunk(i, carry):
        for k in range(width):
            body(low + i * width + k)
        return carry

    if rounds > 1:
        lax.fori_loop(0, rounds, chunk, 0)
    else:
        chunk(0, 0)
    for x in range(low + rounds * width, high):
        body(x)


def lanes_of(rows):
    return lax.broadcasted_iota(jnp.int32, (rows, 128), 1)


def roll(value, shift):
    if isinstance(shift, int):
        shift = shift % 128
        if shift == 0:
            return value
    return pltpu.roll(value, shift, 1)


def flag(condition):
    return jnp.where(condition, 1.0, 0.0).astype(F32)


def dot(left, right):
    return lax.dot_general(
        left,
        right,
        (((1,), (0,)), ((), ())),
        precision=lax.Precision.HIGHEST,
        preferred_element_type=F32,
    )


def pick(match):
    row = lax.broadcasted_iota(jnp.int32, (128, 128), 0)
    col = lax.broadcasted_iota(jnp.int32, (128, 128), 1)
    return jnp.where(match(row, col), 1.0, 0.0).astype(F32)


def coarse_beta(beta, out, rows):
    total = []
    for x in range(8):
        s = beta[4 * x] + beta[4 * x + 1] + beta[4 * x + 2] + beta[4 * x + 3]
        rows[...] = s
        t = rows[pl.ds(0, 8, stride=4), :] + rows[pl.ds(1, 8, stride=4), :]
        t = t + rows[pl.ds(2, 8, stride=4), :] + rows[pl.ds(3, 8, stride=4), :]
        total.append(t * (1.0 / 64.0))
    for half in range(2):
        acc = jnp.zeros((8, 128), F32)
        for quarter in range(4):
            weight = pick(lambda r, c: (r // 4 + 32 * quarter) == c)
            acc = acc + dot(total[half * 4 + quarter], weight)
        out[half * 8 : half * 8 + 8, :] = acc


def pack_y(src, beta, from_lo, from_hi, lo, hi, s_mid, b_mid):
    index = lax.axis_index("gx")
    low = flag(index > 0)
    high = flag(index < lax.axis_size("gx") - 1)
    for field, (ref, mid) in enumerate(((src, s_mid), (beta, b_mid))):
        mid[0:8] = from_lo[field] * low
        mid[8:40] = ref[...]
        mid[40:48] = from_hi[field] * high
        lo[field] = mid[:, 0:8, :]
        hi[field] = mid[:, 24:32, :]


def pack_z(s_mid, b_mid, y_lo, y_hi, s_out, b_out, lo, hi):
    iy = lax.axis_index("gy")
    y_low = flag(iy > 0)
    y_high = flag(iy < lax.axis_size("gy") - 1)
    for field, (mid, out) in enumerate(((s_mid, s_out), (b_mid, b_out))):
        out[:, 8:40, :] = mid[...]
        out[:, 0:8, :] = y_lo[field] * y_low
        out[:, 40:48, :] = y_hi[field] * y_high
    lane = lanes_of(48)

    def body(xx):
        acc_lo = jnp.zeros((48, 128), F32)
        acc_hi = jnp.zeros((48, 128), F32)
        for g in range(8):
            s = s_out[g * 6 + xx]
            b = b_out[g * 6 + xx]
            first = (lane >= g * 16) & (lane < g * 16 + 8)
            second = (lane >= g * 16 + 8) & (lane < g * 16 + 16)
            acc_lo = jnp.where(first, roll(s, g * 16), acc_lo)
            acc_lo = jnp.where(second, roll(b, g * 16 + 8), acc_lo)
            acc_hi = jnp.where(first, roll(s, g * 16 + 8), acc_hi)
            acc_hi = jnp.where(second, roll(b, g * 16 + 16), acc_hi)
        lo[xx] = acc_lo
        hi[xx] = acc_hi

    loop(0, 6, 36, body)


def strip_ghosts(values, ghost):
    lane = lanes_of(48)

    def body(xx):
        acc = jnp.zeros((48, 128), F32)
        for g in range(8):
            acc = jnp.where(lane // 16 == g, roll(values[g * 6 + xx + 1, 8:56, :], g * 16 + 8), acc)
        ghost[xx] = acc

    loop(0, 6, 36, body)


def strip_sides(strip, xx):
    after = strip[xx + 1, 8:56, :] if xx < 5 else roll(strip[0, 8:56, :], -16)
    before = strip[xx - 1, 8:56, :] if xx > 0 else roll(strip[5, 8:56, :], 16)
    return before, after


def strip_z(strip, ghost, xx, lane):
    here = strip[xx, 8:56, :]
    up = jnp.where(lane % 16 == 8, ghost[xx], roll(here, 1))
    down = jnp.where(lane % 16 == 7, ghost[xx], roll(here, -1))
    return down, up


def block_edge(strip, x, first=8, count=48):
    g = x // 6
    return roll(strip[x - g * 6, first : first + count, :], 120 - g * 16)


def weights(here, sides):
    sums = [here + side for side in sides]
    total = sums[0] + sums[1] + sums[2] + sums[3] + sums[4] + sums[5]
    inverse = jnp.where(here > 0.0, 1.0 / total, 0.0)
    return [s * inverse for s in sums], inverse, total


def level0_setup(b_pad, bt_pad, ghost, src, src_t, g_main, g_strip, sp, sp_t, total):
    strip_ghosts(b_pad, ghost)
    lane = lanes_of(48)

    def body(x):
        here = b_pad[x + 1, 8:56, :]
        edge = block_edge(bt_pad, x)
        down = jnp.where(lane == 0, edge, roll(here, 1))
        up = jnp.where(lane == 127, edge, roll(here, -1))
        faces, inverse, tot = weights(
            here,
            (
                b_pad[x, 8:56, :],
                b_pad[x + 2, 8:56, :],
                b_pad[x + 1, 7:55, :],
                b_pad[x + 1, 9:57, :],
                down,
                up,
            ),
        )
        for i in range(4):
            g_main[i, x] = faces[i]
        g_main[4, x] = jnp.where(lane == 0, 0.0, faces[4])
        g_main[5, x] = jnp.where(lane == 127, 0.0, faces[5])
        g_main[6, x] = jnp.where(lane == 0, faces[4], jnp.where(lane == 127, faces[5], 0.0))
        sp[x] = src[x] * (2.0 * inverse)
        if total is not None:
            total[x] = tot

    loop(0, 48, 12, body)
    for xx in range(6):
        before, after = strip_sides(bt_pad, xx)
        down, up = strip_z(bt_pad, ghost, xx, lane)
        faces, inverse, _ = weights(
            bt_pad[xx, 8:56, :],
            (before, after, bt_pad[xx, 7:55, :], bt_pad[xx, 9:57, :], down, up),
        )
        for i in range(6):
            g_strip[i, xx] = faces[i]
        sp_t[xx] = src_t[xx] * (2.0 * inverse)


def block_rest(v, t, g_main, sp, x, skip=0):
    count = 48 - 2 * skip
    first = 8 + skip
    keep = slice(skip, 48 - skip)
    here = v[x + 1, first : first + count, :]
    rest = sp[x, keep] - here
    rest = rest + g_main[0, x, keep] * v[x, first : first + count, :]
    rest = rest + g_main[1, x, keep] * v[x + 2, first : first + count, :]
    rest = rest + g_main[2, x, keep] * v[x + 1, first - 1 : first - 1 + count, :]
    rest = rest + g_main[3, x, keep] * v[x + 1, first + 1 : first + 1 + count, :]
    rest = rest + g_main[4, x, keep] * roll(here, 1) + g_main[5, x, keep] * roll(here, -1)
    rest = rest + g_main[6, x, keep] * block_edge(t, x, first, count)
    return here, rest


def level0_step(v, t, v_out, t_out, ghost, g_main, g_strip, sp, sp_t, u, u_t, low, high, retain, factor):
    strip_ghosts(v, ghost)
    lane = lanes_of(48)

    def body(x):
        here, rest = block_rest(v, t, g_main, sp, x)
        new = factor * rest
        if retain is not None:
            new = retain * u[x] + new
        u[x] = new
        v_out[x + 1, 8:56, :] = here + new

    loop(low, high, 6, body)
    for xx in range(6):
        here = t[xx, 8:56, :]
        before, after = strip_sides(t, xx)
        down, up = strip_z(t, ghost, xx, lane)
        rest = sp_t[xx] - here
        rest = rest + g_strip[0, xx] * before + g_strip[1, xx] * after
        rest = rest + g_strip[2, xx] * t[xx, 7:55, :] + g_strip[3, xx] * t[xx, 9:57, :]
        rest = rest + g_strip[4, xx] * down + g_strip[5, xx] * up
        new = factor * rest
        if retain is not None:
            new = retain * u_t[xx] + new
        u_t[xx] = new
        t_out[xx, 8:56, :] = here + new


def clear_edges(ref, planes, rows):
    width = ref.shape[1]
    ref[0] = jnp.zeros((width, 128), F32)
    ref[planes + 1] = jnp.zeros((width, 128), F32)

    def body(x):
        ref[x, 0:8, :] = jnp.zeros((8, 128), F32)
        ref[x, 8 + rows : width, :] = jnp.zeros((width - 8 - rows, 128), F32)

    loop(0, planes + 2, 4, body)


def clear_strip(ref):
    for xx in range(6):
        ref[xx, 0:8, :] = jnp.zeros((8, 128), F32)
        ref[xx, 56:64, :] = jnp.zeros((8, 128), F32)


def unpack_strip(z_lo, z_hi, src_t, bt_pad):
    iz = lax.axis_index("gz")
    low = flag(iz > 0)
    high = flag(iz < lax.axis_size("gz") - 1)

    def mirror(first, last):
        return pick(lambda r, c: (r // 16 == c // 16) & ((r % 16 < 8) == first) & (r % 16 + c % 16 == last))

    s_lo, s_hi = mirror(True, 15), mirror(True, 7)
    b_lo, b_hi = mirror(False, 23), mirror(False, 15)
    for xx in range(6):
        before = z_lo[xx] * low
        after = z_hi[xx] * high
        src_t[xx] = dot(before, s_lo) + dot(after, s_hi)
        bt_pad[xx, 8:56, :] = dot(before, b_lo) + dot(after, b_hi)


LEVEL0_SCRATCH = [
    vm(50, 64, 128),
    vm(6, 64, 128),
    vm(50, 64, 128),
    vm(50, 64, 128),
    vm(6, 64, 128),
    vm(6, 64, 128),
    vm(6, 48, 128),
    vm(48, 48, 128),
    vm(6, 48, 128),
    vm(6, 48, 128),
    vm(48, 48, 128),
    vm(2, 16, 32, 128),
]


def level0_down(
    src, beta, z_lo, z_hi, iter_out, iter_t_out, c_out, c_lo, c_hi, g_main, g_strip, sp, sp_t, bt_out,
    b_pad, bt_pad, va, vb, ta, tb, ghost, u, u_t, src_t, total, rows,
):
    for ref in (b_pad, va, vb):
        clear_edges(ref, 48, 48)
    for ref in (bt_pad, ta, tb):
        clear_strip(ref)
    b_pad[1:49, 8:56, :] = beta[...]
    unpack_strip(z_lo, z_hi, src_t, bt_pad)
    for xx in range(6):
        bt_out[xx] = bt_pad[xx, 8:56, :]
    level0_setup(b_pad, bt_pad, ghost, src, src_t, g_main, g_strip, sp, sp_t, total)

    first = RECIPE[0][1]

    def start(x):
        u[x] = first * sp[x]
        va[x + 1, 8:56, :] = u[x]

    loop(0, 48, 8, start)
    for xx in range(6):
        u_t[xx] = first * sp_t[xx]
        ta[xx, 8:56, :] = u_t[xx]
    bufs = [(va, ta), (vb, tb)]
    for k in range(1, SMOOTH):
        (v, t), (w, s) = bufs
        retain, factor = RECIPE[k]
        level0_step(v, t, w, s, ghost, g_main, g_strip, sp, sp_t, u, u_t, 0, 48, retain, factor)
        bufs = [(w, s), (v, t)]
    v, t = bufs[0]
    iter_out[...] = v[1:49, 8:56, :]
    for xx in range(6):
        iter_t_out[xx] = t[xx, 8:56, :]

    to_low = pick(lambda r, c: r // 2 == c)
    to_high = pick(lambda r, c: r // 2 + 64 == c)

    def restrict(x2):
        parts = []
        for half in range(2):
            x = 8 + 2 * x2 + half
            _, rest = block_rest(v, t, g_main, sp, x, 8)
            parts.append(rest * total[x, 8:40])
        rows[0, x2] = (parts[0] + parts[1]) * (0.5 / 8.0)
        rows[1, x2] = (b_pad[9 + 2 * x2, 16:48, :] + b_pad[10 + 2 * x2, 16:48, :]) * (1.0 / 8.0)

    loop(0, 16, 8, restrict)

    def compress(x2):
        res = rows[0, x2, pl.ds(0, 16, stride=2), :] + rows[0, x2, pl.ds(1, 16, stride=2), :]
        bet = rows[1, x2, pl.ds(0, 16, stride=2), :] + rows[1, x2, pl.ds(1, 16, stride=2), :]
        c_out[x2] = dot(res, to_low) + dot(bet, to_high)

    loop(0, 16, 8, compress)
    c_lo[...] = c_out[0:10]
    c_hi[...] = c_out[6:16]


def pack1_y(c, from_lo, from_hi, lo, hi):
    index = lax.axis_index("gx")
    low = flag(index > 0)
    high = flag(index < lax.axis_size("gx") - 1)
    for x in range(36):
        if x < 10:
            plane = from_lo[x] * low
        elif x < 26:
            plane = c[x - 10]
        else:
            plane = from_hi[x - 26] * high
        lo[x * 10 : x * 10 + 10, :] = plane[0:10]
        hi[x * 10 : x * 10 + 10, :] = plane[6:16]


def pack1_z(c, x_lo, x_hi, y_lo, y_hi, ext, lo, hi):
    ix = lax.axis_index("gx")
    iy = lax.axis_index("gy")
    x_low = flag(ix > 0)
    x_high = flag(ix < lax.axis_size("gx") - 1)
    y_low = flag(iy > 0)
    y_high = flag(iy < lax.axis_size("gy") - 1)
    ext[0:10, 10:26, :] = x_lo[...] * x_low
    ext[10:26, 10:26, :] = c[...]
    ext[26:36, 10:26, :] = x_hi[...] * x_high
    for x in range(36):
        ext[x, 0:10, :] = y_lo[x * 10 : x * 10 + 10, :] * y_low
        ext[x, 26:36, :] = y_hi[x * 10 : x * 10 + 10, :] * y_high
        ext[x, 36:40, :] = jnp.zeros((4, 128), F32)
    lane = lanes_of(40)

    def body(xx):
        acc_lo = jnp.zeros((40, 128), F32)
        acc_hi = jnp.zeros((40, 128), F32)
        for g in range(6):
            e = ext[g * 6 + xx]
            first = (lane >= g * 20) & (lane < g * 20 + 10)
            second = (lane >= g * 20 + 10) & (lane < g * 20 + 20)
            middle = roll(e, g * 20 - 54)
            acc_lo = jnp.where(first, roll(e, g * 20), acc_lo)
            acc_lo = jnp.where(second, middle, acc_lo)
            acc_hi = jnp.where(first, middle, acc_hi)
            acc_hi = jnp.where(second, roll(e, g * 20 + 20), acc_hi)
        lo[xx] = acc_lo
        hi[xx] = acc_hi

    loop(0, 6, 36, body)


def ring_weights(b_pad, src, g, sp, total, planes, rows, scale, edges=None):
    lane = lanes_of(rows)

    def body(x):
        here = b_pad[x + 1, 8 : 8 + rows, :]
        down = roll(here, 1)
        up = roll(here, -1)
        if edges is not None:
            down = jnp.where(lane == 0, 0.0, down)
            up = jnp.where(lane == 127, 0.0, up)
        faces, inverse, tot = weights(
            here,
            (
                b_pad[x, 8 : 8 + rows, :],
                b_pad[x + 2, 8 : 8 + rows, :],
                b_pad[x + 1, 7 : 7 + rows, :],
                b_pad[x + 1, 9 : 9 + rows, :],
                down,
                up,
            ),
        )
        if edges is not None:
            faces[4] = jnp.where(lane == 0, 0.0, faces[4])
            faces[5] = jnp.where(lane == 127, 0.0, faces[5])
        for i in range(6):
            g[i, x] = faces[i]
        sp[x] = scale * 2.0 * inverse if src is None else src[x] * (scale * 2.0 * inverse)
        if total is not None:
            total[x] = tot

    loop(0, planes, rows // 4, body)


def ring_rest(v, g, sp, x, rows):
    here = v[x + 1, 8 : 8 + rows, :]
    rest = sp[x] - here
    rest = rest + g[0, x] * v[x, 8 : 8 + rows, :] + g[1, x] * v[x + 2, 8 : 8 + rows, :]
    rest = rest + g[2, x] * v[x + 1, 7 : 7 + rows, :] + g[3, x] * v[x + 1, 9 : 9 + rows, :]
    rest = rest + g[4, x] * roll(here, 1) + g[5, x] * roll(here, -1)
    return here, rest


def ring_step(v, v_out, g, sp, u, planes, rows, retain, factor):
    def body(x):
        here, rest = ring_rest(v, g, sp, x, rows)
        new = factor * rest
        if retain is not None:
            new = retain * u[x] + new
        u[x] = new
        v_out[x + 1, 8 : 8 + rows, :] = here + new

    loop(0, planes, rows // 16, body)


def ring_zero_start(v, u, sp, planes, rows, factor):
    def body(x):
        u[x] = factor * sp[x]
        v[x + 1, 8 : 8 + rows, :] = u[x]

    loop(0, planes, rows // 8, body)


def ring_cheb(va, vb, g, sp, u, planes, rows, recipe, from_zero):
    begin = 0
    if from_zero:
        ring_zero_start(va, u, sp, planes, rows, recipe[0][1])
        begin = 1
    for k in range(begin, len(recipe)):
        retain, factor = recipe[k]
        ring_step(va, vb, g, sp, u, planes, rows, None if k == 0 else retain, factor)
        va, vb = vb, va
    return va


LEVEL1_SCRATCH = [
    vm(38, 56, 128),
    vm(38, 56, 128),
    vm(38, 56, 128),
    vm(36, 40, 128),
    vm(36, 40, 128),
    vm(36, 40, 128),
    vm(8, 40, 128),
]


def level1_unpack(ext, z_lo, z_hi, source, b_pad, beta_out):
    iz = lax.axis_index("gz")
    low = flag(iz > 0)
    high = flag(iz < lax.axis_size("gz") - 1)
    lane = lanes_of(40)
    inner = lane < 64
    above = (lane >= 64) & (lane < 74)
    below = lane >= 118

    def unpack(xx):
        before = z_lo[xx] * low
        after = z_hi[xx] * high
        for k in range(6):
            x = k * 6 + xx
            e = ext[x]
            s = jnp.where(inner, e, 0.0)
            s = jnp.where(above, roll(after, 64 - k * 20), s)
            s = jnp.where(below, roll(before, 118 - k * 20), s)
            b = jnp.where(inner, roll(e, 64), 0.0)
            b = jnp.where(above, roll(after, 54 - k * 20), b)
            b = jnp.where(below, roll(before, 108 - k * 20), b)
            source[x] = s
            b_pad[x + 1, 8:48, :] = b
            beta_out[x] = b

    loop(0, 6, 36, unpack)


def level1_down(
    ext, z_lo, z_hi, iter_out, chunk, g, sp, beta_out,
    b_pad, va, vb, u, src, total, rows,
):
    for ref in (b_pad, va, vb):
        clear_edges(ref, 36, 40)
    level1_unpack(ext, z_lo, z_hi, src, b_pad, beta_out)
    ring_weights(b_pad, src, g, sp, total, 36, 40, 4.0)
    v = ring_cheb(va, vb, g, sp, u, 36, 40, RECIPE, True)
    iter_out[...] = v[1:37, 8:48, :]
    summed = []
    for x2 in range(8):
        parts = []
        for half in range(2):
            x = 10 + 2 * x2 + half
            _, rest = ring_rest(v, g, sp, x, 40)
            parts.append(rest * total[x])
        rows[x2] = (parts[0] + parts[1]) * (0.25 * 0.5 / 8.0)
        summed.append(rows[x2, pl.ds(10, 8, stride=2), :] + rows[x2, pl.ds(11, 8, stride=2), :])
    for half in range(2):
        acc = jnp.zeros((8, 128), F32)
        for quarter in range(4):
            weight = pick(lambda r, c: (r < 64) & ((r // 2 + 32 * quarter) == c))
            acc = acc + dot(summed[half * 4 + quarter], weight)
        chunk[half * 8 : half * 8 + 8, :] = acc


def sender(axis, step):
    count = lax.axis_size(axis)
    return lax.rem(lax.axis_index(axis) + count - step, count)


def gather_z(*refs):
    *parts, _, out = refs
    lane = lanes_of(8)
    for half in range(2):
        for quarter in range(4):
            acc = jnp.zeros((8, 128), F32)
            for step, part in enumerate(parts):
                owner = sender("gz", step)
                moved = roll(part[half * 8 : half * 8 + 8, :], lax.rem(owner - quarter + 4, 4) * 32)
                acc = jnp.where(lane // 32 == owner, moved, acc)
            out[half * 4 + quarter] = acc


def gather_x(*refs):
    *parts, _, out = refs
    for step, part in enumerate(parts):
        out[pl.ds(sender("gx", step) * 8, 8)] = part[...]


def gather_y(parts, out):
    for step, part in enumerate(parts):
        row = pl.multiple_of(8 + sender("gy", step) * 8, 8)
        out[8:40, pl.ds(row, 8), :] = part[...]


def clear_whole(ref):
    def clear(x):
        ref[x, 0:8, :] = jnp.zeros((8, 128), F32)
        ref[x, 72:80, :] = jnp.zeros((8, 128), F32)

    loop(0, 48, 2, clear)
    for x in [*range(8), *range(40, 48)]:
        ref[x, 8:72, :] = jnp.zeros((64, 128), F32)


def coarse_prepare(p0, p1, p2, p3, p4, p5, p6, p7, g, inv, total, g3, inv3, gw, invw, b2, b3, bw, rows):
    clear_whole(b2)
    clear_edges(b3, 16, 32)
    clear_edges(bw, 22, 24)
    gather_y((p0, p1, p2, p3, p4, p5, p6, p7), b2)
    ring_weights(b2.at[7:41], None, g, inv, total, 32, 64, 16.0, edges=True)
    half_z = pick(lambda r, c: r // 2 == c)

    def restrict(x2):
        rows[x2] = (b2[8 + 2 * x2, 8:72, :] + b2[9 + 2 * x2, 8:72, :]) * (1.0 / 8.0)

    loop(0, 16, 8, restrict)

    def compress(x2):
        bet = rows[x2, pl.ds(0, 32, stride=2), :] + rows[x2, pl.ds(1, 32, stride=2), :]
        b3[x2 + 1, 8:40, :] = dot(bet, half_z)

    loop(0, 16, 9, compress)
    ring_weights(b3, None, g3, inv3, None, 16, 32, 64.0)
    ix = lax.axis_index("gx")
    row = pl.multiple_of(lax.axis_index("gy") * 8, 8)

    def window(x):
        bw[x + 1, 8:32, :] = b2[ix * 8 + 1 + x, pl.ds(row, 24), :]

    loop(0, 22, 6, window)
    ring_weights(bw, None, gw, invw, None, 22, 24, 16.0, edges=True)


COARSE_SHAPES = [
    (6, 32, 64, 128),
    (32, 64, 128),
    (32, 64, 128),
    (6, 16, 32, 128),
    (16, 32, 128),
    (6, 22, 24, 128),
    (22, 24, 128),
]


def bottom(
    p0, p1, p2, p3, p4, p5, p6, p7, g, inv, total, g3, inv3, gw, invw, out,
    s2, va, vb, sp, u, v3a, v3b, sp3, u3, rows, wa, wb, spw, uw,
):
    for ref in (s2, va, vb):
        clear_whole(ref)
    gather_y((p0, p1, p2, p3, p4, p5, p6, p7), s2)

    def scale(x):
        sp[x] = s2[x + 8, 8:72, :] * inv[x]

    loop(0, 32, 8, scale)
    v = ring_cheb(va.at[7:41], vb.at[7:41], g, sp, u, 32, 64, RECIPE, True)
    iterate = vb if SMOOTH % 2 == 0 else va

    clear_edges(v3a, 16, 32)
    clear_edges(v3b, 16, 32)
    half_z = pick(lambda r, c: r // 2 == c)

    def restrict(x2):
        parts = []
        for half in range(2):
            x = 2 * x2 + half
            _, rest = ring_rest(v, g, sp, x, 64)
            parts.append(rest * total[x])
        rows[x2] = (parts[0] + parts[1]) * (0.0625 * 0.5 / 8.0)

    loop(0, 16, 16, restrict)

    def compress(x2):
        res = rows[x2, pl.ds(0, 32, stride=2), :] + rows[x2, pl.ds(1, 32, stride=2), :]
        sp3[x2] = dot(res, half_z) * inv3[x2]

    loop(0, 16, 9, compress)
    c3 = ring_cheb(v3a, v3b, g3, sp3, u3, 16, 32, BOTTOM_RECIPE, True)

    other = va if iterate is vb else vb
    double_z = pick(lambda r, c: c // 2 == r)

    def prolong(x3):
        wide = dot(c3[x3 + 1, 8:40, :], double_z)
        rows[x3, pl.ds(0, 32, stride=2), :] = wide
        rows[x3, pl.ds(1, 32, stride=2), :] = wide
        for half in range(2):
            x = 8 + 2 * x3 + half
            other[x, 8:72, :] = iterate[x, 8:72, :] + rows[x3]

    loop(0, 16, 18, prolong)
    ix = lax.axis_index("gx")
    iz = lax.axis_index("gz")
    clear_edges(wa, 22, 24)
    clear_edges(wb, 22, 24)
    row = pl.multiple_of(lax.axis_index("gy") * 8, 8)

    def window(x):
        plane = ix * 8 + 1 + x
        wa[x + 1, 8:32, :] = other[plane, pl.ds(row, 24), :]
        spw[x] = s2[plane, pl.ds(row, 24), :] * invw[x]

    loop(0, 22, 6, window)
    c2 = ring_cheb(wa, wb, gw, spw, uw, 22, 24, RECIPE, False)
    shift = (128 - iz * 32) % 128
    for x in range(18):
        out[x] = roll(c2[x + 3, 8:32, :], shift)


COARSE_SCRATCH = [
    vm(48, 80, 128),
    vm(18, 48, 128),
    vm(24, 40, 128),
    vm(16, 64, 128),
]
BOTTOM_SCRATCH = [
    vm(48, 80, 128),
    vm(48, 80, 128),
    vm(48, 80, 128),
    vm(32, 64, 128),
    vm(32, 64, 128),
    vm(18, 48, 128),
    vm(18, 48, 128),
    vm(16, 32, 128),
    vm(16, 32, 128),
    vm(16, 64, 128),
    vm(24, 40, 128),
    vm(24, 40, 128),
    vm(22, 24, 128),
    vm(22, 24, 128),
]


def level1_up(c2, g, sp, beta, iterate, out, va, vb, u, wide, rows):
    for ref in (va, vb):
        clear_edges(ref, 36, 40)
    spread = pick(lambda r, c: ((c < 74) & (c // 2 == r)) | ((c >= 118) & (c // 2 + 64 == r)))
    for x2 in range(18):
        rows[x2, 32:40, :] = jnp.zeros((8, 128), F32)

    def prolong(x2):
        wide[x2] = dot(c2[x2], spread)
        part = wide[x2, 3:21, :]
        rows[x2, pl.ds(0, 18, stride=2), :] = part
        rows[x2, pl.ds(1, 18, stride=2), :] = part
        for half in range(2):
            x = 2 * x2 + half
            va[x + 1, 8:48, :] = jnp.where(beta[x] > 0.0, iterate[x] + rows[x2], 0.0)

    loop(0, 18, 12, prolong)
    v = ring_cheb(va, vb, g, sp, u, 36, 40, RECIPE, False)
    out[...] = v[7:31, 14:38, :]


def level0_up(
    c1, beta, g_main, g_strip, sp, sp_t, beta_t, iterate, iterate_t, out,
    va, vb, ta, tb, ghost, u, u_t, rows,
):
    for ref in (va, vb):
        clear_edges(ref, 48, 48)
    for ref in (ta, tb):
        clear_strip(ref)
    spread = pick(lambda r, c: c // 2 == r)

    def prolong(x1):
        wide = dot(c1[x1], spread)
        rows[x1, pl.ds(0, 24, stride=2), :] = wide
        rows[x1, pl.ds(1, 24, stride=2), :] = wide
        for half in range(2):
            x = 2 * x1 + half
            va[x + 1, 8:56, :] = jnp.where(beta[x] > 0.0, iterate[x] + rows[x1], 0.0)

    loop(0, 24, 12, prolong)

    def prolong_strip(m):
        acc = jnp.zeros((24, 128), F32)
        for k in range(8):
            to = pick(
                lambda r, c: (c // 16 == k)
                & (
                    ((c % 16 < 8) & (r == 64 + (7 - c % 16) // 2))
                    | ((c % 16 >= 8) & (r == 124 + (15 - c % 16) // 2))
                )
            )
            acc = acc + dot(c1[k * 3 + m], to)
        rows[m, pl.ds(0, 24, stride=2), :] = acc
        rows[m, pl.ds(1, 24, stride=2), :] = acc
        for half in range(2):
            xx = 2 * m + half
            ta[xx, 8:56, :] = jnp.where(beta_t[xx] > 0.0, iterate_t[xx] + rows[m], 0.0)

    loop(0, 3, 36, prolong_strip)
    for x in [*range(6), *range(42, 48)]:
        vb[x + 1, 8:56, :] = jnp.zeros((48, 128), F32)
    bufs = [(va, ta), (vb, tb)]
    for k in range(SMOOTH):
        (v, t), (w, s) = bufs
        retain, factor = RECIPE[k]
        if k == 0:
            retain = None
        if k < SMOOTH - 1:
            low, high = (4, 44) if k < 2 else (6, 42)
            level0_step(
                v, t, w, s, ghost, g_main, g_strip, sp, sp_t, u, u_t, low, high, retain, factor
            )
        else:

            def last(x):
                here, rest = block_rest(v, t, g_main, sp, x, 8)
                out[x - 8] = here + retain * u[x, 8:40] + factor * rest

            loop(8, 40, 4, last)
        bufs = [(w, s), (v, t)]


def ring(value, axis, step):
    count = lax.axis_size(axis)
    return lax.ppermute(value, axis, [(i, (i + step) % count) for i in range(count)])


def trade(lo, hi, axis):
    return ring(hi, axis, 1), ring(lo, axis, -1)


def gather(kernel, parts, after, *shape):
    return call(kernel, sds(*shape), name=kernel.__name__, last_unread=len(parts) + 1)(*parts, after)


def around(value, axis):
    return [value] + [ring(value, axis, step) for step in range(1, lax.axis_size(axis))]


def carry(parts, steps, after, *values):
    slab, _ = lax.optimization_barrier((parts[0], after))
    moved = [ring(slab, "gy", step) for step in steps]
    *values, last = lax.optimization_barrier((*values, tuple(moved)))
    parts.extend(last)
    return values


def per_device(source, beta):
    lo = jnp.stack([source[0:8], beta[0:8]])
    hi = jnp.stack([source[24:32], beta[24:32]])
    lo, hi, source, beta = lax.optimization_barrier((lo, hi, source, beta))
    x_lo, x_hi = trade(lo, hi, "gx")
    beta2 = call(coarse_beta, sds(16, 128), [vm(32, 128)], name="coarse_beta")(beta)
    x_lo, x_hi, beta2 = lax.optimization_barrier((x_lo, x_hi, beta2))
    slab = sds(2, 48, 8, 128)
    mid = sds(48, 32, 128)
    lo, hi, s_mid, b_mid = call(pack_y, (slab, slab, mid, mid), name="pack_y", mib=4)(
        source, beta, x_lo, x_hi
    )
    y_lo, y_hi = trade(lo, hi, "gy")
    beta2_block = gather(gather_z, around(beta2, "gz"), lo, 8, 8, 128)
    y_lo, y_hi, beta2_block = lax.optimization_barrier((y_lo, y_hi, beta2_block))
    whole = sds(48, 48, 128)
    strip = sds(6, 48, 128)
    src_ext, beta_ext, lo, hi = call(
        pack_z, (whole, whole, strip, strip), name="pack_z", mib=4
    )(s_mid, b_mid, y_lo, y_hi)
    z_lo, z_hi = trade(lo, hi, "gz")
    beta2_slab = gather(gather_x, around(beta2_block, "gx"), lo, 32, 8, 128)
    z_lo, z_hi, beta2_slab = lax.optimization_barrier((z_lo, z_hi, beta2_slab))
    beta2_y = [beta2_slab]
    iter0, iter0_t, c, lo, hi, *ready = call(
        level0_down,
        (
            whole,
            strip,
            sds(16, 16, 128),
            sds(10, 16, 128),
            sds(10, 16, 128),
            sds(7, 48, 48, 128),
            sds(6, 6, 48, 128),
            whole,
            strip,
            strip,
        ),
        LEVEL0_SCRATCH,
        name="level0_down",
        mib=16,
    )(src_ext, beta_ext, z_lo, z_hi)
    x_lo, x_hi = trade(lo, hi, "gx")
    x_lo, x_hi = carry(beta2_y, (1, 2, 3), lo, x_lo, x_hi)
    lo, hi = call(pack1_y, (sds(360, 128), sds(360, 128)), name="pack1_y")(c, x_lo, x_hi)
    y_lo, y_hi = trade(lo, hi, "gy")
    y_lo, y_hi = carry(beta2_y, (4,), lo, y_lo, y_hi)
    ext, lo, hi = call(
        pack1_z, (sds(36, 40, 128), sds(6, 40, 128), sds(6, 40, 128)), name="pack1_z"
    )(c, x_lo, x_hi, y_lo, y_hi)
    z1_lo, z1_hi = trade(lo, hi, "gz")
    z1_lo, z1_hi = carry(beta2_y, (5, 6, 7), lo, z1_lo, z1_hi)
    level1 = sds(36, 40, 128)
    iter1, chunk, g1, sp1, beta1 = call(
        level1_down,
        (level1, sds(16, 128), sds(6, 36, 40, 128), level1, level1),
        LEVEL1_SCRATCH,
        name="level1_down",
        mib=8,
    )(ext, z1_lo, z1_hi)
    parts = around(chunk, "gz")
    parts = around(gather(gather_z, parts, chunk, 8, 8, 128), "gx")
    slab = gather(gather_x, parts, chunk, 32, 8, 128)
    parts = around(slab, "gy")
    coarse = call(
        coarse_prepare,
        tuple(sds(*shape) for shape in COARSE_SHAPES),
        COARSE_SCRATCH,
        name="coarse_prepare",
        mib=8,
    )(*beta2_y)
    c2 = call(bottom, sds(18, 24, 128), BOTTOM_SCRATCH, name="bottom", mib=18)(*parts, *coarse)
    c1 = call(
        level1_up,
        sds(24, 24, 128),
        [vm(38, 56, 128), vm(38, 56, 128), vm(36, 40, 128), vm(18, 24, 128), vm(18, 40, 128)],
        name="level1_up",
        mib=8,
    )(c2, g1, sp1, beta1, iter1)
    return call(
        level0_up,
        sds(32, 32, 128),
        [vm(50, 64, 128), vm(50, 64, 128), vm(6, 64, 128), vm(6, 64, 128), vm(6, 48, 128)]
        + [vm(48, 48, 128), vm(6, 48, 128), vm(24, 48, 128)],
        name="level0_up",
        mib=14,
    )(c1, beta_ext, *ready, iter0, iter0_t)


def solution(mesh):
    placed = (P(*AXES), P(*AXES))
    return jax.shard_map(
        per_device, mesh=mesh, in_specs=placed, out_specs=P(*AXES), check_vma=False
    )
```

```python
import jax
import jax.numpy as jnp
from jax import lax
from jax.experimental import pallas as pl
from jax.experimental.pallas import tpu as pltpu
from jax.sharding import PartitionSpec as P

SMOOTH = 4
BOTTOM = 12
LOW_EIG = 0.3
HIGH_EIG = 2.0
BOTTOM_LOW = 0.02

AXES = ("gx", "gy", "gz")
F32 = jnp.float32
MIB = 1024 * 1024


def cheb_plan(degree, lowest, highest):
    centre = 0.5 * (highest + lowest)
    radius = 0.5 * (highest - lowest)
    ratio_s = centre / radius
    rho_old = 1.0 / ratio_s
    recipe = [(0.0, 1.0 / centre)]
    for position in range(1, degree):
        rho_new = 1.0 / (2.0 * ratio_s - rho_old)
        recipe.append((rho_new * rho_old, 2.0 * rho_new / radius))
        rho_old = rho_new
    return recipe


RECIPE = cheb_plan(SMOOTH, LOW_EIG, HIGH_EIG)
BOTTOM_RECIPE = cheb_plan(BOTTOM, BOTTOM_LOW, HIGH_EIG)


def sds(*shape):
    return jax.ShapeDtypeStruct(shape, F32)


def vm(*shape):
    return pltpu.VMEM(shape, F32)


def call(body, outs, scratch=(), name=None, mib=2, last_unread=None):
    specs = {}
    if last_unread:
        whole = pl.BlockSpec(memory_space=pltpu.VMEM)
        specs["in_specs"] = [whole] * (last_unread - 1) + [pl.BlockSpec(memory_space=pl.ANY)]
    return pl.pallas_call(
        body,
        out_shape=outs,
        **specs,
        scratch_shapes=list(scratch),
        compiler_params=pltpu.CompilerParams(vmem_limit_bytes=mib * MIB),
        name=name,
    )


def loop(low, high, vectors, body):
    count = high - low
    most = max(1, min(count, 72 // vectors))
    width = max([w for w in range(1, most + 1) if count % w == 0])
    if width * 2 < most:
        width = most
    rounds = count // width

    def chunk(i, carry):
        for k in range(width):
            body(low + i * width + k)
        return carry

    if rounds > 1:
        lax.fori_loop(0, rounds, chunk, 0)
    else:
        chunk(0, 0)
    for x in range(low + rounds * width, high):
        body(x)


def lanes_of(rows):
    return lax.broadcasted_iota(jnp.int32, (rows, 128), 1)


def roll(value, shift):
    if isinstance(shift, int):
        shift = shift % 128
        if shift == 0:
            return value
    return pltpu.roll(value, shift, 1)


def flag(condition):
    return jnp.where(condition, 1.0, 0.0).astype(F32)


def dot(left, right):
    return lax.dot_general(
        left,
        right,
        (((1,), (0,)), ((), ())),
        precision=lax.Precision.HIGHEST,
        preferred_element_type=F32,
    )


def pick(match):
    row = lax.broadcasted_iota(jnp.int32, (128, 128), 0)
    col = lax.broadcasted_iota(jnp.int32, (128, 128), 1)
    return jnp.where(match(row, col), 1.0, 0.0).astype(F32)


def coarse_beta(beta, out, rows):
    total = []
    for x in range(8):
        s = beta[4 * x] + beta[4 * x + 1] + beta[4 * x + 2] + beta[4 * x + 3]
        rows[...] = s
        t = rows[pl.ds(0, 8, stride=4), :] + rows[pl.ds(1, 8, stride=4), :]
        t = t + rows[pl.ds(2, 8, stride=4), :] + rows[pl.ds(3, 8, stride=4), :]
        total.append(t * (1.0 / 64.0))
    for half in range(2):
        acc = jnp.zeros((8, 128), F32)
        for quarter in range(4):
            weight = pick(lambda r, c: (r // 4 + 32 * quarter) == c)
            acc = acc + dot(total[half * 4 + quarter], weight)
        out[half * 8 : half * 8 + 8, :] = acc


def pack_y(src, beta, from_lo, from_hi, lo, hi, s_mid, b_mid):
    index = lax.axis_index("gx")
    low = flag(index > 0)
    high = flag(index < lax.axis_size("gx") - 1)
    for field, (ref, mid) in enumerate(((src, s_mid), (beta, b_mid))):
        mid[0:8] = from_lo[field] * low
        mid[8:40] = ref[...]
        mid[40:48] = from_hi[field] * high
        lo[field] = mid[:, 0:8, :]
        hi[field] = mid[:, 24:32, :]


def pack_z(s_mid, b_mid, y_lo, y_hi, s_out, b_out, lo, hi):
    iy = lax.axis_index("gy")
    y_low = flag(iy > 0)
    y_high = flag(iy < lax.axis_size("gy") - 1)
    for field, (mid, out) in enumerate(((s_mid, s_out), (b_mid, b_out))):
        out[:, 8:40, :] = mid[...]
        out[:, 0:8, :] = y_lo[field] * y_low
        out[:, 40:48, :] = y_hi[field] * y_high
    lane = lanes_of(48)

    def body(xx):
        acc_lo = jnp.zeros((48, 128), F32)
        acc_hi = jnp.zeros((48, 128), F32)
        for g in range(8):
            s = s_out[g * 6 + xx]
            b = b_out[g * 6 + xx]
            first = (lane >= g * 16) & (lane < g * 16 + 8)
            second = (lane >= g * 16 + 8) & (lane < g * 16 + 16)
            acc_lo = jnp.where(first, roll(s, g * 16), acc_lo)
            acc_lo = jnp.where(second, roll(b, g * 16 + 8), acc_lo)
            acc_hi = jnp.where(first, roll(s, g * 16 + 8), acc_hi)
            acc_hi = jnp.where(second, roll(b, g * 16 + 16), acc_hi)
        lo[xx] = acc_lo
        hi[xx] = acc_hi

    loop(0, 6, 36, body)


def strip_ghosts(values, ghost):
    lane = lanes_of(48)

    def body(xx):
        acc = jnp.zeros((48, 128), F32)
        for g in range(8):
            acc = jnp.where(lane // 16 == g, roll(values[g * 6 + xx + 1, 8:56, :], g * 16 + 8), acc)
        ghost[xx] = acc

    loop(0, 6, 36, body)


def strip_sides(strip, xx):
    after = strip[xx + 1, 8:56, :] if xx < 5 else roll(strip[0, 8:56, :], -16)
    before = strip[xx - 1, 8:56, :] if xx > 0 else roll(strip[5, 8:56, :], 16)
    return before, after


def strip_z(strip, ghost, xx, lane):
    here = strip[xx, 8:56, :]
    up = jnp.where(lane % 16 == 8, ghost[xx], roll(here, 1))
    down = jnp.where(lane % 16 == 7, ghost[xx], roll(here, -1))
    return down, up


def block_edge(strip, x, first=8, count=48):
    g = x // 6
    return roll(strip[x - g * 6, first : first + count, :], 120 - g * 16)


def weights(here, sides):
    sums = [here + side for side in sides]
    total = sums[0] + sums[1] + sums[2] + sums[3] + sums[4] + sums[5]
    inverse = jnp.where(here > 0.0, 1.0 / total, 0.0)
    return [s * inverse for s in sums], inverse, total


def level0_setup(b_pad, bt_pad, ghost, src, src_t, g_main, g_strip, sp, sp_t, total):
    strip_ghosts(b_pad, ghost)
    lane = lanes_of(48)

    def body(x):
        here = b_pad[x + 1, 8:56, :]
        edge = block_edge(bt_pad, x)
        down = jnp.where(lane == 0, edge, roll(here, 1))
        up = jnp.where(lane == 127, edge, roll(here, -1))
        faces, inverse, tot = weights(
            here,
            (
                b_pad[x, 8:56, :],
                b_pad[x + 2, 8:56, :],
                b_pad[x + 1, 7:55, :],
                b_pad[x + 1, 9:57, :],
                down,
                up,
            ),
        )
        for i in range(4):
            g_main[i, x] = faces[i]
        g_main[4, x] = jnp.where(lane == 0, 0.0, faces[4])
        g_main[5, x] = jnp.where(lane == 127, 0.0, faces[5])
        g_main[6, x] = jnp.where(lane == 0, faces[4], jnp.where(lane == 127, faces[5], 0.0))
        sp[x] = src[x] * (2.0 * inverse)
        if total is not None:
            total[x] = tot

    loop(0, 48, 12, body)
    for xx in range(6):
        before, after = strip_sides(bt_pad, xx)
        down, up = strip_z(bt_pad, ghost, xx, lane)
        faces, inverse, _ = weights(
            bt_pad[xx, 8:56, :],
            (before, after, bt_pad[xx, 7:55, :], bt_pad[xx, 9:57, :], down, up),
        )
        for i in range(6):
            g_strip[i, xx] = faces[i]
        sp_t[xx] = src_t[xx] * (2.0 * inverse)


def block_rest(v, t, g_main, sp, x, skip=0):
    count = 48 - 2 * skip
    first = 8 + skip
    keep = slice(skip, 48 - skip)
    here = v[x + 1, first : first + count, :]
    rest = sp[x, keep] - here
    rest = rest + g_main[0, x, keep] * v[x, first : first + count, :]
    rest = rest + g_main[1, x, keep] * v[x + 2, first : first + count, :]
    rest = rest + g_main[2, x, keep] * v[x + 1, first - 1 : first - 1 + count, :]
    rest = rest + g_main[3, x, keep] * v[x + 1, first + 1 : first + 1 + count, :]
    rest = rest + g_main[4, x, keep] * roll(here, 1) + g_main[5, x, keep] * roll(here, -1)
    rest = rest + g_main[6, x, keep] * block_edge(t, x, first, count)
    return here, rest


def level0_step(v, t, v_out, t_out, ghost, g_main, g_strip, sp, sp_t, u, u_t, low, high, retain, factor):
    strip_ghosts(v, ghost)
    lane = lanes_of(48)

    def body(x):
        here, rest = block_rest(v, t, g_main, sp, x)
        new = factor * rest
        if retain is not None:
            new = retain * u[x] + new
        u[x] = new
        v_out[x + 1, 8:56, :] = here + new

    loop(low, high, 6, body)
    for xx in range(6):
        here = t[xx, 8:56, :]
        before, after = strip_sides(t, xx)
        down, up = strip_z(t, ghost, xx, lane)
        rest = sp_t[xx] - here
        rest = rest + g_strip[0, xx] * before + g_strip[1, xx] * after
        rest = rest + g_strip[2, xx] * t[xx, 7:55, :] + g_strip[3, xx] * t[xx, 9:57, :]
        rest = rest + g_strip[4, xx] * down + g_strip[5, xx] * up
        new = factor * rest
        if retain is not None:
            new = retain * u_t[xx] + new
        u_t[xx] = new
        t_out[xx, 8:56, :] = here + new


def clear_edges(ref, planes, rows):
    width = ref.shape[1]
    ref[0] = jnp.zeros((width, 128), F32)
    ref[planes + 1] = jnp.zeros((width, 128), F32)

    def body(x):
        ref[x, 0:8, :] = jnp.zeros((8, 128), F32)
        ref[x, 8 + rows : width, :] = jnp.zeros((width - 8 - rows, 128), F32)

    loop(0, planes + 2, 4, body)


def clear_strip(ref):
    for xx in range(6):
        ref[xx, 0:8, :] = jnp.zeros((8, 128), F32)
        ref[xx, 56:64, :] = jnp.zeros((8, 128), F32)


def unpack_strip(z_lo, z_hi, src_t, bt_pad):
    iz = lax.axis_index("gz")
    low = flag(iz > 0)
    high = flag(iz < lax.axis_size("gz") - 1)

    def mirror(first, last):
        return pick(lambda r, c: (r // 16 == c // 16) & ((r % 16 < 8) == first) & (r % 16 + c % 16 == last))

    s_lo, s_hi = mirror(True, 15), mirror(True, 7)
    b_lo, b_hi = mirror(False, 23), mirror(False, 15)
    for xx in range(6):
        before = z_lo[xx] * low
        after = z_hi[xx] * high
        src_t[xx] = dot(before, s_lo) + dot(after, s_hi)
        bt_pad[xx, 8:56, :] = dot(before, b_lo) + dot(after, b_hi)


LEVEL0_SCRATCH = [
    vm(50, 64, 128),
    vm(6, 64, 128),
    vm(50, 64, 128),
    vm(50, 64, 128),
    vm(6, 64, 128),
    vm(6, 64, 128),
    vm(6, 48, 128),
    vm(48, 48, 128),
    vm(6, 48, 128),
    vm(6, 48, 128),
    vm(48, 48, 128),
    vm(2, 16, 32, 128),
]


def level0_down(
    src, beta, z_lo, z_hi, iter_out, iter_t_out, c_out, c_lo, c_hi, g_main, g_strip, sp, sp_t, bt_out,
    b_pad, bt_pad, va, vb, ta, tb, ghost, u, u_t, src_t, total, rows,
):
    for ref in (b_pad, va, vb):
        clear_edges(ref, 48, 48)
    for ref in (bt_pad, ta, tb):
        clear_strip(ref)
    b_pad[1:49, 8:56, :] = beta[...]
    unpack_strip(z_lo, z_hi, src_t, bt_pad)
    for xx in range(6):
        bt_out[xx] = bt_pad[xx, 8:56, :]
    level0_setup(b_pad, bt_pad, ghost, src, src_t, g_main, g_strip, sp, sp_t, total)

    first = RECIPE[0][1]

    def start(x):
        u[x] = first * sp[x]
        va[x + 1, 8:56, :] = u[x]

    loop(0, 48, 8, start)
    for xx in range(6):
        u_t[xx] = first * sp_t[xx]
        ta[xx, 8:56, :] = u_t[xx]
    bufs = [(va, ta), (vb, tb)]
    for k in range(1, SMOOTH):
        (v, t), (w, s) = bufs
        retain, factor = RECIPE[k]
        level0_step(v, t, w, s, ghost, g_main, g_strip, sp, sp_t, u, u_t, 0, 48, retain, factor)
        bufs = [(w, s), (v, t)]
    v, t = bufs[0]
    iter_out[...] = v[1:49, 8:56, :]
    for xx in range(6):
        iter_t_out[xx] = t[xx, 8:56, :]

    to_low = pick(lambda r, c: r // 2 == c)
    to_high = pick(lambda r, c: r // 2 + 64 == c)

    def restrict(x2):
        parts = []
        for half in range(2):
            x = 8 + 2 * x2 + half
            _, rest = block_rest(v, t, g_main, sp, x, 8)
            parts.append(rest * total[x, 8:40])
        rows[0, x2] = (parts[0] + parts[1]) * (0.5 / 8.0)
        rows[1, x2] = (b_pad[9 + 2 * x2, 16:48, :] + b_pad[10 + 2 * x2, 16:48, :]) * (1.0 / 8.0)

    loop(0, 16, 8, restrict)

    def compress(x2):
        res = rows[0, x2, pl.ds(0, 16, stride=2), :] + rows[0, x2, pl.ds(1, 16, stride=2), :]
        bet = rows[1, x2, pl.ds(0, 16, stride=2), :] + rows[1, x2, pl.ds(1, 16, stride=2), :]
        c_out[x2] = dot(res, to_low) + dot(bet, to_high)

    loop(0, 16, 8, compress)
    c_lo[...] = c_out[0:10]
    c_hi[...] = c_out[6:16]


def pack1_y(c, from_lo, from_hi, lo, hi):
    index = lax.axis_index("gx")
    low = flag(index > 0)
    high = flag(index < lax.axis_size("gx") - 1)
    for x in range(36):
        if x < 10:
            plane = from_lo[x] * low
        elif x < 26:
            plane = c[x - 10]
        else:
            plane = from_hi[x - 26] * high
        lo[x * 10 : x * 10 + 10, :] = plane[0:10]
        hi[x * 10 : x * 10 + 10, :] = plane[6:16]


def pack1_z(c, x_lo, x_hi, y_lo, y_hi, ext, lo, hi):
    ix = lax.axis_index("gx")
    iy = lax.axis_index("gy")
    x_low = flag(ix > 0)
    x_high = flag(ix < lax.axis_size("gx") - 1)
    y_low = flag(iy > 0)
    y_high = flag(iy < lax.axis_size("gy") - 1)
    ext[0:10, 10:26, :] = x_lo[...] * x_low
    ext[10:26, 10:26, :] = c[...]
    ext[26:36, 10:26, :] = x_hi[...] * x_high
    for x in range(36):
        ext[x, 0:10, :] = y_lo[x * 10 : x * 10 + 10, :] * y_low
        ext[x, 26:36, :] = y_hi[x * 10 : x * 10 + 10, :] * y_high
        ext[x, 36:40, :] = jnp.zeros((4, 128), F32)
    lane = lanes_of(40)

    def body(xx):
        acc_lo = jnp.zeros((40, 128), F32)
        acc_hi = jnp.zeros((40, 128), F32)
        for g in range(6):
            e = ext[g * 6 + xx]
            first = (lane >= g * 20) & (lane < g * 20 + 10)
            second = (lane >= g * 20 + 10) & (lane < g * 20 + 20)
            middle = roll(e, g * 20 - 54)
            acc_lo = jnp.where(first, roll(e, g * 20), acc_lo)
            acc_lo = jnp.where(second, middle, acc_lo)
            acc_hi = jnp.where(first, middle, acc_hi)
            acc_hi = jnp.where(second, roll(e, g * 20 + 20), acc_hi)
        lo[xx] = acc_lo
        hi[xx] = acc_hi

    loop(0, 6, 36, body)


def ring_weights(b_pad, src, g, sp, total, planes, rows, scale, edges=None):
    lane = lanes_of(rows)

    def body(x):
        here = b_pad[x + 1, 8 : 8 + rows, :]
        down = roll(here, 1)
        up = roll(here, -1)
        if edges is not None:
            down = jnp.where(lane == 0, 0.0, down)
            up = jnp.where(lane == 127, 0.0, up)
        faces, inverse, tot = weights(
            here,
            (
                b_pad[x, 8 : 8 + rows, :],
                b_pad[x + 2, 8 : 8 + rows, :],
                b_pad[x + 1, 7 : 7 + rows, :],
                b_pad[x + 1, 9 : 9 + rows, :],
                down,
                up,
            ),
        )
        if edges is not None:
            faces[4] = jnp.where(lane == 0, 0.0, faces[4])
            faces[5] = jnp.where(lane == 127, 0.0, faces[5])
        for i in range(6):
            g[i, x] = faces[i]
        sp[x] = scale * 2.0 * inverse if src is None else src[x] * (scale * 2.0 * inverse)
        if total is not None:
            total[x] = tot

    loop(0, planes, rows // 4, body)


def ring_rest(v, g, sp, x, rows):
    here = v[x + 1, 8 : 8 + rows, :]
    rest = sp[x] - here
    rest = rest + g[0, x] * v[x, 8 : 8 + rows, :] + g[1, x] * v[x + 2, 8 : 8 + rows, :]
    rest = rest + g[2, x] * v[x + 1, 7 : 7 + rows, :] + g[3, x] * v[x + 1, 9 : 9 + rows, :]
    rest = rest + g[4, x] * roll(here, 1) + g[5, x] * roll(here, -1)
    return here, rest


def ring_step(v, v_out, g, sp, u, planes, rows, retain, factor):
    def body(x):
        here, rest = ring_rest(v, g, sp, x, rows)
        new = factor * rest
        if retain is not None:
            new = retain * u[x] + new
        u[x] = new
        v_out[x + 1, 8 : 8 + rows, :] = here + new

    loop(0, planes, rows // 16, body)


def ring_zero_start(v, u, sp, planes, rows, factor):
    def body(x):
        u[x] = factor * sp[x]
        v[x + 1, 8 : 8 + rows, :] = u[x]

    loop(0, planes, rows // 8, body)


def ring_cheb(va, vb, g, sp, u, planes, rows, recipe, from_zero):
    begin = 0
    if from_zero:
        ring_zero_start(va, u, sp, planes, rows, recipe[0][1])
        begin = 1
    for k in range(begin, len(recipe)):
        retain, factor = recipe[k]
        ring_step(va, vb, g, sp, u, planes, rows, None if k == 0 else retain, factor)
        va, vb = vb, va
    return va


LEVEL1_SCRATCH = [
    vm(38, 56, 128),
    vm(38, 56, 128),
    vm(38, 56, 128),
    vm(36, 40, 128),
    vm(36, 40, 128),
    vm(36, 40, 128),
    vm(8, 40, 128),
]


def level1_unpack(ext, z_lo, z_hi, source, b_pad, beta_out):
    iz = lax.axis_index("gz")
    low = flag(iz > 0)
    high = flag(iz < lax.axis_size("gz") - 1)
    lane = lanes_of(40)
    inner = lane < 64
    above = (lane >= 64) & (lane < 74)
    below = lane >= 118

    def unpack(xx):
        before = z_lo[xx] * low
        after = z_hi[xx] * high
        for k in range(6):
            x = k * 6 + xx
            e = ext[x]
            s = jnp.where(inner, e, 0.0)
            s = jnp.where(above, roll(after, 64 - k * 20), s)
            s = jnp.where(below, roll(before, 118 - k * 20), s)
            b = jnp.where(inner, roll(e, 64), 0.0)
            b = jnp.where(above, roll(after, 54 - k * 20), b)
            b = jnp.where(below, roll(before, 108 - k * 20), b)
            source[x] = s
            b_pad[x + 1, 8:48, :] = b
            beta_out[x] = b

    loop(0, 6, 36, unpack)


def level1_down(
    ext, z_lo, z_hi, iter_out, chunk, g, sp, beta_out,
    b_pad, va, vb, u, src, total, rows,
):
    for ref in (b_pad, va, vb):
        clear_edges(ref, 36, 40)
    level1_unpack(ext, z_lo, z_hi, src, b_pad, beta_out)
    ring_weights(b_pad, src, g, sp, total, 36, 40, 4.0)
    v = ring_cheb(va, vb, g, sp, u, 36, 40, RECIPE, True)
    iter_out[...] = v[1:37, 8:48, :]
    summed = []
    for x2 in range(8):
        parts = []
        for half in range(2):
            x = 10 + 2 * x2 + half
            _, rest = ring_rest(v, g, sp, x, 40)
            parts.append(rest * total[x])
        rows[x2] = (parts[0] + parts[1]) * (0.25 * 0.5 / 8.0)
        summed.append(rows[x2, pl.ds(10, 8, stride=2), :] + rows[x2, pl.ds(11, 8, stride=2), :])
    for half in range(2):
        acc = jnp.zeros((8, 128), F32)
        for quarter in range(4):
            weight = pick(lambda r, c: (r < 64) & ((r // 2 + 32 * quarter) == c))
            acc = acc + dot(summed[half * 4 + quarter], weight)
        chunk[half * 8 : half * 8 + 8, :] = acc


def sender(axis, step):
    count = lax.axis_size(axis)
    return lax.rem(lax.axis_index(axis) + count - step, count)


def gather_z(*refs):
    *parts, _, out = refs
    lane = lanes_of(8)
    for half in range(2):
        for quarter in range(4):
            acc = jnp.zeros((8, 128), F32)
            for step, part in enumerate(parts):
                owner = sender("gz", step)
                moved = roll(part[half * 8 : half * 8 + 8, :], lax.rem(owner - quarter + 4, 4) * 32)
                acc = jnp.where(lane // 32 == owner, moved, acc)
            out[half * 4 + quarter] = acc


def gather_x(*refs):
    *parts, _, out = refs
    for step, part in enumerate(parts):
        out[pl.ds(sender("gx", step) * 8, 8)] = part[...]


def stack_y(*refs):
    *parts, _, out = refs
    for step, part in enumerate(parts):
        out[step] = part[...]


def gather_y(same, other, out):
    count = lax.axis_size("gy")
    index = lax.axis_index("gy")
    sibling = index + 1 - 2 * lax.rem(index, 2)
    for stack, first in ((same, index), (other, sibling)):
        for step in range(4):
            owner = lax.rem(first + count - 2 * step, count)
            row = pl.multiple_of(8 + owner * 8, 8)
            out[8:40, pl.ds(row, 8), :] = stack[step]


def clear_whole(ref):
    def clear(x):
        ref[x, 0:8, :] = jnp.zeros((8, 128), F32)
        ref[x, 72:80, :] = jnp.zeros((8, 128), F32)

    loop(0, 48, 2, clear)
    for x in [*range(8), *range(40, 48)]:
        ref[x, 8:72, :] = jnp.zeros((64, 128), F32)


def coarse_prepare(same, sibling, g, inv, total, g3, inv3, gw, invw, b2, b3, bw, rows):
    clear_whole(b2)
    clear_edges(b3, 16, 32)
    clear_edges(bw, 22, 24)
    gather_y(same, sibling, b2)
    ring_weights(b2.at[7:41], None, g, inv, total, 32, 64, 16.0, edges=True)
    half_z = pick(lambda r, c: r // 2 == c)

    def restrict(x2):
        rows[x2] = (b2[8 + 2 * x2, 8:72, :] + b2[9 + 2 * x2, 8:72, :]) * (1.0 / 8.0)

    loop(0, 16, 8, restrict)

    def compress(x2):
        bet = rows[x2, pl.ds(0, 32, stride=2), :] + rows[x2, pl.ds(1, 32, stride=2), :]
        b3[x2 + 1, 8:40, :] = dot(bet, half_z)

    loop(0, 16, 9, compress)
    ring_weights(b3, None, g3, inv3, None, 16, 32, 64.0)
    ix = lax.axis_index("gx")
    row = pl.multiple_of(lax.axis_index("gy") * 8, 8)

    def window(x):
        bw[x + 1, 8:32, :] = b2[ix * 8 + 1 + x, pl.ds(row, 24), :]

    loop(0, 22, 6, window)
    ring_weights(bw, None, gw, invw, None, 22, 24, 16.0, edges=True)


COARSE_SHAPES = [
    (6, 32, 64, 128),
    (32, 64, 128),
    (32, 64, 128),
    (6, 16, 32, 128),
    (16, 32, 128),
    (6, 22, 24, 128),
    (22, 24, 128),
]


def bottom(
    same, sibling, g, inv, total, g3, inv3, gw, invw, out,
    s2, va, vb, sp, u, v3a, v3b, sp3, u3, rows, wa, wb, spw, uw,
):
    for ref in (s2, va, vb):
        clear_whole(ref)
    gather_y(same, sibling, s2)

    def scale(x):
        sp[x] = s2[x + 8, 8:72, :] * inv[x]

    loop(0, 32, 8, scale)
    v = ring_cheb(va.at[7:41], vb.at[7:41], g, sp, u, 32, 64, RECIPE, True)
    iterate = vb if SMOOTH % 2 == 0 else va

    clear_edges(v3a, 16, 32)
    clear_edges(v3b, 16, 32)
    half_z = pick(lambda r, c: r // 2 == c)

    def restrict(x2):
        parts = []
        for half in range(2):
            x = 2 * x2 + half
            _, rest = ring_rest(v, g, sp, x, 64)
            parts.append(rest * total[x])
        rows[x2] = (parts[0] + parts[1]) * (0.0625 * 0.5 / 8.0)

    loop(0, 16, 16, restrict)

    def compress(x2):
        res = rows[x2, pl.ds(0, 32, stride=2), :] + rows[x2, pl.ds(1, 32, stride=2), :]
        sp3[x2] = dot(res, half_z) * inv3[x2]

    loop(0, 16, 9, compress)
    c3 = ring_cheb(v3a, v3b, g3, sp3, u3, 16, 32, BOTTOM_RECIPE, True)

    other = va if iterate is vb else vb
    double_z = pick(lambda r, c: c // 2 == r)

    def prolong(x3):
        wide = dot(c3[x3 + 1, 8:40, :], double_z)
        rows[x3, pl.ds(0, 32, stride=2), :] = wide
        rows[x3, pl.ds(1, 32, stride=2), :] = wide
        for half in range(2):
            x = 8 + 2 * x3 + half
            other[x, 8:72, :] = iterate[x, 8:72, :] + rows[x3]

    loop(0, 16, 18, prolong)
    ix = lax.axis_index("gx")
    iz = lax.axis_index("gz")
    clear_edges(wa, 22, 24)
    clear_edges(wb, 22, 24)
    row = pl.multiple_of(lax.axis_index("gy") * 8, 8)

    def window(x):
        plane = ix * 8 + 1 + x
        wa[x + 1, 8:32, :] = other[plane, pl.ds(row, 24), :]
        spw[x] = s2[plane, pl.ds(row, 24), :] * invw[x]

    loop(0, 22, 6, window)
    c2 = ring_cheb(wa, wb, gw, spw, uw, 22, 24, RECIPE, False)
    shift = (128 - iz * 32) % 128
    for x in range(18):
        out[x] = roll(c2[x + 3, 8:32, :], shift)


COARSE_SCRATCH = [
    vm(48, 80, 128),
    vm(18, 48, 128),
    vm(24, 40, 128),
    vm(16, 64, 128),
]
BOTTOM_SCRATCH = [
    vm(48, 80, 128),
    vm(48, 80, 128),
    vm(48, 80, 128),
    vm(32, 64, 128),
    vm(32, 64, 128),
    vm(18, 48, 128),
    vm(18, 48, 128),
    vm(16, 32, 128),
    vm(16, 32, 128),
    vm(16, 64, 128),
    vm(24, 40, 128),
    vm(24, 40, 128),
    vm(22, 24, 128),
    vm(22, 24, 128),
]


def level1_up(c2, g, sp, beta, iterate, out, va, vb, u, wide, rows):
    for ref in (va, vb):
        clear_edges(ref, 36, 40)
    spread = pick(lambda r, c: ((c < 74) & (c // 2 == r)) | ((c >= 118) & (c // 2 + 64 == r)))
    for x2 in range(18):
        rows[x2, 32:40, :] = jnp.zeros((8, 128), F32)

    def prolong(x2):
        wide[x2] = dot(c2[x2], spread)
        part = wide[x2, 3:21, :]
        rows[x2, pl.ds(0, 18, stride=2), :] = part
        rows[x2, pl.ds(1, 18, stride=2), :] = part
        for half in range(2):
            x = 2 * x2 + half
            va[x + 1, 8:48, :] = jnp.where(beta[x] > 0.0, iterate[x] + rows[x2], 0.0)

    loop(0, 18, 12, prolong)
    v = ring_cheb(va, vb, g, sp, u, 36, 40, RECIPE, False)
    out[...] = v[7:31, 14:38, :]


def level0_up(
    c1, beta, g_main, g_strip, sp, sp_t, beta_t, iterate, iterate_t, out,
    va, vb, ta, tb, ghost, u, u_t, rows,
):
    for ref in (va, vb):
        clear_edges(ref, 48, 48)
    for ref in (ta, tb):
        clear_strip(ref)
    spread = pick(lambda r, c: c // 2 == r)

    def prolong(x1):
        wide = dot(c1[x1], spread)
        rows[x1, pl.ds(0, 24, stride=2), :] = wide
        rows[x1, pl.ds(1, 24, stride=2), :] = wide
        for half in range(2):
            x = 2 * x1 + half
            va[x + 1, 8:56, :] = jnp.where(beta[x] > 0.0, iterate[x] + rows[x1], 0.0)

    loop(0, 24, 12, prolong)

    def prolong_strip(m):
        acc = jnp.zeros((24, 128), F32)
        for k in range(8):
            to = pick(
                lambda r, c: (c // 16 == k)
                & (
                    ((c % 16 < 8) & (r == 64 + (7 - c % 16) // 2))
                    | ((c % 16 >= 8) & (r == 124 + (15 - c % 16) // 2))
                )
            )
            acc = acc + dot(c1[k * 3 + m], to)
        rows[m, pl.ds(0, 24, stride=2), :] = acc
        rows[m, pl.ds(1, 24, stride=2), :] = acc
        for half in range(2):
            xx = 2 * m + half
            ta[xx, 8:56, :] = jnp.where(beta_t[xx] > 0.0, iterate_t[xx] + rows[m], 0.0)

    loop(0, 3, 36, prolong_strip)
    for x in [*range(6), *range(42, 48)]:
        vb[x + 1, 8:56, :] = jnp.zeros((48, 128), F32)
    bufs = [(va, ta), (vb, tb)]
    for k in range(SMOOTH):
        (v, t), (w, s) = bufs
        retain, factor = RECIPE[k]
        if k == 0:
            retain = None
        if k < SMOOTH - 1:
            low, high = (4, 44) if k < 2 else (6, 42)
            level0_step(
                v, t, w, s, ghost, g_main, g_strip, sp, sp_t, u, u_t, low, high, retain, factor
            )
        else:

            def last(x):
                here, rest = block_rest(v, t, g_main, sp, x, 8)
                out[x - 8] = here + retain * u[x, 8:40] + factor * rest

            loop(8, 40, 4, last)
        bufs = [(w, s), (v, t)]


def ring(value, axis, step):
    count = lax.axis_size(axis)
    return lax.ppermute(value, axis, [(i, (i + step) % count) for i in range(count)])


def trade(lo, hi, axis):
    return ring(hi, axis, 1), ring(lo, axis, -1)


def gather(kernel, parts, after, *shape):
    return call(kernel, sds(*shape), name=kernel.__name__, last_unread=len(parts) + 1)(*parts, after)


def around(value, axis):
    return [value] + [ring(value, axis, step) for step in range(1, lax.axis_size(axis))]


def chips(value):
    return [value] + [ring(value, "gy", 2 * step) for step in (1, 2, 3)]


def across(value):
    count = lax.axis_size("gy")
    return lax.ppermute(value, "gy", [(i, i + 1 - 2 * (i % 2)) for i in range(count)])


def per_device(source, beta):
    lo = jnp.stack([source[0:8], beta[0:8]])
    hi = jnp.stack([source[24:32], beta[24:32]])
    lo, hi, source, beta = lax.optimization_barrier((lo, hi, source, beta))
    x_lo, x_hi = trade(lo, hi, "gx")
    beta2 = call(coarse_beta, sds(16, 128), [vm(32, 128)], name="coarse_beta")(beta)
    beta2_block = gather(gather_z, around(beta2, "gz"), lo, 8, 8, 128)
    x_lo, x_hi, beta2_block = lax.optimization_barrier((x_lo, x_hi, beta2_block))
    slab = sds(2, 48, 8, 128)
    mid = sds(48, 32, 128)
    lo, hi, s_mid, b_mid = call(pack_y, (slab, slab, mid, mid), name="pack_y", mib=4)(
        source, beta, x_lo, x_hi
    )
    y_lo, y_hi = trade(lo, hi, "gy")
    beta2_slab = gather(gather_x, around(beta2_block, "gx"), lo, 32, 8, 128)
    y_lo, y_hi, beta2_slab = lax.optimization_barrier((y_lo, y_hi, beta2_slab))
    whole = sds(48, 48, 128)
    strip = sds(6, 48, 128)
    src_ext, beta_ext, lo, hi = call(
        pack_z, (whole, whole, strip, strip), name="pack_z", mib=4
    )(s_mid, b_mid, y_lo, y_hi)
    z_lo, z_hi = trade(lo, hi, "gz")
    beta2_stack = gather(stack_y, chips(beta2_slab), lo, 4, 32, 8, 128)
    z_lo, z_hi, beta2_stack = lax.optimization_barrier((z_lo, z_hi, beta2_stack))
    iter0, iter0_t, c, lo, hi, *ready = call(
        level0_down,
        (
            whole,
            strip,
            sds(16, 16, 128),
            sds(10, 16, 128),
            sds(10, 16, 128),
            sds(7, 48, 48, 128),
            sds(6, 6, 48, 128),
            whole,
            strip,
            strip,
        ),
        LEVEL0_SCRATCH,
        name="level0_down",
        mib=16,
    )(src_ext, beta_ext, z_lo, z_hi)
    x_lo, x_hi = trade(lo, hi, "gx")
    lo, hi = call(pack1_y, (sds(360, 128), sds(360, 128)), name="pack1_y")(c, x_lo, x_hi)
    y_lo, y_hi = trade(lo, hi, "gy")
    ext, lo, hi = call(
        pack1_z, (sds(36, 40, 128), sds(6, 40, 128), sds(6, 40, 128)), name="pack1_z"
    )(c, x_lo, x_hi, y_lo, y_hi)
    z1_lo, z1_hi = trade(lo, hi, "gz")
    beta2_stack, _ = lax.optimization_barrier((beta2_stack, lo))
    beta2_other = across(beta2_stack)
    z1_lo, z1_hi, beta2_other = lax.optimization_barrier((z1_lo, z1_hi, beta2_other))
    level1 = sds(36, 40, 128)
    iter1, chunk, g1, sp1, beta1 = call(
        level1_down,
        (level1, sds(16, 128), sds(6, 36, 40, 128), level1, level1),
        LEVEL1_SCRATCH,
        name="level1_down",
        mib=8,
    )(ext, z1_lo, z1_hi)
    parts = around(chunk, "gz")
    parts = around(gather(gather_z, parts, chunk, 8, 8, 128), "gx")
    slab = gather(gather_x, parts, chunk, 32, 8, 128)
    stack = gather(stack_y, chips(slab), slab, 4, 32, 8, 128)
    stack_other = across(stack)
    coarse = call(
        coarse_prepare,
        tuple(sds(*shape) for shape in COARSE_SHAPES),
        COARSE_SCRATCH,
        name="coarse_prepare",
        mib=8,
    )(beta2_stack, beta2_other)
    c2 = call(bottom, sds(18, 24, 128), BOTTOM_SCRATCH, name="bottom", mib=18)(
        stack, stack_other, *coarse
    )
    c1 = call(
        level1_up,
        sds(24, 24, 128),
        [vm(38, 56, 128), vm(38, 56, 128), vm(36, 40, 128), vm(18, 24, 128), vm(18, 40, 128)],
        name="level1_up",
        mib=8,
    )(c2, g1, sp1, beta1, iter1)
    return call(
        level0_up,
        sds(32, 32, 128),
        [vm(50, 64, 128), vm(50, 64, 128), vm(6, 64, 128), vm(6, 64, 128), vm(6, 48, 128)]
        + [vm(48, 48, 128), vm(6, 48, 128), vm(24, 48, 128)],
        name="level0_up",
        mib=14,
    )(c1, beta_ext, *ready, iter0, iter0_t)


def solution(mesh):
    placed = (P(*AXES), P(*AXES))
    return jax.shard_map(
        per_device, mesh=mesh, in_specs=placed, out_specs=P(*AXES), check_vma=False
    )
```

```python
import jax
import jax.numpy as jnp
from jax import lax
from jax.experimental import pallas as pl
from jax.experimental.pallas import tpu as pltpu
from jax.sharding import PartitionSpec as P

SMOOTH = 4
BOTTOM = 12
LOW_EIG = 0.3
HIGH_EIG = 2.0
BOTTOM_LOW = 0.02

AXES = ("gx", "gy", "gz")
F32 = jnp.float32
MIB = 1024 * 1024


def cheb_plan(degree, lowest, highest):
    centre = 0.5 * (highest + lowest)
    radius = 0.5 * (highest - lowest)
    ratio_s = centre / radius
    rho_old = 1.0 / ratio_s
    recipe = [(0.0, 1.0 / centre)]
    for position in range(1, degree):
        rho_new = 1.0 / (2.0 * ratio_s - rho_old)
        recipe.append((rho_new * rho_old, 2.0 * rho_new / radius))
        rho_old = rho_new
    return recipe


RECIPE = cheb_plan(SMOOTH, LOW_EIG, HIGH_EIG)
BOTTOM_RECIPE = cheb_plan(BOTTOM, BOTTOM_LOW, HIGH_EIG)


def sds(*shape):
    return jax.ShapeDtypeStruct(shape, F32)


def vm(*shape):
    return pltpu.VMEM(shape, F32)


def call(body, outs, scratch=(), name=None, mib=2, last_unread=None):
    specs = {}
    if last_unread:
        whole = pl.BlockSpec(memory_space=pltpu.VMEM)
        specs["in_specs"] = [whole] * (last_unread - 1) + [pl.BlockSpec(memory_space=pl.ANY)]
    return pl.pallas_call(
        body,
        out_shape=outs,
        **specs,
        scratch_shapes=list(scratch),
        compiler_params=pltpu.CompilerParams(vmem_limit_bytes=mib * MIB),
        name=name,
    )


def loop(low, high, vectors, body):
    count = high - low
    most = max(1, min(count, 72 // vectors))
    width = max([w for w in range(1, most + 1) if count % w == 0])
    if width * 2 < most:
        width = most
    rounds = count // width

    def chunk(i, carry):
        for k in range(width):
            body(low + i * width + k)
        return carry

    if rounds > 1:
        lax.fori_loop(0, rounds, chunk, 0)
    else:
        chunk(0, 0)
    for x in range(low + rounds * width, high):
        body(x)


def lanes_of(rows):
    return lax.broadcasted_iota(jnp.int32, (rows, 128), 1)


def roll(value, shift):
    if isinstance(shift, int):
        shift = shift % 128
        if shift == 0:
            return value
    return pltpu.roll(value, shift, 1)


def flag(condition):
    return jnp.where(condition, 1.0, 0.0).astype(F32)


def dot(left, right):
    return lax.dot_general(
        left,
        right,
        (((1,), (0,)), ((), ())),
        precision=lax.Precision.HIGHEST,
        preferred_element_type=F32,
    )


def pick(match):
    row = lax.broadcasted_iota(jnp.int32, (128, 128), 0)
    col = lax.broadcasted_iota(jnp.int32, (128, 128), 1)
    return jnp.where(match(row, col), 1.0, 0.0).astype(F32)


def coarse_beta(beta, out, rows):
    total = []
    for x in range(8):
        s = beta[4 * x] + beta[4 * x + 1] + beta[4 * x + 2] + beta[4 * x + 3]
        rows[...] = s
        t = rows[pl.ds(0, 8, stride=4), :] + rows[pl.ds(1, 8, stride=4), :]
        t = t + rows[pl.ds(2, 8, stride=4), :] + rows[pl.ds(3, 8, stride=4), :]
        total.append(t * (1.0 / 64.0))
    for half in range(2):
        acc = jnp.zeros((8, 128), F32)
        for quarter in range(4):
            weight = pick(lambda r, c: (r // 4 + 32 * quarter) == c)
            acc = acc + dot(total[half * 4 + quarter], weight)
        out[half * 8 : half * 8 + 8, :] = acc


def pack_y(src, beta, from_lo, from_hi, lo, hi, s_mid, b_mid):
    index = lax.axis_index("gx")
    low = flag(index > 0)
    high = flag(index < lax.axis_size("gx") - 1)
    for field, (ref, mid) in enumerate(((src, s_mid), (beta, b_mid))):
        mid[0:8] = from_lo[field] * low
        mid[8:40] = ref[...]
        mid[40:48] = from_hi[field] * high
        lo[field] = mid[:, 0:8, :]
        hi[field] = mid[:, 24:32, :]


def pack_z(s_mid, b_mid, y_lo, y_hi, s_out, b_out, lo, hi):
    iy = lax.axis_index("gy")
    y_low = flag(iy > 0)
    y_high = flag(iy < lax.axis_size("gy") - 1)
    for field, (mid, out) in enumerate(((s_mid, s_out), (b_mid, b_out))):
        out[:, 8:40, :] = mid[...]
        out[:, 0:8, :] = y_lo[field] * y_low
        out[:, 40:48, :] = y_hi[field] * y_high
    lane = lanes_of(48)

    def body(xx):
        acc_lo = jnp.zeros((48, 128), F32)
        acc_hi = jnp.zeros((48, 128), F32)
        for g in range(8):
            s = s_out[g * 6 + xx]
            b = b_out[g * 6 + xx]
            first = (lane >= g * 16) & (lane < g * 16 + 8)
            second = (lane >= g * 16 + 8) & (lane < g * 16 + 16)
            acc_lo = jnp.where(first, roll(s, g * 16), acc_lo)
            acc_lo = jnp.where(second, roll(b, g * 16 + 8), acc_lo)
            acc_hi = jnp.where(first, roll(s, g * 16 + 8), acc_hi)
            acc_hi = jnp.where(second, roll(b, g * 16 + 16), acc_hi)
        lo[xx] = acc_lo
        hi[xx] = acc_hi

    loop(0, 6, 36, body)


def strip_ghosts(values, ghost):
    lane = lanes_of(48)

    def body(xx):
        acc = jnp.zeros((48, 128), F32)
        for g in range(8):
            acc = jnp.where(lane // 16 == g, roll(values[g * 6 + xx + 1, 8:56, :], g * 16 + 8), acc)
        ghost[xx] = acc

    loop(0, 6, 36, body)


def strip_sides(strip, xx):
    after = strip[xx + 1, 8:56, :] if xx < 5 else roll(strip[0, 8:56, :], -16)
    before = strip[xx - 1, 8:56, :] if xx > 0 else roll(strip[5, 8:56, :], 16)
    return before, after


def strip_z(strip, ghost, xx, lane):
    here = strip[xx, 8:56, :]
    up = jnp.where(lane % 16 == 8, ghost[xx], roll(here, 1))
    down = jnp.where(lane % 16 == 7, ghost[xx], roll(here, -1))
    return down, up


def block_edge(strip, x, first=8, count=48):
    g = x // 6
    return roll(strip[x - g * 6, first : first + count, :], 120 - g * 16)


def weights(here, sides):
    sums = [here + side for side in sides]
    total = sums[0] + sums[1] + sums[2] + sums[3] + sums[4] + sums[5]
    inverse = jnp.where(here > 0.0, 1.0 / total, 0.0)
    return [s * inverse for s in sums], inverse, total


def level0_setup(b_pad, bt_pad, ghost, src, src_t, g_main, g_strip, sp, sp_t, total):
    strip_ghosts(b_pad, ghost)
    lane = lanes_of(48)

    def body(x):
        here = b_pad[x + 1, 8:56, :]
        edge = block_edge(bt_pad, x)
        down = jnp.where(lane == 0, edge, roll(here, 1))
        up = jnp.where(lane == 127, edge, roll(here, -1))
        faces, inverse, tot = weights(
            here,
            (
                b_pad[x, 8:56, :],
                b_pad[x + 2, 8:56, :],
                b_pad[x + 1, 7:55, :],
                b_pad[x + 1, 9:57, :],
                down,
                up,
            ),
        )
        for i in range(4):
            g_main[i, x] = faces[i]
        g_main[4, x] = jnp.where(lane == 0, 0.0, faces[4])
        g_main[5, x] = jnp.where(lane == 127, 0.0, faces[5])
        g_main[6, x] = jnp.where(lane == 0, faces[4], jnp.where(lane == 127, faces[5], 0.0))
        sp[x] = src[x] * (2.0 * inverse)
        if total is not None:
            total[x] = tot

    loop(0, 48, 6, body)
    for xx in range(6):
        before, after = strip_sides(bt_pad, xx)
        down, up = strip_z(bt_pad, ghost, xx, lane)
        faces, inverse, _ = weights(
            bt_pad[xx, 8:56, :],
            (before, after, bt_pad[xx, 7:55, :], bt_pad[xx, 9:57, :], down, up),
        )
        for i in range(6):
            g_strip[i, xx] = faces[i]
        sp_t[xx] = src_t[xx] * (2.0 * inverse)


def block_rest(v, t, g_main, sp, x, skip=0):
    count = 48 - 2 * skip
    first = 8 + skip
    keep = slice(skip, 48 - skip)
    here = v[x + 1, first : first + count, :]
    rest = sp[x, keep] - here
    rest = rest + g_main[0, x, keep] * v[x, first : first + count, :]
    rest = rest + g_main[1, x, keep] * v[x + 2, first : first + count, :]
    rest = rest + g_main[2, x, keep] * v[x + 1, first - 1 : first - 1 + count, :]
    rest = rest + g_main[3, x, keep] * v[x + 1, first + 1 : first + 1 + count, :]
    rest = rest + g_main[4, x, keep] * roll(here, 1) + g_main[5, x, keep] * roll(here, -1)
    rest = rest + g_main[6, x, keep] * block_edge(t, x, first, count)
    return here, rest


def level0_step(v, t, v_out, t_out, ghost, g_main, g_strip, sp, sp_t, u, u_t, low, high, retain, factor):
    strip_ghosts(v, ghost)
    lane = lanes_of(48)

    def body(x):
        here, rest = block_rest(v, t, g_main, sp, x)
        new = factor * rest
        if retain is not None:
            new = retain * u[x] + new
        u[x] = new
        v_out[x + 1, 8:56, :] = here + new

    loop(low, high, 6, body)
    for xx in range(6):
        here = t[xx, 8:56, :]
        before, after = strip_sides(t, xx)
        down, up = strip_z(t, ghost, xx, lane)
        rest = sp_t[xx] - here
        rest = rest + g_strip[0, xx] * before + g_strip[1, xx] * after
        rest = rest + g_strip[2, xx] * t[xx, 7:55, :] + g_strip[3, xx] * t[xx, 9:57, :]
        rest = rest + g_strip[4, xx] * down + g_strip[5, xx] * up
        new = factor * rest
        if retain is not None:
            new = retain * u_t[xx] + new
        u_t[xx] = new
        t_out[xx, 8:56, :] = here + new


def clear_edges(ref, planes, rows):
    width = ref.shape[1]
    ref[0] = jnp.zeros((width, 128), F32)
    ref[planes + 1] = jnp.zeros((width, 128), F32)

    def body(x):
        ref[x, 0:8, :] = jnp.zeros((8, 128), F32)
        ref[x, 8 + rows : width, :] = jnp.zeros((width - 8 - rows, 128), F32)

    loop(0, planes + 2, 4, body)


def clear_strip(ref):
    for xx in range(6):
        ref[xx, 0:8, :] = jnp.zeros((8, 128), F32)
        ref[xx, 56:64, :] = jnp.zeros((8, 128), F32)


def unpack_strip(z_lo, z_hi, src_t, bt_pad):
    iz = lax.axis_index("gz")
    low = flag(iz > 0)
    high = flag(iz < lax.axis_size("gz") - 1)

    def mirror(first, last):
        return pick(lambda r, c: (r // 16 == c // 16) & ((r % 16 < 8) == first) & (r % 16 + c % 16 == last))

    s_lo, s_hi = mirror(True, 15), mirror(True, 7)
    b_lo, b_hi = mirror(False, 23), mirror(False, 15)
    for xx in range(6):
        before = z_lo[xx] * low
        after = z_hi[xx] * high
        src_t[xx] = dot(before, s_lo) + dot(after, s_hi)
        bt_pad[xx, 8:56, :] = dot(before, b_lo) + dot(after, b_hi)


LEVEL0_SCRATCH = [
    vm(50, 64, 128),
    vm(6, 64, 128),
    vm(50, 64, 128),
    vm(50, 64, 128),
    vm(6, 64, 128),
    vm(6, 64, 128),
    vm(6, 48, 128),
    vm(48, 48, 128),
    vm(6, 48, 128),
    vm(6, 48, 128),
    vm(48, 48, 128),
    vm(2, 16, 32, 128),
]


def level0_down(
    src, beta, z_lo, z_hi, iter_out, iter_t_out, c_out, c_lo, c_hi, g_main, g_strip, sp, sp_t, bt_out,
    b_pad, bt_pad, va, vb, ta, tb, ghost, u, u_t, src_t, total, rows,
):
    for ref in (b_pad, va, vb):
        clear_edges(ref, 48, 48)
    for ref in (bt_pad, ta, tb):
        clear_strip(ref)
    b_pad[1:49, 8:56, :] = beta[...]
    unpack_strip(z_lo, z_hi, src_t, bt_pad)
    for xx in range(6):
        bt_out[xx] = bt_pad[xx, 8:56, :]
    level0_setup(b_pad, bt_pad, ghost, src, src_t, g_main, g_strip, sp, sp_t, total)

    first = RECIPE[0][1]

    def start(x):
        u[x] = first * sp[x]
        va[x + 1, 8:56, :] = u[x]

    loop(0, 48, 8, start)
    for xx in range(6):
        u_t[xx] = first * sp_t[xx]
        ta[xx, 8:56, :] = u_t[xx]
    bufs = [(va, ta), (vb, tb)]
    for k in range(1, SMOOTH):
        (v, t), (w, s) = bufs
        retain, factor = RECIPE[k]
        level0_step(v, t, w, s, ghost, g_main, g_strip, sp, sp_t, u, u_t, 0, 48, retain, factor)
        bufs = [(w, s), (v, t)]
    v, t = bufs[0]
    iter_out[...] = v[1:49, 8:56, :]
    for xx in range(6):
        iter_t_out[xx] = t[xx, 8:56, :]

    to_low = pick(lambda r, c: r // 2 == c)
    to_high = pick(lambda r, c: r // 2 + 64 == c)

    def restrict(x2):
        parts = []
        for half in range(2):
            x = 8 + 2 * x2 + half
            _, rest = block_rest(v, t, g_main, sp, x, 8)
            parts.append(rest * total[x, 8:40])
        rows[0, x2] = (parts[0] + parts[1]) * (0.5 / 8.0)
        rows[1, x2] = (b_pad[9 + 2 * x2, 16:48, :] + b_pad[10 + 2 * x2, 16:48, :]) * (1.0 / 8.0)

    loop(0, 16, 8, restrict)

    def compress(x2):
        res = rows[0, x2, pl.ds(0, 16, stride=2), :] + rows[0, x2, pl.ds(1, 16, stride=2), :]
        bet = rows[1, x2, pl.ds(0, 16, stride=2), :] + rows[1, x2, pl.ds(1, 16, stride=2), :]
        c_out[x2] = dot(res, to_low) + dot(bet, to_high)

    loop(0, 16, 8, compress)
    c_lo[...] = c_out[0:10]
    c_hi[...] = c_out[6:16]


def pack1_y(c, from_lo, from_hi, lo, hi):
    index = lax.axis_index("gx")
    low = flag(index > 0)
    high = flag(index < lax.axis_size("gx") - 1)
    for x in range(36):
        if x < 10:
            plane = from_lo[x] * low
        elif x < 26:
            plane = c[x - 10]
        else:
            plane = from_hi[x - 26] * high
        lo[x * 10 : x * 10 + 10, :] = plane[0:10]
        hi[x * 10 : x * 10 + 10, :] = plane[6:16]


def pack1_z(c, x_lo, x_hi, y_lo, y_hi, ext, lo, hi):
    ix = lax.axis_index("gx")
    iy = lax.axis_index("gy")
    x_low = flag(ix > 0)
    x_high = flag(ix < lax.axis_size("gx") - 1)
    y_low = flag(iy > 0)
    y_high = flag(iy < lax.axis_size("gy") - 1)
    ext[0:10, 10:26, :] = x_lo[...] * x_low
    ext[10:26, 10:26, :] = c[...]
    ext[26:36, 10:26, :] = x_hi[...] * x_high
    for x in range(36):
        ext[x, 0:10, :] = y_lo[x * 10 : x * 10 + 10, :] * y_low
        ext[x, 26:36, :] = y_hi[x * 10 : x * 10 + 10, :] * y_high
        ext[x, 36:40, :] = jnp.zeros((4, 128), F32)
    lane = lanes_of(40)

    def body(xx):
        acc_lo = jnp.zeros((40, 128), F32)
        acc_hi = jnp.zeros((40, 128), F32)
        for g in range(6):
            e = ext[g * 6 + xx]
            first = (lane >= g * 20) & (lane < g * 20 + 10)
            second = (lane >= g * 20 + 10) & (lane < g * 20 + 20)
            middle = roll(e, g * 20 - 54)
            acc_lo = jnp.where(first, roll(e, g * 20), acc_lo)
            acc_lo = jnp.where(second, middle, acc_lo)
            acc_hi = jnp.where(first, middle, acc_hi)
            acc_hi = jnp.where(second, roll(e, g * 20 + 20), acc_hi)
        lo[xx] = acc_lo
        hi[xx] = acc_hi

    loop(0, 6, 36, body)


def ring_weights(b_pad, src, g, sp, total, planes, rows, scale, edges=None):
    lane = lanes_of(rows)

    def body(x):
        here = b_pad[x + 1, 8 : 8 + rows, :]
        down = roll(here, 1)
        up = roll(here, -1)
        if edges is not None:
            down = jnp.where(lane == 0, 0.0, down)
            up = jnp.where(lane == 127, 0.0, up)
        faces, inverse, tot = weights(
            here,
            (
                b_pad[x, 8 : 8 + rows, :],
                b_pad[x + 2, 8 : 8 + rows, :],
                b_pad[x + 1, 7 : 7 + rows, :],
                b_pad[x + 1, 9 : 9 + rows, :],
                down,
                up,
            ),
        )
        if edges is not None:
            faces[4] = jnp.where(lane == 0, 0.0, faces[4])
            faces[5] = jnp.where(lane == 127, 0.0, faces[5])
        for i in range(6):
            g[i, x] = faces[i]
        sp[x] = scale * 2.0 * inverse if src is None else src[x] * (scale * 2.0 * inverse)
        if total is not None:
            total[x] = tot

    loop(0, planes, rows // 5, body)


def ring_rest(v, g, sp, x, rows):
    here = v[x + 1, 8 : 8 + rows, :]
    rest = sp[x] - here
    rest = rest + g[0, x] * v[x, 8 : 8 + rows, :] + g[1, x] * v[x + 2, 8 : 8 + rows, :]
    rest = rest + g[2, x] * v[x + 1, 7 : 7 + rows, :] + g[3, x] * v[x + 1, 9 : 9 + rows, :]
    rest = rest + g[4, x] * roll(here, 1) + g[5, x] * roll(here, -1)
    return here, rest


def ring_step(v, v_out, g, sp, u, planes, rows, retain, factor):
    def body(x):
        here, rest = ring_rest(v, g, sp, x, rows)
        new = factor * rest
        if retain is not None:
            new = retain * u[x] + new
        u[x] = new
        v_out[x + 1, 8 : 8 + rows, :] = here + new

    loop(0, planes, rows // 16, body)


def ring_zero_start(v, u, sp, planes, rows, factor):
    def body(x):
        u[x] = factor * sp[x]
        v[x + 1, 8 : 8 + rows, :] = u[x]

    loop(0, planes, rows // 8, body)


def ring_cheb(va, vb, g, sp, u, planes, rows, recipe, from_zero):
    begin = 0
    if from_zero:
        ring_zero_start(va, u, sp, planes, rows, recipe[0][1])
        begin = 1
    for k in range(begin, len(recipe)):
        retain, factor = recipe[k]
        ring_step(va, vb, g, sp, u, planes, rows, None if k == 0 else retain, factor)
        va, vb = vb, va
    return va


LEVEL1_SCRATCH = [
    vm(38, 56, 128),
    vm(38, 56, 128),
    vm(38, 56, 128),
    vm(36, 40, 128),
    vm(36, 40, 128),
    vm(36, 40, 128),
    vm(8, 40, 128),
]


def level1_unpack(ext, z_lo, z_hi, source, b_pad, beta_out):
    iz = lax.axis_index("gz")
    low = flag(iz > 0)
    high = flag(iz < lax.axis_size("gz") - 1)
    lane = lanes_of(40)
    inner = lane < 64
    above = (lane >= 64) & (lane < 74)
    below = lane >= 118

    def unpack(xx):
        before = z_lo[xx] * low
        after = z_hi[xx] * high
        for k in range(6):
            x = k * 6 + xx
            e = ext[x]
            s = jnp.where(inner, e, 0.0)
            s = jnp.where(above, roll(after, 64 - k * 20), s)
            s = jnp.where(below, roll(before, 118 - k * 20), s)
            b = jnp.where(inner, roll(e, 64), 0.0)
            b = jnp.where(above, roll(after, 54 - k * 20), b)
            b = jnp.where(below, roll(before, 108 - k * 20), b)
            source[x] = s
            b_pad[x + 1, 8:48, :] = b
            beta_out[x] = b

    loop(0, 6, 36, unpack)


def level1_down(
    ext, z_lo, z_hi, iter_out, chunk, g, sp, beta_out,
    b_pad, va, vb, u, src, total, rows,
):
    for ref in (b_pad, va, vb):
        clear_edges(ref, 36, 40)
    level1_unpack(ext, z_lo, z_hi, src, b_pad, beta_out)
    ring_weights(b_pad, src, g, sp, total, 36, 40, 4.0)
    v = ring_cheb(va, vb, g, sp, u, 36, 40, RECIPE, True)
    iter_out[...] = v[1:37, 8:48, :]
    summed = []
    for x2 in range(8):
        parts = []
        for half in range(2):
            x = 10 + 2 * x2 + half
            _, rest = ring_rest(v, g, sp, x, 40)
            parts.append(rest * total[x])
        rows[x2] = (parts[0] + parts[1]) * (0.25 * 0.5 / 8.0)
        summed.append(rows[x2, pl.ds(10, 8, stride=2), :] + rows[x2, pl.ds(11, 8, stride=2), :])
    for half in range(2):
        acc = jnp.zeros((8, 128), F32)
        for quarter in range(4):
            weight = pick(lambda r, c: (r < 64) & ((r // 2 + 32 * quarter) == c))
            acc = acc + dot(summed[half * 4 + quarter], weight)
        chunk[half * 8 : half * 8 + 8, :] = acc


def sender(axis, step):
    count = lax.axis_size(axis)
    return lax.rem(lax.axis_index(axis) + count - step, count)


def singles(parts):
    return [part.at[i] for part in parts for i in range(2)] if len(parts) == 2 else parts


def gather_z(*refs):
    *parts, _, out = refs
    parts = singles(parts)
    lane = lanes_of(8)
    for half in range(2):
        for quarter in range(4):
            acc = jnp.zeros((8, 128), F32)
            for step, part in enumerate(parts):
                owner = sender("gz", step)
                moved = roll(part[half * 8 : half * 8 + 8, :], lax.rem(owner - quarter + 4, 4) * 32)
                acc = jnp.where(lane // 32 == owner, moved, acc)
            out[half * 4 + quarter] = acc


def gather_x(*refs):
    *parts, _, out = refs
    parts = singles(parts)
    for step, part in enumerate(parts):
        out[pl.ds(sender("gx", step) * 8, 8)] = part[...]


def stack_y(*refs):
    *parts, _, out = refs
    for step, part in enumerate(singles(parts)):
        out[step] = part[...]


def pair(mine, other, _, out):
    out[0] = mine[...]
    out[1] = other[...]


def gather_y(same, other, out):
    count = lax.axis_size("gy")
    index = lax.axis_index("gy")
    sibling = index + 1 - 2 * lax.rem(index, 2)
    for stack, first in ((same, index), (other, sibling)):
        for step in range(4):
            owner = lax.rem(first + count - 2 * step, count)
            row = pl.multiple_of(8 + owner * 8, 8)
            out[8:40, pl.ds(row, 8), :] = stack[step]


def clear_whole(ref):
    def clear(x):
        ref[x, 0:8, :] = jnp.zeros((8, 128), F32)
        ref[x, 72:80, :] = jnp.zeros((8, 128), F32)

    loop(0, 48, 2, clear)
    for x in [*range(8), *range(40, 48)]:
        ref[x, 8:72, :] = jnp.zeros((64, 128), F32)


def coarse_prepare(same, sibling, g, inv, total, g3, inv3, gw, invw, b2, b3, bw, rows):
    clear_whole(b2)
    clear_edges(b3, 16, 32)
    clear_edges(bw, 22, 24)
    gather_y(same, sibling, b2)
    ring_weights(b2.at[7:41], None, g, inv, total, 32, 64, 16.0, edges=True)
    half_z = pick(lambda r, c: r // 2 == c)

    def restrict(x2):
        rows[x2] = (b2[8 + 2 * x2, 8:72, :] + b2[9 + 2 * x2, 8:72, :]) * (1.0 / 8.0)

    loop(0, 16, 8, restrict)

    def compress(x2):
        bet = rows[x2, pl.ds(0, 32, stride=2), :] + rows[x2, pl.ds(1, 32, stride=2), :]
        b3[x2 + 1, 8:40, :] = dot(bet, half_z)

    loop(0, 16, 9, compress)
    ring_weights(b3, None, g3, inv3, None, 16, 32, 64.0)
    ix = lax.axis_index("gx")
    row = pl.multiple_of(lax.axis_index("gy") * 8, 8)

    def window(x):
        bw[x + 1, 8:32, :] = b2[ix * 8 + 1 + x, pl.ds(row, 24), :]

    loop(0, 22, 6, window)
    ring_weights(bw, None, gw, invw, None, 22, 24, 16.0, edges=True)


COARSE_SHAPES = [
    (6, 32, 64, 128),
    (32, 64, 128),
    (32, 64, 128),
    (6, 16, 32, 128),
    (16, 32, 128),
    (6, 22, 24, 128),
    (22, 24, 128),
]


def bottom(
    same, sibling, g, inv, total, g3, inv3, gw, invw, out,
    s2, va, vb, sp, u, v3a, v3b, sp3, u3, rows, wa, wb, spw, uw,
):
    for ref in (s2, va, vb):
        clear_whole(ref)
    gather_y(same, sibling, s2)

    def scale(x):
        sp[x] = s2[x + 8, 8:72, :] * inv[x]

    loop(0, 32, 8, scale)
    v = ring_cheb(va.at[7:41], vb.at[7:41], g, sp, u, 32, 64, RECIPE, True)
    iterate = vb if SMOOTH % 2 == 0 else va

    clear_edges(v3a, 16, 32)
    clear_edges(v3b, 16, 32)
    half_z = pick(lambda r, c: r // 2 == c)

    def restrict(x2):
        parts = []
        for half in range(2):
            x = 2 * x2 + half
            _, rest = ring_rest(v, g, sp, x, 64)
            parts.append(rest * total[x])
        rows[x2] = (parts[0] + parts[1]) * (0.0625 * 0.5 / 8.0)

    loop(0, 16, 16, restrict)

    def compress(x2):
        res = rows[x2, pl.ds(0, 32, stride=2), :] + rows[x2, pl.ds(1, 32, stride=2), :]
        sp3[x2] = dot(res, half_z) * inv3[x2]

    loop(0, 16, 9, compress)
    c3 = ring_cheb(v3a, v3b, g3, sp3, u3, 16, 32, BOTTOM_RECIPE, True)

    other = va if iterate is vb else vb
    double_z = pick(lambda r, c: c // 2 == r)

    def prolong(x3):
        wide = dot(c3[x3 + 1, 8:40, :], double_z)
        rows[x3, pl.ds(0, 32, stride=2), :] = wide
        rows[x3, pl.ds(1, 32, stride=2), :] = wide
        for half in range(2):
            x = 8 + 2 * x3 + half
            other[x, 8:72, :] = iterate[x, 8:72, :] + rows[x3]

    loop(0, 16, 18, prolong)
    ix = lax.axis_index("gx")
    iz = lax.axis_index("gz")
    clear_edges(wa, 22, 24)
    clear_edges(wb, 22, 24)
    row = pl.multiple_of(lax.axis_index("gy") * 8, 8)

    def window(x):
        plane = ix * 8 + 1 + x
        wa[x + 1, 8:32, :] = other[plane, pl.ds(row, 24), :]
        spw[x] = s2[plane, pl.ds(row, 24), :] * invw[x]

    loop(0, 22, 6, window)
    c2 = ring_cheb(wa, wb, gw, spw, uw, 22, 24, RECIPE, False)
    shift = (128 - iz * 32) % 128
    for x in range(18):
        out[x] = roll(c2[x + 3, 8:32, :], shift)


COARSE_SCRATCH = [
    vm(48, 80, 128),
    vm(18, 48, 128),
    vm(24, 40, 128),
    vm(16, 64, 128),
]
BOTTOM_SCRATCH = [
    vm(48, 80, 128),
    vm(48, 80, 128),
    vm(48, 80, 128),
    vm(32, 64, 128),
    vm(32, 64, 128),
    vm(18, 48, 128),
    vm(18, 48, 128),
    vm(16, 32, 128),
    vm(16, 32, 128),
    vm(16, 64, 128),
    vm(24, 40, 128),
    vm(24, 40, 128),
    vm(22, 24, 128),
    vm(22, 24, 128),
]


def level1_up(c2, g, sp, beta, iterate, out, va, vb, u, wide, rows):
    for ref in (va, vb):
        clear_edges(ref, 36, 40)
    spread = pick(lambda r, c: ((c < 74) & (c // 2 == r)) | ((c >= 118) & (c // 2 + 64 == r)))
    for x2 in range(18):
        rows[x2, 32:40, :] = jnp.zeros((8, 128), F32)

    def prolong(x2):
        wide[x2] = dot(c2[x2], spread)
        part = wide[x2, 3:21, :]
        rows[x2, pl.ds(0, 18, stride=2), :] = part
        rows[x2, pl.ds(1, 18, stride=2), :] = part
        for half in range(2):
            x = 2 * x2 + half
            va[x + 1, 8:48, :] = jnp.where(beta[x] > 0.0, iterate[x] + rows[x2], 0.0)

    loop(0, 18, 12, prolong)
    v = ring_cheb(va, vb, g, sp, u, 36, 40, RECIPE, False)
    out[...] = v[7:31, 14:38, :]


def level0_up(
    c1, beta, g_main, g_strip, sp, sp_t, beta_t, iterate, iterate_t, out,
    va, vb, ta, tb, ghost, u, u_t, rows,
):
    for ref in (va, vb):
        clear_edges(ref, 48, 48)
    for ref in (ta, tb):
        clear_strip(ref)
    spread = pick(lambda r, c: c // 2 == r)

    def prolong(x1):
        wide = dot(c1[x1], spread)
        rows[x1, pl.ds(0, 24, stride=2), :] = wide
        rows[x1, pl.ds(1, 24, stride=2), :] = wide
        for half in range(2):
            x = 2 * x1 + half
            va[x + 1, 8:56, :] = jnp.where(beta[x] > 0.0, iterate[x] + rows[x1], 0.0)

    loop(0, 24, 12, prolong)

    def prolong_strip(m):
        acc = jnp.zeros((24, 128), F32)
        for k in range(8):
            to = pick(
                lambda r, c: (c // 16 == k)
                & (
                    ((c % 16 < 8) & (r == 64 + (7 - c % 16) // 2))
                    | ((c % 16 >= 8) & (r == 124 + (15 - c % 16) // 2))
                )
            )
            acc = acc + dot(c1[k * 3 + m], to)
        rows[m, pl.ds(0, 24, stride=2), :] = acc
        rows[m, pl.ds(1, 24, stride=2), :] = acc
        for half in range(2):
            xx = 2 * m + half
            ta[xx, 8:56, :] = jnp.where(beta_t[xx] > 0.0, iterate_t[xx] + rows[m], 0.0)

    loop(0, 3, 36, prolong_strip)
    for x in [*range(6), *range(42, 48)]:
        vb[x + 1, 8:56, :] = jnp.zeros((48, 128), F32)
    bufs = [(va, ta), (vb, tb)]
    for k in range(SMOOTH):
        (v, t), (w, s) = bufs
        retain, factor = RECIPE[k]
        if k == 0:
            retain = None
        if k < SMOOTH - 1:
            low, high = (4, 44) if k < 2 else (6, 42)
            level0_step(
                v, t, w, s, ghost, g_main, g_strip, sp, sp_t, u, u_t, low, high, retain, factor
            )
        else:

            def last(x):
                here, rest = block_rest(v, t, g_main, sp, x, 8)
                out[x - 8] = here + retain * u[x, 8:40] + factor * rest

            loop(8, 40, 4, last)
        bufs = [(w, s), (v, t)]


def ring(value, axis, step):
    count = lax.axis_size(axis)
    return lax.ppermute(value, axis, [(i, (i + step) % count) for i in range(count)])


def trade(lo, hi, axis):
    return ring(hi, axis, 1), ring(lo, axis, -1)


def gather(kernel, parts, after, *shape):
    return call(kernel, sds(*shape), name=kernel.__name__, last_unread=len(parts) + 1)(*parts, after)


def around(value, axis):
    return [value] + [ring(value, axis, step) for step in range(1, lax.axis_size(axis))]


def chips(value):
    return [value] + [ring(value, "gy", 2 * step) for step in (1, 2, 3)]


def across(value):
    count = lax.axis_size("gy")
    return lax.ppermute(value, "gy", [(i, i + 1 - 2 * (i % 2)) for i in range(count)])


def per_device(source, beta):
    lo = jnp.stack([source[0:8], beta[0:8]])
    hi = jnp.stack([source[24:32], beta[24:32]])
    lo, hi, source, beta = lax.optimization_barrier((lo, hi, source, beta))
    x_lo, x_hi = trade(lo, hi, "gx")
    beta2 = call(coarse_beta, sds(16, 128), [vm(32, 128)], name="coarse_beta")(beta)
    beta2_pair = gather(pair, [beta2, ring(beta2, "gz", 1)], lo, 2, 16, 128)
    x_lo, x_hi, beta2_pair = lax.optimization_barrier((x_lo, x_hi, beta2_pair))
    slab = sds(2, 48, 8, 128)
    mid = sds(48, 32, 128)
    lo, hi, s_mid, b_mid = call(pack_y, (slab, slab, mid, mid), name="pack_y", mib=4)(
        source, beta, x_lo, x_hi
    )
    y_lo, y_hi = trade(lo, hi, "gy")
    beta2_block = gather(gather_z, [beta2_pair, ring(beta2_pair, "gz", 2)], lo, 8, 8, 128)
    y_lo, y_hi, beta2_block = lax.optimization_barrier((y_lo, y_hi, beta2_block))
    whole = sds(48, 48, 128)
    strip = sds(6, 48, 128)
    src_ext, beta_ext, lo, hi = call(
        pack_z, (whole, whole, strip, strip), name="pack_z", mib=4
    )(s_mid, b_mid, y_lo, y_hi)
    z_lo, z_hi = trade(lo, hi, "gz")
    beta2_pair = gather(pair, [beta2_block, ring(beta2_block, "gx", 1)], lo, 2, 8, 8, 128)
    z_lo, z_hi, beta2_pair = lax.optimization_barrier((z_lo, z_hi, beta2_pair))
    iter0, iter0_t, c, lo, hi, *ready = call(
        level0_down,
        (
            whole,
            strip,
            sds(16, 16, 128),
            sds(10, 16, 128),
            sds(10, 16, 128),
            sds(7, 48, 48, 128),
            sds(6, 6, 48, 128),
            whole,
            strip,
            strip,
        ),
        LEVEL0_SCRATCH,
        name="level0_down",
        mib=16,
    )(src_ext, beta_ext, z_lo, z_hi)
    x_lo, x_hi = trade(lo, hi, "gx")
    beta2_pair, _ = lax.optimization_barrier((beta2_pair, lo))
    beta2_slab = gather(gather_x, [beta2_pair, ring(beta2_pair, "gx", 2)], lo, 32, 8, 128)
    x_lo, x_hi, beta2_slab = lax.optimization_barrier((x_lo, x_hi, beta2_slab))
    lo, hi = call(pack1_y, (sds(360, 128), sds(360, 128)), name="pack1_y")(c, x_lo, x_hi)
    y_lo, y_hi = trade(lo, hi, "gy")
    beta2_pair = gather(pair, [beta2_slab, ring(beta2_slab, "gy", 2)], lo, 2, 32, 8, 128)
    y_lo, y_hi, beta2_pair = lax.optimization_barrier((y_lo, y_hi, beta2_pair))
    ext, lo, hi = call(
        pack1_z, (sds(36, 40, 128), sds(6, 40, 128), sds(6, 40, 128)), name="pack1_z"
    )(c, x_lo, x_hi, y_lo, y_hi)
    z1_lo, z1_hi = trade(lo, hi, "gz")
    beta2_pair, _ = lax.optimization_barrier((beta2_pair, lo))
    beta2_stack = gather(stack_y, [beta2_pair, ring(beta2_pair, "gy", 4)], lo, 4, 32, 8, 128)
    z1_lo, z1_hi, beta2_stack = lax.optimization_barrier((z1_lo, z1_hi, beta2_stack))
    level1 = sds(36, 40, 128)
    iter1, chunk, g1, sp1, beta1 = call(
        level1_down,
        (level1, sds(16, 128), sds(6, 36, 40, 128), level1, level1),
        LEVEL1_SCRATCH,
        name="level1_down",
        mib=8,
    )(ext, z1_lo, z1_hi)
    parts = around(chunk, "gz")
    beta2_stack, _ = lax.optimization_barrier((beta2_stack, chunk))
    *parts, beta2_other = lax.optimization_barrier((*parts, across(beta2_stack)))
    parts = around(gather(gather_z, parts, chunk, 8, 8, 128), "gx")
    slab = gather(gather_x, parts, chunk, 32, 8, 128)
    stack = gather(stack_y, chips(slab), slab, 4, 32, 8, 128)
    stack_other = across(stack)
    coarse = call(
        coarse_prepare,
        tuple(sds(*shape) for shape in COARSE_SHAPES),
        COARSE_SCRATCH,
        name="coarse_prepare",
        mib=8,
    )(beta2_stack, beta2_other)
    c2 = call(bottom, sds(18, 24, 128), BOTTOM_SCRATCH, name="bottom", mib=18)(
        stack, stack_other, *coarse
    )
    c1 = call(
        level1_up,
        sds(24, 24, 128),
        [vm(38, 56, 128), vm(38, 56, 128), vm(36, 40, 128), vm(18, 24, 128), vm(18, 40, 128)],
        name="level1_up",
        mib=8,
    )(c2, g1, sp1, beta1, iter1)
    return call(
        level0_up,
        sds(32, 32, 128),
        [vm(50, 64, 128), vm(50, 64, 128), vm(6, 64, 128), vm(6, 64, 128), vm(6, 48, 128)]
        + [vm(48, 48, 128), vm(6, 48, 128), vm(24, 48, 128)],
        name="level0_up",
        mib=14,
    )(c1, beta_ext, *ready, iter0, iter0_t)


def solution(mesh):
    placed = (P(*AXES), P(*AXES))
    return jax.shard_map(
        per_device, mesh=mesh, in_specs=placed, out_specs=P(*AXES), check_vma=False
    )
```

```python
import jax
import jax.numpy as jnp
from jax import lax
from jax.experimental import pallas as pl
from jax.experimental.pallas import tpu as pltpu
from jax.sharding import PartitionSpec as P

SMOOTH = 4
BOTTOM = 12
LOW_EIG = 0.3
HIGH_EIG = 2.0
BOTTOM_LOW = 0.02

AXES = ("gx", "gy", "gz")
F32 = jnp.float32
MIB = 1024 * 1024


def cheb_plan(degree, lowest, highest):
    centre = 0.5 * (highest + lowest)
    radius = 0.5 * (highest - lowest)
    ratio_s = centre / radius
    rho_old = 1.0 / ratio_s
    recipe = [(0.0, 1.0 / centre)]
    for position in range(1, degree):
        rho_new = 1.0 / (2.0 * ratio_s - rho_old)
        recipe.append((rho_new * rho_old, 2.0 * rho_new / radius))
        rho_old = rho_new
    return recipe


RECIPE = cheb_plan(SMOOTH, LOW_EIG, HIGH_EIG)
BOTTOM_RECIPE = cheb_plan(BOTTOM, BOTTOM_LOW, HIGH_EIG)


def sds(*shape):
    return jax.ShapeDtypeStruct(shape, F32)


def vm(*shape):
    return pltpu.VMEM(shape, F32)


def call(body, outs, scratch=(), name=None, mib=2, last_unread=None):
    specs = {}
    if last_unread:
        whole = pl.BlockSpec(memory_space=pltpu.VMEM)
        specs["in_specs"] = [whole] * (last_unread - 1) + [pl.BlockSpec(memory_space=pl.ANY)]
    return pl.pallas_call(
        body,
        out_shape=outs,
        **specs,
        scratch_shapes=list(scratch),
        compiler_params=pltpu.CompilerParams(vmem_limit_bytes=mib * MIB),
        name=name,
    )


def loop(low, high, vectors, body):
    count = high - low
    most = max(1, min(count, 72 // vectors))
    width = max([w for w in range(1, most + 1) if count % w == 0])
    if width * 2 < most:
        width = most
    rounds = count // width

    def chunk(i, carry):
        for k in range(width):
            body(low + i * width + k)
        return carry

    if rounds > 1:
        lax.fori_loop(0, rounds, chunk, 0)
    else:
        chunk(0, 0)
    for x in range(low + rounds * width, high):
        body(x)


def lanes_of(rows):
    return lax.broadcasted_iota(jnp.int32, (rows, 128), 1)


def roll(value, shift):
    if isinstance(shift, int):
        shift = shift % 128
        if shift == 0:
            return value
    return pltpu.roll(value, shift, 1)


def flag(condition):
    return jnp.where(condition, 1.0, 0.0).astype(F32)


def dot(left, right):
    return lax.dot_general(
        left,
        right,
        (((1,), (0,)), ((), ())),
        precision=lax.Precision.HIGHEST,
        preferred_element_type=F32,
    )


def pick(match):
    row = lax.broadcasted_iota(jnp.int32, (128, 128), 0)
    col = lax.broadcasted_iota(jnp.int32, (128, 128), 1)
    return jnp.where(match(row, col), 1.0, 0.0).astype(F32)


def coarse_beta(beta, out, rows):
    total = []
    for x in range(8):
        s = beta[4 * x] + beta[4 * x + 1] + beta[4 * x + 2] + beta[4 * x + 3]
        rows[...] = s
        t = rows[pl.ds(0, 8, stride=4), :] + rows[pl.ds(1, 8, stride=4), :]
        t = t + rows[pl.ds(2, 8, stride=4), :] + rows[pl.ds(3, 8, stride=4), :]
        total.append(t * (1.0 / 64.0))
    for half in range(2):
        acc = jnp.zeros((8, 128), F32)
        for quarter in range(4):
            weight = pick(lambda r, c: (r // 4 + 32 * quarter) == c)
            acc = acc + dot(total[half * 4 + quarter], weight)
        out[half * 8 : half * 8 + 8, :] = acc


def pack_y(src, beta, from_lo, from_hi, lo, hi, s_mid, b_mid):
    index = lax.axis_index("gx")
    low = flag(index > 0)
    high = flag(index < lax.axis_size("gx") - 1)
    for field, (ref, mid) in enumerate(((src, s_mid), (beta, b_mid))):
        mid[0:8] = from_lo[field] * low
        mid[8:40] = ref[...]
        mid[40:48] = from_hi[field] * high
        lo[field] = mid[:, 0:8, :]
        hi[field] = mid[:, 24:32, :]


def pack_z(s_mid, b_mid, y_lo, y_hi, s_out, b_out, lo, hi):
    iy = lax.axis_index("gy")
    y_low = flag(iy > 0)
    y_high = flag(iy < lax.axis_size("gy") - 1)
    for field, (mid, out) in enumerate(((s_mid, s_out), (b_mid, b_out))):
        out[:, 8:40, :] = mid[...]
        out[:, 0:8, :] = y_lo[field] * y_low
        out[:, 40:48, :] = y_hi[field] * y_high
    lane = lanes_of(48)

    def body(xx):
        acc_lo = jnp.zeros((48, 128), F32)
        acc_hi = jnp.zeros((48, 128), F32)
        for g in range(8):
            s = s_out[g * 6 + xx]
            b = b_out[g * 6 + xx]
            first = (lane >= g * 16) & (lane < g * 16 + 8)
            second = (lane >= g * 16 + 8) & (lane < g * 16 + 16)
            acc_lo = jnp.where(first, roll(s, g * 16), acc_lo)
            acc_lo = jnp.where(second, roll(b, g * 16 + 8), acc_lo)
            acc_hi = jnp.where(first, roll(s, g * 16 + 8), acc_hi)
            acc_hi = jnp.where(second, roll(b, g * 16 + 16), acc_hi)
        lo[xx] = acc_lo
        hi[xx] = acc_hi

    loop(0, 6, 36, body)


def strip_ghosts(values, ghost):
    lane = lanes_of(48)

    def body(xx):
        acc = jnp.zeros((48, 128), F32)
        for g in range(8):
            acc = jnp.where(lane // 16 == g, roll(values[g * 6 + xx + 1, 8:56, :], g * 16 + 8), acc)
        ghost[xx] = acc

    loop(0, 6, 36, body)


def strip_sides(strip, xx):
    after = strip[xx + 1, 8:56, :] if xx < 5 else roll(strip[0, 8:56, :], -16)
    before = strip[xx - 1, 8:56, :] if xx > 0 else roll(strip[5, 8:56, :], 16)
    return before, after


def strip_z(strip, ghost, xx, lane):
    here = strip[xx, 8:56, :]
    up = jnp.where(lane % 16 == 8, ghost[xx], roll(here, 1))
    down = jnp.where(lane % 16 == 7, ghost[xx], roll(here, -1))
    return down, up


def block_edge(strip, x, first=8, count=48):
    g = x // 6
    return roll(strip[x - g * 6, first : first + count, :], 120 - g * 16)


def weights(here, sides):
    sums = [here + side for side in sides]
    total = sums[0] + sums[1] + sums[2] + sums[3] + sums[4] + sums[5]
    inverse = jnp.where(here > 0.0, 1.0 / total, 0.0)
    return [s * inverse for s in sums], inverse, total


def level0_setup(b_pad, bt_pad, ghost, src, src_t, g_main, g_strip, sp, sp_t, total):
    strip_ghosts(b_pad, ghost)
    lane = lanes_of(48)

    def body(x):
        here = b_pad[x + 1, 8:56, :]
        edge = block_edge(bt_pad, x)
        down = jnp.where(lane == 0, edge, roll(here, 1))
        up = jnp.where(lane == 127, edge, roll(here, -1))
        faces, inverse, tot = weights(
            here,
            (
                b_pad[x, 8:56, :],
                b_pad[x + 2, 8:56, :],
                b_pad[x + 1, 7:55, :],
                b_pad[x + 1, 9:57, :],
                down,
                up,
            ),
        )
        for i in range(4):
            g_main[i, x] = faces[i]
        g_main[4, x] = jnp.where(lane == 0, 0.0, faces[4])
        g_main[5, x] = jnp.where(lane == 127, 0.0, faces[5])
        g_main[6, x] = jnp.where(lane == 0, faces[4], jnp.where(lane == 127, faces[5], 0.0))
        sp[x] = src[x] * (2.0 * inverse)
        if total is not None:
            total[x] = tot

    loop(0, 48, 6, body)
    for xx in range(6):
        before, after = strip_sides(bt_pad, xx)
        down, up = strip_z(bt_pad, ghost, xx, lane)
        faces, inverse, _ = weights(
            bt_pad[xx, 8:56, :],
            (before, after, bt_pad[xx, 7:55, :], bt_pad[xx, 9:57, :], down, up),
        )
        for i in range(6):
            g_strip[i, xx] = faces[i]
        sp_t[xx] = src_t[xx] * (2.0 * inverse)


def block_rest(v, t, g_main, sp, x, skip=0):
    count = 48 - 2 * skip
    first = 8 + skip
    keep = slice(skip, 48 - skip)
    here = v[x + 1, first : first + count, :]
    rest = sp[x, keep] - here
    rest = rest + g_main[0, x, keep] * v[x, first : first + count, :]
    rest = rest + g_main[1, x, keep] * v[x + 2, first : first + count, :]
    rest = rest + g_main[2, x, keep] * v[x + 1, first - 1 : first - 1 + count, :]
    rest = rest + g_main[3, x, keep] * v[x + 1, first + 1 : first + 1 + count, :]
    rest = rest + g_main[4, x, keep] * roll(here, 1) + g_main[5, x, keep] * roll(here, -1)
    rest = rest + g_main[6, x, keep] * block_edge(t, x, first, count)
    return here, rest


def level0_step(v, t, v_out, t_out, ghost, g_main, g_strip, sp, sp_t, u, u_t, low, high, retain, factor):
    strip_ghosts(v, ghost)
    lane = lanes_of(48)

    def body(x):
        here, rest = block_rest(v, t, g_main, sp, x)
        new = factor * rest
        if retain is not None:
            new = retain * u[x] + new
        u[x] = new
        v_out[x + 1, 8:56, :] = here + new

    loop(low, high, 6, body)
    for xx in range(6):
        here = t[xx, 8:56, :]
        before, after = strip_sides(t, xx)
        down, up = strip_z(t, ghost, xx, lane)
        rest = sp_t[xx] - here
        rest = rest + g_strip[0, xx] * before + g_strip[1, xx] * after
        rest = rest + g_strip[2, xx] * t[xx, 7:55, :] + g_strip[3, xx] * t[xx, 9:57, :]
        rest = rest + g_strip[4, xx] * down + g_strip[5, xx] * up
        new = factor * rest
        if retain is not None:
            new = retain * u_t[xx] + new
        u_t[xx] = new
        t_out[xx, 8:56, :] = here + new


def clear_edges(ref, planes, rows):
    width = ref.shape[1]
    ref[0] = jnp.zeros((width, 128), F32)
    ref[planes + 1] = jnp.zeros((width, 128), F32)

    def body(x):
        ref[x, 0:8, :] = jnp.zeros((8, 128), F32)
        ref[x, 8 + rows : width, :] = jnp.zeros((width - 8 - rows, 128), F32)

    loop(0, planes + 2, 4, body)


def clear_strip(ref):
    for xx in range(6):
        ref[xx, 0:8, :] = jnp.zeros((8, 128), F32)
        ref[xx, 56:64, :] = jnp.zeros((8, 128), F32)


def unpack_strip(z_lo, z_hi, src_t, bt_pad):
    iz = lax.axis_index("gz")
    low = flag(iz > 0)
    high = flag(iz < lax.axis_size("gz") - 1)

    def mirror(first, last):
        return pick(lambda r, c: (r // 16 == c // 16) & ((r % 16 < 8) == first) & (r % 16 + c % 16 == last))

    s_lo, s_hi = mirror(True, 15), mirror(True, 7)
    b_lo, b_hi = mirror(False, 23), mirror(False, 15)
    for xx in range(6):
        before = z_lo[xx] * low
        after = z_hi[xx] * high
        src_t[xx] = dot(before, s_lo) + dot(after, s_hi)
        bt_pad[xx, 8:56, :] = dot(before, b_lo) + dot(after, b_hi)


LEVEL0_SCRATCH = [
    vm(50, 64, 128),
    vm(6, 64, 128),
    vm(50, 64, 128),
    vm(50, 64, 128),
    vm(6, 64, 128),
    vm(6, 64, 128),
    vm(6, 48, 128),
    vm(48, 48, 128),
    vm(6, 48, 128),
    vm(6, 48, 128),
    vm(48, 48, 128),
    vm(2, 16, 32, 128),
]


def level0_down(
    src, beta, z_lo, z_hi, iter_out, iter_t_out, c_out, c_lo, c_hi, g_main, g_strip, sp, sp_t, bt_out,
    b_pad, bt_pad, va, vb, ta, tb, ghost, u, u_t, src_t, total, rows,
):
    for ref in (b_pad, va, vb):
        clear_edges(ref, 48, 48)
    for ref in (bt_pad, ta, tb):
        clear_strip(ref)
    b_pad[1:49, 8:56, :] = beta[...]
    unpack_strip(z_lo, z_hi, src_t, bt_pad)
    for xx in range(6):
        bt_out[xx] = bt_pad[xx, 8:56, :]
    level0_setup(b_pad, bt_pad, ghost, src, src_t, g_main, g_strip, sp, sp_t, total)

    first = RECIPE[0][1]

    def start(x):
        u[x] = first * sp[x]
        va[x + 1, 8:56, :] = u[x]

    loop(0, 48, 8, start)
    for xx in range(6):
        u_t[xx] = first * sp_t[xx]
        ta[xx, 8:56, :] = u_t[xx]
    bufs = [(va, ta), (vb, tb)]
    for k in range(1, SMOOTH):
        (v, t), (w, s) = bufs
        retain, factor = RECIPE[k]
        level0_step(v, t, w, s, ghost, g_main, g_strip, sp, sp_t, u, u_t, 0, 48, retain, factor)
        bufs = [(w, s), (v, t)]
    v, t = bufs[0]
    iter_out[...] = v[1:49, 8:56, :]
    for xx in range(6):
        iter_t_out[xx] = t[xx, 8:56, :]

    to_low = pick(lambda r, c: r // 2 == c)
    to_high = pick(lambda r, c: r // 2 + 64 == c)

    def restrict(x2):
        parts = []
        for half in range(2):
            x = 8 + 2 * x2 + half
            _, rest = block_rest(v, t, g_main, sp, x, 8)
            parts.append(rest * total[x, 8:40])
        rows[0, x2] = (parts[0] + parts[1]) * (0.5 / 8.0)
        rows[1, x2] = (b_pad[9 + 2 * x2, 16:48, :] + b_pad[10 + 2 * x2, 16:48, :]) * (1.0 / 8.0)

    loop(0, 16, 8, restrict)

    def compress(x2):
        res = rows[0, x2, pl.ds(0, 16, stride=2), :] + rows[0, x2, pl.ds(1, 16, stride=2), :]
        bet = rows[1, x2, pl.ds(0, 16, stride=2), :] + rows[1, x2, pl.ds(1, 16, stride=2), :]
        c_out[x2] = dot(res, to_low) + dot(bet, to_high)

    loop(0, 16, 8, compress)
    c_lo[...] = c_out[0:10]
    c_hi[...] = c_out[6:16]


def pack1_y(c, from_lo, from_hi, lo, hi):
    index = lax.axis_index("gx")
    low = flag(index > 0)
    high = flag(index < lax.axis_size("gx") - 1)
    for x in range(36):
        if x < 10:
            plane = from_lo[x] * low
        elif x < 26:
            plane = c[x - 10]
        else:
            plane = from_hi[x - 26] * high
        lo[x * 10 : x * 10 + 10, :] = plane[0:10]
        hi[x * 10 : x * 10 + 10, :] = plane[6:16]


def pack1_z(c, x_lo, x_hi, y_lo, y_hi, ext, lo, hi):
    ix = lax.axis_index("gx")
    iy = lax.axis_index("gy")
    x_low = flag(ix > 0)
    x_high = flag(ix < lax.axis_size("gx") - 1)
    y_low = flag(iy > 0)
    y_high = flag(iy < lax.axis_size("gy") - 1)
    ext[0:10, 10:26, :] = x_lo[...] * x_low
    ext[10:26, 10:26, :] = c[...]
    ext[26:36, 10:26, :] = x_hi[...] * x_high
    for x in range(36):
        ext[x, 0:10, :] = y_lo[x * 10 : x * 10 + 10, :] * y_low
        ext[x, 26:36, :] = y_hi[x * 10 : x * 10 + 10, :] * y_high
        ext[x, 36:40, :] = jnp.zeros((4, 128), F32)
    lane = lanes_of(40)

    def body(xx):
        acc_lo = jnp.zeros((40, 128), F32)
        acc_hi = jnp.zeros((40, 128), F32)
        for g in range(6):
            e = ext[g * 6 + xx]
            first = (lane >= g * 20) & (lane < g * 20 + 10)
            second = (lane >= g * 20 + 10) & (lane < g * 20 + 20)
            middle = roll(e, g * 20 - 54)
            acc_lo = jnp.where(first, roll(e, g * 20), acc_lo)
            acc_lo = jnp.where(second, middle, acc_lo)
            acc_hi = jnp.where(first, middle, acc_hi)
            acc_hi = jnp.where(second, roll(e, g * 20 + 20), acc_hi)
        lo[xx] = acc_lo
        hi[xx] = acc_hi

    loop(0, 6, 36, body)


def ring_weights(b_pad, src, g, sp, total, planes, rows, scale, edges=None):
    lane = lanes_of(rows)

    def body(x):
        here = b_pad[x + 1, 8 : 8 + rows, :]
        down = roll(here, 1)
        up = roll(here, -1)
        if edges is not None:
            down = jnp.where(lane == 0, 0.0, down)
            up = jnp.where(lane == 127, 0.0, up)
        faces, inverse, tot = weights(
            here,
            (
                b_pad[x, 8 : 8 + rows, :],
                b_pad[x + 2, 8 : 8 + rows, :],
                b_pad[x + 1, 7 : 7 + rows, :],
                b_pad[x + 1, 9 : 9 + rows, :],
                down,
                up,
            ),
        )
        if edges is not None:
            faces[4] = jnp.where(lane == 0, 0.0, faces[4])
            faces[5] = jnp.where(lane == 127, 0.0, faces[5])
        for i in range(6):
            g[i, x] = faces[i]
        sp[x] = scale * 2.0 * inverse if src is None else src[x] * (scale * 2.0 * inverse)
        if total is not None:
            total[x] = tot

    loop(0, planes, rows // 5, body)


def ring_rest(v, g, sp, x, rows):
    here = v[x + 1, 8 : 8 + rows, :]
    rest = sp[x] - here
    rest = rest + g[0, x] * v[x, 8 : 8 + rows, :] + g[1, x] * v[x + 2, 8 : 8 + rows, :]
    rest = rest + g[2, x] * v[x + 1, 7 : 7 + rows, :] + g[3, x] * v[x + 1, 9 : 9 + rows, :]
    rest = rest + g[4, x] * roll(here, 1) + g[5, x] * roll(here, -1)
    return here, rest


def ring_step(v, v_out, g, sp, u, planes, rows, retain, factor):
    def body(x):
        here, rest = ring_rest(v, g, sp, x, rows)
        new = factor * rest
        if retain is not None:
            new = retain * u[x] + new
        u[x] = new
        v_out[x + 1, 8 : 8 + rows, :] = here + new

    loop(0, planes, rows // 16, body)


def ring_zero_start(v, u, sp, planes, rows, factor):
    def body(x):
        u[x] = factor * sp[x]
        v[x + 1, 8 : 8 + rows, :] = u[x]

    loop(0, planes, rows // 8, body)


def ring_cheb(va, vb, g, sp, u, planes, rows, recipe, from_zero):
    begin = 0
    if from_zero:
        ring_zero_start(va, u, sp, planes, rows, recipe[0][1])
        begin = 1
    for k in range(begin, len(recipe)):
        retain, factor = recipe[k]
        ring_step(va, vb, g, sp, u, planes, rows, None if k == 0 else retain, factor)
        va, vb = vb, va
    return va


LEVEL1_SCRATCH = [
    vm(38, 56, 128),
    vm(38, 56, 128),
    vm(38, 56, 128),
    vm(36, 40, 128),
    vm(36, 40, 128),
    vm(36, 40, 128),
    vm(8, 40, 128),
]


def level1_unpack(ext, z_lo, z_hi, source, b_pad, beta_out):
    iz = lax.axis_index("gz")
    low = flag(iz > 0)
    high = flag(iz < lax.axis_size("gz") - 1)
    lane = lanes_of(40)
    inner = lane < 64
    above = (lane >= 64) & (lane < 74)
    below = lane >= 118

    def unpack(xx):
        before = z_lo[xx] * low
        after = z_hi[xx] * high
        for k in range(6):
            x = k * 6 + xx
            e = ext[x]
            s = jnp.where(inner, e, 0.0)
            s = jnp.where(above, roll(after, 64 - k * 20), s)
            s = jnp.where(below, roll(before, 118 - k * 20), s)
            b = jnp.where(inner, roll(e, 64), 0.0)
            b = jnp.where(above, roll(after, 54 - k * 20), b)
            b = jnp.where(below, roll(before, 108 - k * 20), b)
            source[x] = s
            b_pad[x + 1, 8:48, :] = b
            beta_out[x] = b

    loop(0, 6, 36, unpack)


def level1_down(
    ext, z_lo, z_hi, iter_out, chunk, g, sp, beta_out,
    b_pad, va, vb, u, src, total, rows,
):
    for ref in (b_pad, va, vb):
        clear_edges(ref, 36, 40)
    level1_unpack(ext, z_lo, z_hi, src, b_pad, beta_out)
    ring_weights(b_pad, src, g, sp, total, 36, 40, 4.0)
    v = ring_cheb(va, vb, g, sp, u, 36, 40, RECIPE, True)
    iter_out[...] = v[1:37, 8:48, :]
    summed = []
    for x2 in range(8):
        parts = []
        for half in range(2):
            x = 10 + 2 * x2 + half
            _, rest = ring_rest(v, g, sp, x, 40)
            parts.append(rest * total[x])
        rows[x2] = (parts[0] + parts[1]) * (0.25 * 0.5 / 8.0)
        summed.append(rows[x2, pl.ds(10, 8, stride=2), :] + rows[x2, pl.ds(11, 8, stride=2), :])
    for half in range(2):
        acc = jnp.zeros((8, 128), F32)
        for quarter in range(4):
            weight = pick(lambda r, c: (r < 64) & ((r // 2 + 32 * quarter) == c))
            acc = acc + dot(summed[half * 4 + quarter], weight)
        chunk[half * 8 : half * 8 + 8, :] = acc


def sender(axis, step):
    count = lax.axis_size(axis)
    return lax.rem(lax.axis_index(axis) + count - step, count)


def singles(parts):
    return [part.at[i] for part in parts for i in range(2)] if len(parts) == 2 else parts


def gather_z(*refs):
    *parts, _, out = refs
    parts = singles(parts)
    lane = lanes_of(8)
    for half in range(2):
        for quarter in range(4):
            acc = jnp.zeros((8, 128), F32)
            for step, part in enumerate(parts):
                owner = sender("gz", step)
                moved = roll(part[half * 8 : half * 8 + 8, :], lax.rem(owner - quarter + 4, 4) * 32)
                acc = jnp.where(lane // 32 == owner, moved, acc)
            out[half * 4 + quarter] = acc


def gather_x(*refs):
    *parts, _, out = refs
    parts = singles(parts)
    for step, part in enumerate(parts):
        out[pl.ds(sender("gx", step) * 8, 8)] = part[...]


def stack_y(*refs):
    *parts, _, out = refs
    for step, part in enumerate(singles(parts)):
        out[step] = part[...]


def pair(mine, other, _, out):
    out[0] = mine[...]
    out[1] = other[...]


def gather_y(same, other, out):
    count = lax.axis_size("gy")
    index = lax.axis_index("gy")
    sibling = index + 1 - 2 * lax.rem(index, 2)
    for stack, first in ((same, index), (other, sibling)):
        for step in range(4):
            owner = lax.rem(first + count - 2 * step, count)
            row = pl.multiple_of(8 + owner * 8, 8)
            out[8:40, pl.ds(row, 8), :] = stack[step]


def clear_whole(ref):
    def clear(x):
        ref[x, 0:8, :] = jnp.zeros((8, 128), F32)
        ref[x, 72:80, :] = jnp.zeros((8, 128), F32)

    loop(0, 48, 2, clear)
    for x in [*range(8), *range(40, 48)]:
        ref[x, 8:72, :] = jnp.zeros((64, 128), F32)


def coarse_prepare(same, sibling, g, inv, total, g3, inv3, gw, invw, b2, b3, bw, rows):
    clear_whole(b2)
    clear_edges(b3, 16, 32)
    clear_edges(bw, 22, 24)
    gather_y(same, sibling, b2)
    ring_weights(b2.at[7:41], None, g, inv, total, 32, 64, 16.0, edges=True)
    half_z = pick(lambda r, c: r // 2 == c)

    def restrict(x2):
        rows[x2] = (b2[8 + 2 * x2, 8:72, :] + b2[9 + 2 * x2, 8:72, :]) * (1.0 / 8.0)

    loop(0, 16, 8, restrict)

    def compress(x2):
        bet = rows[x2, pl.ds(0, 32, stride=2), :] + rows[x2, pl.ds(1, 32, stride=2), :]
        b3[x2 + 1, 8:40, :] = dot(bet, half_z)

    loop(0, 16, 9, compress)
    ring_weights(b3, None, g3, inv3, None, 16, 32, 64.0)
    ix = lax.axis_index("gx")
    row = pl.multiple_of(lax.axis_index("gy") * 8, 8)

    def window(x):
        bw[x + 1, 8:32, :] = b2[ix * 8 + 1 + x, pl.ds(row, 24), :]

    loop(0, 22, 6, window)
    ring_weights(bw, None, gw, invw, None, 22, 24, 16.0, edges=True)


COARSE_SHAPES = [
    (6, 32, 64, 128),
    (32, 64, 128),
    (32, 64, 128),
    (6, 16, 32, 128),
    (16, 32, 128),
    (6, 22, 24, 128),
    (22, 24, 128),
]


def bottom(
    same, sibling, g, inv, total, g3, inv3, gw, invw, out,
    s2, va, vb, sp, u, v3a, v3b, sp3, u3, rows, wa, wb, spw, uw,
):
    for ref in (s2, va, vb):
        clear_whole(ref)
    gather_y(same, sibling, s2)

    def scale(x):
        sp[x] = s2[x + 8, 8:72, :] * inv[x]

    loop(0, 32, 8, scale)
    v = ring_cheb(va.at[7:41], vb.at[7:41], g, sp, u, 32, 64, RECIPE, True)
    iterate = vb if SMOOTH % 2 == 0 else va

    clear_edges(v3a, 16, 32)
    clear_edges(v3b, 16, 32)
    half_z = pick(lambda r, c: r // 2 == c)

    def restrict(x2):
        parts = []
        for half in range(2):
            x = 2 * x2 + half
            _, rest = ring_rest(v, g, sp, x, 64)
            parts.append(rest * total[x])
        rows[x2] = (parts[0] + parts[1]) * (0.0625 * 0.5 / 8.0)

    loop(0, 16, 16, restrict)

    def compress(x2):
        res = rows[x2, pl.ds(0, 32, stride=2), :] + rows[x2, pl.ds(1, 32, stride=2), :]
        sp3[x2] = dot(res, half_z) * inv3[x2]

    loop(0, 16, 9, compress)
    c3 = ring_cheb(v3a, v3b, g3, sp3, u3, 16, 32, BOTTOM_RECIPE, True)

    other = va if iterate is vb else vb
    double_z = pick(lambda r, c: c // 2 == r)

    def prolong(x3):
        wide = dot(c3[x3 + 1, 8:40, :], double_z)
        rows[x3, pl.ds(0, 32, stride=2), :] = wide
        rows[x3, pl.ds(1, 32, stride=2), :] = wide
        for half in range(2):
            x = 8 + 2 * x3 + half
            other[x, 8:72, :] = iterate[x, 8:72, :] + rows[x3]

    loop(0, 16, 18, prolong)
    ix = lax.axis_index("gx")
    iz = lax.axis_index("gz")
    clear_edges(wa, 22, 24)
    clear_edges(wb, 22, 24)
    row = pl.multiple_of(lax.axis_index("gy") * 8, 8)

    def window(x):
        plane = ix * 8 + 1 + x
        wa[x + 1, 8:32, :] = other[plane, pl.ds(row, 24), :]
        spw[x] = s2[plane, pl.ds(row, 24), :] * invw[x]

    loop(0, 22, 6, window)
    c2 = ring_cheb(wa, wb, gw, spw, uw, 22, 24, RECIPE, False)
    shift = (128 - iz * 32) % 128
    for x in range(18):
        out[x] = roll(c2[x + 3, 8:32, :], shift)


COARSE_SCRATCH = [
    vm(48, 80, 128),
    vm(18, 48, 128),
    vm(24, 40, 128),
    vm(16, 64, 128),
]
BOTTOM_SCRATCH = [
    vm(48, 80, 128),
    vm(48, 80, 128),
    vm(48, 80, 128),
    vm(32, 64, 128),
    vm(32, 64, 128),
    vm(18, 48, 128),
    vm(18, 48, 128),
    vm(16, 32, 128),
    vm(16, 32, 128),
    vm(16, 64, 128),
    vm(24, 40, 128),
    vm(24, 40, 128),
    vm(22, 24, 128),
    vm(22, 24, 128),
]


def level1_up(c2, g, sp, beta, iterate, out, va, vb, u, wide, rows):
    for ref in (va, vb):
        clear_edges(ref, 36, 40)
    spread = pick(lambda r, c: ((c < 74) & (c // 2 == r)) | ((c >= 118) & (c // 2 + 64 == r)))
    for x2 in range(18):
        rows[x2, 32:40, :] = jnp.zeros((8, 128), F32)

    def prolong(x2):
        wide[x2] = dot(c2[x2], spread)
        part = wide[x2, 3:21, :]
        rows[x2, pl.ds(0, 18, stride=2), :] = part
        rows[x2, pl.ds(1, 18, stride=2), :] = part
        for half in range(2):
            x = 2 * x2 + half
            va[x + 1, 8:48, :] = jnp.where(beta[x] > 0.0, iterate[x] + rows[x2], 0.0)

    loop(0, 18, 12, prolong)
    v = ring_cheb(va, vb, g, sp, u, 36, 40, RECIPE, False)
    out[...] = v[7:31, 14:38, :]


def level0_up(
    c1, beta, g_main, g_strip, sp, sp_t, beta_t, iterate, iterate_t, out,
    va, vb, ta, tb, ghost, u, u_t, rows,
):
    for ref in (va, vb):
        clear_edges(ref, 48, 48)
    for ref in (ta, tb):
        clear_strip(ref)
    spread = pick(lambda r, c: c // 2 == r)

    def prolong(x1):
        wide = dot(c1[x1], spread)
        rows[x1, pl.ds(0, 24, stride=2), :] = wide
        rows[x1, pl.ds(1, 24, stride=2), :] = wide
        for half in range(2):
            x = 2 * x1 + half
            va[x + 1, 8:56, :] = jnp.where(beta[x] > 0.0, iterate[x] + rows[x1], 0.0)

    loop(0, 24, 12, prolong)

    def prolong_strip(m):
        acc = jnp.zeros((24, 128), F32)
        for k in range(8):
            to = pick(
                lambda r, c: (c // 16 == k)
                & (
                    ((c % 16 < 8) & (r == 64 + (7 - c % 16) // 2))
                    | ((c % 16 >= 8) & (r == 124 + (15 - c % 16) // 2))
                )
            )
            acc = acc + dot(c1[k * 3 + m], to)
        rows[m, pl.ds(0, 24, stride=2), :] = acc
        rows[m, pl.ds(1, 24, stride=2), :] = acc
        for half in range(2):
            xx = 2 * m + half
            ta[xx, 8:56, :] = jnp.where(beta_t[xx] > 0.0, iterate_t[xx] + rows[m], 0.0)

    loop(0, 3, 36, prolong_strip)
    for x in [*range(6), *range(42, 48)]:
        vb[x + 1, 8:56, :] = jnp.zeros((48, 128), F32)
    bufs = [(va, ta), (vb, tb)]
    for k in range(SMOOTH):
        (v, t), (w, s) = bufs
        retain, factor = RECIPE[k]
        if k == 0:
            retain = None
        if k < SMOOTH - 1:
            low, high = (4, 44) if k < 2 else (6, 42)
            level0_step(
                v, t, w, s, ghost, g_main, g_strip, sp, sp_t, u, u_t, low, high, retain, factor
            )
        else:

            def last(x):
                here, rest = block_rest(v, t, g_main, sp, x, 8)
                out[x - 8] = here + retain * u[x, 8:40] + factor * rest

            loop(8, 40, 4, last)
        bufs = [(w, s), (v, t)]


def ring(value, axis, step):
    count = lax.axis_size(axis)
    return lax.ppermute(value, axis, [(i, (i + step) % count) for i in range(count)])


def trade(lo, hi, axis):
    return ring(hi, axis, 1), ring(lo, axis, -1)


def gather(kernel, parts, after, *shape):
    return call(kernel, sds(*shape), name=kernel.__name__, last_unread=len(parts) + 1)(*parts, after)


def around(value, axis):
    return [value] + [ring(value, axis, step) for step in range(1, lax.axis_size(axis))]


def chips(value):
    return [value] + [ring(value, "gy", 2 * step) for step in (1, 2, 3)]


def across(value):
    count = lax.axis_size("gy")
    return lax.ppermute(value, "gy", [(i, i + 1 - 2 * (i % 2)) for i in range(count)])


def per_device(source, beta):
    lo = jnp.stack([source[0:8], beta[0:8]])
    hi = jnp.stack([source[24:32], beta[24:32]])
    lo, hi, source, beta = lax.optimization_barrier((lo, hi, source, beta))
    x_lo, x_hi = trade(lo, hi, "gx")
    beta2 = call(coarse_beta, sds(16, 128), [vm(32, 128)], name="coarse_beta")(beta)
    beta2_pair = gather(pair, [beta2, ring(beta2, "gz", 1)], lo, 2, 16, 128)
    x_lo, x_hi, beta2_pair = lax.optimization_barrier((x_lo, x_hi, beta2_pair))
    slab = sds(2, 48, 8, 128)
    mid = sds(48, 32, 128)
    lo, hi, s_mid, b_mid = call(pack_y, (slab, slab, mid, mid), name="pack_y", mib=4)(
        source, beta, x_lo, x_hi
    )
    y_lo, y_hi = trade(lo, hi, "gy")
    beta2_block = gather(gather_z, [beta2_pair, ring(beta2_pair, "gz", 2)], lo, 8, 8, 128)
    y_lo, y_hi, beta2_block = lax.optimization_barrier((y_lo, y_hi, beta2_block))
    whole = sds(48, 48, 128)
    strip = sds(6, 48, 128)
    src_ext, beta_ext, lo, hi = call(
        pack_z, (whole, whole, strip, strip), name="pack_z", mib=4
    )(s_mid, b_mid, y_lo, y_hi)
    z_lo, z_hi = trade(lo, hi, "gz")
    beta2_pair = gather(pair, [beta2_block, ring(beta2_block, "gx", 1)], lo, 2, 8, 8, 128)
    z_lo, z_hi, beta2_pair = lax.optimization_barrier((z_lo, z_hi, beta2_pair))
    iter0, iter0_t, c, lo, hi, *ready = call(
        level0_down,
        (
            whole,
            strip,
            sds(16, 16, 128),
            sds(10, 16, 128),
            sds(10, 16, 128),
            sds(7, 48, 48, 128),
            sds(6, 6, 48, 128),
            whole,
            strip,
            strip,
        ),
        LEVEL0_SCRATCH,
        name="level0_down",
        mib=16,
    )(src_ext, beta_ext, z_lo, z_hi)
    x_lo, x_hi = trade(lo, hi, "gx")
    lo, hi = call(pack1_y, (sds(360, 128), sds(360, 128)), name="pack1_y")(c, x_lo, x_hi)
    y_lo, y_hi = trade(lo, hi, "gy")
    beta2_pair, _ = lax.optimization_barrier((beta2_pair, lo))
    beta2_slab = gather(gather_x, [beta2_pair, ring(beta2_pair, "gx", 2)], lo, 32, 8, 128)
    y_lo, y_hi, beta2_slab = lax.optimization_barrier((y_lo, y_hi, beta2_slab))
    ext, lo, hi = call(
        pack1_z, (sds(36, 40, 128), sds(6, 40, 128), sds(6, 40, 128)), name="pack1_z"
    )(c, x_lo, x_hi, y_lo, y_hi)
    z1_lo, z1_hi = trade(lo, hi, "gz")
    beta2_slab, _ = lax.optimization_barrier((beta2_slab, lo))
    beta2_pair = gather(pair, [beta2_slab, ring(beta2_slab, "gy", 2)], lo, 2, 32, 8, 128)
    z1_lo, z1_hi, beta2_pair = lax.optimization_barrier((z1_lo, z1_hi, beta2_pair))
    level1 = sds(36, 40, 128)
    iter1, chunk, g1, sp1, beta1 = call(
        level1_down,
        (level1, sds(16, 128), sds(6, 36, 40, 128), level1, level1),
        LEVEL1_SCRATCH,
        name="level1_down",
        mib=8,
    )(ext, z1_lo, z1_hi)
    parts = around(chunk, "gz")
    beta2_pair, _ = lax.optimization_barrier((beta2_pair, chunk))
    beta2_stack = gather(stack_y, [beta2_pair, ring(beta2_pair, "gy", 4)], chunk, 4, 32, 8, 128)
    *parts, beta2_stack = lax.optimization_barrier((*parts, beta2_stack))
    block = gather(gather_z, parts, chunk, 8, 8, 128)
    parts = around(block, "gx")
    beta2_sent, _ = lax.optimization_barrier((beta2_stack, block))
    *parts, beta2_other = lax.optimization_barrier((*parts, across(beta2_sent)))
    slab = gather(gather_x, parts, chunk, 32, 8, 128)
    stack = gather(stack_y, chips(slab), slab, 4, 32, 8, 128)
    stack_other = across(stack)
    coarse = call(
        coarse_prepare,
        tuple(sds(*shape) for shape in COARSE_SHAPES),
        COARSE_SCRATCH,
        name="coarse_prepare",
        mib=8,
    )(beta2_stack, beta2_other)
    c2 = call(bottom, sds(18, 24, 128), BOTTOM_SCRATCH, name="bottom", mib=18)(
        stack, stack_other, *coarse
    )
    c1 = call(
        level1_up,
        sds(24, 24, 128),
        [vm(38, 56, 128), vm(38, 56, 128), vm(36, 40, 128), vm(18, 24, 128), vm(18, 40, 128)],
        name="level1_up",
        mib=8,
    )(c2, g1, sp1, beta1, iter1)
    return call(
        level0_up,
        sds(32, 32, 128),
        [vm(50, 64, 128), vm(50, 64, 128), vm(6, 64, 128), vm(6, 64, 128), vm(6, 48, 128)]
        + [vm(48, 48, 128), vm(6, 48, 128), vm(24, 48, 128)],
        name="level0_up",
        mib=14,
    )(c1, beta_ext, *ready, iter0, iter0_t)


def solution(mesh):
    placed = (P(*AXES), P(*AXES))
    return jax.shard_map(
        per_device, mesh=mesh, in_specs=placed, out_specs=P(*AXES), check_vma=False
    )
```

```python
import jax
import jax.numpy as jnp
from jax import lax
from jax.experimental import pallas as pl
from jax.experimental.pallas import tpu as pltpu
from jax.sharding import PartitionSpec as P

SMOOTH = 4
BOTTOM = 12
LOW_EIG = 0.3
HIGH_EIG = 2.0
BOTTOM_LOW = 0.02

AXES = ("gx", "gy", "gz")
F32 = jnp.float32
MIB = 1024 * 1024


def cheb_plan(degree, lowest, highest):
    centre = 0.5 * (highest + lowest)
    radius = 0.5 * (highest - lowest)
    ratio_s = centre / radius
    rho_old = 1.0 / ratio_s
    recipe = [(0.0, 1.0 / centre)]
    for position in range(1, degree):
        rho_new = 1.0 / (2.0 * ratio_s - rho_old)
        recipe.append((rho_new * rho_old, 2.0 * rho_new / radius))
        rho_old = rho_new
    return recipe


RECIPE = cheb_plan(SMOOTH, LOW_EIG, HIGH_EIG)
BOTTOM_RECIPE = cheb_plan(BOTTOM, BOTTOM_LOW, HIGH_EIG)


def sds(*shape):
    return jax.ShapeDtypeStruct(shape, F32)


def vm(*shape):
    return pltpu.VMEM(shape, F32)


def call(body, outs, scratch=(), name=None, mib=2, last_unread=None):
    specs = {}
    if last_unread:
        whole = pl.BlockSpec(memory_space=pltpu.VMEM)
        specs["in_specs"] = [whole] * (last_unread - 1) + [pl.BlockSpec(memory_space=pl.ANY)]
    return pl.pallas_call(
        body,
        out_shape=outs,
        **specs,
        scratch_shapes=list(scratch),
        compiler_params=pltpu.CompilerParams(vmem_limit_bytes=mib * MIB),
        name=name,
    )


def loop(low, high, vectors, body):
    count = high - low
    most = max(1, min(count, 72 // vectors))
    width = max([w for w in range(1, most + 1) if count % w == 0])
    if width * 2 < most:
        width = most
    rounds = count // width

    def chunk(i, carry):
        for k in range(width):
            body(low + i * width + k)
        return carry

    if rounds > 1:
        lax.fori_loop(0, rounds, chunk, 0)
    else:
        chunk(0, 0)
    for x in range(low + rounds * width, high):
        body(x)


def lanes_of(rows):
    return lax.broadcasted_iota(jnp.int32, (rows, 128), 1)


def roll(value, shift):
    if isinstance(shift, int):
        shift = shift % 128
        if shift == 0:
            return value
    return pltpu.roll(value, shift, 1)


def flag(condition):
    return jnp.where(condition, 1.0, 0.0).astype(F32)


def dot(left, right):
    return lax.dot_general(
        left,
        right,
        (((1,), (0,)), ((), ())),
        precision=lax.Precision.HIGHEST,
        preferred_element_type=F32,
    )


def pick(match):
    row = lax.broadcasted_iota(jnp.int32, (128, 128), 0)
    col = lax.broadcasted_iota(jnp.int32, (128, 128), 1)
    return jnp.where(match(row, col), 1.0, 0.0).astype(F32)


def coarse_beta(beta, out, rows):
    total = []
    for x in range(8):
        s = beta[4 * x] + beta[4 * x + 1] + beta[4 * x + 2] + beta[4 * x + 3]
        rows[...] = s
        t = rows[pl.ds(0, 8, stride=4), :] + rows[pl.ds(1, 8, stride=4), :]
        t = t + rows[pl.ds(2, 8, stride=4), :] + rows[pl.ds(3, 8, stride=4), :]
        total.append(t * (1.0 / 64.0))
    for half in range(2):
        acc = jnp.zeros((8, 128), F32)
        for quarter in range(4):
            weight = pick(lambda r, c: (r // 4 + 32 * quarter) == c)
            acc = acc + dot(total[half * 4 + quarter], weight)
        out[half * 8 : half * 8 + 8, :] = acc


def pack_y(src, beta, from_lo, from_hi, lo, hi, s_mid, b_mid):
    index = lax.axis_index("gx")
    low = flag(index > 0)
    high = flag(index < lax.axis_size("gx") - 1)
    for field, (ref, mid) in enumerate(((src, s_mid), (beta, b_mid))):
        mid[0:8] = from_lo[field] * low
        mid[8:40] = ref[...]
        mid[40:48] = from_hi[field] * high
        lo[field] = mid[:, 0:8, :]
        hi[field] = mid[:, 24:32, :]


def pack_z(s_mid, b_mid, y_lo, y_hi, s_out, b_out, lo, hi):
    iy = lax.axis_index("gy")
    y_low = flag(iy > 0)
    y_high = flag(iy < lax.axis_size("gy") - 1)
    for field, (mid, out) in enumerate(((s_mid, s_out), (b_mid, b_out))):
        out[:, 8:40, :] = mid[...]
        out[:, 0:8, :] = y_lo[field] * y_low
        out[:, 40:48, :] = y_hi[field] * y_high
    lane = lanes_of(48)

    def body(xx):
        acc_lo = jnp.zeros((48, 128), F32)
        acc_hi = jnp.zeros((48, 128), F32)
        for g in range(8):
            s = s_out[g * 6 + xx]
            b = b_out[g * 6 + xx]
            first = (lane >= g * 16) & (lane < g * 16 + 8)
            second = (lane >= g * 16 + 8) & (lane < g * 16 + 16)
            acc_lo = jnp.where(first, roll(s, g * 16), acc_lo)
            acc_lo = jnp.where(second, roll(b, g * 16 + 8), acc_lo)
            acc_hi = jnp.where(first, roll(s, g * 16 + 8), acc_hi)
            acc_hi = jnp.where(second, roll(b, g * 16 + 16), acc_hi)
        lo[xx] = acc_lo
        hi[xx] = acc_hi

    loop(0, 6, 36, body)


def strip_ghosts(values, ghost):
    lane = lanes_of(48)

    def body(xx):
        acc = jnp.zeros((48, 128), F32)
        for g in range(8):
            acc = jnp.where(lane // 16 == g, roll(values[g * 6 + xx + 1, 8:56, :], g * 16 + 8), acc)
        ghost[xx] = acc

    loop(0, 6, 36, body)


def strip_sides(strip, xx):
    after = strip[xx + 1, 8:56, :] if xx < 5 else roll(strip[0, 8:56, :], -16)
    before = strip[xx - 1, 8:56, :] if xx > 0 else roll(strip[5, 8:56, :], 16)
    return before, after


def strip_z(strip, ghost, xx, lane):
    here = strip[xx, 8:56, :]
    up = jnp.where(lane % 16 == 8, ghost[xx], roll(here, 1))
    down = jnp.where(lane % 16 == 7, ghost[xx], roll(here, -1))
    return down, up


def block_edge(strip, x, first=8, count=48):
    g = x // 6
    return roll(strip[x - g * 6, first : first + count, :], 120 - g * 16)


def weights(here, sides):
    sums = [here + side for side in sides]
    total = sums[0] + sums[1] + sums[2] + sums[3] + sums[4] + sums[5]
    inverse = jnp.where(here > 0.0, 1.0 / total, 0.0)
    return [s * inverse for s in sums], inverse, total


def level0_setup(b_pad, bt_pad, ghost, src, src_t, g_main, g_strip, sp, sp_t, total, v, t, u, u_t, first):
    strip_ghosts(b_pad, ghost)
    lane = lanes_of(48)

    def body(x):
        here = b_pad[x + 1, 8:56, :]
        edge = block_edge(bt_pad, x)
        down = jnp.where(lane == 0, edge, roll(here, 1))
        up = jnp.where(lane == 127, edge, roll(here, -1))
        faces, inverse, tot = weights(
            here,
            (
                b_pad[x, 8:56, :],
                b_pad[x + 2, 8:56, :],
                b_pad[x + 1, 7:55, :],
                b_pad[x + 1, 9:57, :],
                down,
                up,
            ),
        )
        for i in range(4):
            g_main[i, x] = faces[i]
        g_main[4, x] = jnp.where(lane == 0, 0.0, faces[4])
        g_main[5, x] = jnp.where(lane == 127, 0.0, faces[5])
        g_main[6, x] = jnp.where(lane == 0, faces[4], jnp.where(lane == 127, faces[5], 0.0))
        scaled = src[x] * (2.0 * inverse)
        sp[x] = scaled
        u[x] = first * scaled
        v[x + 1, 8:56, :] = first * scaled
        total[x] = tot

    loop(0, 48, 6, body)
    for xx in range(6):
        before, after = strip_sides(bt_pad, xx)
        down, up = strip_z(bt_pad, ghost, xx, lane)
        faces, inverse, _ = weights(
            bt_pad[xx, 8:56, :],
            (before, after, bt_pad[xx, 7:55, :], bt_pad[xx, 9:57, :], down, up),
        )
        for i in range(6):
            g_strip[i, xx] = faces[i]
        scaled = src_t[xx] * (2.0 * inverse)
        sp_t[xx] = scaled
        u_t[xx] = first * scaled
        t[xx, 8:56, :] = first * scaled


def block_rest(v, t, g_main, sp, x, skip=0):
    count = 48 - 2 * skip
    first = 8 + skip
    keep = slice(skip, 48 - skip)
    here = v[x + 1, first : first + count, :]
    rest = sp[x, keep] - here
    rest = rest + g_main[0, x, keep] * v[x, first : first + count, :]
    rest = rest + g_main[1, x, keep] * v[x + 2, first : first + count, :]
    rest = rest + g_main[2, x, keep] * v[x + 1, first - 1 : first - 1 + count, :]
    rest = rest + g_main[3, x, keep] * v[x + 1, first + 1 : first + 1 + count, :]
    rest = rest + g_main[4, x, keep] * roll(here, 1) + g_main[5, x, keep] * roll(here, -1)
    rest = rest + g_main[6, x, keep] * block_edge(t, x, first, count)
    return here, rest


def level0_step(v, t, v_out, t_out, ghost, g_main, g_strip, sp, sp_t, u, u_t, low, high, retain, factor):
    strip_ghosts(v, ghost)
    lane = lanes_of(48)

    def body(x):
        here, rest = block_rest(v, t, g_main, sp, x)
        new = factor * rest
        if retain is not None:
            new = retain * u[x] + new
        u[x] = new
        v_out[x + 1, 8:56, :] = here + new

    loop(low, high, 4, body)
    for xx in range(6):
        here = t[xx, 8:56, :]
        before, after = strip_sides(t, xx)
        down, up = strip_z(t, ghost, xx, lane)
        rest = sp_t[xx] - here
        rest = rest + g_strip[0, xx] * before + g_strip[1, xx] * after
        rest = rest + g_strip[2, xx] * t[xx, 7:55, :] + g_strip[3, xx] * t[xx, 9:57, :]
        rest = rest + g_strip[4, xx] * down + g_strip[5, xx] * up
        new = factor * rest
        if retain is not None:
            new = retain * u_t[xx] + new
        u_t[xx] = new
        t_out[xx, 8:56, :] = here + new


def clear_edges(ref, planes, rows):
    width = ref.shape[1]
    ref[0] = jnp.zeros((width, 128), F32)
    ref[planes + 1] = jnp.zeros((width, 128), F32)

    def body(x):
        ref[x, 0:8, :] = jnp.zeros((8, 128), F32)
        ref[x, 8 + rows : width, :] = jnp.zeros((width - 8 - rows, 128), F32)

    loop(0, planes + 2, 4, body)


def clear_strip(ref):
    for xx in range(6):
        ref[xx, 0:8, :] = jnp.zeros((8, 128), F32)
        ref[xx, 56:64, :] = jnp.zeros((8, 128), F32)


def unpack_strip(z_lo, z_hi, src_t, bt_pad):
    iz = lax.axis_index("gz")
    low = flag(iz > 0)
    high = flag(iz < lax.axis_size("gz") - 1)

    def mirror(first, last):
        return pick(lambda r, c: (r // 16 == c // 16) & ((r % 16 < 8) == first) & (r % 16 + c % 16 == last))

    s_lo, s_hi = mirror(True, 15), mirror(True, 7)
    b_lo, b_hi = mirror(False, 23), mirror(False, 15)
    for xx in range(6):
        before = z_lo[xx] * low
        after = z_hi[xx] * high
        src_t[xx] = dot(before, s_lo) + dot(after, s_hi)
        bt_pad[xx, 8:56, :] = dot(before, b_lo) + dot(after, b_hi)


LEVEL0_SCRATCH = [
    vm(50, 64, 128),
    vm(6, 64, 128),
    vm(50, 64, 128),
    vm(6, 64, 128),
    vm(6, 48, 128),
    vm(48, 48, 128),
    vm(6, 48, 128),
    vm(6, 48, 128),
    vm(48, 48, 128),
    vm(2, 16, 32, 128),
]


def level0_down(
    src, beta, z_lo, z_hi, vb, tb, c_out, c_lo, c_hi, g_main, g_strip, sp, sp_t, bt_out,
    b_pad, bt_pad, va, ta, ghost, u, u_t, src_t, total, rows,
):
    for ref in (b_pad, va, vb):
        clear_edges(ref, 48, 48)
    for ref in (bt_pad, ta, tb):
        clear_strip(ref)
    b_pad[1:49, 8:56, :] = beta[...]
    unpack_strip(z_lo, z_hi, src_t, bt_pad)
    for xx in range(6):
        bt_out[xx] = bt_pad[xx, 8:56, :]
    level0_setup(
        b_pad, bt_pad, ghost, src, src_t, g_main, g_strip, sp, sp_t, total, va, ta, u, u_t, RECIPE[0][1]
    )
    for x in (0, 1, 46, 47):
        vb[x + 1, 8:56, :] = jnp.zeros((48, 128), F32)
    bufs = [(va, ta), (vb, tb)]
    for k in range(1, SMOOTH):
        (v, t), (w, s) = bufs
        retain, factor = RECIPE[k]
        level0_step(
            v, t, w, s, ghost, g_main, g_strip, sp, sp_t, u, u_t, 1 + k, 47 - k, retain, factor
        )
        bufs = [(w, s), (v, t)]
    v, t = bufs[0]
    assert v is vb and t is tb

    to_low = pick(lambda r, c: r // 2 == c)
    to_high = pick(lambda r, c: r // 2 + 64 == c)

    def restrict(x2):
        parts = []
        for half in range(2):
            x = 8 + 2 * x2 + half
            _, rest = block_rest(v, t, g_main, sp, x, 8)
            parts.append(rest * total[x, 8:40])
        rows[0, x2] = (parts[0] + parts[1]) * (0.5 / 8.0)
        rows[1, x2] = (b_pad[9 + 2 * x2, 16:48, :] + b_pad[10 + 2 * x2, 16:48, :]) * (1.0 / 8.0)

    loop(0, 16, 8, restrict)

    def compress(x2):
        res = rows[0, x2, pl.ds(0, 16, stride=2), :] + rows[0, x2, pl.ds(1, 16, stride=2), :]
        bet = rows[1, x2, pl.ds(0, 16, stride=2), :] + rows[1, x2, pl.ds(1, 16, stride=2), :]
        c_out[x2] = dot(res, to_low) + dot(bet, to_high)

    loop(0, 16, 8, compress)
    c_lo[...] = c_out[0:10]
    c_hi[...] = c_out[6:16]


def pack1_y(c, from_lo, from_hi, lo, hi):
    index = lax.axis_index("gx")
    low = flag(index > 0)
    high = flag(index < lax.axis_size("gx") - 1)
    for x in range(36):
        if x < 10:
            plane = from_lo[x] * low
        elif x < 26:
            plane = c[x - 10]
        else:
            plane = from_hi[x - 26] * high
        lo[x * 10 : x * 10 + 10, :] = plane[0:10]
        hi[x * 10 : x * 10 + 10, :] = plane[6:16]


def pack1_z(c, x_lo, x_hi, y_lo, y_hi, ext, lo, hi):
    ix = lax.axis_index("gx")
    iy = lax.axis_index("gy")
    x_low = flag(ix > 0)
    x_high = flag(ix < lax.axis_size("gx") - 1)
    y_low = flag(iy > 0)
    y_high = flag(iy < lax.axis_size("gy") - 1)
    ext[0:10, 10:26, :] = x_lo[...] * x_low
    ext[10:26, 10:26, :] = c[...]
    ext[26:36, 10:26, :] = x_hi[...] * x_high
    for x in range(36):
        ext[x, 0:10, :] = y_lo[x * 10 : x * 10 + 10, :] * y_low
        ext[x, 26:36, :] = y_hi[x * 10 : x * 10 + 10, :] * y_high
        ext[x, 36:40, :] = jnp.zeros((4, 128), F32)
    lane = lanes_of(40)

    def body(xx):
        acc_lo = jnp.zeros((40, 128), F32)
        acc_hi = jnp.zeros((40, 128), F32)
        for g in range(6):
            e = ext[g * 6 + xx]
            first = (lane >= g * 20) & (lane < g * 20 + 10)
            second = (lane >= g * 20 + 10) & (lane < g * 20 + 20)
            middle = roll(e, g * 20 - 54)
            acc_lo = jnp.where(first, roll(e, g * 20), acc_lo)
            acc_lo = jnp.where(second, middle, acc_lo)
            acc_hi = jnp.where(first, middle, acc_hi)
            acc_hi = jnp.where(second, roll(e, g * 20 + 20), acc_hi)
        lo[xx] = acc_lo
        hi[xx] = acc_hi

    loop(0, 6, 36, body)


def ring_weights(b_pad, src, g, sp, total, planes, rows, scale, edges=None):
    lane = lanes_of(rows)

    def body(x):
        here = b_pad[x + 1, 8 : 8 + rows, :]
        down = roll(here, 1)
        up = roll(here, -1)
        if edges is not None:
            down = jnp.where(lane == 0, 0.0, down)
            up = jnp.where(lane == 127, 0.0, up)
        faces, inverse, tot = weights(
            here,
            (
                b_pad[x, 8 : 8 + rows, :],
                b_pad[x + 2, 8 : 8 + rows, :],
                b_pad[x + 1, 7 : 7 + rows, :],
                b_pad[x + 1, 9 : 9 + rows, :],
                down,
                up,
            ),
        )
        if edges is not None:
            faces[4] = jnp.where(lane == 0, 0.0, faces[4])
            faces[5] = jnp.where(lane == 127, 0.0, faces[5])
        for i in range(6):
            g[i, x] = faces[i]
        sp[x] = scale * 2.0 * inverse if src is None else src[x] * (scale * 2.0 * inverse)
        if total is not None:
            total[x] = tot

    loop(0, planes, rows // 5, body)


def ring_rest(v, g, sp, x, rows):
    here = v[x + 1, 8 : 8 + rows, :]
    rest = sp[x] - here
    rest = rest + g[0, x] * v[x, 8 : 8 + rows, :] + g[1, x] * v[x + 2, 8 : 8 + rows, :]
    rest = rest + g[2, x] * v[x + 1, 7 : 7 + rows, :] + g[3, x] * v[x + 1, 9 : 9 + rows, :]
    rest = rest + g[4, x] * roll(here, 1) + g[5, x] * roll(here, -1)
    return here, rest


def ring_step(v, v_out, g, sp, u, planes, rows, retain, factor):
    def body(x):
        here, rest = ring_rest(v, g, sp, x, rows)
        new = factor * rest
        if retain is not None:
            new = retain * u[x] + new
        u[x] = new
        v_out[x + 1, 8 : 8 + rows, :] = here + new

    loop(0, planes, rows // 16, body)


def ring_zero_start(v, u, sp, planes, rows, factor):
    def body(x):
        u[x] = factor * sp[x]
        v[x + 1, 8 : 8 + rows, :] = u[x]

    loop(0, planes, rows // 8, body)


def ring_cheb(va, vb, g, sp, u, planes, rows, recipe, from_zero):
    begin = 0
    if from_zero:
        ring_zero_start(va, u, sp, planes, rows, recipe[0][1])
        begin = 1
    for k in range(begin, len(recipe)):
        retain, factor = recipe[k]
        ring_step(va, vb, g, sp, u, planes, rows, None if k == 0 else retain, factor)
        va, vb = vb, va
    return va


LEVEL1_SCRATCH = [
    vm(38, 56, 128),
    vm(38, 56, 128),
    vm(36, 40, 128),
    vm(36, 40, 128),
    vm(36, 40, 128),
    vm(8, 40, 128),
]


def level1_unpack(ext, z_lo, z_hi, source, b_pad, beta_out):
    iz = lax.axis_index("gz")
    low = flag(iz > 0)
    high = flag(iz < lax.axis_size("gz") - 1)
    lane = lanes_of(40)
    inner = lane < 64
    above = (lane >= 64) & (lane < 74)
    below = lane >= 118

    def unpack(xx):
        before = z_lo[xx] * low
        after = z_hi[xx] * high
        for k in range(6):
            x = k * 6 + xx
            e = ext[x]
            s = jnp.where(inner, e, 0.0)
            s = jnp.where(above, roll(after, 64 - k * 20), s)
            s = jnp.where(below, roll(before, 118 - k * 20), s)
            b = jnp.where(inner, roll(e, 64), 0.0)
            b = jnp.where(above, roll(after, 54 - k * 20), b)
            b = jnp.where(below, roll(before, 108 - k * 20), b)
            source[x] = s
            b_pad[x + 1, 8:48, :] = b
            beta_out[x] = b

    loop(0, 6, 36, unpack)


def level1_down(
    ext, z_lo, z_hi, vb, chunk, g, sp, beta_out,
    b_pad, va, u, src, total, rows,
):
    for ref in (b_pad, va, vb):
        clear_edges(ref, 36, 40)
    level1_unpack(ext, z_lo, z_hi, src, b_pad, beta_out)
    ring_weights(b_pad, src, g, sp, total, 36, 40, 4.0)
    v = ring_cheb(va, vb, g, sp, u, 36, 40, RECIPE, True)
    assert v is vb
    summed = []
    for x2 in range(8):
        parts = []
        for half in range(2):
            x = 10 + 2 * x2 + half
            _, rest = ring_rest(v, g, sp, x, 40)
            parts.append(rest * total[x])
        rows[x2] = (parts[0] + parts[1]) * (0.25 * 0.5 / 8.0)
        summed.append(rows[x2, pl.ds(10, 8, stride=2), :] + rows[x2, pl.ds(11, 8, stride=2), :])
    for half in range(2):
        acc = jnp.zeros((8, 128), F32)
        for quarter in range(4):
            weight = pick(lambda r, c: (r < 64) & ((r // 2 + 32 * quarter) == c))
            acc = acc + dot(summed[half * 4 + quarter], weight)
        chunk[half * 8 : half * 8 + 8, :] = acc


def sender(axis, step):
    count = lax.axis_size(axis)
    return lax.rem(lax.axis_index(axis) + count - step, count)


def singles(parts):
    return [part.at[i] for part in parts for i in range(2)] if len(parts) == 2 else parts


def gather_z(*refs):
    *parts, _, out = refs
    parts = singles(parts)
    lane = lanes_of(8)
    for half in range(2):
        for quarter in range(4):
            acc = jnp.zeros((8, 128), F32)
            for step, part in enumerate(parts):
                owner = sender("gz", step)
                moved = roll(part[half * 8 : half * 8 + 8, :], lax.rem(owner - quarter + 4, 4) * 32)
                acc = jnp.where(lane // 32 == owner, moved, acc)
            out[half * 4 + quarter] = acc


def gather_x(*refs):
    *parts, _, out = refs
    parts = singles(parts)
    for step, part in enumerate(parts):
        out[pl.ds(sender("gx", step) * 8, 8)] = part[...]


def stack_y(*refs):
    *parts, _, out = refs
    for step, part in enumerate(singles(parts)):
        out[step] = part[...]


def pair(mine, other, _, out):
    out[0] = mine[...]
    out[1] = other[...]


def gather_y(same, other, out):
    count = lax.axis_size("gy")
    index = lax.axis_index("gy")
    sibling = index + 1 - 2 * lax.rem(index, 2)
    for stack, first in ((same, index), (other, sibling)):
        for step in range(4):
            owner = lax.rem(first + count - 2 * step, count)
            row = pl.multiple_of(8 + owner * 8, 8)
            out[8:40, pl.ds(row, 8), :] = stack[step]


def clear_whole(ref):
    def clear(x):
        ref[x, 0:8, :] = jnp.zeros((8, 128), F32)
        ref[x, 72:80, :] = jnp.zeros((8, 128), F32)

    loop(0, 48, 2, clear)
    for x in [*range(8), *range(40, 48)]:
        ref[x, 8:72, :] = jnp.zeros((64, 128), F32)


def coarse_prepare(same, sibling, g, inv, total, g3, inv3, gw, invw, b2, b3, bw, rows):
    clear_whole(b2)
    clear_edges(b3, 16, 32)
    clear_edges(bw, 22, 24)
    gather_y(same, sibling, b2)
    ring_weights(b2.at[7:41], None, g, inv, total, 32, 64, 16.0, edges=True)
    half_z = pick(lambda r, c: r // 2 == c)

    def restrict(x2):
        rows[x2] = (b2[8 + 2 * x2, 8:72, :] + b2[9 + 2 * x2, 8:72, :]) * (1.0 / 8.0)

    loop(0, 16, 8, restrict)

    def compress(x2):
        bet = rows[x2, pl.ds(0, 32, stride=2), :] + rows[x2, pl.ds(1, 32, stride=2), :]
        b3[x2 + 1, 8:40, :] = dot(bet, half_z)

    loop(0, 16, 9, compress)
    ring_weights(b3, None, g3, inv3, None, 16, 32, 64.0)
    ix = lax.axis_index("gx")
    row = pl.multiple_of(lax.axis_index("gy") * 8, 8)

    def window(x):
        bw[x + 1, 8:32, :] = b2[ix * 8 + 1 + x, pl.ds(row, 24), :]

    loop(0, 22, 6, window)
    ring_weights(bw, None, gw, invw, None, 22, 24, 16.0, edges=True)


COARSE_SHAPES = [
    (6, 32, 64, 128),
    (32, 64, 128),
    (32, 64, 128),
    (6, 16, 32, 128),
    (16, 32, 128),
    (6, 22, 24, 128),
    (22, 24, 128),
]


def bottom(
    same, sibling, g, inv, total, g3, inv3, gw, invw, out,
    s2, va, vb, sp, u, v3a, v3b, sp3, u3, rows, wa, wb, spw, uw,
):
    for ref in (s2, va, vb):
        clear_whole(ref)
    gather_y(same, sibling, s2)

    def scale(x):
        sp[x] = s2[x + 8, 8:72, :] * inv[x]

    loop(0, 32, 8, scale)
    v = ring_cheb(va.at[7:41], vb.at[7:41], g, sp, u, 32, 64, RECIPE, True)
    iterate = vb if SMOOTH % 2 == 0 else va

    clear_edges(v3a, 16, 32)
    clear_edges(v3b, 16, 32)
    half_z = pick(lambda r, c: r // 2 == c)

    def restrict(x2):
        parts = []
        for half in range(2):
            x = 2 * x2 + half
            _, rest = ring_rest(v, g, sp, x, 64)
            parts.append(rest * total[x])
        rows[x2] = (parts[0] + parts[1]) * (0.0625 * 0.5 / 8.0)

    loop(0, 16, 16, restrict)

    def compress(x2):
        res = rows[x2, pl.ds(0, 32, stride=2), :] + rows[x2, pl.ds(1, 32, stride=2), :]
        sp3[x2] = dot(res, half_z) * inv3[x2]

    loop(0, 16, 9, compress)
    c3 = ring_cheb(v3a, v3b, g3, sp3, u3, 16, 32, BOTTOM_RECIPE, True)

    other = va if iterate is vb else vb
    double_z = pick(lambda r, c: c // 2 == r)

    def prolong(x3):
        wide = dot(c3[x3 + 1, 8:40, :], double_z)
        rows[x3, pl.ds(0, 32, stride=2), :] = wide
        rows[x3, pl.ds(1, 32, stride=2), :] = wide
        for half in range(2):
            x = 8 + 2 * x3 + half
            other[x, 8:72, :] = iterate[x, 8:72, :] + rows[x3]

    loop(0, 16, 18, prolong)
    ix = lax.axis_index("gx")
    iz = lax.axis_index("gz")
    clear_edges(wa, 22, 24)
    clear_edges(wb, 22, 24)
    row = pl.multiple_of(lax.axis_index("gy") * 8, 8)

    def window(x):
        plane = ix * 8 + 1 + x
        wa[x + 1, 8:32, :] = other[plane, pl.ds(row, 24), :]
        spw[x] = s2[plane, pl.ds(row, 24), :] * invw[x]

    loop(0, 22, 6, window)
    c2 = ring_cheb(wa, wb, gw, spw, uw, 22, 24, RECIPE, False)
    shift = (128 - iz * 32) % 128
    for x in range(18):
        out[x] = roll(c2[x + 3, 8:32, :], shift)


COARSE_SCRATCH = [
    vm(48, 80, 128),
    vm(18, 48, 128),
    vm(24, 40, 128),
    vm(16, 64, 128),
]
BOTTOM_SCRATCH = [
    vm(48, 80, 128),
    vm(48, 80, 128),
    vm(48, 80, 128),
    vm(32, 64, 128),
    vm(32, 64, 128),
    vm(18, 48, 128),
    vm(18, 48, 128),
    vm(16, 32, 128),
    vm(16, 32, 128),
    vm(16, 64, 128),
    vm(24, 40, 128),
    vm(24, 40, 128),
    vm(22, 24, 128),
    vm(22, 24, 128),
]


def level1_up(c2, g, sp, beta, iterate, out, va, vb, u, wide, rows):
    for ref in (va, vb):
        clear_edges(ref, 36, 40)
    spread = pick(lambda r, c: ((c < 74) & (c // 2 == r)) | ((c >= 118) & (c // 2 + 64 == r)))
    for x2 in range(18):
        rows[x2, 32:40, :] = jnp.zeros((8, 128), F32)

    def prolong(x2):
        wide[x2] = dot(c2[x2], spread)
        part = wide[x2, 3:21, :]
        rows[x2, pl.ds(0, 18, stride=2), :] = part
        rows[x2, pl.ds(1, 18, stride=2), :] = part
        for half in range(2):
            x = 2 * x2 + half
            va[x + 1, 8:48, :] = jnp.where(beta[x] > 0.0, iterate[x + 1, 8:48, :] + rows[x2], 0.0)

    loop(0, 18, 12, prolong)
    v = ring_cheb(va, vb, g, sp, u, 36, 40, RECIPE, False)
    out[...] = v[7:31, 14:38, :]


def level0_up(
    c1, beta, g_main, g_strip, sp, sp_t, beta_t, iterate, iterate_t, out,
    va, vb, ta, tb, ghost, u, u_t, rows,
):
    for ref in (va, vb):
        clear_edges(ref, 48, 48)
    for ref in (ta, tb):
        clear_strip(ref)
    spread = pick(lambda r, c: c // 2 == r)

    def prolong(x1):
        wide = dot(c1[x1], spread)
        rows[x1, pl.ds(0, 24, stride=2), :] = wide
        rows[x1, pl.ds(1, 24, stride=2), :] = wide
        for half in range(2):
            x = 2 * x1 + half
            va[x + 1, 8:56, :] = jnp.where(beta[x] > 0.0, iterate[x + 1, 8:56, :] + rows[x1], 0.0)

    loop(0, 24, 12, prolong)

    def prolong_strip(m):
        acc = jnp.zeros((24, 128), F32)
        for k in range(8):
            to = pick(
                lambda r, c: (c // 16 == k)
                & (
                    ((c % 16 < 8) & (r == 64 + (7 - c % 16) // 2))
                    | ((c % 16 >= 8) & (r == 124 + (15 - c % 16) // 2))
                )
            )
            acc = acc + dot(c1[k * 3 + m], to)
        rows[m, pl.ds(0, 24, stride=2), :] = acc
        rows[m, pl.ds(1, 24, stride=2), :] = acc
        for half in range(2):
            xx = 2 * m + half
            ta[xx, 8:56, :] = jnp.where(beta_t[xx] > 0.0, iterate_t[xx, 8:56, :] + rows[m], 0.0)

    loop(0, 3, 36, prolong_strip)
    for x in [*range(6), *range(42, 48)]:
        vb[x + 1, 8:56, :] = jnp.zeros((48, 128), F32)
    bufs = [(va, ta), (vb, tb)]
    for k in range(SMOOTH):
        (v, t), (w, s) = bufs
        retain, factor = RECIPE[k]
        if k == 0:
            retain = None
        if k < SMOOTH - 1:
            low, high = (4, 44) if k < 2 else (6, 42)
            level0_step(
                v, t, w, s, ghost, g_main, g_strip, sp, sp_t, u, u_t, low, high, retain, factor
            )
        else:

            def last(x):
                here, rest = block_rest(v, t, g_main, sp, x, 8)
                out[x - 8] = here + retain * u[x, 8:40] + factor * rest

            loop(8, 40, 4, last)
        bufs = [(w, s), (v, t)]


def ring(value, axis, step):
    count = lax.axis_size(axis)
    return lax.ppermute(value, axis, [(i, (i + step) % count) for i in range(count)])


def trade(lo, hi, axis):
    return ring(hi, axis, 1), ring(lo, axis, -1)


def gather(kernel, parts, after, *shape):
    return call(kernel, sds(*shape), name=kernel.__name__, last_unread=len(parts) + 1)(*parts, after)


def around(value, axis):
    return [value] + [ring(value, axis, step) for step in range(1, lax.axis_size(axis))]


def chips(value):
    return [value] + [ring(value, "gy", 2 * step) for step in (1, 2, 3)]


def across(value):
    count = lax.axis_size("gy")
    return lax.ppermute(value, "gy", [(i, i + 1 - 2 * (i % 2)) for i in range(count)])


def per_device(source, beta):
    lo = jnp.stack([source[0:8], beta[0:8]])
    hi = jnp.stack([source[24:32], beta[24:32]])
    lo, hi, source, beta = lax.optimization_barrier((lo, hi, source, beta))
    x_lo, x_hi = trade(lo, hi, "gx")
    beta2 = call(coarse_beta, sds(16, 128), [vm(32, 128)], name="coarse_beta")(beta)
    beta2_pair = gather(pair, [beta2, ring(beta2, "gz", 1)], lo, 2, 16, 128)
    x_lo, x_hi, beta2_pair = lax.optimization_barrier((x_lo, x_hi, beta2_pair))
    slab = sds(2, 48, 8, 128)
    mid = sds(48, 32, 128)
    lo, hi, s_mid, b_mid = call(pack_y, (slab, slab, mid, mid), name="pack_y", mib=4)(
        source, beta, x_lo, x_hi
    )
    y_lo, y_hi = trade(lo, hi, "gy")
    beta2_block = gather(gather_z, [beta2_pair, ring(beta2_pair, "gz", 2)], lo, 8, 8, 128)
    y_lo, y_hi, beta2_block = lax.optimization_barrier((y_lo, y_hi, beta2_block))
    whole = sds(48, 48, 128)
    strip = sds(6, 48, 128)
    src_ext, beta_ext, lo, hi = call(
        pack_z, (whole, whole, strip, strip), name="pack_z", mib=4
    )(s_mid, b_mid, y_lo, y_hi)
    z_lo, z_hi = trade(lo, hi, "gz")
    beta2_pair = gather(pair, [beta2_block, ring(beta2_block, "gx", 1)], lo, 2, 8, 8, 128)
    z_lo, z_hi, beta2_pair = lax.optimization_barrier((z_lo, z_hi, beta2_pair))
    iter0, iter0_t, c, lo, hi, *ready = call(
        level0_down,
        (
            sds(50, 64, 128),
            sds(6, 64, 128),
            sds(16, 16, 128),
            sds(10, 16, 128),
            sds(10, 16, 128),
            sds(7, 48, 48, 128),
            sds(6, 6, 48, 128),
            whole,
            strip,
            strip,
        ),
        LEVEL0_SCRATCH,
        name="level0_down",
        mib=16,
    )(src_ext, beta_ext, z_lo, z_hi)
    x_lo, x_hi = trade(lo, hi, "gx")
    beta2_pair, _ = lax.optimization_barrier((beta2_pair, lo))
    beta2_slab = gather(gather_x, [beta2_pair, ring(beta2_pair, "gx", 2)], lo, 32, 8, 128)
    x_lo, x_hi, beta2_slab = lax.optimization_barrier((x_lo, x_hi, beta2_slab))
    lo, hi = call(pack1_y, (sds(360, 128), sds(360, 128)), name="pack1_y")(c, x_lo, x_hi)
    y_lo, y_hi = trade(lo, hi, "gy")
    beta2_pair = gather(pair, [beta2_slab, ring(beta2_slab, "gy", 2)], lo, 2, 32, 8, 128)
    y_lo, y_hi, beta2_pair = lax.optimization_barrier((y_lo, y_hi, beta2_pair))
    ext, lo, hi = call(
        pack1_z, (sds(36, 40, 128), sds(6, 40, 128), sds(6, 40, 128)), name="pack1_z"
    )(c, x_lo, x_hi, y_lo, y_hi)
    z1_lo, z1_hi = trade(lo, hi, "gz")
    beta2_pair, _ = lax.optimization_barrier((beta2_pair, lo))
    beta2_stack = gather(stack_y, [beta2_pair, ring(beta2_pair, "gy", 4)], lo, 4, 32, 8, 128)
    z1_lo, z1_hi, beta2_stack = lax.optimization_barrier((z1_lo, z1_hi, beta2_stack))
    level1 = sds(36, 40, 128)
    iter1, chunk, g1, sp1, beta1 = call(
        level1_down,
        (sds(38, 56, 128), sds(16, 128), sds(6, 36, 40, 128), level1, level1),
        LEVEL1_SCRATCH,
        name="level1_down",
        mib=8,
    )(ext, z1_lo, z1_hi)
    parts = around(chunk, "gz")
    beta2_stack, _ = lax.optimization_barrier((beta2_stack, chunk))
    *parts, beta2_other = lax.optimization_barrier((*parts, across(beta2_stack)))
    parts = around(gather(gather_z, parts, chunk, 8, 8, 128), "gx")
    slab = gather(gather_x, parts, chunk, 32, 8, 128)
    stack = gather(stack_y, chips(slab), slab, 4, 32, 8, 128)
    stack_other = across(stack)
    coarse = call(
        coarse_prepare,
        tuple(sds(*shape) for shape in COARSE_SHAPES),
        COARSE_SCRATCH,
        name="coarse_prepare",
        mib=8,
    )(beta2_stack, beta2_other)
    c2 = call(bottom, sds(18, 24, 128), BOTTOM_SCRATCH, name="bottom", mib=18)(
        stack, stack_other, *coarse
    )
    c1 = call(
        level1_up,
        sds(24, 24, 128),
        [vm(38, 56, 128), vm(38, 56, 128), vm(36, 40, 128), vm(18, 24, 128), vm(18, 40, 128)],
        name="level1_up",
        mib=8,
    )(c2, g1, sp1, beta1, iter1)
    return call(
        level0_up,
        sds(32, 32, 128),
        [vm(50, 64, 128), vm(50, 64, 128), vm(6, 64, 128), vm(6, 64, 128), vm(6, 48, 128)]
        + [vm(48, 48, 128), vm(6, 48, 128), vm(24, 48, 128)],
        name="level0_up",
        mib=14,
    )(c1, beta_ext, *ready, iter0, iter0_t)


def solution(mesh):
    placed = (P(*AXES), P(*AXES))
    return jax.shard_map(
        per_device, mesh=mesh, in_specs=placed, out_specs=P(*AXES), check_vma=False
    )
```

```python
import jax
import jax.numpy as jnp
from jax import lax
from jax.experimental import pallas as pl
from jax.experimental.pallas import tpu as pltpu
from jax.sharding import PartitionSpec as P

SMOOTH = 4
BOTTOM = 12
LOW_EIG = 0.3
HIGH_EIG = 2.0
BOTTOM_LOW = 0.02

AXES = ("gx", "gy", "gz")
F32 = jnp.float32
MIB = 1024 * 1024


def cheb_plan(degree, lowest, highest):
    centre = 0.5 * (highest + lowest)
    radius = 0.5 * (highest - lowest)
    ratio_s = centre / radius
    rho_old = 1.0 / ratio_s
    recipe = [(0.0, 1.0 / centre)]
    for position in range(1, degree):
        rho_new = 1.0 / (2.0 * ratio_s - rho_old)
        recipe.append((rho_new * rho_old, 2.0 * rho_new / radius))
        rho_old = rho_new
    return recipe


RECIPE = cheb_plan(SMOOTH, LOW_EIG, HIGH_EIG)
BOTTOM_RECIPE = cheb_plan(BOTTOM, BOTTOM_LOW, HIGH_EIG)


def sds(*shape):
    return jax.ShapeDtypeStruct(shape, F32)


def vm(*shape):
    return pltpu.VMEM(shape, F32)


def call(body, outs, scratch=(), name=None, mib=2, last_unread=None):
    specs = {}
    if last_unread:
        whole = pl.BlockSpec(memory_space=pltpu.VMEM)
        specs["in_specs"] = [whole] * (last_unread - 1) + [pl.BlockSpec(memory_space=pl.ANY)]
    return pl.pallas_call(
        body,
        out_shape=outs,
        **specs,
        scratch_shapes=list(scratch),
        compiler_params=pltpu.CompilerParams(vmem_limit_bytes=mib * MIB),
        name=name,
    )


def loop(low, high, vectors, body):
    count = high - low
    most = max(1, min(count, 72 // vectors))
    width = max([w for w in range(1, most + 1) if count % w == 0])
    if width * 2 < most:
        width = most
    rounds = count // width

    def chunk(i, carry):
        for k in range(width):
            body(low + i * width + k)
        return carry

    if rounds > 1:
        lax.fori_loop(0, rounds, chunk, 0)
    else:
        chunk(0, 0)
    for x in range(low + rounds * width, high):
        body(x)


def lanes_of(rows):
    return lax.broadcasted_iota(jnp.int32, (rows, 128), 1)


def roll(value, shift):
    if isinstance(shift, int):
        shift = shift % 128
        if shift == 0:
            return value
    return pltpu.roll(value, shift, 1)


def flag(condition):
    return jnp.where(condition, 1.0, 0.0).astype(F32)


def dot(left, right):
    return lax.dot_general(
        left,
        right,
        (((1,), (0,)), ((), ())),
        precision=lax.Precision.HIGHEST,
        preferred_element_type=F32,
    )


def pick(match):
    row = lax.broadcasted_iota(jnp.int32, (128, 128), 0)
    col = lax.broadcasted_iota(jnp.int32, (128, 128), 1)
    return jnp.where(match(row, col), 1.0, 0.0).astype(F32)


def coarse_beta(beta, out, rows):
    total = []
    for x in range(8):
        s = beta[4 * x] + beta[4 * x + 1] + beta[4 * x + 2] + beta[4 * x + 3]
        rows[...] = s
        t = rows[pl.ds(0, 8, stride=4), :] + rows[pl.ds(1, 8, stride=4), :]
        t = t + rows[pl.ds(2, 8, stride=4), :] + rows[pl.ds(3, 8, stride=4), :]
        total.append(t * (1.0 / 64.0))
    for half in range(2):
        acc = jnp.zeros((8, 128), F32)
        for quarter in range(4):
            weight = pick(lambda r, c: (r // 4 + 32 * quarter) == c)
            acc = acc + dot(total[half * 4 + quarter], weight)
        out[half * 8 : half * 8 + 8, :] = acc


def pack_y(src, beta, from_lo, from_hi, lo, hi, s_mid, b_mid):
    index = lax.axis_index("gx")
    low = flag(index > 0)
    high = flag(index < lax.axis_size("gx") - 1)
    for field, (ref, mid) in enumerate(((src, s_mid), (beta, b_mid))):
        mid[0:8] = from_lo[field] * low
        mid[8:40] = ref[...]
        mid[40:48] = from_hi[field] * high
        lo[field] = mid[:, 0:8, :]
        hi[field] = mid[:, 24:32, :]


def pack_z(s_mid, b_mid, y_lo, y_hi, s_out, b_out, lo, hi):
    iy = lax.axis_index("gy")
    y_low = flag(iy > 0)
    y_high = flag(iy < lax.axis_size("gy") - 1)
    for field, (mid, out) in enumerate(((s_mid, s_out), (b_mid, b_out))):
        out[:, 8:40, :] = mid[...]
        out[:, 0:8, :] = y_lo[field] * y_low
        out[:, 40:48, :] = y_hi[field] * y_high
    lane = lanes_of(48)

    def body(xx):
        acc_lo = jnp.zeros((48, 128), F32)
        acc_hi = jnp.zeros((48, 128), F32)
        for g in range(8):
            s = s_out[g * 6 + xx]
            b = b_out[g * 6 + xx]
            first = (lane >= g * 16) & (lane < g * 16 + 8)
            second = (lane >= g * 16 + 8) & (lane < g * 16 + 16)
            acc_lo = jnp.where(first, roll(s, g * 16), acc_lo)
            acc_lo = jnp.where(second, roll(b, g * 16 + 8), acc_lo)
            acc_hi = jnp.where(first, roll(s, g * 16 + 8), acc_hi)
            acc_hi = jnp.where(second, roll(b, g * 16 + 16), acc_hi)
        lo[xx] = acc_lo
        hi[xx] = acc_hi

    loop(0, 6, 36, body)


def strip_ghosts(values, ghost):
    lane = lanes_of(48)

    def body(xx):
        acc = jnp.zeros((48, 128), F32)
        for g in range(8):
            acc = jnp.where(lane // 16 == g, roll(values[g * 6 + xx + 1, 8:56, :], g * 16 + 8), acc)
        ghost[xx] = acc

    loop(0, 6, 36, body)


def strip_sides(strip, xx):
    after = strip[xx + 1, 8:56, :] if xx < 5 else roll(strip[0, 8:56, :], -16)
    before = strip[xx - 1, 8:56, :] if xx > 0 else roll(strip[5, 8:56, :], 16)
    return before, after


def strip_z(strip, ghost, xx, lane):
    here = strip[xx, 8:56, :]
    up = jnp.where(lane % 16 == 8, ghost[xx], roll(here, 1))
    down = jnp.where(lane % 16 == 7, ghost[xx], roll(here, -1))
    return down, up


def block_edge(strip, x, first=8, count=48):
    g = x // 6
    return roll(strip[x - g * 6, first : first + count, :], 120 - g * 16)


def weights(here, sides):
    sums = [here + side for side in sides]
    total = sums[0] + sums[1] + sums[2] + sums[3] + sums[4] + sums[5]
    inverse = jnp.where(here > 0.0, 1.0 / total, 0.0)
    return [s * inverse for s in sums], inverse, total


def level0_setup(b_pad, bt_pad, ghost, src, src_t, g_main, g_strip, sp, sp_t, total, v, t, u, u_t, first):
    strip_ghosts(b_pad, ghost)
    lane = lanes_of(48)

    def body(x):
        here = b_pad[x + 1, 8:56, :]
        edge = block_edge(bt_pad, x)
        down = jnp.where(lane == 0, edge, roll(here, 1))
        up = jnp.where(lane == 127, edge, roll(here, -1))
        faces, inverse, tot = weights(
            here,
            (
                b_pad[x, 8:56, :],
                b_pad[x + 2, 8:56, :],
                b_pad[x + 1, 7:55, :],
                b_pad[x + 1, 9:57, :],
                down,
                up,
            ),
        )
        for i in range(4):
            g_main[i, x] = faces[i]
        g_main[4, x] = jnp.where(lane == 0, 0.0, faces[4])
        g_main[5, x] = jnp.where(lane == 127, 0.0, faces[5])
        g_main[6, x] = jnp.where(lane == 0, faces[4], jnp.where(lane == 127, faces[5], 0.0))
        scaled = src[x] * (2.0 * inverse)
        sp[x] = scaled
        u[x] = first * scaled
        v[x + 1, 8:56, :] = first * scaled
        total[x] = tot

    loop(0, 48, 6, body)
    for xx in range(6):
        before, after = strip_sides(bt_pad, xx)
        down, up = strip_z(bt_pad, ghost, xx, lane)
        faces, inverse, _ = weights(
            bt_pad[xx, 8:56, :],
            (before, after, bt_pad[xx, 7:55, :], bt_pad[xx, 9:57, :], down, up),
        )
        for i in range(6):
            g_strip[i, xx] = faces[i]
        scaled = src_t[xx] * (2.0 * inverse)
        sp_t[xx] = scaled
        u_t[xx] = first * scaled
        t[xx, 8:56, :] = first * scaled


def block_rest(v, t, g_main, sp, x, skip=0):
    count = 48 - 2 * skip
    first = 8 + skip
    keep = slice(skip, 48 - skip)
    here = v[x + 1, first : first + count, :]
    rest = sp[x, keep] - here
    rest = rest + g_main[0, x, keep] * v[x, first : first + count, :]
    rest = rest + g_main[1, x, keep] * v[x + 2, first : first + count, :]
    rest = rest + g_main[2, x, keep] * v[x + 1, first - 1 : first - 1 + count, :]
    rest = rest + g_main[3, x, keep] * v[x + 1, first + 1 : first + 1 + count, :]
    rest = rest + g_main[4, x, keep] * roll(here, 1) + g_main[5, x, keep] * roll(here, -1)
    rest = rest + g_main[6, x, keep] * block_edge(t, x, first, count)
    return here, rest


def level0_step(v, t, v_out, t_out, ghost, g_main, g_strip, sp, sp_t, u, u_t, low, high, retain, factor):
    strip_ghosts(v, ghost)
    lane = lanes_of(48)

    def body(x):
        here, rest = block_rest(v, t, g_main, sp, x)
        new = factor * rest
        if retain is not None:
            new = retain * u[x] + new
        u[x] = new
        v_out[x + 1, 8:56, :] = here + new

    loop(low, high, 4, body)
    for xx in range(6):
        here = t[xx, 8:56, :]
        before, after = strip_sides(t, xx)
        down, up = strip_z(t, ghost, xx, lane)
        rest = sp_t[xx] - here
        rest = rest + g_strip[0, xx] * before + g_strip[1, xx] * after
        rest = rest + g_strip[2, xx] * t[xx, 7:55, :] + g_strip[3, xx] * t[xx, 9:57, :]
        rest = rest + g_strip[4, xx] * down + g_strip[5, xx] * up
        new = factor * rest
        if retain is not None:
            new = retain * u_t[xx] + new
        u_t[xx] = new
        t_out[xx, 8:56, :] = here + new


def clear_edges(ref, planes, rows):
    width = ref.shape[1]
    ref[0] = jnp.zeros((width, 128), F32)
    ref[planes + 1] = jnp.zeros((width, 128), F32)

    def body(x):
        ref[x, 0:8, :] = jnp.zeros((8, 128), F32)
        ref[x, 8 + rows : width, :] = jnp.zeros((width - 8 - rows, 128), F32)

    loop(0, planes + 2, 4, body)


def clear_strip(ref):
    for xx in range(6):
        ref[xx, 0:8, :] = jnp.zeros((8, 128), F32)
        ref[xx, 56:64, :] = jnp.zeros((8, 128), F32)


def unpack_strip(z_lo, z_hi, src_t, bt_pad):
    iz = lax.axis_index("gz")
    low = flag(iz > 0)
    high = flag(iz < lax.axis_size("gz") - 1)

    def mirror(first, last):
        return pick(lambda r, c: (r // 16 == c // 16) & ((r % 16 < 8) == first) & (r % 16 + c % 16 == last))

    s_lo, s_hi = mirror(True, 15), mirror(True, 7)
    b_lo, b_hi = mirror(False, 23), mirror(False, 15)
    for xx in range(6):
        before = z_lo[xx] * low
        after = z_hi[xx] * high
        src_t[xx] = dot(before, s_lo) + dot(after, s_hi)
        bt_pad[xx, 8:56, :] = dot(before, b_lo) + dot(after, b_hi)


LEVEL0_SCRATCH = [
    vm(50, 64, 128),
    vm(6, 64, 128),
    vm(50, 64, 128),
    vm(6, 64, 128),
    vm(6, 48, 128),
    vm(48, 48, 128),
    vm(6, 48, 128),
    vm(6, 48, 128),
    vm(48, 48, 128),
    vm(2, 16, 32, 128),
]


def level0_down(
    src, beta, z_lo, z_hi, vb, tb, c_out, c_lo, c_hi, g_main, g_strip, sp, sp_t, bt_out,
    b_pad, bt_pad, va, ta, ghost, u, u_t, src_t, total, rows,
):
    for ref in (b_pad, va, vb):
        clear_edges(ref, 48, 48)
    for ref in (bt_pad, ta, tb):
        clear_strip(ref)
    b_pad[1:49, 8:56, :] = beta[...]
    unpack_strip(z_lo, z_hi, src_t, bt_pad)
    for xx in range(6):
        bt_out[xx] = bt_pad[xx, 8:56, :]
    level0_setup(
        b_pad, bt_pad, ghost, src, src_t, g_main, g_strip, sp, sp_t, total, va, ta, u, u_t, RECIPE[0][1]
    )
    for x in (0, 1, 46, 47):
        vb[x + 1, 8:56, :] = jnp.zeros((48, 128), F32)
    bufs = [(va, ta), (vb, tb)]
    for k in range(1, SMOOTH):
        (v, t), (w, s) = bufs
        retain, factor = RECIPE[k]
        level0_step(
            v, t, w, s, ghost, g_main, g_strip, sp, sp_t, u, u_t, 1 + k, 47 - k, retain, factor
        )
        bufs = [(w, s), (v, t)]
    v, t = bufs[0]
    assert v is vb and t is tb

    to_low = pick(lambda r, c: r // 2 == c)
    to_high = pick(lambda r, c: r // 2 + 64 == c)

    def restrict(x2):
        parts = []
        for half in range(2):
            x = 8 + 2 * x2 + half
            _, rest = block_rest(v, t, g_main, sp, x, 8)
            parts.append(rest * total[x, 8:40])
        rows[0, x2] = (parts[0] + parts[1]) * (0.5 / 8.0)
        rows[1, x2] = (b_pad[9 + 2 * x2, 16:48, :] + b_pad[10 + 2 * x2, 16:48, :]) * (1.0 / 8.0)

    loop(0, 16, 8, restrict)

    def compress(x2):
        res = rows[0, x2, pl.ds(0, 16, stride=2), :] + rows[0, x2, pl.ds(1, 16, stride=2), :]
        bet = rows[1, x2, pl.ds(0, 16, stride=2), :] + rows[1, x2, pl.ds(1, 16, stride=2), :]
        c_out[x2] = dot(res, to_low) + dot(bet, to_high)

    loop(0, 16, 8, compress)
    c_lo[...] = c_out[0:10]
    c_hi[...] = c_out[6:16]


def pack1_y(c, from_lo, from_hi, lo, hi):
    index = lax.axis_index("gx")
    low = flag(index > 0)
    high = flag(index < lax.axis_size("gx") - 1)
    for x in range(36):
        if x < 10:
            plane = from_lo[x] * low
        elif x < 26:
            plane = c[x - 10]
        else:
            plane = from_hi[x - 26] * high
        lo[x * 10 : x * 10 + 10, :] = plane[0:10]
        hi[x * 10 : x * 10 + 10, :] = plane[6:16]


def pack1_z(c, x_lo, x_hi, y_lo, y_hi, ext, lo, hi):
    ix = lax.axis_index("gx")
    iy = lax.axis_index("gy")
    x_low = flag(ix > 0)
    x_high = flag(ix < lax.axis_size("gx") - 1)
    y_low = flag(iy > 0)
    y_high = flag(iy < lax.axis_size("gy") - 1)
    ext[0:10, 10:26, :] = x_lo[...] * x_low
    ext[10:26, 10:26, :] = c[...]
    ext[26:36, 10:26, :] = x_hi[...] * x_high
    for x in range(36):
        ext[x, 0:10, :] = y_lo[x * 10 : x * 10 + 10, :] * y_low
        ext[x, 26:36, :] = y_hi[x * 10 : x * 10 + 10, :] * y_high
        ext[x, 36:40, :] = jnp.zeros((4, 128), F32)
    lane = lanes_of(40)

    def body(xx):
        acc_lo = jnp.zeros((40, 128), F32)
        acc_hi = jnp.zeros((40, 128), F32)
        for g in range(6):
            e = ext[g * 6 + xx]
            first = (lane >= g * 20) & (lane < g * 20 + 10)
            second = (lane >= g * 20 + 10) & (lane < g * 20 + 20)
            middle = roll(e, g * 20 - 54)
            acc_lo = jnp.where(first, roll(e, g * 20), acc_lo)
            acc_lo = jnp.where(second, middle, acc_lo)
            acc_hi = jnp.where(first, middle, acc_hi)
            acc_hi = jnp.where(second, roll(e, g * 20 + 20), acc_hi)
        lo[xx] = acc_lo
        hi[xx] = acc_hi

    loop(0, 6, 36, body)


def ring_weights(b_pad, src, g, sp, total, planes, rows, scale, edges=None):
    lane = lanes_of(rows)

    def body(x):
        here = b_pad[x + 1, 8 : 8 + rows, :]
        down = roll(here, 1)
        up = roll(here, -1)
        if edges is not None:
            down = jnp.where(lane == 0, 0.0, down)
            up = jnp.where(lane == 127, 0.0, up)
        faces, inverse, tot = weights(
            here,
            (
                b_pad[x, 8 : 8 + rows, :],
                b_pad[x + 2, 8 : 8 + rows, :],
                b_pad[x + 1, 7 : 7 + rows, :],
                b_pad[x + 1, 9 : 9 + rows, :],
                down,
                up,
            ),
        )
        if edges is not None:
            faces[4] = jnp.where(lane == 0, 0.0, faces[4])
            faces[5] = jnp.where(lane == 127, 0.0, faces[5])
        for i in range(6):
            g[i, x] = faces[i]
        sp[x] = scale * 2.0 * inverse if src is None else src[x] * (scale * 2.0 * inverse)
        if total is not None:
            total[x] = tot

    loop(0, planes, rows // 5, body)


def ring_rest(v, g, sp, x, rows):
    here = v[x + 1, 8 : 8 + rows, :]
    rest = sp[x] - here
    rest = rest + g[0, x] * v[x, 8 : 8 + rows, :] + g[1, x] * v[x + 2, 8 : 8 + rows, :]
    rest = rest + g[2, x] * v[x + 1, 7 : 7 + rows, :] + g[3, x] * v[x + 1, 9 : 9 + rows, :]
    rest = rest + g[4, x] * roll(here, 1) + g[5, x] * roll(here, -1)
    return here, rest


def ring_step(v, v_out, g, sp, u, planes, rows, retain, factor):
    def body(x):
        here, rest = ring_rest(v, g, sp, x, rows)
        new = factor * rest
        if retain is not None:
            new = retain * u[x] + new
        u[x] = new
        v_out[x + 1, 8 : 8 + rows, :] = here + new

    loop(0, planes, rows // 16, body)


def ring_zero_start(v, u, sp, planes, rows, factor):
    def body(x):
        u[x] = factor * sp[x]
        v[x + 1, 8 : 8 + rows, :] = u[x]

    loop(0, planes, rows // 8, body)


def ring_cheb(va, vb, g, sp, u, planes, rows, recipe, from_zero):
    begin = 0
    if from_zero:
        ring_zero_start(va, u, sp, planes, rows, recipe[0][1])
        begin = 1
    for k in range(begin, len(recipe)):
        retain, factor = recipe[k]
        ring_step(va, vb, g, sp, u, planes, rows, None if k == 0 else retain, factor)
        va, vb = vb, va
    return va


LEVEL1_SCRATCH = [
    vm(38, 56, 128),
    vm(38, 56, 128),
    vm(36, 40, 128),
    vm(36, 40, 128),
    vm(36, 40, 128),
    vm(8, 40, 128),
]


def level1_unpack(ext, z_lo, z_hi, source, b_pad, beta_out):
    iz = lax.axis_index("gz")
    low = flag(iz > 0)
    high = flag(iz < lax.axis_size("gz") - 1)
    lane = lanes_of(40)
    inner = lane < 64
    above = (lane >= 64) & (lane < 74)
    below = lane >= 118

    def unpack(xx):
        before = z_lo[xx] * low
        after = z_hi[xx] * high
        for k in range(6):
            x = k * 6 + xx
            e = ext[x]
            s = jnp.where(inner, e, 0.0)
            s = jnp.where(above, roll(after, 64 - k * 20), s)
            s = jnp.where(below, roll(before, 118 - k * 20), s)
            b = jnp.where(inner, roll(e, 64), 0.0)
            b = jnp.where(above, roll(after, 54 - k * 20), b)
            b = jnp.where(below, roll(before, 108 - k * 20), b)
            source[x] = s
            b_pad[x + 1, 8:48, :] = b
            beta_out[x] = b

    loop(0, 6, 36, unpack)


def level1_down(
    ext, z_lo, z_hi, vb, chunk, g, sp, beta_out,
    b_pad, va, u, src, total, rows,
):
    for ref in (b_pad, va, vb):
        clear_edges(ref, 36, 40)
    level1_unpack(ext, z_lo, z_hi, src, b_pad, beta_out)
    ring_weights(b_pad, src, g, sp, total, 36, 40, 4.0)
    v = ring_cheb(va, vb, g, sp, u, 36, 40, RECIPE, True)
    assert v is vb
    summed = []
    for x2 in range(8):
        parts = []
        for half in range(2):
            x = 10 + 2 * x2 + half
            _, rest = ring_rest(v, g, sp, x, 40)
            parts.append(rest * total[x])
        rows[x2] = (parts[0] + parts[1]) * (0.25 * 0.5 / 8.0)
        summed.append(rows[x2, pl.ds(10, 8, stride=2), :] + rows[x2, pl.ds(11, 8, stride=2), :])
    for half in range(2):
        acc = jnp.zeros((8, 128), F32)
        for quarter in range(4):
            weight = pick(lambda r, c: (r < 64) & ((r // 2 + 32 * quarter) == c))
            acc = acc + dot(summed[half * 4 + quarter], weight)
        chunk[half * 8 : half * 8 + 8, :] = acc


def sender(axis, step):
    count = lax.axis_size(axis)
    return lax.rem(lax.axis_index(axis) + count - step, count)


def singles(parts):
    return [part.at[i] for part in parts for i in range(2)] if len(parts) == 2 else parts


def gather_z(*refs):
    *parts, _, out = refs
    parts = singles(parts)
    lane = lanes_of(8)
    for half in range(2):
        for quarter in range(4):
            acc = jnp.zeros((8, 128), F32)
            for step, part in enumerate(parts):
                owner = sender("gz", step)
                moved = roll(part[half * 8 : half * 8 + 8, :], lax.rem(owner - quarter + 4, 4) * 32)
                acc = jnp.where(lane // 32 == owner, moved, acc)
            out[half * 4 + quarter] = acc


def gather_x(*refs):
    *parts, _, out = refs
    parts = singles(parts)
    for step, part in enumerate(parts):
        out[pl.ds(sender("gx", step) * 8, 8)] = part[...]


def stack_y(*refs):
    *parts, _, out = refs
    for step, part in enumerate(singles(parts)):
        out[step] = part[...]


def pair(mine, other, _, out):
    out[0] = mine[...]
    out[1] = other[...]


def gather_y(same, other, out):
    count = lax.axis_size("gy")
    index = lax.axis_index("gy")
    sibling = index + 1 - 2 * lax.rem(index, 2)
    for stack, first in ((same, index), (other, sibling)):
        for step in range(4):
            owner = lax.rem(first + count - 2 * step, count)
            row = pl.multiple_of(8 + owner * 8, 8)
            out[8:40, pl.ds(row, 8), :] = stack[step]


def clear_whole(ref):
    def clear(x):
        ref[x, 0:8, :] = jnp.zeros((8, 128), F32)
        ref[x, 72:80, :] = jnp.zeros((8, 128), F32)

    loop(0, 48, 2, clear)
    for x in [*range(8), *range(40, 48)]:
        ref[x, 8:72, :] = jnp.zeros((64, 128), F32)


def coarse_prepare(same, sibling, g, inv, total, g3, inv3, gw, invw, b2, b3, bw, rows):
    clear_whole(b2)
    clear_edges(b3, 16, 32)
    clear_edges(bw, 22, 24)
    gather_y(same, sibling, b2)
    ring_weights(b2.at[7:41], None, g, inv, total, 32, 64, 16.0, edges=True)
    half_z = pick(lambda r, c: r // 2 == c)

    def restrict(x2):
        rows[x2] = (b2[8 + 2 * x2, 8:72, :] + b2[9 + 2 * x2, 8:72, :]) * (1.0 / 8.0)

    loop(0, 16, 8, restrict)

    def compress(x2):
        bet = rows[x2, pl.ds(0, 32, stride=2), :] + rows[x2, pl.ds(1, 32, stride=2), :]
        b3[x2 + 1, 8:40, :] = dot(bet, half_z)

    loop(0, 16, 9, compress)
    ring_weights(b3, None, g3, inv3, None, 16, 32, 64.0)
    ix = lax.axis_index("gx")
    row = pl.multiple_of(lax.axis_index("gy") * 8, 8)

    def window(x):
        bw[x + 1, 8:32, :] = b2[ix * 8 + 1 + x, pl.ds(row, 24), :]

    loop(0, 22, 6, window)
    ring_weights(bw, None, gw, invw, None, 22, 24, 16.0, edges=True)


COARSE_SHAPES = [
    (6, 32, 64, 128),
    (32, 64, 128),
    (32, 64, 128),
    (6, 16, 32, 128),
    (16, 32, 128),
    (6, 22, 24, 128),
    (22, 24, 128),
]


def bottom(
    same, sibling, g, inv, total, g3, inv3, gw, invw, out,
    s2, va, vb, sp, u, v3a, v3b, sp3, u3, rows, wa, wb, spw, uw,
):
    for ref in (s2, va, vb):
        clear_whole(ref)
    gather_y(same, sibling, s2)

    def scale(x):
        sp[x] = s2[x + 8, 8:72, :] * inv[x]

    loop(0, 32, 8, scale)
    v = ring_cheb(va.at[7:41], vb.at[7:41], g, sp, u, 32, 64, RECIPE, True)
    iterate = vb if SMOOTH % 2 == 0 else va

    clear_edges(v3a, 16, 32)
    clear_edges(v3b, 16, 32)
    half_z = pick(lambda r, c: r // 2 == c)

    def restrict(x2):
        parts = []
        for half in range(2):
            x = 2 * x2 + half
            _, rest = ring_rest(v, g, sp, x, 64)
            parts.append(rest * total[x])
        rows[x2] = (parts[0] + parts[1]) * (0.0625 * 0.5 / 8.0)

    loop(0, 16, 16, restrict)

    def compress(x2):
        res = rows[x2, pl.ds(0, 32, stride=2), :] + rows[x2, pl.ds(1, 32, stride=2), :]
        sp3[x2] = dot(res, half_z) * inv3[x2]

    loop(0, 16, 9, compress)
    c3 = ring_cheb(v3a, v3b, g3, sp3, u3, 16, 32, BOTTOM_RECIPE, True)

    other = va if iterate is vb else vb
    double_z = pick(lambda r, c: c // 2 == r)

    def prolong(x3):
        wide = dot(c3[x3 + 1, 8:40, :], double_z)
        rows[x3, pl.ds(0, 32, stride=2), :] = wide
        rows[x3, pl.ds(1, 32, stride=2), :] = wide
        for half in range(2):
            x = 8 + 2 * x3 + half
            other[x, 8:72, :] = iterate[x, 8:72, :] + rows[x3]

    loop(0, 16, 18, prolong)
    ix = lax.axis_index("gx")
    iz = lax.axis_index("gz")
    clear_edges(wa, 22, 24)
    clear_edges(wb, 22, 24)
    row = pl.multiple_of(lax.axis_index("gy") * 8, 8)

    def window(x):
        plane = ix * 8 + 1 + x
        wa[x + 1, 8:32, :] = other[plane, pl.ds(row, 24), :]
        spw[x] = s2[plane, pl.ds(row, 24), :] * invw[x]

    loop(0, 22, 6, window)
    c2 = ring_cheb(wa, wb, gw, spw, uw, 22, 24, RECIPE, False)
    shift = (128 - iz * 32) % 128
    for x in range(18):
        out[x] = roll(c2[x + 3, 8:32, :], shift)


COARSE_SCRATCH = [
    vm(48, 80, 128),
    vm(18, 48, 128),
    vm(24, 40, 128),
    vm(16, 64, 128),
]
BOTTOM_SCRATCH = [
    vm(48, 80, 128),
    vm(48, 80, 128),
    vm(48, 80, 128),
    vm(32, 64, 128),
    vm(32, 64, 128),
    vm(18, 48, 128),
    vm(18, 48, 128),
    vm(16, 32, 128),
    vm(16, 32, 128),
    vm(16, 64, 128),
    vm(24, 40, 128),
    vm(24, 40, 128),
    vm(22, 24, 128),
    vm(22, 24, 128),
]


def level1_up(c2, g, sp, beta, iterate, out, va, vb, u, wide, rows):
    for ref in (va, vb):
        clear_edges(ref, 36, 40)
    spread = pick(lambda r, c: ((c < 74) & (c // 2 == r)) | ((c >= 118) & (c // 2 + 64 == r)))
    for x2 in range(18):
        rows[x2, 32:40, :] = jnp.zeros((8, 128), F32)

    def prolong(x2):
        wide[x2] = dot(c2[x2], spread)
        part = wide[x2, 3:21, :]
        rows[x2, pl.ds(0, 18, stride=2), :] = part
        rows[x2, pl.ds(1, 18, stride=2), :] = part
        for half in range(2):
            x = 2 * x2 + half
            va[x + 1, 8:48, :] = jnp.where(beta[x] > 0.0, iterate[x + 1, 8:48, :] + rows[x2], 0.0)

    loop(0, 18, 12, prolong)
    v = ring_cheb(va, vb, g, sp, u, 36, 40, RECIPE, False)
    out[...] = v[7:31, 14:38, :]


def level0_up(
    c1, beta, g_main, g_strip, sp, sp_t, beta_t, iterate, iterate_t, out,
    va, vb, ta, tb, ghost, u, u_t, rows,
):
    for ref in (va, vb):
        clear_edges(ref, 48, 48)
    for ref in (ta, tb):
        clear_strip(ref)
    spread = pick(lambda r, c: c // 2 == r)

    def prolong(x1):
        wide = dot(c1[x1], spread)
        rows[x1, pl.ds(0, 24, stride=2), :] = wide
        rows[x1, pl.ds(1, 24, stride=2), :] = wide
        for half in range(2):
            x = 2 * x1 + half
            va[x + 1, 8:56, :] = jnp.where(beta[x] > 0.0, iterate[x + 1, 8:56, :] + rows[x1], 0.0)

    loop(0, 24, 12, prolong)

    def prolong_strip(m):
        acc = jnp.zeros((24, 128), F32)
        for k in range(8):
            to = pick(
                lambda r, c: (c // 16 == k)
                & (
                    ((c % 16 < 8) & (r == 64 + (7 - c % 16) // 2))
                    | ((c % 16 >= 8) & (r == 124 + (15 - c % 16) // 2))
                )
            )
            acc = acc + dot(c1[k * 3 + m], to)
        rows[m, pl.ds(0, 24, stride=2), :] = acc
        rows[m, pl.ds(1, 24, stride=2), :] = acc
        for half in range(2):
            xx = 2 * m + half
            ta[xx, 8:56, :] = jnp.where(beta_t[xx] > 0.0, iterate_t[xx, 8:56, :] + rows[m], 0.0)

    loop(0, 3, 36, prolong_strip)
    for x in [*range(6), *range(42, 48)]:
        vb[x + 1, 8:56, :] = jnp.zeros((48, 128), F32)
    bufs = [(va, ta), (vb, tb)]
    for k in range(SMOOTH):
        (v, t), (w, s) = bufs
        retain, factor = RECIPE[k]
        if k == 0:
            retain = None
        if k < SMOOTH - 1:
            low, high = (4, 44) if k < 2 else (6, 42)
            level0_step(
                v, t, w, s, ghost, g_main, g_strip, sp, sp_t, u, u_t, low, high, retain, factor
            )
        else:

            def last(x):
                here, rest = block_rest(v, t, g_main, sp, x, 8)
                out[x - 8] = here + retain * u[x, 8:40] + factor * rest

            loop(8, 40, 4, last)
        bufs = [(w, s), (v, t)]


def ring(value, axis, step):
    count = lax.axis_size(axis)
    return lax.ppermute(value, axis, [(i, (i + step) % count) for i in range(count)])


def trade(lo, hi, axis):
    return ring(hi, axis, 1), ring(lo, axis, -1)


def gather(kernel, parts, after, *shape):
    return call(kernel, sds(*shape), name=kernel.__name__, last_unread=len(parts) + 1)(*parts, after)


def around(value, axis):
    return [value] + [ring(value, axis, step) for step in range(1, lax.axis_size(axis))]


def chips(value):
    return [value] + [ring(value, "gy", 2 * step) for step in (1, 2, 3)]


def across(value):
    count = lax.axis_size("gy")
    return lax.ppermute(value, "gy", [(i, i + 1 - 2 * (i % 2)) for i in range(count)])


def per_device(source, beta):
    lo = jnp.stack([source[0:8], beta[0:8]])
    hi = jnp.stack([source[24:32], beta[24:32]])
    lo, hi, source, beta = lax.optimization_barrier((lo, hi, source, beta))
    x_lo, x_hi = trade(lo, hi, "gx")
    beta2 = call(coarse_beta, sds(16, 128), [vm(32, 128)], name="coarse_beta")(beta)
    beta2_pair = gather(pair, [beta2, ring(beta2, "gz", 1)], lo, 2, 16, 128)
    x_lo, x_hi, beta2_pair = lax.optimization_barrier((x_lo, x_hi, beta2_pair))
    slab = sds(2, 48, 8, 128)
    mid = sds(48, 32, 128)
    lo, hi, s_mid, b_mid = call(pack_y, (slab, slab, mid, mid), name="pack_y", mib=4)(
        source, beta, x_lo, x_hi
    )
    y_lo, y_hi = trade(lo, hi, "gy")
    beta2_block = gather(gather_z, [beta2_pair, ring(beta2_pair, "gz", 2)], lo, 8, 8, 128)
    y_lo, y_hi, beta2_block = lax.optimization_barrier((y_lo, y_hi, beta2_block))
    whole = sds(48, 48, 128)
    strip = sds(6, 48, 128)
    src_ext, beta_ext, lo, hi = call(
        pack_z, (whole, whole, strip, strip), name="pack_z", mib=4
    )(s_mid, b_mid, y_lo, y_hi)
    z_lo, z_hi = trade(lo, hi, "gz")
    beta2_pair = gather(pair, [beta2_block, ring(beta2_block, "gx", 1)], lo, 2, 8, 8, 128)
    z_lo, z_hi, beta2_pair = lax.optimization_barrier((z_lo, z_hi, beta2_pair))
    iter0, iter0_t, c, lo, hi, *ready = call(
        level0_down,
        (
            sds(50, 64, 128),
            sds(6, 64, 128),
            sds(16, 16, 128),
            sds(10, 16, 128),
            sds(10, 16, 128),
            sds(7, 48, 48, 128),
            sds(6, 6, 48, 128),
            whole,
            strip,
            strip,
        ),
        LEVEL0_SCRATCH,
        name="level0_down",
        mib=16,
    )(src_ext, beta_ext, z_lo, z_hi)
    x_lo, x_hi = trade(lo, hi, "gx")
    beta2_pair, _ = lax.optimization_barrier((beta2_pair, lo))
    beta2_far = ring(beta2_pair, "gx", 2)
    lo, hi = call(pack1_y, (sds(360, 128), sds(360, 128)), name="pack1_y")(c, x_lo, x_hi)
    y_lo, y_hi = trade(lo, hi, "gy")
    beta2_slab = gather(gather_x, [beta2_pair, beta2_far], lo, 32, 8, 128)
    y_lo, y_hi, beta2_slab = lax.optimization_barrier((y_lo, y_hi, beta2_slab))
    ext, lo, hi = call(
        pack1_z, (sds(36, 40, 128), sds(6, 40, 128), sds(6, 40, 128)), name="pack1_z"
    )(c, x_lo, x_hi, y_lo, y_hi)
    z1_lo, z1_hi = trade(lo, hi, "gz")
    beta2_slab, _ = lax.optimization_barrier((beta2_slab, lo))
    beta2_pair = gather(pair, [beta2_slab, ring(beta2_slab, "gy", 2)], lo, 2, 32, 8, 128)
    z1_lo, z1_hi, beta2_pair = lax.optimization_barrier((z1_lo, z1_hi, beta2_pair))
    level1 = sds(36, 40, 128)
    iter1, chunk, g1, sp1, beta1 = call(
        level1_down,
        (sds(38, 56, 128), sds(16, 128), sds(6, 36, 40, 128), level1, level1),
        LEVEL1_SCRATCH,
        name="level1_down",
        mib=8,
    )(ext, z1_lo, z1_hi)
    parts = around(chunk, "gz")
    beta2_pair, _ = lax.optimization_barrier((beta2_pair, chunk))
    beta2_far = ring(beta2_pair, "gy", 4)
    parts = around(gather(gather_z, parts, chunk, 8, 8, 128), "gx")
    beta2_stack = gather(stack_y, [beta2_pair, beta2_far], chunk, 4, 32, 8, 128)
    *parts, beta2_stack = lax.optimization_barrier((*parts, beta2_stack))
    slab = gather(gather_x, parts, chunk, 32, 8, 128)
    parts = chips(slab)
    beta2_sent, _ = lax.optimization_barrier((beta2_stack, slab))
    *parts, beta2_other = lax.optimization_barrier((*parts, across(beta2_sent)))
    stack = gather(stack_y, parts, slab, 4, 32, 8, 128)
    stack_other = across(stack)
    coarse = call(
        coarse_prepare,
        tuple(sds(*shape) for shape in COARSE_SHAPES),
        COARSE_SCRATCH,
        name="coarse_prepare",
        mib=8,
    )(beta2_stack, beta2_other)
    c2 = call(bottom, sds(18, 24, 128), BOTTOM_SCRATCH, name="bottom", mib=18)(
        stack, stack_other, *coarse
    )
    c1 = call(
        level1_up,
        sds(24, 24, 128),
        [vm(38, 56, 128), vm(38, 56, 128), vm(36, 40, 128), vm(18, 24, 128), vm(18, 40, 128)],
        name="level1_up",
        mib=8,
    )(c2, g1, sp1, beta1, iter1)
    return call(
        level0_up,
        sds(32, 32, 128),
        [vm(50, 64, 128), vm(50, 64, 128), vm(6, 64, 128), vm(6, 64, 128), vm(6, 48, 128)]
        + [vm(48, 48, 128), vm(6, 48, 128), vm(24, 48, 128)],
        name="level0_up",
        mib=14,
    )(c1, beta_ext, *ready, iter0, iter0_t)


def solution(mesh):
    placed = (P(*AXES), P(*AXES))
    return jax.shard_map(
        per_device, mesh=mesh, in_specs=placed, out_specs=P(*AXES), check_vma=False
    )
```

```python
import jax
import jax.numpy as jnp
from jax import lax
from jax.experimental import pallas as pl
from jax.experimental.pallas import tpu as pltpu
from jax.sharding import PartitionSpec as P

SMOOTH = 4
BOTTOM = 12
LOW_EIG = 0.3
HIGH_EIG = 2.0
BOTTOM_LOW = 0.02

AXES = ("gx", "gy", "gz")
F32 = jnp.float32
MIB = 1024 * 1024


def cheb_plan(degree, lowest, highest):
    centre = 0.5 * (highest + lowest)
    radius = 0.5 * (highest - lowest)
    ratio_s = centre / radius
    rho_old = 1.0 / ratio_s
    recipe = [(0.0, 1.0 / centre)]
    for position in range(1, degree):
        rho_new = 1.0 / (2.0 * ratio_s - rho_old)
        recipe.append((rho_new * rho_old, 2.0 * rho_new / radius))
        rho_old = rho_new
    return recipe


RECIPE = cheb_plan(SMOOTH, LOW_EIG, HIGH_EIG)
BOTTOM_RECIPE = cheb_plan(BOTTOM, BOTTOM_LOW, HIGH_EIG)


def sds(*shape):
    return jax.ShapeDtypeStruct(shape, F32)


def vm(*shape):
    return pltpu.VMEM(shape, F32)


def call(body, outs, scratch=(), name=None, mib=2, last_unread=None):
    specs = {}
    if last_unread:
        whole = pl.BlockSpec(memory_space=pltpu.VMEM)
        specs["in_specs"] = [whole] * (last_unread - 1) + [pl.BlockSpec(memory_space=pl.ANY)]
    return pl.pallas_call(
        body,
        out_shape=outs,
        **specs,
        scratch_shapes=list(scratch),
        compiler_params=pltpu.CompilerParams(vmem_limit_bytes=mib * MIB),
        name=name,
    )


def loop(low, high, vectors, body):
    count = high - low
    most = max(1, min(count, 72 // vectors))
    width = max([w for w in range(1, most + 1) if count % w == 0])
    if width * 2 < most:
        width = most
    rounds = count // width

    def chunk(i, carry):
        for k in range(width):
            body(low + i * width + k)
        return carry

    if rounds > 1:
        lax.fori_loop(0, rounds, chunk, 0)
    else:
        chunk(0, 0)
    for x in range(low + rounds * width, high):
        body(x)


def lanes_of(rows):
    return lax.broadcasted_iota(jnp.int32, (rows, 128), 1)


def roll(value, shift):
    if isinstance(shift, int):
        shift = shift % 128
        if shift == 0:
            return value
    return pltpu.roll(value, shift, 1)


def flag(condition):
    return jnp.where(condition, 1.0, 0.0).astype(F32)


def dot(left, right):
    return lax.dot_general(
        left,
        right,
        (((1,), (0,)), ((), ())),
        precision=lax.Precision.HIGHEST,
        preferred_element_type=F32,
    )


def pick(match):
    row = lax.broadcasted_iota(jnp.int32, (128, 128), 0)
    col = lax.broadcasted_iota(jnp.int32, (128, 128), 1)
    return jnp.where(match(row, col), 1.0, 0.0).astype(F32)


def coarse_beta(beta, out, rows):
    total = []
    for x in range(8):
        s = beta[4 * x] + beta[4 * x + 1] + beta[4 * x + 2] + beta[4 * x + 3]
        rows[...] = s
        t = rows[pl.ds(0, 8, stride=4), :] + rows[pl.ds(1, 8, stride=4), :]
        t = t + rows[pl.ds(2, 8, stride=4), :] + rows[pl.ds(3, 8, stride=4), :]
        total.append(t * (1.0 / 64.0))
    for half in range(2):
        acc = jnp.zeros((8, 128), F32)
        for quarter in range(4):
            weight = pick(lambda r, c: (r // 4 + 32 * quarter) == c)
            acc = acc + dot(total[half * 4 + quarter], weight)
        out[half * 8 : half * 8 + 8, :] = acc


def pack_y(src, beta, from_lo, from_hi, lo, hi, s_mid, b_mid):
    index = lax.axis_index("gx")
    low = flag(index > 0)
    high = flag(index < lax.axis_size("gx") - 1)
    for field, (ref, mid) in enumerate(((src, s_mid), (beta, b_mid))):
        mid[0:8] = from_lo[field] * low
        mid[8:40] = ref[...]
        mid[40:48] = from_hi[field] * high
        lo[field] = mid[:, 0:8, :]
        hi[field] = mid[:, 24:32, :]


def pack_z(s_mid, b_mid, y_lo, y_hi, s_out, b_out, lo, hi):
    iy = lax.axis_index("gy")
    y_low = flag(iy > 0)
    y_high = flag(iy < lax.axis_size("gy") - 1)
    for field, (mid, out) in enumerate(((s_mid, s_out), (b_mid, b_out))):
        out[:, 8:40, :] = mid[...]
        out[:, 0:8, :] = y_lo[field] * y_low
        out[:, 40:48, :] = y_hi[field] * y_high
    lane = lanes_of(48)

    def body(xx):
        acc_lo = jnp.zeros((48, 128), F32)
        acc_hi = jnp.zeros((48, 128), F32)
        for g in range(8):
            s = s_out[g * 6 + xx]
            b = b_out[g * 6 + xx]
            first = (lane >= g * 16) & (lane < g * 16 + 8)
            second = (lane >= g * 16 + 8) & (lane < g * 16 + 16)
            acc_lo = jnp.where(first, roll(s, g * 16), acc_lo)
            acc_lo = jnp.where(second, roll(b, g * 16 + 8), acc_lo)
            acc_hi = jnp.where(first, roll(s, g * 16 + 8), acc_hi)
            acc_hi = jnp.where(second, roll(b, g * 16 + 16), acc_hi)
        lo[xx] = acc_lo
        hi[xx] = acc_hi

    loop(0, 6, 36, body)


def strip_ghosts(values, ghost):
    lane = lanes_of(48)

    def body(xx):
        acc = jnp.zeros((48, 128), F32)
        for g in range(8):
            acc = jnp.where(lane // 16 == g, roll(values[g * 6 + xx + 1, 8:56, :], g * 16 + 8), acc)
        ghost[xx] = acc

    loop(0, 6, 36, body)


def strip_sides(strip, xx):
    after = strip[xx + 1, 8:56, :] if xx < 5 else roll(strip[0, 8:56, :], -16)
    before = strip[xx - 1, 8:56, :] if xx > 0 else roll(strip[5, 8:56, :], 16)
    return before, after


def strip_z(strip, ghost, xx, lane):
    here = strip[xx, 8:56, :]
    up = jnp.where(lane % 16 == 8, ghost[xx], roll(here, 1))
    down = jnp.where(lane % 16 == 7, ghost[xx], roll(here, -1))
    return down, up


def block_edge(strip, x, first=8, count=48):
    g = x // 6
    return roll(strip[x - g * 6, first : first + count, :], 120 - g * 16)


def weights(here, sides):
    sums = [here + side for side in sides]
    total = sums[0] + sums[1] + sums[2] + sums[3] + sums[4] + sums[5]
    inverse = jnp.where(here > 0.0, 1.0 / total, 0.0)
    return [s * inverse for s in sums], inverse, total


def level0_setup(b_pad, bt_pad, ghost, src, src_t, g_main, g_strip, sp, sp_t, total, v, t, u, u_t, first):
    strip_ghosts(b_pad, ghost)
    lane = lanes_of(48)

    def body(x):
        here = b_pad[x + 1, 8:56, :]
        edge = block_edge(bt_pad, x)
        down = jnp.where(lane == 0, edge, roll(here, 1))
        up = jnp.where(lane == 127, edge, roll(here, -1))
        faces, inverse, tot = weights(
            here,
            (
                b_pad[x, 8:56, :],
                b_pad[x + 2, 8:56, :],
                b_pad[x + 1, 7:55, :],
                b_pad[x + 1, 9:57, :],
                down,
                up,
            ),
        )
        for i in range(4):
            g_main[i, x] = faces[i]
        g_main[4, x] = jnp.where(lane == 0, 0.0, faces[4])
        g_main[5, x] = jnp.where(lane == 127, 0.0, faces[5])
        g_main[6, x] = jnp.where(lane == 0, faces[4], jnp.where(lane == 127, faces[5], 0.0))
        scaled = src[x] * (2.0 * inverse)
        sp[x] = scaled
        u[x] = first * scaled
        v[x + 1, 8:56, :] = first * scaled
        total[x] = tot

    loop(0, 48, 6, body)
    for xx in range(6):
        before, after = strip_sides(bt_pad, xx)
        down, up = strip_z(bt_pad, ghost, xx, lane)
        faces, inverse, _ = weights(
            bt_pad[xx, 8:56, :],
            (before, after, bt_pad[xx, 7:55, :], bt_pad[xx, 9:57, :], down, up),
        )
        for i in range(6):
            g_strip[i, xx] = faces[i]
        scaled = src_t[xx] * (2.0 * inverse)
        sp_t[xx] = scaled
        u_t[xx] = first * scaled
        t[xx, 8:56, :] = first * scaled


def block_rest(v, t, g_main, sp, x, skip=0):
    count = 48 - 2 * skip
    first = 8 + skip
    keep = slice(skip, 48 - skip)
    here = v[x + 1, first : first + count, :]
    rest = sp[x, keep] - here
    rest = rest + g_main[0, x, keep] * v[x, first : first + count, :]
    rest = rest + g_main[1, x, keep] * v[x + 2, first : first + count, :]
    rest = rest + g_main[2, x, keep] * v[x + 1, first - 1 : first - 1 + count, :]
    rest = rest + g_main[3, x, keep] * v[x + 1, first + 1 : first + 1 + count, :]
    rest = rest + g_main[4, x, keep] * roll(here, 1) + g_main[5, x, keep] * roll(here, -1)
    rest = rest + g_main[6, x, keep] * block_edge(t, x, first, count)
    return here, rest


def level0_step(v, t, v_out, t_out, ghost, g_main, g_strip, sp, sp_t, u, u_t, low, high, retain, factor):
    strip_ghosts(v, ghost)
    lane = lanes_of(48)

    def body(x):
        here, rest = block_rest(v, t, g_main, sp, x)
        new = factor * rest
        if retain is not None:
            new = retain * u[x] + new
        u[x] = new
        v_out[x + 1, 8:56, :] = here + new

    loop(low, high, 4, body)
    for xx in range(6):
        here = t[xx, 8:56, :]
        before, after = strip_sides(t, xx)
        down, up = strip_z(t, ghost, xx, lane)
        rest = sp_t[xx] - here
        rest = rest + g_strip[0, xx] * before + g_strip[1, xx] * after
        rest = rest + g_strip[2, xx] * t[xx, 7:55, :] + g_strip[3, xx] * t[xx, 9:57, :]
        rest = rest + g_strip[4, xx] * down + g_strip[5, xx] * up
        new = factor * rest
        if retain is not None:
            new = retain * u_t[xx] + new
        u_t[xx] = new
        t_out[xx, 8:56, :] = here + new


def clear_edges(ref, planes, rows):
    width = ref.shape[1]
    ref[0] = jnp.zeros((width, 128), F32)
    ref[planes + 1] = jnp.zeros((width, 128), F32)

    def body(x):
        ref[x, 0:8, :] = jnp.zeros((8, 128), F32)
        ref[x, 8 + rows : width, :] = jnp.zeros((width - 8 - rows, 128), F32)

    loop(0, planes + 2, 4, body)


def clear_strip(ref):
    for xx in range(6):
        ref[xx, 0:8, :] = jnp.zeros((8, 128), F32)
        ref[xx, 56:64, :] = jnp.zeros((8, 128), F32)


def unpack_strip(z_lo, z_hi, src_t, bt_pad):
    iz = lax.axis_index("gz")
    low = flag(iz > 0)
    high = flag(iz < lax.axis_size("gz") - 1)

    def mirror(first, last):
        return pick(lambda r, c: (r // 16 == c // 16) & ((r % 16 < 8) == first) & (r % 16 + c % 16 == last))

    s_lo, s_hi = mirror(True, 15), mirror(True, 7)
    b_lo, b_hi = mirror(False, 23), mirror(False, 15)
    for xx in range(6):
        before = z_lo[xx] * low
        after = z_hi[xx] * high
        src_t[xx] = dot(before, s_lo) + dot(after, s_hi)
        bt_pad[xx, 8:56, :] = dot(before, b_lo) + dot(after, b_hi)


LEVEL0_SCRATCH = [
    vm(50, 64, 128),
    vm(6, 64, 128),
    vm(50, 64, 128),
    vm(6, 64, 128),
    vm(6, 48, 128),
    vm(48, 48, 128),
    vm(6, 48, 128),
    vm(6, 48, 128),
    vm(48, 48, 128),
    vm(2, 16, 32, 128),
]


def level0_down(
    src, beta, z_lo, z_hi, vb, tb, c_out, c_lo, c_hi, g_main, g_strip, sp, sp_t, bt_out,
    b_pad, bt_pad, va, ta, ghost, u, u_t, src_t, total, rows,
):
    for ref in (b_pad, va, vb):
        clear_edges(ref, 48, 48)
    for ref in (bt_pad, ta, tb):
        clear_strip(ref)
    b_pad[1:49, 8:56, :] = beta[...]
    unpack_strip(z_lo, z_hi, src_t, bt_pad)
    for xx in range(6):
        bt_out[xx] = bt_pad[xx, 8:56, :]
    level0_setup(
        b_pad, bt_pad, ghost, src, src_t, g_main, g_strip, sp, sp_t, total, va, ta, u, u_t, RECIPE[0][1]
    )
    for x in (0, 1, 46, 47):
        vb[x + 1, 8:56, :] = jnp.zeros((48, 128), F32)
    bufs = [(va, ta), (vb, tb)]
    for k in range(1, SMOOTH):
        (v, t), (w, s) = bufs
        retain, factor = RECIPE[k]
        level0_step(
            v, t, w, s, ghost, g_main, g_strip, sp, sp_t, u, u_t, 1 + k, 47 - k, retain, factor
        )
        bufs = [(w, s), (v, t)]
    v, t = bufs[0]
    assert v is vb and t is tb

    to_low = pick(lambda r, c: r // 2 == c)
    to_high = pick(lambda r, c: r // 2 + 64 == c)

    def restrict(x2):
        parts = []
        for half in range(2):
            x = 8 + 2 * x2 + half
            _, rest = block_rest(v, t, g_main, sp, x, 8)
            parts.append(rest * total[x, 8:40])
        rows[0, x2] = (parts[0] + parts[1]) * (0.5 / 8.0)
        rows[1, x2] = (b_pad[9 + 2 * x2, 16:48, :] + b_pad[10 + 2 * x2, 16:48, :]) * (1.0 / 8.0)

    loop(0, 16, 8, restrict)

    def compress(x2):
        res = rows[0, x2, pl.ds(0, 16, stride=2), :] + rows[0, x2, pl.ds(1, 16, stride=2), :]
        bet = rows[1, x2, pl.ds(0, 16, stride=2), :] + rows[1, x2, pl.ds(1, 16, stride=2), :]
        c_out[x2] = dot(res, to_low) + dot(bet, to_high)

    loop(0, 16, 8, compress)
    c_lo[...] = c_out[0:10]
    c_hi[...] = c_out[6:16]


def pack1_y(c, from_lo, from_hi, lo, hi):
    index = lax.axis_index("gx")
    low = flag(index > 0)
    high = flag(index < lax.axis_size("gx") - 1)
    for x in range(36):
        if x < 10:
            plane = from_lo[x] * low
        elif x < 26:
            plane = c[x - 10]
        else:
            plane = from_hi[x - 26] * high
        lo[x * 10 : x * 10 + 10, :] = plane[0:10]
        hi[x * 10 : x * 10 + 10, :] = plane[6:16]


def pack1_z(c, x_lo, x_hi, y_lo, y_hi, ext, lo, hi):
    ix = lax.axis_index("gx")
    iy = lax.axis_index("gy")
    x_low = flag(ix > 0)
    x_high = flag(ix < lax.axis_size("gx") - 1)
    y_low = flag(iy > 0)
    y_high = flag(iy < lax.axis_size("gy") - 1)
    ext[0:10, 10:26, :] = x_lo[...] * x_low
    ext[10:26, 10:26, :] = c[...]
    ext[26:36, 10:26, :] = x_hi[...] * x_high
    for x in range(36):
        ext[x, 0:10, :] = y_lo[x * 10 : x * 10 + 10, :] * y_low
        ext[x, 26:36, :] = y_hi[x * 10 : x * 10 + 10, :] * y_high
        ext[x, 36:40, :] = jnp.zeros((4, 128), F32)
    lane = lanes_of(40)

    def body(xx):
        acc_lo = jnp.zeros((40, 128), F32)
        acc_hi = jnp.zeros((40, 128), F32)
        for g in range(6):
            e = ext[g * 6 + xx]
            first = (lane >= g * 20) & (lane < g * 20 + 10)
            second = (lane >= g * 20 + 10) & (lane < g * 20 + 20)
            middle = roll(e, g * 20 - 54)
            acc_lo = jnp.where(first, roll(e, g * 20), acc_lo)
            acc_lo = jnp.where(second, middle, acc_lo)
            acc_hi = jnp.where(first, middle, acc_hi)
            acc_hi = jnp.where(second, roll(e, g * 20 + 20), acc_hi)
        lo[xx] = acc_lo
        hi[xx] = acc_hi

    loop(0, 6, 36, body)


def ring_weights(b_pad, src, g, sp, total, planes, rows, scale, edges=None):
    lane = lanes_of(rows)

    def body(x):
        here = b_pad[x + 1, 8 : 8 + rows, :]
        down = roll(here, 1)
        up = roll(here, -1)
        if edges is not None:
            down = jnp.where(lane == 0, 0.0, down)
            up = jnp.where(lane == 127, 0.0, up)
        faces, inverse, tot = weights(
            here,
            (
                b_pad[x, 8 : 8 + rows, :],
                b_pad[x + 2, 8 : 8 + rows, :],
                b_pad[x + 1, 7 : 7 + rows, :],
                b_pad[x + 1, 9 : 9 + rows, :],
                down,
                up,
            ),
        )
        if edges is not None:
            faces[4] = jnp.where(lane == 0, 0.0, faces[4])
            faces[5] = jnp.where(lane == 127, 0.0, faces[5])
        for i in range(6):
            g[i, x] = faces[i]
        sp[x] = scale * 2.0 * inverse if src is None else src[x] * (scale * 2.0 * inverse)
        if total is not None:
            total[x] = tot

    loop(0, planes, rows // 5, body)


def ring_rest(v, g, sp, x, rows):
    here = v[x + 1, 8 : 8 + rows, :]
    rest = sp[x] - here
    rest = rest + g[0, x] * v[x, 8 : 8 + rows, :] + g[1, x] * v[x + 2, 8 : 8 + rows, :]
    rest = rest + g[2, x] * v[x + 1, 7 : 7 + rows, :] + g[3, x] * v[x + 1, 9 : 9 + rows, :]
    rest = rest + g[4, x] * roll(here, 1) + g[5, x] * roll(here, -1)
    return here, rest


def ring_step(v, v_out, g, sp, u, low, high, rows, retain, factor):
    def body(x):
        here, rest = ring_rest(v, g, sp, x, rows)
        new = factor * rest
        if retain is not None:
            new = retain * u[x] + new
        u[x] = new
        v_out[x + 1, 8 : 8 + rows, :] = here + new

    loop(low, high, rows // 16, body)


def ring_zero_start(v, u, sp, planes, rows, factor):
    def body(x):
        u[x] = factor * sp[x]
        v[x + 1, 8 : 8 + rows, :] = u[x]

    loop(0, planes, rows // 8, body)


def ring_cheb(va, vb, g, sp, u, planes, rows, recipe, from_zero, trim=None):
    begin = 0
    if from_zero:
        ring_zero_start(va, u, sp, planes, rows, recipe[0][1])
        begin = 1
    for k in range(begin, len(recipe)):
        retain, factor = recipe[k]
        skip = 0 if trim is None else trim + k
        ring_step(
            va, vb, g, sp, u, skip, planes - skip, rows, None if k == 0 else retain, factor
        )
        va, vb = vb, va
    return va


LEVEL1_SCRATCH = [
    vm(38, 56, 128),
    vm(38, 56, 128),
    vm(36, 40, 128),
    vm(36, 40, 128),
    vm(36, 40, 128),
    vm(8, 40, 128),
]


def level1_unpack(ext, z_lo, z_hi, source, b_pad, beta_out):
    iz = lax.axis_index("gz")
    low = flag(iz > 0)
    high = flag(iz < lax.axis_size("gz") - 1)
    lane = lanes_of(40)
    inner = lane < 64
    above = (lane >= 64) & (lane < 74)
    below = lane >= 118

    def unpack(xx):
        before = z_lo[xx] * low
        after = z_hi[xx] * high
        for k in range(6):
            x = k * 6 + xx
            e = ext[x]
            s = jnp.where(inner, e, 0.0)
            s = jnp.where(above, roll(after, 64 - k * 20), s)
            s = jnp.where(below, roll(before, 118 - k * 20), s)
            b = jnp.where(inner, roll(e, 64), 0.0)
            b = jnp.where(above, roll(after, 54 - k * 20), b)
            b = jnp.where(below, roll(before, 108 - k * 20), b)
            source[x] = s
            b_pad[x + 1, 8:48, :] = b
            beta_out[x] = b

    loop(0, 6, 36, unpack)


def level1_down(
    ext, z_lo, z_hi, vb, chunk, g, sp, beta_out,
    b_pad, va, u, src, total, rows,
):
    for ref in (b_pad, va, vb):
        clear_edges(ref, 36, 40)
    level1_unpack(ext, z_lo, z_hi, src, b_pad, beta_out)
    ring_weights(b_pad, src, g, sp, total, 36, 40, 4.0)
    for x in (0, 1, 34, 35):
        vb[x + 1, 8:48, :] = jnp.zeros((40, 128), F32)
    v = ring_cheb(va, vb, g, sp, u, 36, 40, RECIPE, True, trim=1)
    assert v is vb
    summed = []
    for x2 in range(8):
        parts = []
        for half in range(2):
            x = 10 + 2 * x2 + half
            _, rest = ring_rest(v, g, sp, x, 40)
            parts.append(rest * total[x])
        rows[x2] = (parts[0] + parts[1]) * (0.25 * 0.5 / 8.0)
        summed.append(rows[x2, pl.ds(10, 8, stride=2), :] + rows[x2, pl.ds(11, 8, stride=2), :])
    for half in range(2):
        acc = jnp.zeros((8, 128), F32)
        for quarter in range(4):
            weight = pick(lambda r, c: (r < 64) & ((r // 2 + 32 * quarter) == c))
            acc = acc + dot(summed[half * 4 + quarter], weight)
        chunk[half * 8 : half * 8 + 8, :] = acc


def sender(axis, step):
    count = lax.axis_size(axis)
    return lax.rem(lax.axis_index(axis) + count - step, count)


def singles(parts):
    return [part.at[i] for part in parts for i in range(2)] if len(parts) == 2 else parts


def gather_z(*refs):
    *parts, _, out = refs
    parts = singles(parts)
    lane = lanes_of(8)
    for half in range(2):
        for quarter in range(4):
            acc = jnp.zeros((8, 128), F32)
            for step, part in enumerate(parts):
                owner = sender("gz", step)
                moved = roll(part[half * 8 : half * 8 + 8, :], lax.rem(owner - quarter + 4, 4) * 32)
                acc = jnp.where(lane // 32 == owner, moved, acc)
            out[half * 4 + quarter] = acc


def gather_x(*refs):
    *parts, _, out = refs
    parts = singles(parts)
    for step, part in enumerate(parts):
        out[pl.ds(sender("gx", step) * 8, 8)] = part[...]


def stack_y(*refs):
    *parts, _, out = refs
    for step, part in enumerate(singles(parts)):
        out[step] = part[...]


def pair(mine, other, _, out):
    out[0] = mine[...]
    out[1] = other[...]


def gather_y(same, other, out):
    count = lax.axis_size("gy")
    index = lax.axis_index("gy")
    sibling = index + 1 - 2 * lax.rem(index, 2)
    for stack, first in ((same, index), (other, sibling)):
        for step in range(4):
            owner = lax.rem(first + count - 2 * step, count)
            row = pl.multiple_of(8 + owner * 8, 8)
            out[8:40, pl.ds(row, 8), :] = stack[step]


def clear_whole(ref):
    def clear(x):
        ref[x, 0:8, :] = jnp.zeros((8, 128), F32)
        ref[x, 72:80, :] = jnp.zeros((8, 128), F32)

    loop(0, 48, 2, clear)
    for x in [*range(8), *range(40, 48)]:
        ref[x, 8:72, :] = jnp.zeros((64, 128), F32)


def coarse_prepare(same, sibling, g, inv, total, g3, inv3, gw, invw, b2, b3, bw, rows):
    clear_whole(b2)
    clear_edges(b3, 16, 32)
    clear_edges(bw, 22, 24)
    gather_y(same, sibling, b2)
    ring_weights(b2.at[7:41], None, g, inv, total, 32, 64, 16.0, edges=True)
    half_z = pick(lambda r, c: r // 2 == c)

    def restrict(x2):
        rows[x2] = (b2[8 + 2 * x2, 8:72, :] + b2[9 + 2 * x2, 8:72, :]) * (1.0 / 8.0)

    loop(0, 16, 8, restrict)

    def compress(x2):
        bet = rows[x2, pl.ds(0, 32, stride=2), :] + rows[x2, pl.ds(1, 32, stride=2), :]
        b3[x2 + 1, 8:40, :] = dot(bet, half_z)

    loop(0, 16, 9, compress)
    ring_weights(b3, None, g3, inv3, None, 16, 32, 64.0)
    ix = lax.axis_index("gx")
    row = pl.multiple_of(lax.axis_index("gy") * 8, 8)

    def window(x):
        bw[x + 1, 8:32, :] = b2[ix * 8 + 1 + x, pl.ds(row, 24), :]

    loop(0, 22, 6, window)
    ring_weights(bw, None, gw, invw, None, 22, 24, 16.0, edges=True)


COARSE_SHAPES = [
    (6, 32, 64, 128),
    (32, 64, 128),
    (32, 64, 128),
    (6, 16, 32, 128),
    (16, 32, 128),
    (6, 22, 24, 128),
    (22, 24, 128),
]


def bottom(
    same, sibling, g, inv, total, g3, inv3, gw, invw, out,
    s2, va, vb, sp, u, v3a, v3b, sp3, u3, rows, wa, wb, spw, uw,
):
    for ref in (s2, va, vb):
        clear_whole(ref)
    gather_y(same, sibling, s2)

    def scale(x):
        sp[x] = s2[x + 8, 8:72, :] * inv[x]

    loop(0, 32, 8, scale)
    v = ring_cheb(va.at[7:41], vb.at[7:41], g, sp, u, 32, 64, RECIPE, True)
    iterate = vb if SMOOTH % 2 == 0 else va

    clear_edges(v3a, 16, 32)
    clear_edges(v3b, 16, 32)
    half_z = pick(lambda r, c: r // 2 == c)

    def restrict(x2):
        parts = []
        for half in range(2):
            x = 2 * x2 + half
            _, rest = ring_rest(v, g, sp, x, 64)
            parts.append(rest * total[x])
        rows[x2] = (parts[0] + parts[1]) * (0.0625 * 0.5 / 8.0)

    loop(0, 16, 16, restrict)

    def compress(x2):
        res = rows[x2, pl.ds(0, 32, stride=2), :] + rows[x2, pl.ds(1, 32, stride=2), :]
        sp3[x2] = dot(res, half_z) * inv3[x2]

    loop(0, 16, 9, compress)
    c3 = ring_cheb(v3a, v3b, g3, sp3, u3, 16, 32, BOTTOM_RECIPE, True)

    other = va if iterate is vb else vb
    double_z = pick(lambda r, c: c // 2 == r)

    def prolong(x3):
        wide = dot(c3[x3 + 1, 8:40, :], double_z)
        rows[x3, pl.ds(0, 32, stride=2), :] = wide
        rows[x3, pl.ds(1, 32, stride=2), :] = wide
        for half in range(2):
            x = 8 + 2 * x3 + half
            other[x, 8:72, :] = iterate[x, 8:72, :] + rows[x3]

    loop(0, 16, 18, prolong)
    ix = lax.axis_index("gx")
    iz = lax.axis_index("gz")
    clear_edges(wa, 22, 24)
    clear_edges(wb, 22, 24)
    row = pl.multiple_of(lax.axis_index("gy") * 8, 8)

    def window(x):
        plane = ix * 8 + 1 + x
        wa[x + 1, 8:32, :] = other[plane, pl.ds(row, 24), :]
        spw[x] = s2[plane, pl.ds(row, 24), :] * invw[x]

    loop(0, 22, 6, window)
    c2 = ring_cheb(wa, wb, gw, spw, uw, 22, 24, RECIPE, False, trim=1)
    shift = (128 - iz * 32) % 128
    for x in range(18):
        out[x] = roll(c2[x + 3, 8:32, :], shift)


COARSE_SCRATCH = [
    vm(48, 80, 128),
    vm(18, 48, 128),
    vm(24, 40, 128),
    vm(16, 64, 128),
]
BOTTOM_SCRATCH = [
    vm(48, 80, 128),
    vm(48, 80, 128),
    vm(48, 80, 128),
    vm(32, 64, 128),
    vm(32, 64, 128),
    vm(18, 48, 128),
    vm(18, 48, 128),
    vm(16, 32, 128),
    vm(16, 32, 128),
    vm(16, 64, 128),
    vm(24, 40, 128),
    vm(24, 40, 128),
    vm(22, 24, 128),
    vm(22, 24, 128),
]


def level1_up(c2, g, sp, beta, iterate, out, va, vb, u, wide, rows):
    for ref in (va, vb):
        clear_edges(ref, 36, 40)
    spread = pick(lambda r, c: ((c < 74) & (c // 2 == r)) | ((c >= 118) & (c // 2 + 64 == r)))
    for x2 in range(18):
        rows[x2, 32:40, :] = jnp.zeros((8, 128), F32)

    def prolong(x2):
        wide[x2] = dot(c2[x2], spread)
        part = wide[x2, 3:21, :]
        rows[x2, pl.ds(0, 18, stride=2), :] = part
        rows[x2, pl.ds(1, 18, stride=2), :] = part
        for half in range(2):
            x = 2 * x2 + half
            va[x + 1, 8:48, :] = jnp.where(beta[x] > 0.0, iterate[x + 1, 8:48, :] + rows[x2], 0.0)

    loop(0, 18, 12, prolong)
    v = ring_cheb(va, vb, g, sp, u, 36, 40, RECIPE, False, trim=5)
    out[...] = v[7:31, 14:38, :]


def level0_up(
    c1, beta, g_main, g_strip, sp, sp_t, beta_t, iterate, iterate_t, out,
    va, vb, ta, tb, ghost, u, u_t, rows,
):
    for ref in (va, vb):
        clear_edges(ref, 48, 48)
    for ref in (ta, tb):
        clear_strip(ref)
    spread = pick(lambda r, c: c // 2 == r)

    def prolong(x1):
        wide = dot(c1[x1], spread)
        rows[x1, pl.ds(0, 24, stride=2), :] = wide
        rows[x1, pl.ds(1, 24, stride=2), :] = wide
        for half in range(2):
            x = 2 * x1 + half
            va[x + 1, 8:56, :] = jnp.where(beta[x] > 0.0, iterate[x + 1, 8:56, :] + rows[x1], 0.0)

    loop(0, 24, 12, prolong)

    def prolong_strip(m):
        acc = jnp.zeros((24, 128), F32)
        for k in range(8):
            to = pick(
                lambda r, c: (c // 16 == k)
                & (
                    ((c % 16 < 8) & (r == 64 + (7 - c % 16) // 2))
                    | ((c % 16 >= 8) & (r == 124 + (15 - c % 16) // 2))
                )
            )
            acc = acc + dot(c1[k * 3 + m], to)
        rows[m, pl.ds(0, 24, stride=2), :] = acc
        rows[m, pl.ds(1, 24, stride=2), :] = acc
        for half in range(2):
            xx = 2 * m + half
            ta[xx, 8:56, :] = jnp.where(beta_t[xx] > 0.0, iterate_t[xx, 8:56, :] + rows[m], 0.0)

    loop(0, 3, 36, prolong_strip)
    for x in [*range(6), *range(42, 48)]:
        vb[x + 1, 8:56, :] = jnp.zeros((48, 128), F32)
    bufs = [(va, ta), (vb, tb)]
    for k in range(SMOOTH):
        (v, t), (w, s) = bufs
        retain, factor = RECIPE[k]
        if k == 0:
            retain = None
        if k < SMOOTH - 1:
            low, high = 5 + k, 43 - k
            level0_step(
                v, t, w, s, ghost, g_main, g_strip, sp, sp_t, u, u_t, low, high, retain, factor
            )
        else:

            def last(x):
                here, rest = block_rest(v, t, g_main, sp, x, 8)
                out[x - 8] = here + retain * u[x, 8:40] + factor * rest

            loop(8, 40, 4, last)
        bufs = [(w, s), (v, t)]


def ring(value, axis, step):
    count = lax.axis_size(axis)
    return lax.ppermute(value, axis, [(i, (i + step) % count) for i in range(count)])


def trade(lo, hi, axis):
    return ring(hi, axis, 1), ring(lo, axis, -1)


def gather(kernel, parts, after, *shape):
    return call(kernel, sds(*shape), name=kernel.__name__, last_unread=len(parts) + 1)(*parts, after)


def around(value, axis):
    return [value] + [ring(value, axis, step) for step in range(1, lax.axis_size(axis))]


def chips(value):
    return [value] + [ring(value, "gy", 2 * step) for step in (1, 2, 3)]


def across(value):
    count = lax.axis_size("gy")
    return lax.ppermute(value, "gy", [(i, i + 1 - 2 * (i % 2)) for i in range(count)])


def per_device(source, beta):
    lo = jnp.stack([source[0:8], beta[0:8]])
    hi = jnp.stack([source[24:32], beta[24:32]])
    lo, hi, source, beta = lax.optimization_barrier((lo, hi, source, beta))
    x_lo, x_hi = trade(lo, hi, "gx")
    beta2 = call(coarse_beta, sds(16, 128), [vm(32, 128)], name="coarse_beta")(beta)
    beta2_pair = gather(pair, [beta2, ring(beta2, "gz", 1)], lo, 2, 16, 128)
    x_lo, x_hi, beta2_pair = lax.optimization_barrier((x_lo, x_hi, beta2_pair))
    slab = sds(2, 48, 8, 128)
    mid = sds(48, 32, 128)
    lo, hi, s_mid, b_mid = call(pack_y, (slab, slab, mid, mid), name="pack_y", mib=4)(
        source, beta, x_lo, x_hi
    )
    y_lo, y_hi = trade(lo, hi, "gy")
    beta2_block = gather(gather_z, [beta2_pair, ring(beta2_pair, "gz", 2)], lo, 8, 8, 128)
    y_lo, y_hi, beta2_block = lax.optimization_barrier((y_lo, y_hi, beta2_block))
    whole = sds(48, 48, 128)
    strip = sds(6, 48, 128)
    src_ext, beta_ext, lo, hi = call(
        pack_z, (whole, whole, strip, strip), name="pack_z", mib=4
    )(s_mid, b_mid, y_lo, y_hi)
    z_lo, z_hi = trade(lo, hi, "gz")
    beta2_pair = gather(pair, [beta2_block, ring(beta2_block, "gx", 1)], lo, 2, 8, 8, 128)
    z_lo, z_hi, beta2_pair = lax.optimization_barrier((z_lo, z_hi, beta2_pair))
    iter0, iter0_t, c, lo, hi, *ready = call(
        level0_down,
        (
            sds(50, 64, 128),
            sds(6, 64, 128),
            sds(16, 16, 128),
            sds(10, 16, 128),
            sds(10, 16, 128),
            sds(7, 48, 48, 128),
            sds(6, 6, 48, 128),
            whole,
            strip,
            strip,
        ),
        LEVEL0_SCRATCH,
        name="level0_down",
        mib=16,
    )(src_ext, beta_ext, z_lo, z_hi)
    x_lo, x_hi = trade(lo, hi, "gx")
    beta2_pair, _ = lax.optimization_barrier((beta2_pair, lo))
    beta2_slab = gather(gather_x, [beta2_pair, ring(beta2_pair, "gx", 2)], lo, 32, 8, 128)
    x_lo, x_hi, beta2_slab = lax.optimization_barrier((x_lo, x_hi, beta2_slab))
    lo, hi = call(pack1_y, (sds(360, 128), sds(360, 128)), name="pack1_y")(c, x_lo, x_hi)
    y_lo, y_hi = trade(lo, hi, "gy")
    beta2_pair = gather(pair, [beta2_slab, ring(beta2_slab, "gy", 2)], lo, 2, 32, 8, 128)
    y_lo, y_hi, beta2_pair = lax.optimization_barrier((y_lo, y_hi, beta2_pair))
    ext, lo, hi = call(
        pack1_z, (sds(36, 40, 128), sds(6, 40, 128), sds(6, 40, 128)), name="pack1_z"
    )(c, x_lo, x_hi, y_lo, y_hi)
    z1_lo, z1_hi = trade(lo, hi, "gz")
    beta2_pair, _ = lax.optimization_barrier((beta2_pair, lo))
    beta2_stack = gather(stack_y, [beta2_pair, ring(beta2_pair, "gy", 4)], lo, 4, 32, 8, 128)
    z1_lo, z1_hi, beta2_stack = lax.optimization_barrier((z1_lo, z1_hi, beta2_stack))
    level1 = sds(36, 40, 128)
    iter1, chunk, g1, sp1, beta1 = call(
        level1_down,
        (sds(38, 56, 128), sds(16, 128), sds(6, 36, 40, 128), level1, level1),
        LEVEL1_SCRATCH,
        name="level1_down",
        mib=8,
    )(ext, z1_lo, z1_hi)
    parts = around(chunk, "gz")
    beta2_stack, _ = lax.optimization_barrier((beta2_stack, chunk))
    *parts, beta2_other = lax.optimization_barrier((*parts, across(beta2_stack)))
    parts = around(gather(gather_z, parts, chunk, 8, 8, 128), "gx")
    slab = gather(gather_x, parts, chunk, 32, 8, 128)
    stack = gather(stack_y, chips(slab), slab, 4, 32, 8, 128)
    stack_other = across(stack)
    coarse = call(
        coarse_prepare,
        tuple(sds(*shape) for shape in COARSE_SHAPES),
        COARSE_SCRATCH,
        name="coarse_prepare",
        mib=8,
    )(beta2_stack, beta2_other)
    c2 = call(bottom, sds(18, 24, 128), BOTTOM_SCRATCH, name="bottom", mib=18)(
        stack, stack_other, *coarse
    )
    c1 = call(
        level1_up,
        sds(24, 24, 128),
        [vm(38, 56, 128), vm(38, 56, 128), vm(36, 40, 128), vm(18, 24, 128), vm(18, 40, 128)],
        name="level1_up",
        mib=8,
    )(c2, g1, sp1, beta1, iter1)
    return call(
        level0_up,
        sds(32, 32, 128),
        [vm(50, 64, 128), vm(50, 64, 128), vm(6, 64, 128), vm(6, 64, 128), vm(6, 48, 128)]
        + [vm(48, 48, 128), vm(6, 48, 128), vm(24, 48, 128)],
        name="level0_up",
        mib=14,
    )(c1, beta_ext, *ready, iter0, iter0_t)


def solution(mesh):
    placed = (P(*AXES), P(*AXES))
    return jax.shard_map(
        per_device, mesh=mesh, in_specs=placed, out_specs=P(*AXES), check_vma=False
    )
```
